32 devices in a mesh: cp: 16 (over z, y, core), hd: 2 (over x).
Axes of the slice: x: 2, y: 2, z: 4, core: 2. Of those that a mesh axis runs over, the one named last changes fastest.
Arguments:
- tokens: bfloat16 [8192, 768], P(('cp', 'hd')), may hold values from -6 to 6
- qkv_weight: bfloat16 [768, 2304], P(('cp', 'hd')), may hold values from -0.21875 to 0.21875
- out_weight: bfloat16 [768, 768], P(('cp', 'hd')), may hold values from -3 to 3
- gate_weight: bfloat16 [768, 3072], P(('cp', 'hd')), may hold values from -0.21875 to 0.21875
- up_weight: bfloat16 [768, 3072], P(('cp', 'hd')), may hold values from -0.21875 to 0.21875
- down_weight: bfloat16 [3072, 768], P(('cp', 'hd')), may hold values from -0.109375 to 0.109375
- first_gain: bfloat16 [768], P(('cp', 'hd')), may hold values from 0.5 to 1.5
- first_bias: bfloat16 [768], P(('cp', 'hd')), may hold values from -3 to 3
- second_gain: bfloat16 [768], P(('cp', 'hd')), may hold values from 0.5 to 1.5
- second_bias: bfloat16 [768], P(('cp', 'hd')), may hold values from -3 to 3
- doc_lengths: int32 [8], replicated, may hold values from 1 to 4096, 8192 in all
- cotangent: bfloat16 [8192, 768], P(('cp', 'hd')), may hold values from -6 to 6
Outputs:
- layer_out: bfloat16 [8192, 768], P(('cp', 'hd'))
- tokens_grad: bfloat16 [8192, 768], P(('cp', 'hd'))
- qkv_grad: float32 [768, 2304], P(('cp', 'hd'))
- out_grad: float32 [768, 768], P(('cp', 'hd'))
- gate_grad: float32 [768, 3072], P(('cp', 'hd'))
- up_grad: float32 [768, 3072], P(('cp', 'hd'))
- down_grad: float32 [3072, 768], P(('cp', 'hd'))
- first_gain_grad: float32 [768], P(('cp', 'hd'))
- first_bias_grad: float32 [768], P(('cp', 'hd'))
- second_gain_grad: float32 [768], P(('cp', 'hd'))
- second_bias_grad: float32 [768], P(('cp', 'hd'))
The draws below stay inside these ranges and needn't reach their ends.
Inputs may be any that keep to these rules, and one draw needn't show every extreme that they name: `doc_lengths`: the lengths of the documents packed in order; they sum to 8192, and the longest is exactly 4096.
All inputs are finite; a program needn't handle non-finite values.
Results may differ from the reference program's by a relative error of at most 0.018.
The reference program's roundings to bfloat16 on the way count: a program that leaves them out, or rounds other values in their place, can miss the bound.
Values may be sent and summed in bfloat16 or wider, within the bound.
A program may use at most 320 MiB of HBM per device.

```python
import math
import jax
import jax.numpy as jnp
import numpy as np
from jax import lax

D = 768
H = 12
HD = 64
FF = 3072
TOK_DEV = 256
REACH = 8
TOKENS = 8192
MAXDOC = 4096
NDOCS = 8
N_CP = 16
N_HD = 2


def level_of(key, extent, shards, low, high):
    loudness, own = 1.0, jax.random.fold_in(key, 6)
    for dim, blocks in shards:
        heights = jnp.exp(jax.random.uniform(jax.random.fold_in(own, dim), (blocks,), jnp.float32, low / len(shards), high / len(shards)))
        loudness = loudness * jnp.repeat(heights, extent[dim] // blocks).reshape([-1 if axis == dim else 1 for axis in range(len(extent))])
    return loudness


def split_up(count, total, limit, lean):
    weights = [(1 << 20) // math.isqrt(rank ** lean) + 1 for rank in range(2, count + 1)]
    surplus, counts = total - limit - (count - 1), [1] * (count - 1)
    while surplus > 0:
        candidates = [i for i in range(count - 1) if counts[i] < limit]
        whole, budget = sum([weights[i] for i in candidates]), surplus
        for i in candidates:
            more = min(limit - counts[i], max(1, budget * weights[i] // whole), surplus)
            counts[i] = counts[i] + more
            surplus = surplus - more
    return np.array([limit] + counts)


def uneven(own_key, number_of, total, bound, lean):
    if number_of == 2:
        one = jax.random.randint(own_key, (), max(1, total - bound), min(bound, total - 1) + 1)
        return jnp.stack([one, total - one])
    sizes = jnp.asarray(split_up(number_of, total, bound, lean), jnp.int32)
    couples = (number_of - 1) // 2
    giver, taker = sizes[1:1 + 2 * couples:2], sizes[2:2 + 2 * couples:2]
    room = jnp.minimum(giver - 1, bound - taker)
    shifted = jax.random.randint(jax.random.fold_in(own_key, 1), (couples,), 0, 1 << 20) % (room + 1)
    sizes = sizes.at[1:1 + 2 * couples:2].set(giver - shifted).at[2:2 + 2 * couples:2].set(taker + shifted)
    return sizes[jax.random.permutation(jax.random.fold_in(own_key, 2), number_of)]


def centred(own_key, dims, width, limit, split=(), held_as=jnp.bfloat16):
    array = jax.random.normal(own_key, dims, jnp.float32) * width
    if len(split) > 0:
        array = level_of(own_key, dims, split, -0.22, 0.18) * array
    return jnp.clip(array, min=-limit, max=limit).astype(held_as)


def setup_inputs(seed: int = 0) -> dict:
    streams_of = jax.random.split(jax.random.key(seed), 13)
    tokens = centred(streams_of[0], (TOKENS, D), 1.0, 6.0, ((0, 32),))
    qkv_weight = centred(streams_of[1], (D, 3 * D), D ** -0.5, 0.21875, ((0, 32),))
    out_weight = centred(streams_of[2], (D, D), 4 ** -0.5, 3.0, ((0, 32),))
    gate_weight = centred(streams_of[3], (D, FF), D ** -0.5, 0.21875, ((0, 32),))
    up_weight = centred(streams_of[4], (D, FF), D ** -0.5, 0.21875, ((0, 32),))
    down_weight = centred(streams_of[5], (FF, D), FF ** -0.5, 0.109375, ((0, 32),))
    first_gain = jnp.clip(1.0 + 0.1 * jax.random.normal(streams_of[6], (D,), jnp.float32), 0.5, 1.5).astype(jnp.bfloat16)
    first_bias = centred(streams_of[7], (D,), 0.5, 3.0, ((0, 32),))
    second_gain = jnp.clip(1.0 + 0.1 * jax.random.normal(streams_of[8], (D,), jnp.float32), 0.5, 1.5).astype(jnp.bfloat16)
    second_bias = centred(streams_of[9], (D,), 0.5, 3.0, ((0, 32),))
    doc_lengths = uneven(streams_of[10], NDOCS, TOKENS, MAXDOC, 2).astype(jnp.int32)
    cotangent = centred(streams_of[11], (TOKENS, D), 1.0, 6.0, ((0, 32),))
    return dict(tokens=tokens, qkv_weight=qkv_weight, out_weight=out_weight, gate_weight=gate_weight, up_weight=up_weight, down_weight=down_weight, first_gain=first_gain, first_bias=first_bias, second_gain=second_gain, second_bias=second_bias, doc_lengths=doc_lengths, cotangent=cotangent)


@jax.custom_vjp
def low(v):
    return lax.optimization_barrier(v.astype(jnp.bfloat16)).astype(jnp.float32)

@jax.custom_vjp
def low_back(v):
    return v

def low_keep(v):
    return (low(v), None)

def low_pass(kept, grad):
    return (grad,)

def back_keep(v):
    return (v, None)

def back_low(kept, grad):
    return (low(grad),)
low.defvjp(low_keep, low_pass)
low_back.defvjp(back_keep, back_low)
rope_base = 1000.0
norm_eps = 1e-12
score_scale = 0.125
masked_score = -1000000000.0

def doc_layout(lengths, first_row, row_count):
    starts = (jnp.cumsum(lengths) - lengths).astype(jnp.int32)
    position = (first_row + jnp.arange(row_count, dtype=jnp.int32)).astype(jnp.int32)
    at_or_after = position[:, None] >= starts[None, :]
    doc_ids = (lax.optimization_barrier(jnp.sum(at_or_after.astype(jnp.int32), axis=1)) - 1).astype(jnp.int32)
    doc_begin = lax.optimization_barrier(jnp.max(jnp.where(at_or_after, starts[None, :], 0), axis=1)).astype(jnp.int32)
    return (doc_ids, (position - doc_begin).astype(jnp.int32))

def rope_tables(offsets, head_size):
    half_size = head_size // 2
    frequency = rope_base ** (-(jnp.arange(half_size, dtype=jnp.float32) * 2.0) / head_size)
    angles = offsets.astype(jnp.float32)[:, None] * frequency[None, :]
    return (jnp.cos(angles), jnp.sin(angles))

def rotate(values, cosine, sine):
    half_size = values.shape[-1] // 2
    first_half = values[..., :half_size]
    second_half = values[..., half_size:]
    cos_rows = cosine[:, None, :]
    sin_rows = sine[:, None, :]
    return jnp.concatenate([first_half * cos_rows - second_half * sin_rows, second_half * cos_rows + first_half * sin_rows], axis=-1)

def normalize(hidden_in, gain_vec, bias_vec):
    average = lax.optimization_barrier(jnp.mean(hidden_in, axis=-1, keepdims=True))
    centered = hidden_in - average
    variance = lax.optimization_barrier(jnp.mean(centered * centered, axis=-1, keepdims=True))
    return centered * lax.rsqrt(variance + norm_eps) * gain_vec + bias_vec

def matmul(left, right):
    return jnp.dot(left, right, precision=lax.Precision.HIGHEST)

def reference(tokens, qkv_weight, out_weight, gate_weight, up_weight, down_weight, first_gain, first_bias, second_gain, second_bias, doc_lengths, cotangent):
    block_rows = TOK_DEV * N_HD
    all_rows = block_rows * N_CP
    margin = REACH * block_rows
    window = (2 * REACH + 1) * block_rows
    model_width = H * HD
    lengths = doc_lengths.astype(jnp.int32)
    doc_ids, offsets = doc_layout(lengths, jnp.int32(0), all_rows)
    cosine, sine = rope_tables(offsets, HD)
    edge_docs = jnp.full((margin,), -2, jnp.int32)
    padded_docs = jnp.concatenate([edge_docs, doc_ids, edge_docs]).astype(jnp.int32)

    def attention(queries, key_rows, value_rows):
        key_pad = jnp.pad(key_rows, ((margin, margin), (0, 0), (0, 0)))
        value_pad = jnp.pad(value_rows, ((margin, margin), (0, 0), (0, 0)))

        def one_block(block_index):
            start = (block_index * block_rows).astype(jnp.int32)
            query_block = lax.dynamic_slice_in_dim(queries, start, block_rows, 0)
            key_block = lax.dynamic_slice_in_dim(key_pad, start, window, 0)
            value_block = lax.dynamic_slice_in_dim(value_pad, start, window, 0)
            query_docs = lax.dynamic_slice_in_dim(doc_ids, start, block_rows, 0)
            key_docs = lax.dynamic_slice_in_dim(padded_docs, start, window, 0)
            scores = jnp.einsum('qhd,khd->hqk', query_block, key_block, precision=lax.Precision.HIGHEST) * score_scale
            same_doc = (query_docs[:, None] == key_docs[None, :])[None]
            scores = low_back(jnp.where(same_doc, scores, masked_score))
            weights = low(jax.nn.softmax(scores, axis=-1))
            return jnp.einsum('hqk,khd->qhd', weights, value_block, precision=lax.Precision.HIGHEST)
        blocks = lax.map(jax.checkpoint(one_block), jnp.arange(N_CP, dtype=jnp.int32))
        return blocks.reshape(all_rows, H, HD)

    def forward(x_rows, w_qkv, w_out, w_gate, w_up, w_down, gain_one, bias_one, gain_two, bias_two):
        raw = low_back(low(matmul(x_rows, w_qkv)))
        queries = low(rotate(raw[:, :model_width].reshape(all_rows, H, HD), cosine, sine))
        key_rows = low(rotate(raw[:, model_width:2 * model_width].reshape(all_rows, H, HD), cosine, sine))
        value_rows = raw[:, 2 * model_width:].reshape(all_rows, H, HD)
        attended = low_back(low(attention(queries, key_rows, value_rows).reshape(all_rows, model_width)))
        attn_out = low_back(matmul(attended, w_out))
        first = normalize(x_rows + attn_out, gain_one, bias_one)
        first_low = low(first)
        gate_proj = low_back(matmul(first_low, w_gate))
        up_proj = low_back(matmul(first_low, w_up))
        hidden = low(jax.nn.silu(gate_proj) * up_proj)
        branch = low_back(matmul(hidden, w_down))
        return normalize(first + branch, gain_two, bias_two)
    inputs = tuple((item.astype(jnp.float32) for item in (tokens, qkv_weight, out_weight, gate_weight, up_weight, down_weight, first_gain, first_bias, second_gain, second_bias)))
    result, pullback = jax.vjp(forward, *inputs)
    grads = pullback(cotangent.astype(jnp.float32))
    return (result.astype(jnp.bfloat16), grads[0].astype(jnp.bfloat16), grads[1], grads[2], grads[3], grads[4], grads[5], grads[6], grads[7], grads[8], grads[9])
```

```python
import functools

import jax
import jax.numpy as jnp
from jax import lax
from jax.experimental import pallas as pl
from jax.experimental.pallas import tpu as pltpu
from jax.sharding import PartitionSpec as P

HD = 64
REACH = 8


rope_base = 1000.0
norm_eps = 1e-12
score_scale = 0.125
masked_score = -1000000000.0


def shifted(block, axis, distance):
    devices = range(lax.axis_size(axis))
    route = [(i - distance, i) for i in devices if i - distance in devices]
    return lax.ppermute(block, axis, route)


def doc_layout(lengths, first_row, row_count):
    starts = jnp.cumsum(lengths) - lengths
    position = first_row + jnp.arange(row_count, dtype=jnp.int32)
    at_or_after = position[:, None] >= starts[None, :]
    doc_ids = jnp.sum(at_or_after.astype(jnp.int32), axis=1) - 1
    doc_begin = jnp.max(jnp.where(at_or_after, starts[None, :], 0), axis=1)
    return (doc_ids, position - doc_begin)


def rope_tables(offsets, head_size):
    half_size = head_size // 2
    frequency = rope_base ** (-(jnp.arange(half_size, dtype=jnp.float32) * 2.0) / head_size)
    angles = offsets.astype(jnp.float32)[:, None] * frequency[None, :]
    return (jnp.cos(angles), jnp.sin(angles))


def rotate(values, cosine, sine):
    half_size = values.shape[-1] // 2
    first_half = values[..., :half_size]
    second_half = values[..., half_size:]
    cos_rows = cosine[:, None, :]
    sin_rows = sine[:, None, :]
    return jnp.concatenate(
        [
            first_half * cos_rows - second_half * sin_rows,
            second_half * cos_rows + first_half * sin_rows,
        ],
        axis=-1,
    )


def rotate_back(grads, cosine, sine):
    half_size = grads.shape[-1] // 2
    first_half = grads[..., :half_size]
    second_half = grads[..., half_size:]
    cos_rows = cosine[:, None, :]
    sin_rows = sine[:, None, :]
    return jnp.concatenate(
        [
            first_half * cos_rows + second_half * sin_rows,
            second_half * cos_rows - first_half * sin_rows,
        ],
        axis=-1,
    )


def normalize(hidden_in, gain_vec, bias_vec):
    average = jnp.mean(hidden_in, axis=-1, keepdims=True)
    centered = hidden_in - average
    variance = jnp.mean(centered * centered, axis=-1, keepdims=True)
    inv_std = lax.rsqrt(variance + norm_eps)
    scaled = centered * inv_std
    return (scaled * gain_vec + bias_vec, scaled, inv_std)


def normalize_back(upstream, scaled, inv_std, gain_vec):
    weighted = upstream * gain_vec
    inner = (
        weighted
        - jnp.mean(weighted, axis=-1, keepdims=True)
        - scaled * jnp.mean(weighted * scaled, axis=-1, keepdims=True)
    )
    return (inv_std * inner, jnp.sum(upstream * scaled, axis=0), jnp.sum(upstream, axis=0))


def product(left, right):
    return jnp.dot(left, right, preferred_element_type=jnp.float32)


def local_any(
    tokens,
    qkv_weight,
    out_weight,
    gate_weight,
    up_weight,
    down_weight,
    first_gain,
    first_bias,
    second_gain,
    second_bias,
    doc_lengths,
    cotangent,
):
    rows_here = tokens.shape[0]
    model_width = tokens.shape[1]
    hd_count = lax.axis_size("hd")
    cp_count = lax.axis_size("cp")
    cp_index = lax.axis_index("cp")
    block_rows = rows_here * hd_count
    local_width = model_width // hd_count
    local_heads = local_width // HD
    shifts = [0]
    for distance in range(1, REACH + 1):
        shifts = shifts + [-distance, distance]
    shards = (
        qkv_weight,
        out_weight,
        gate_weight,
        up_weight,
        down_weight,
        first_gain,
        first_bias,
        second_gain,
        second_bias,
    )
    weights = (
        lax.all_gather(shards[0], ("cp", "hd"), axis=0, tiled=True),
        lax.all_gather(shards[1], ("cp", "hd"), axis=0, tiled=True),
        lax.all_gather(shards[2], ("cp", "hd"), axis=0, tiled=True),
        lax.all_gather(shards[3], ("cp", "hd"), axis=0, tiled=True),
        lax.all_gather(shards[4], ("cp", "hd"), axis=0, tiled=True),
        lax.all_gather(shards[5], ("cp", "hd"), axis=0, tiled=True),
        lax.all_gather(shards[6], ("cp", "hd"), axis=0, tiled=True),
        lax.all_gather(shards[7], ("cp", "hd"), axis=0, tiled=True),
        lax.all_gather(shards[8], ("cp", "hd"), axis=0, tiled=True),
    )
    (
        qkv_full,
        out_full,
        gate_full,
        up_full,
        down_full,
        gain_first,
        bias_first,
        gain_second,
        bias_second,
    ) = weights
    raw_rows = product(tokens, qkv_full).astype(jnp.bfloat16)
    grouped = lax.all_to_all(
        raw_rows.reshape(rows_here, 3, hd_count, local_width),
        "hd",
        split_axis=2,
        concat_axis=0,
        tiled=True,
    )
    grouped = grouped.reshape(block_rows, 3, local_width)
    query_docs, offsets = doc_layout(doc_lengths, cp_index * block_rows, block_rows)
    cosine, sine = rope_tables(offsets, HD)
    queries = rotate(
        grouped[:, 0].astype(jnp.float32).reshape(block_rows, local_heads, HD), cosine, sine
    ).astype(jnp.bfloat16)
    key_rows = rotate(
        grouped[:, 1].astype(jnp.float32).reshape(block_rows, local_heads, HD), cosine, sine
    ).astype(jnp.bfloat16)
    own_block = jnp.stack([key_rows.reshape(block_rows, local_width), grouped[:, 2]], axis=1)

    def key_docs(distance):
        source = cp_index - distance
        doc_ids, unused_offsets = doc_layout(doc_lengths, source * block_rows, block_rows)
        inside = jnp.logical_and(source >= 0, source < cp_count)
        return jnp.where(inside, doc_ids, -2)

    remote = [own_block] + [shifted(own_block, "cp", distance) for distance in shifts[1:]]
    masks = [query_docs[:, None] == key_docs(distance)[None, :] for distance in shifts]

    def scores_with(query_part, remote_block, key_mask):
        key_part = remote_block[:, 0].reshape(block_rows, local_heads, HD)
        raw_scores = (
            jnp.einsum("qhd,khd->hqk", query_part, key_part, preferred_element_type=jnp.float32)
            * score_scale
        )
        return jnp.where(key_mask[None], raw_scores, masked_score)

    def scores_for(remote_block, key_mask):
        return scores_with(queries, remote_block, key_mask)

    running_max = jnp.full((local_heads, block_rows), masked_score, jnp.float32)
    running_sum = jnp.zeros((local_heads, block_rows), jnp.float32)
    for remote_block, key_mask in zip(remote, masks):
        block_scores = scores_for(remote_block, key_mask)
        new_max = jnp.maximum(running_max, jnp.max(block_scores, axis=-1))
        running_sum = running_sum * jnp.exp(running_max - new_max) + jnp.sum(
            jnp.exp(block_scores - new_max[:, :, None]), axis=-1
        )
        running_max = new_max
    log_total = running_max + jnp.log(running_sum)
    attended = jnp.zeros((block_rows, local_heads, HD), jnp.float32)
    for remote_block, key_mask in zip(remote, masks):
        block_scores = scores_for(remote_block, key_mask)
        probs = jnp.exp(block_scores - log_total[:, :, None]).astype(jnp.bfloat16)
        value_part = remote_block[:, 1].reshape(block_rows, local_heads, HD)
        attended = attended + jnp.einsum(
            "hqk,khd->qhd", probs, value_part, preferred_element_type=jnp.float32
        )
    attended_send = attended.reshape(block_rows, 1, local_width).astype(jnp.bfloat16)
    attended_low = lax.all_to_all(
        attended_send, "hd", split_axis=0, concat_axis=1, tiled=True
    ).reshape(rows_here, model_width)
    gain_one = gain_first.astype(jnp.float32)
    gain_two = gain_second.astype(jnp.float32)
    attn_out = product(attended_low, out_full)
    first, scaled_one, inv_one = normalize(
        tokens.astype(jnp.float32) + attn_out, gain_one, bias_first.astype(jnp.float32)
    )
    first_low = first.astype(jnp.bfloat16)
    gate_proj = product(first_low, gate_full)
    up_proj = product(first_low, up_full)
    sigmoid_gate = jax.nn.sigmoid(gate_proj)
    silu_gate = gate_proj * sigmoid_gate
    hidden = (silu_gate * up_proj).astype(jnp.bfloat16)
    branch = product(hidden, down_full)
    second, scaled_two, inv_two = normalize(
        first + branch, gain_two, bias_second.astype(jnp.float32)
    )
    layer_out = second.astype(jnp.bfloat16)
    weights = (
        lax.all_gather(shards[0], ("cp", "hd"), axis=0, tiled=True),
        lax.all_gather(shards[1], ("cp", "hd"), axis=0, tiled=True),
        lax.all_gather(shards[2], ("cp", "hd"), axis=0, tiled=True),
        lax.all_gather(shards[3], ("cp", "hd"), axis=0, tiled=True),
        lax.all_gather(shards[4], ("cp", "hd"), axis=0, tiled=True),
        lax.all_gather(shards[5], ("cp", "hd"), axis=0, tiled=True),
        lax.all_gather(shards[6], ("cp", "hd"), axis=0, tiled=True),
        lax.all_gather(shards[7], ("cp", "hd"), axis=0, tiled=True),
        lax.all_gather(shards[8], ("cp", "hd"), axis=0, tiled=True),
    )
    (
        qkv_full,
        out_full,
        gate_full,
        up_full,
        down_full,
        gain_first,
        bias_first,
        gain_second,
        bias_second,
    ) = weights
    upstream = cotangent.astype(jnp.float32)
    dz_two, gain_two_grad, bias_two_grad = normalize_back(upstream, scaled_two, inv_two, gain_two)
    dz_two_low = dz_two.astype(jnp.bfloat16)
    down_sum = product(hidden.T, dz_two_low)
    hidden_grad = product(dz_two_low, down_full.T)
    gate_back = (
        hidden_grad * up_proj * sigmoid_gate * (1.0 + gate_proj * (1.0 - sigmoid_gate))
    ).astype(jnp.bfloat16)
    up_back = (hidden_grad * silu_gate).astype(jnp.bfloat16)
    gate_sum = product(first_low.T, gate_back)
    up_sum = product(first_low.T, up_back)
    first_back = dz_two + product(gate_back, gate_full.T) + product(up_back, up_full.T)
    dz_one, gain_one_grad, bias_one_grad = normalize_back(first_back, scaled_one, inv_one, gain_one)
    dz_one_low = dz_one.astype(jnp.bfloat16)
    out_sum = product(attended_low.T, dz_one_low)
    attended_back = product(dz_one_low, out_full.T).astype(jnp.bfloat16)
    heads_back = lax.all_to_all(
        attended_back.reshape(rows_here, hd_count, local_width),
        "hd",
        split_axis=1,
        concat_axis=0,
        tiled=True,
    )
    heads_back = heads_back.reshape(block_rows, local_heads, HD)
    delta = jnp.transpose(jnp.sum(heads_back.astype(jnp.float32) * attended, axis=-1))
    query_grad = jnp.zeros((block_rows, local_heads, HD), jnp.float32)
    pair_total = jnp.zeros((block_rows, 2, local_width), jnp.float32)
    remote = [own_block] + [shifted(own_block, "cp", distance) for distance in shifts[1:]]
    for distance, remote_block, key_mask in zip(shifts, remote, masks):
        pair_block_scores = scores_with(queries, remote_block, key_mask)
        pair_probs = jnp.exp(pair_block_scores - log_total[:, :, None])
        pair_key_part = remote_block[:, 0].reshape(block_rows, local_heads, HD)
        pair_value_part = remote_block[:, 1].reshape(block_rows, local_heads, HD)
        value_grad = jnp.einsum(
            "hqk,qhd->khd",
            pair_probs.astype(jnp.bfloat16),
            heads_back,
            preferred_element_type=jnp.float32,
        )
        prob_grad = jnp.einsum(
            "qhd,khd->hqk", heads_back, pair_value_part, preferred_element_type=jnp.float32
        )
        score_grad = (pair_probs * (prob_grad - delta[:, :, None])).astype(jnp.bfloat16)
        query_term = (
            jnp.einsum(
                "hqk,khd->qhd", score_grad, pair_key_part, preferred_element_type=jnp.float32
            )
            * score_scale
        )
        key_grad = (
            jnp.einsum("hqk,qhd->khd", score_grad, queries, preferred_element_type=jnp.float32)
            * score_scale
        )
        grad_pair = jnp.stack(
            [
                key_grad.reshape(block_rows, local_width),
                value_grad.reshape(block_rows, local_width),
            ],
            axis=1,
        )
        query_term, grad_pair = (query_term, grad_pair)
        query_grad = query_grad + query_term
        if distance == 0:
            pair_total = grad_pair
        else:
            pair_total = pair_total + shifted(
                grad_pair.astype(jnp.bfloat16), "cp", -distance
            ).astype(grad_pair.dtype)
    query_back = rotate_back(query_grad, cosine, sine).reshape(block_rows, local_width)
    key_back = rotate_back(
        pair_total[:, 0].reshape(block_rows, local_heads, HD), cosine, sine
    ).reshape(block_rows, local_width)
    raw_back = jnp.stack([query_back, key_back, pair_total[:, 1]], axis=1).astype(jnp.bfloat16)
    raw_back = lax.all_to_all(
        raw_back.reshape(block_rows, 3, 1, local_width),
        "hd",
        split_axis=0,
        concat_axis=2,
        tiled=True,
    )
    raw_back = raw_back.reshape(rows_here, 3 * model_width)
    qkv_sum = product(tokens.T, raw_back)
    tokens_grad = (dz_one + product(raw_back, qkv_full.T)).astype(jnp.bfloat16)
    summed = (
        lax.psum_scatter(qkv_sum, ("cp", "hd"), scatter_dimension=0, tiled=True),
        lax.psum_scatter(out_sum, ("cp", "hd"), scatter_dimension=0, tiled=True),
        lax.psum_scatter(gate_sum, ("cp", "hd"), scatter_dimension=0, tiled=True),
        lax.psum_scatter(up_sum, ("cp", "hd"), scatter_dimension=0, tiled=True),
        lax.psum_scatter(down_sum, ("cp", "hd"), scatter_dimension=0, tiled=True),
        lax.psum_scatter(gain_one_grad, ("cp", "hd"), scatter_dimension=0, tiled=True),
        lax.psum_scatter(bias_one_grad, ("cp", "hd"), scatter_dimension=0, tiled=True),
        lax.psum_scatter(gain_two_grad, ("cp", "hd"), scatter_dimension=0, tiled=True),
        lax.psum_scatter(bias_two_grad, ("cp", "hd"), scatter_dimension=0, tiled=True),
    )
    return (
        layer_out,
        tokens_grad,
        summed[0],
        summed[1],
        summed[2],
        summed[3],
        summed[4],
        summed[5],
        summed[6],
        summed[7],
        summed[8],
    )


MESH = pl.DeviceIdType.MESH
ZN, YN, CN, XN = 4, 2, 2, 2
BLOCKS = ZN * YN * CN * XN


def place():
    cp = lax.axis_index("cp")
    x = lax.axis_index("hd")
    return x, lax.rem(cp // CN, YN), cp // (YN * CN), lax.rem(cp, CN)


def device(x, y, z, c):
    return ((z * YN + y) * CN + c, x)


def block(x, y, z, c):
    return ((z * YN + y) * CN + c) * XN + x


def when(cond, fn):
    if cond is None:
        fn()
    else:
        pl.when(cond)(fn)


def both(a, b):
    if a is None:
        return b
    if b is None:
        return a
    return jnp.logical_and(a, b)


def halves(ref):
    rows, cols = ref.shape[-2:]
    if rows % 32 == 0:
        return ref.at[pl.ds(0, rows // 2)], ref.at[pl.ds(rows // 2, rows // 2)]
    if cols % 256 == 0:
        return ref.at[:, pl.ds(0, cols // 2)], ref.at[:, pl.ds(cols // 2, cols // 2)]
    return ref, None


def greet(x, y, z, c, far):
    barrier = pltpu.get_barrier_semaphore()
    for peer in (device(1 - x, y, z, c), device(x, 1 - y, z, c), device(x, y, z, 1 - c)):
        pl.semaphore_signal(barrier, inc=1, device_id=peer, device_id_type=MESH)
    count = 3
    if far:
        for k in range(1, ZN):
            peer = device(x, y, lax.rem(z + k, ZN), c)
            pl.semaphore_signal(barrier, inc=1, device_id=peer, device_id_type=MESH)
        count = count + ZN - 1
    else:
        pl.when(z > 0)(lambda: pl.semaphore_signal(barrier, inc=1, device_id=device(x, y, z - 1, c), device_id_type=MESH))
        pl.when(z < ZN - 1)(lambda: pl.semaphore_signal(barrier, inc=1, device_id=device(x, y, z + 1, c), device_id_type=MESH))
        count = count + (z > 0).astype(jnp.int32) + (z < ZN - 1).astype(jnp.int32)
    pl.semaphore_wait(barrier, count)


SENDS = 40
RECVS = 36


def gather_kernel(modes, *refs):
    n = len(modes)
    ins, outs, (lsem, ssem, rsem) = refs[:n], refs[n : 2 * n], refs[2 * n :]
    x, y, z, c = place()
    ox, oy, oc = 1 - x, 1 - y, 1 - c
    greet(x, y, z, c, any(m != "bcast" for m in modes))
    sent = []

    def copy(k, src, dst, s, r, peer):
        return pltpu.make_async_remote_copy(
            src_ref=src,
            dst_ref=dst,
            send_sem=ssem.at[k, s],
            recv_sem=rsem.at[k, r],
            device_id=peer,
            device_id_type=MESH,
        )

    def send(cond, *args):
        when(cond, lambda: copy(*args).start())
        sent.append((cond, args))

    def arrived(cond, k, ref, r):
        when(cond, lambda: copy(k, ref, ref, 0, r, device(ox, y, z, c)).wait_recv())

    for k, mode in enumerate(modes):
        if mode == "bcast":
            mine, spot = ins[k], outs[k].at[block(x, y, z, c)]
        elif mode == "swap":
            mine, spot = ins[k].at[z], outs[k].at[z]
        else:
            mine, spot = ins[k].at[z], outs[k].at[block(x, y, z, c)]
        pltpu.make_async_copy(mine, spot, lsem.at[k]).start()

    def spread(k, cond, b, src, up, down):
        here = outs[k].at[block(x, y, b, c)]
        if modes[k] == "bcast":
            if up is not False:
                send(both(cond, up), k, src, here, b, b, device(x, y, lax.rem(z + 1, ZN), c))
            if down is not False:
                send(both(cond, down), k, src, here, 4 + b, b, device(x, y, lax.rem(z + ZN - 1, ZN), c))
        send(cond, k, src, here, 8 + b, 4 + b, device(ox, y, z, c))
        send(cond, k, src, here, 16 + b, 12 + b, device(x, oy, z, c))
        send(cond, k, src, here, 24 + b, 20 + b, device(x, y, z, oc))

    def sides(k, cond, b):
        fx = outs[k].at[block(ox, y, b, c)]
        fy = outs[k].at[block(x, oy, b, c)]
        arrived(cond, k, fx, 4 + b)
        first, _ = halves(fx)
        send(cond, k, first, first, 20 + b, 16 + b, device(x, oy, z, c))
        send(cond, k, fx, fx, 28 + b, 24 + b, device(x, y, z, oc))
        arrived(cond, k, fy, 12 + b)
        _, second = halves(fy)
        if second is not None:
            send(cond, k, second, second, 12 + b, 8 + b, device(ox, y, z, c))
        send(cond, k, fy, fy, 32 + b, 28 + b, device(x, y, z, oc))

    def corner(k, cond, b):
        far = outs[k].at[block(ox, oy, b, c)]
        first, second = halves(far)
        arrived(cond, k, first, 16 + b)
        if second is not None:
            arrived(cond, k, second, 8 + b)
        send(cond, k, far, far, 36 + b, 32 + b, device(x, y, z, oc))

    def steps(distance):
        if distance == 0:
            return [(None, z)]
        return [(z >= distance, jnp.maximum(z - distance, 0)), (z + distance < ZN, jnp.minimum(z + distance, ZN - 1))]

    for k, mode in enumerate(modes):
        if mode == "bcast":
            spread(k, None, z, ins[k], z < ZN - 1, z > 0)
        else:
            for d in range(1, ZN):
                to = lax.rem(z + d, ZN)
                spot = outs[k].at[z] if mode == "swap" else outs[k].at[block(x, y, z, c)]
                send(None, k, ins[k].at[to], spot, to, z, device(x, y, to, c))
            if mode == "cross":
                spread(k, None, z, ins[k].at[z], False, False)

    active = [k for k, mode in enumerate(modes) if mode != "swap"]
    for distance in range(1, ZN + 2):
        if distance < ZN:
            for side, (cond, b) in enumerate(steps(distance)):
                for k in active:
                    arrived(cond, k, outs[k].at[block(x, y, b, c)], b)
                    here = outs[k].at[block(x, y, b, c)]
                    spread(k, cond, b, here, z < ZN - 1 if side == 0 else False, z > 0 if side == 1 else False)
        if 0 <= distance - 1 < ZN:
            for cond, b in steps(distance - 1):
                for k in active:
                    sides(k, cond, b)
        if 0 <= distance - 2 < ZN:
            for cond, b in steps(distance - 2):
                for k in active:
                    corner(k, cond, b)
    for k, mode in enumerate(modes):
        if mode == "swap":
            for d in range(1, ZN):
                frm = lax.rem(z + d, ZN)
                arrived(None, k, outs[k].at[frm], frm)
            pltpu.make_async_copy(ins[k].at[z], outs[k].at[z], lsem.at[k]).wait()
        else:
            for b in range(ZN):
                for j, (px, py) in enumerate(((x, y), (ox, y), (x, oy), (ox, oy))):
                    arrived(None, k, outs[k].at[block(px, py, b, oc)], 20 + 4 * j + b)
            spot = outs[k].at[block(x, y, z, c)]
            pltpu.make_async_copy(ins[k] if mode == "bcast" else ins[k].at[z], spot, lsem.at[k]).wait()
    for cond, args in sent:
        when(cond, lambda args=args: copy(*args).wait_send())


def gather(arrays, modes, collective_id):
    shapes = []
    for a, mode in zip(arrays, modes):
        if mode == "bcast":
            shapes.append((BLOCKS,) + a.shape)
        elif mode == "swap":
            shapes.append(a.shape)
        else:
            shapes.append((BLOCKS,) + a.shape[1:])
    n = len(arrays)
    return pl.pallas_call(
        functools.partial(gather_kernel, tuple(modes)),
        out_shape=[jax.ShapeDtypeStruct(s, a.dtype) for s, a in zip(shapes, arrays)],
        in_specs=[pl.BlockSpec(memory_space=pl.ANY)] * n,
        out_specs=[pl.BlockSpec(memory_space=pl.ANY)] * n,
        scratch_shapes=[
            pltpu.SemaphoreType.DMA((n,)),
            pltpu.SemaphoreType.DMA((n, SENDS)),
            pltpu.SemaphoreType.DMA((n, RECVS)),
        ],
        compiler_params=pltpu.CompilerParams(collective_id=collective_id, has_side_effects=True),
    )(*arrays)


def chunk_of(cols):
    for size in (768, 640, 512, 384, 256, 128):
        if cols % size == 0:
            return size
    return cols


def add_up(dst, sources):
    rows, cols = dst.shape[-2:]
    size = chunk_of(cols)

    def step(i, carry):
        span = pl.ds(pl.multiple_of(i * size, size), size)
        total = sources[0][:, span].astype(jnp.float32)
        for source in sources[1:]:
            total = total + source[:, span].astype(jnp.float32)
        dst[:, span] = total.astype(dst.dtype)
        return carry

    if cols == size:
        total = sources[0][...].astype(jnp.float32)
        for source in sources[1:]:
            total = total + source[...].astype(jnp.float32)
        dst[...] = total.astype(dst.dtype)
    else:
        lax.fori_loop(0, cols // size, step, 0)


def reduce_kernel(modes, *refs):
    n = len(modes)
    ins, outs = refs[:n], refs[n : 2 * n]
    lsem, ssem, rsem = refs[2 * n : 2 * n + 3]
    scratch = refs[2 * n + 3 :]
    bufs = []
    for mode in modes:
        count = 0 if mode == "swap" else (4 if mode == "reduce" else 3)
        bufs.append(scratch[:count])
        scratch = scratch[count:]
    x, y, z, c = place()
    ox, oy, oc = 1 - x, 1 - y, 1 - c
    greet(x, y, z, c, any(m != "reduce" for m in modes))
    sent = []

    def copy(k, src, dst, s, r, peer):
        return pltpu.make_async_remote_copy(
            src_ref=src,
            dst_ref=dst,
            send_sem=ssem.at[k, s],
            recv_sem=rsem.at[k, r],
            device_id=peer,
            device_id_type=MESH,
        )

    def send(cond, *args):
        when(cond, lambda: copy(*args).start())
        sent.append((cond, args))

    def arrived(cond, k, ref, r):
        when(cond, lambda: copy(k, ref, ref, 0, r, device(ox, y, z, c)).wait_recv())

    half = z // 2
    order = [3 - 3 * half, 2 - half, 1 - z + 4 * half, z]
    quads = ((ox, oy), (ox, y), (x, oy), (x, y))
    active = [k for k, mode in enumerate(modes) if mode != "swap"]

    for i, b in enumerate(order):
        for k in active:
            acc, cor = bufs[k][:2]
            for j, (px, py) in enumerate(quads):
                send(None, k, ins[k].at[block(px, py, b, oc)], cor.at[4 * i + j], 4 * i + j, 4 * i + j, device(x, y, z, oc))
                pltpu.make_async_copy(ins[k].at[block(px, py, b, c)], acc.at[4 * i + j], lsem.at[k, 4 * i + j]).start()
    for k, mode in enumerate(modes):
        if mode == "swap":
            for d in range(1, ZN):
                to = lax.rem(z + d, ZN)
                send(None, k, ins[k].at[to], outs[k].at[z], d, z, device(x, y, to, c))
            pltpu.make_async_copy(ins[k].at[z], outs[k].at[z], lsem.at[k, 0]).start()

    def loaded(k, i, j):
        acc, cor = bufs[k][:2]
        pltpu.make_async_copy(ins[k].at[0], acc.at[4 * i + j], lsem.at[k, 4 * i + j]).wait()
        arrived(None, k, cor.at[4 * i + j], 4 * i + j)

    for i, b in enumerate(order):
        for k in active:
            acc, cor, side = bufs[k][:3]
            loaded(k, i, 0)
            add_up(acc.at[4 * i], (acc.at[4 * i], cor.at[4 * i]))
            first, second = halves(acc.at[4 * i])
            send(None, k, first, halves(side.at[i])[0], 16 + i, 16 + i, device(x, oy, z, c))
            if second is not None:
                send(None, k, second, halves(side.at[4 + i])[1], 20 + i, 20 + i, device(ox, y, z, c))
    for i, b in enumerate(order):
        for k in active:
            acc, cor, side = bufs[k][:3]
            loaded(k, i, 1)
            add_up(acc.at[4 * i + 1], (acc.at[4 * i + 1], cor.at[4 * i + 1]))
            part = halves(side.at[i])[0]
            arrived(None, k, part, 16 + i)
            mine = halves(acc.at[4 * i + 1])[0]
            add_up(mine, (mine, part))
            send(None, k, acc.at[4 * i + 1], side.at[8 + i], 24 + i, 24 + i, device(ox, y, z, c))
            loaded(k, i, 2)
            add_up(acc.at[4 * i + 2], (acc.at[4 * i + 2], cor.at[4 * i + 2]))
            part = halves(side.at[4 + i])[1]
            if part is not None:
                arrived(None, k, part, 20 + i)
                mine = halves(acc.at[4 * i + 2])[1]
                add_up(mine, (mine, part))
            send(None, k, acc.at[4 * i + 2], side.at[12 + i], 28 + i, 28 + i, device(x, oy, z, c))
    for i, b in enumerate(order):
        for k in active:
            acc, cor, side = bufs[k][:3]
            loaded(k, i, 3)
            own = acc.at[4 * i + 3]
            arrived(None, k, side.at[8 + i], 24 + i)
            arrived(None, k, side.at[12 + i], 28 + i)
            terms = (own, cor.at[4 * i + 3], side.at[8 + i], side.at[12 + i])
            if modes[k] == "cross":
                add_up(own, terms)
                if i < ZN - 1:
                    send(None, k, own, outs[k].at[z], 32 + i, 32 + z, device(x, y, b, c))
                else:
                    pltpu.make_async_copy(own, outs[k].at[z], lsem.at[k, 16]).start()
                continue
            chain = bufs[k][3]
            if i == ZN - 1:
                add_up(outs[k], terms)

                def lower(k=k, chain=chain):
                    arrived(None, k, chain.at[z], 32 + z)
                    add_up(outs[k], (outs[k], chain.at[z]))

                def upper(k=k, chain=chain):
                    arrived(None, k, chain.at[4 + z], 36 + z)
                    add_up(outs[k], (outs[k], chain.at[4 + z]))

                pl.when(z > 0)(lower)
                pl.when(z < ZN - 1)(upper)
            else:
                add_up(own, terms)
                below = both(b > z, z > 0)
                above = both(b < z, z < ZN - 1)

                def lower(k=k, chain=chain, own=own, b=b):
                    arrived(None, k, chain.at[b], 32 + b)
                    add_up(own, (own, chain.at[b]))

                def upper(k=k, chain=chain, own=own, b=b):
                    arrived(None, k, chain.at[4 + b], 36 + b)
                    add_up(own, (own, chain.at[4 + b]))

                pl.when(below)(lower)
                pl.when(above)(upper)
                send(b > z, k, own, chain.at[b], 32 + i, 32 + b, device(x, y, lax.rem(z + 1, ZN), c))
                send(b < z, k, own, chain.at[4 + b], 32 + i, 36 + b, device(x, y, lax.rem(z + ZN - 1, ZN), c))
    for k, mode in enumerate(modes):
        if mode == "reduce":
            continue
        for d in range(1, ZN):
            frm = lax.rem(z + d, ZN)
            arrived(None, k, outs[k].at[frm], frm if mode == "swap" else 32 + frm)
        if mode == "swap":
            pltpu.make_async_copy(ins[k].at[z], outs[k].at[z], lsem.at[k, 0]).wait()
        else:
            pltpu.make_async_copy(bufs[k][0].at[15], outs[k].at[z], lsem.at[k, 16]).wait()
    for cond, args in sent:
        when(cond, lambda args=args: copy(*args).wait_send())


def reduce(arrays, modes, collective_id):
    shapes, specs, scratch = [], [], []
    for a, mode in zip(arrays, modes):
        if mode == "swap":
            shapes.append(jax.ShapeDtypeStruct(a.shape, a.dtype))
            specs.append(pl.BlockSpec(memory_space=pl.ANY))
            continue
        rows, cols = a.shape[1:]
        scratch = scratch + [pltpu.VMEM((16, rows, cols), a.dtype)] * 3
        if mode == "cross":
            shapes.append(jax.ShapeDtypeStruct((ZN, rows, cols), a.dtype))
            specs.append(pl.BlockSpec(memory_space=pl.ANY))
        else:
            scratch = scratch + [pltpu.VMEM((8, rows, cols), a.dtype)]
            shapes.append(jax.ShapeDtypeStruct((rows, cols), jnp.float32))
            specs.append(pl.BlockSpec(memory_space=pltpu.VMEM))
    n = len(arrays)
    return pl.pallas_call(
        functools.partial(reduce_kernel, tuple(modes)),
        out_shape=shapes,
        in_specs=[pl.BlockSpec(memory_space=pl.ANY)] * n,
        out_specs=specs,
        scratch_shapes=[
            pltpu.SemaphoreType.DMA((n, 17)),
            pltpu.SemaphoreType.DMA((n, SENDS)),
            pltpu.SemaphoreType.DMA((n, SENDS)),
        ]
        + scratch,
        compiler_params=pltpu.CompilerParams(
            collective_id=collective_id, has_side_effects=True, vmem_limit_bytes=67043328
        ),
    )(*arrays)


HEAD = 64
GROUP = 3
TILE = 512
FAR = 1 << 30


def doc_bounds(lengths, first, count):
    docs = lengths.shape[0]
    last = first + count - 1
    lane = first + lax.broadcasted_iota(jnp.int32, (1, count), 1)
    begin = jnp.int32(0)
    low, low_last = jnp.int32(0), jnp.int32(0)
    high, high_first = jnp.int32(FAR), jnp.int32(FAR)
    lane_low = jnp.zeros((1, count), jnp.int32)
    lane_high = jnp.full((1, count), FAR, jnp.int32)
    for j in range(docs):
        end = begin + lengths[j]
        low = jnp.where(begin <= first, begin, low)
        low_last = jnp.where(begin <= last, begin, low_last)
        high = jnp.where(end > last, jnp.minimum(high, end), high)
        high_first = jnp.where(end > first, jnp.minimum(high_first, end), high_first)
        lane_low = jnp.where(lane >= begin, begin, lane_low)
        lane_high = jnp.where(lane < end, jnp.minimum(lane_high, end), lane_high)
        begin = end
    return low, high, low_last, high_first, lane_low, lane_high


def keys_in(tile, lane_low, lane_high):
    at = tile * TILE + lax.broadcasted_iota(jnp.int32, (TILE, lane_low.shape[1]), 0)
    return jnp.logical_and(at >= lane_low, at < lane_high)


def dot(a, b):
    return jnp.dot(a, b, preferred_element_type=jnp.float32)


def pad_heads(rows, h, slots):
    part = rows[h * HEAD : (h + 1) * HEAD]
    zero = jnp.zeros_like(part)
    return jnp.concatenate([part if s == h else zero for s in slots], axis=0)


Q_SLOTS = (0, 1, 2, -1)
V_SLOTS = (-1, 2, 0, 1)


def forward_kernel(lengths, qt, kv, low_out, out, lse_out, qm, acc):
    x, y, z, c = place()
    count = qt.shape[2]

    def one_block(b, carry):
        first = block(x, y, b, c) * count
        low, high, low_last, high_first, lane_low, lane_high = doc_bounds(lengths, first, count)
        rows = qt[b] * jnp.bfloat16(0.125)
        for h in range(GROUP):
            qm[h] = pad_heads(rows, h, Q_SLOTS)
        acc[...] = jnp.zeros_like(acc)

        def tile_step(tile, stats, masked):
            span = pl.ds(pl.multiple_of(tile * TILE, TILE), TILE)
            keys = kv[span, 0:256]
            values = kv[span, 128:384].T
            mask = keys_in(tile, lane_low, lane_high) if masked else None
            fresh = []
            for h in range(GROUP):
                top, total = stats[2 * h], stats[2 * h + 1]
                scores = dot(keys, qm[h])
                if masked:
                    scores = jnp.where(mask, scores, -1e9)
                new_top = jnp.maximum(top, jnp.max(scores, axis=0, keepdims=True))
                shrink = jnp.exp(top - new_top)
                weights = jnp.exp(scores - new_top)
                total = total * shrink + jnp.sum(weights, axis=0, keepdims=True)
                at = V_SLOTS.index(h) * HEAD
                acc[h] = acc[h] * shrink + dot(values[at : at + HEAD], weights.astype(jnp.bfloat16))
                fresh = fresh + [new_top, total]
            return tuple(fresh)

        def step(tile, stats):
            inside = jnp.logical_and(tile * TILE >= low_last, (tile + 1) * TILE <= high_first)
            return lax.cond(
                inside,
                lambda s: tile_step(tile, s, False),
                lambda s: tile_step(tile, s, True),
                stats,
            )

        init = (jnp.full((1, count), -1e9, jnp.float32), jnp.zeros((1, count), jnp.float32)) * GROUP
        stats = lax.fori_loop(low // TILE, (high + TILE - 1) // TILE, step, init)
        for h in range(GROUP):
            top, total = stats[2 * h], stats[2 * h + 1]
            value = acc[h] / total
            out[b, h * HEAD : (h + 1) * HEAD] = value
            low_out[b, h * HEAD : (h + 1) * HEAD] = value.astype(low_out.dtype)
            lse_out[b, h : h + 1] = top + jnp.log(total)
        return carry

    lax.fori_loop(0, qt.shape[0], one_block, 0)


def attend(lengths, qt, kv):
    blocks, rows, count = qt.shape
    whole = pl.BlockSpec(memory_space=pltpu.VMEM)
    return pl.pallas_call(
        forward_kernel,
        out_shape=[
            jax.ShapeDtypeStruct(qt.shape, jnp.bfloat16),
            jax.ShapeDtypeStruct(qt.shape, jnp.float32),
            jax.ShapeDtypeStruct((blocks, 8, count), jnp.float32),
        ],
        in_specs=[pl.BlockSpec(memory_space=pltpu.SMEM), whole, whole],
        out_specs=[whole] * 3,
        scratch_shapes=[
            pltpu.VMEM((GROUP, 256, count), jnp.bfloat16),
            pltpu.VMEM((GROUP, HEAD, count), jnp.float32),
        ],
        compiler_params=pltpu.CompilerParams(vmem_limit_bytes=67043328),
    )(lengths, qt, kv)


def backward_kernel(lengths, qt, kv, out, lse, dot_in, cosine, sine, dq_out, dkv_out, qmt, qm, dmt, dm, dq, acc):
    x, y, z, c = place()
    count = qt.shape[2]
    tiles = kv.shape[0] // TILE

    def clear(tile, carry):
        acc[pl.ds(pl.multiple_of(tile * TILE, TILE), TILE), :] = jnp.zeros((TILE, acc.shape[1]), jnp.float32)
        return carry

    lax.fori_loop(0, tiles, clear, 0)

    def one_block(b, carry):
        first = block(x, y, b, c) * count
        low, high, low_last, high_first, lane_low, lane_high = doc_bounds(lengths, first, count)
        rows = qt[b] * jnp.bfloat16(0.125)
        grads = dot_in[b]
        deltas, levels = [], []
        for h in range(GROUP):
            part = slice(h * HEAD, (h + 1) * HEAD)
            padded = pad_heads(rows, h, Q_SLOTS)
            qmt[h] = padded
            qm[h * count : (h + 1) * count] = padded.T
            padded = pad_heads(grads, h, V_SLOTS)
            dmt[h] = padded
            dm[h * count : (h + 1) * count] = padded.T
            deltas.append(jnp.sum(grads[part].astype(jnp.float32) * out[b, part], axis=0, keepdims=True))
            levels.append(lse[b, h : h + 1])
        dq[...] = jnp.zeros_like(dq)

        def tile_step(tile, masked):
            span = pl.ds(pl.multiple_of(tile * TILE, TILE), TILE)
            keys = kv[span, 0:256]
            values = kv[span, 128:384]
            turned = keys.T
            mask = keys_in(tile, lane_low, lane_high) if masked else None
            probs, slopes = [], []
            for h in range(GROUP):
                weights = jnp.exp(dot(keys, qmt[h]) - levels[h])
                if masked:
                    weights = jnp.where(mask, weights, 0.0)
                slope = (weights * (dot(values, dmt[h]) - deltas[h])).astype(jnp.bfloat16)
                dq[h] += dot(turned[h * HEAD : (h + 1) * HEAD], slope)
                probs.append(weights.astype(jnp.bfloat16))
                slopes.append(slope)
            dv = dot(jnp.concatenate(probs, axis=1), dm[...])
            dk = dot(jnp.concatenate(slopes, axis=1), qm[...])
            acc[span, 0:128] += dk[:, :128]
            acc[span, 128:256] += dk[:, 128:] + dv[:, :128]
            acc[span, 256:384] += dv[:, 128:]

        def step(tile, inner):
            inside = jnp.logical_and(tile * TILE >= low_last, (tile + 1) * TILE <= high_first)
            pl.when(inside)(lambda: tile_step(tile, False))
            pl.when(jnp.logical_not(inside))(lambda: tile_step(tile, True))
            return inner

        lax.fori_loop(low // TILE, (high + TILE - 1) // TILE, step, 0)
        cos_rows, sin_rows = cosine[b], sine[b]
        half = HEAD // 2
        for h in range(GROUP):
            w1, w2 = dq[h, :half] * 0.125, dq[h, half:] * 0.125
            at = h * HEAD
            dq_out[b, at : at + half] = (w1 * cos_rows + w2 * sin_rows).astype(dq_out.dtype)
            dq_out[b, at + half : at + HEAD] = (w2 * cos_rows - w1 * sin_rows).astype(dq_out.dtype)
        return carry

    lax.fori_loop(0, qt.shape[0], one_block, 0)

    def finish(tile, carry):
        span = pl.ds(pl.multiple_of(tile * TILE, TILE), TILE)
        dkv_out[span, :] = acc[span, :].astype(dkv_out.dtype)
        return carry

    lax.fori_loop(0, tiles, finish, 0)


def attend_back(lengths, qt, kv, out, lse, dots, cosine, sine):
    blocks, rows, count = qt.shape
    whole = pl.BlockSpec(memory_space=pltpu.VMEM)
    return pl.pallas_call(
        backward_kernel,
        out_shape=[
            jax.ShapeDtypeStruct(qt.shape, jnp.bfloat16),
            jax.ShapeDtypeStruct(kv.shape, jnp.bfloat16),
        ],
        in_specs=[pl.BlockSpec(memory_space=pltpu.SMEM)] + [whole] * 7,
        out_specs=[whole] * 2,
        scratch_shapes=[
            pltpu.VMEM((GROUP, 256, count), jnp.bfloat16),
            pltpu.VMEM((GROUP * count, 256), jnp.bfloat16),
            pltpu.VMEM((GROUP, 256, count), jnp.bfloat16),
            pltpu.VMEM((GROUP * count, 256), jnp.bfloat16),
            pltpu.VMEM((GROUP, HEAD, count), jnp.float32),
            pltpu.VMEM(kv.shape, jnp.float32),
        ],
        compiler_params=pltpu.CompilerParams(vmem_limit_bytes=67043328),
    )(lengths, qt, kv, out, lse, dots, cosine, sine)


KV_SLOTS = (0, 1, 2, 5, 3, 4)


def turn(rows, cosine, sine):
    first, second = rows[:, 0], rows[:, 1]
    return jnp.stack([first * cosine - second * sine, second * cosine + first * sine], axis=1)


def turn_back(rows, cosine, sine):
    first, second = rows[:, 0], rows[:, 1]
    return jnp.stack([first * cosine + second * sine, second * cosine - first * sine], axis=1)


def tables(lengths, first, count):
    starts = jnp.cumsum(lengths) - lengths
    position = first[:, None] + jnp.arange(count, dtype=jnp.int32)[None, :]
    begun = position[..., None] >= starts
    offsets = position - jnp.max(jnp.where(begun, starts, 0), axis=-1)
    half = HEAD // 2
    frequency = rope_base ** (-(jnp.arange(half, dtype=jnp.float32) * 2.0) / HEAD)
    angles = offsets.astype(jnp.float32)[:, None, :] * frequency[None, :, None]
    return jnp.cos(angles), jnp.sin(angles)


def contract(left, right, dims):
    return lax.dot_general(left, right, (dims, ((), ())), preferred_element_type=jnp.float32)


def local_grid(
    tokens,
    qkv_weight,
    out_weight,
    gate_weight,
    up_weight,
    down_weight,
    first_gain,
    first_bias,
    second_gain,
    second_bias,
    lengths,
    cotangent,
):
    bf16 = jnp.bfloat16
    rows, width = tokens.shape
    share = first_gain.shape[0]
    heads = width // HEAD
    half = HEAD // 2
    x, y, z, c = place()
    small = jnp.stack([first_gain, first_bias, second_gain, second_bias])
    small = jnp.pad(small, ((0, 4), (0, 128 - share)))
    hidden_width = gate_weight.shape[1]

    (qkv_blocks,) = gather([qkv_weight], ["bcast"], 1)
    qkv_full = qkv_blocks.reshape(width, 3 * width)
    turned = jnp.stack([block(x, y, b, c) for b in range(ZN)]) * rows
    cos_all, sin_all = tables(lengths, turned, rows)
    cosine = lax.dynamic_index_in_dim(cos_all, z, 0, keepdims=False)
    sine = lax.dynamic_index_in_dim(sin_all, z, 0, keepdims=False)

    raw = contract(qkv_full, tokens, ((0,), (1,))).astype(bf16)
    raw = raw.reshape(3, heads, 2, half, rows)
    queries = turn(raw[0].astype(jnp.float32), cosine, sine).astype(bf16)
    keys = turn(raw[1].astype(jnp.float32), cosine, sine).astype(bf16)
    queries = queries.reshape(ZN, GROUP * HEAD, rows)
    pairs = jnp.concatenate(
        [keys.reshape(ZN, GROUP, HEAD, rows), raw[2].reshape(ZN, GROUP, HEAD, rows)], axis=1
    )
    pairs = jnp.concatenate([pairs[:, s : s + 1] for s in KV_SLOTS], axis=1)
    pairs = jnp.swapaxes(pairs.reshape(ZN, 2 * GROUP * HEAD, rows), 1, 2)

    wide = jnp.concatenate([out_weight, gate_weight, up_weight], axis=1)
    pairs_all, queries, wide, down_full, small = gather(
        [pairs, queries, wide, down_weight, small], ["cross", "swap", "bcast", "bcast", "bcast"], 2
    )
    wide = wide.reshape(width, -1)
    out_full = wide[:, :width]
    both_full = wide[:, width:]
    down_full = down_full.reshape(hidden_width, width)
    gain_one, bias_one, gain_two, bias_two = [
        small[:, i, :share].reshape(width).astype(jnp.float32) for i in range(4)
    ]
    pairs_all = pairs_all.reshape(-1, 2 * GROUP * HEAD)
    low, attended, lse = attend(lengths, queries, pairs_all)
    (low,) = gather([low], ["swap"], 3)
    low = low.reshape(width, rows)

    attn_out = contract(low, out_full, ((0,), (0,)))
    first, scaled_one, inv_one = normalize(tokens.astype(jnp.float32) + attn_out, gain_one, bias_one)
    first_low = first.astype(bf16)
    both = product(first_low, both_full)
    gate_proj, up_proj = both[:, :hidden_width], both[:, hidden_width:]
    sigmoid_gate = jax.nn.sigmoid(gate_proj)
    silu_gate = gate_proj * sigmoid_gate
    hidden = (silu_gate * up_proj).astype(bf16)
    branch = product(hidden, down_full)
    second, scaled_two, inv_two = normalize(first + branch, gain_two, bias_two)
    layer_out = second.astype(bf16)

    upstream = cotangent.astype(jnp.float32)
    dz_two, gain_two_grad, bias_two_grad = normalize_back(upstream, scaled_two, inv_two, gain_two)
    dz_two_low = dz_two.astype(bf16)
    down_sum = contract(hidden, dz_two_low, ((0,), (0,))).astype(bf16)
    hidden_grad = contract(dz_two_low, down_full, ((1,), (1,)))
    gate_back = (
        hidden_grad * up_proj * sigmoid_gate * (1.0 + gate_proj * (1.0 - sigmoid_gate))
    ).astype(bf16)
    up_back = (hidden_grad * silu_gate).astype(bf16)
    both_back = jnp.concatenate([gate_back, up_back], axis=1)
    both_sum = contract(first_low, both_back, ((0,), (0,))).astype(bf16)
    first_back = dz_two + contract(both_back, both_full, ((1,), (1,)))
    dz_one, gain_one_grad, bias_one_grad = normalize_back(first_back, scaled_one, inv_one, gain_one)
    dz_one_low = dz_one.astype(bf16)
    out_sum = product(low, dz_one_low).astype(bf16)
    attended_back = contract(out_full, dz_one_low, ((1,), (1,))).astype(bf16)
    (attended_back,) = gather([attended_back.reshape(ZN, GROUP * HEAD, rows)], ["swap"], 4)

    query_back, pair_back = attend_back(
        lengths, queries, pairs_all, attended, lse, attended_back, cos_all, sin_all
    )
    small_sum = jnp.stack([gain_one_grad, bias_one_grad, gain_two_grad, bias_two_grad])
    small_sum = jnp.swapaxes(small_sum.reshape(4, BLOCKS, share), 0, 1)
    small_sum = jnp.pad(small_sum, ((0, 0), (0, 4), (0, 128 - share)))
    pair_back, query_back, out_grad, both_grad, down_grad, small_grad = reduce(
        [
            pair_back.reshape(BLOCKS, rows, 2 * GROUP * HEAD),
            query_back,
            out_sum.reshape(BLOCKS, share, width),
            both_sum.reshape(BLOCKS, share, 2 * hidden_width),
            down_sum.reshape(BLOCKS, -1, width),
            small_sum,
        ],
        ["cross", "swap", "reduce", "reduce", "reduce", "reduce"],
        5,
    )
    pair_back = jnp.swapaxes(pair_back, 1, 2).reshape(ZN, 2 * GROUP, HEAD, rows)
    pair_back = [pair_back[:, KV_SLOTS.index(s)] for s in range(2 * GROUP)]
    key_back = jnp.stack(pair_back[:GROUP], axis=1).reshape(heads, 2, half, rows)
    key_back = turn_back(key_back.astype(jnp.float32), cosine, sine).astype(bf16)
    value_back = jnp.stack(pair_back[GROUP:], axis=1)
    raw_back = jnp.concatenate(
        [
            query_back.reshape(width, rows),
            key_back.reshape(width, rows),
            value_back.reshape(width, rows),
        ],
        axis=0,
    )
    qkv_sum = contract(tokens, raw_back, ((0,), (1,))).astype(bf16)
    tokens_grad = (dz_one + contract(raw_back, qkv_full, ((0,), (1,)))).astype(bf16)
    (qkv_grad,) = reduce([qkv_sum.reshape(BLOCKS, share, 3 * width)], ["reduce"], 6)
    return (
        layer_out,
        tokens_grad,
        qkv_grad,
        out_grad,
        both_grad[:, :hidden_width],
        both_grad[:, hidden_width:],
        down_grad,
        small_grad[0, :share],
        small_grad[1, :share],
        small_grad[2, :share],
        small_grad[3, :share],
    )


def solution(mesh):
    rows = P(("cp", "hd"), None)
    line = P(("cp", "hd"))
    local = local_grid if (mesh.shape["cp"], mesh.shape["hd"]) == (ZN * YN * CN, XN) else local_any
    return jax.shard_map(
        local,
        mesh=mesh,
        in_specs=(rows,) * 6 + (line,) * 4 + (P(), rows),
        out_specs=(rows,) * 7 + (line,) * 4,
        check_vma=False,
    )
```

```python
import functools

import jax
import jax.numpy as jnp
from jax import lax
from jax.experimental import pallas as pl
from jax.experimental.pallas import tpu as pltpu
from jax.sharding import PartitionSpec as P

HD = 64
REACH = 8


rope_base = 1000.0
norm_eps = 1e-12
score_scale = 0.125
masked_score = -1000000000.0


def shifted(block, axis, distance):
    devices = range(lax.axis_size(axis))
    route = [(i - distance, i) for i in devices if i - distance in devices]
    return lax.ppermute(block, axis, route)


def doc_layout(lengths, first_row, row_count):
    starts = jnp.cumsum(lengths) - lengths
    position = first_row + jnp.arange(row_count, dtype=jnp.int32)
    at_or_after = position[:, None] >= starts[None, :]
    doc_ids = jnp.sum(at_or_after.astype(jnp.int32), axis=1) - 1
    doc_begin = jnp.max(jnp.where(at_or_after, starts[None, :], 0), axis=1)
    return (doc_ids, position - doc_begin)


def rope_tables(offsets, head_size):
    half_size = head_size // 2
    frequency = rope_base ** (-(jnp.arange(half_size, dtype=jnp.float32) * 2.0) / head_size)
    angles = offsets.astype(jnp.float32)[:, None] * frequency[None, :]
    return (jnp.cos(angles), jnp.sin(angles))


def rotate(values, cosine, sine):
    half_size = values.shape[-1] // 2
    first_half = values[..., :half_size]
    second_half = values[..., half_size:]
    cos_rows = cosine[:, None, :]
    sin_rows = sine[:, None, :]
    return jnp.concatenate(
        [
            first_half * cos_rows - second_half * sin_rows,
            second_half * cos_rows + first_half * sin_rows,
        ],
        axis=-1,
    )


def rotate_back(grads, cosine, sine):
    half_size = grads.shape[-1] // 2
    first_half = grads[..., :half_size]
    second_half = grads[..., half_size:]
    cos_rows = cosine[:, None, :]
    sin_rows = sine[:, None, :]
    return jnp.concatenate(
        [
            first_half * cos_rows + second_half * sin_rows,
            second_half * cos_rows - first_half * sin_rows,
        ],
        axis=-1,
    )


def normalize(hidden_in, gain_vec, bias_vec):
    average = jnp.mean(hidden_in, axis=-1, keepdims=True)
    centered = hidden_in - average
    variance = jnp.mean(centered * centered, axis=-1, keepdims=True)
    inv_std = lax.rsqrt(variance + norm_eps)
    scaled = centered * inv_std
    return (scaled * gain_vec + bias_vec, scaled, inv_std)


def normalize_back(upstream, scaled, inv_std, gain_vec):
    weighted = upstream * gain_vec
    inner = (
        weighted
        - jnp.mean(weighted, axis=-1, keepdims=True)
        - scaled * jnp.mean(weighted * scaled, axis=-1, keepdims=True)
    )
    return (inv_std * inner, jnp.sum(upstream * scaled, axis=0), jnp.sum(upstream, axis=0))


def product(left, right):
    return jnp.dot(left, right, preferred_element_type=jnp.float32)


def local_any(
    tokens,
    qkv_weight,
    out_weight,
    gate_weight,
    up_weight,
    down_weight,
    first_gain,
    first_bias,
    second_gain,
    second_bias,
    doc_lengths,
    cotangent,
):
    rows_here = tokens.shape[0]
    model_width = tokens.shape[1]
    hd_count = lax.axis_size("hd")
    cp_count = lax.axis_size("cp")
    cp_index = lax.axis_index("cp")
    block_rows = rows_here * hd_count
    local_width = model_width // hd_count
    local_heads = local_width // HD
    shifts = [0]
    for distance in range(1, REACH + 1):
        shifts = shifts + [-distance, distance]
    shards = (
        qkv_weight,
        out_weight,
        gate_weight,
        up_weight,
        down_weight,
        first_gain,
        first_bias,
        second_gain,
        second_bias,
    )
    weights = (
        lax.all_gather(shards[0], ("cp", "hd"), axis=0, tiled=True),
        lax.all_gather(shards[1], ("cp", "hd"), axis=0, tiled=True),
        lax.all_gather(shards[2], ("cp", "hd"), axis=0, tiled=True),
        lax.all_gather(shards[3], ("cp", "hd"), axis=0, tiled=True),
        lax.all_gather(shards[4], ("cp", "hd"), axis=0, tiled=True),
        lax.all_gather(shards[5], ("cp", "hd"), axis=0, tiled=True),
        lax.all_gather(shards[6], ("cp", "hd"), axis=0, tiled=True),
        lax.all_gather(shards[7], ("cp", "hd"), axis=0, tiled=True),
        lax.all_gather(shards[8], ("cp", "hd"), axis=0, tiled=True),
    )
    (
        qkv_full,
        out_full,
        gate_full,
        up_full,
        down_full,
        gain_first,
        bias_first,
        gain_second,
        bias_second,
    ) = weights
    raw_rows = product(tokens, qkv_full).astype(jnp.bfloat16)
    grouped = lax.all_to_all(
        raw_rows.reshape(rows_here, 3, hd_count, local_width),
        "hd",
        split_axis=2,
        concat_axis=0,
        tiled=True,
    )
    grouped = grouped.reshape(block_rows, 3, local_width)
    query_docs, offsets = doc_layout(doc_lengths, cp_index * block_rows, block_rows)
    cosine, sine = rope_tables(offsets, HD)
    queries = rotate(
        grouped[:, 0].astype(jnp.float32).reshape(block_rows, local_heads, HD), cosine, sine
    ).astype(jnp.bfloat16)
    key_rows = rotate(
        grouped[:, 1].astype(jnp.float32).reshape(block_rows, local_heads, HD), cosine, sine
    ).astype(jnp.bfloat16)
    own_block = jnp.stack([key_rows.reshape(block_rows, local_width), grouped[:, 2]], axis=1)

    def key_docs(distance):
        source = cp_index - distance
        doc_ids, unused_offsets = doc_layout(doc_lengths, source * block_rows, block_rows)
        inside = jnp.logical_and(source >= 0, source < cp_count)
        return jnp.where(inside, doc_ids, -2)

    remote = [own_block] + [shifted(own_block, "cp", distance) for distance in shifts[1:]]
    masks = [query_docs[:, None] == key_docs(distance)[None, :] for distance in shifts]

    def scores_with(query_part, remote_block, key_mask):
        key_part = remote_block[:, 0].reshape(block_rows, local_heads, HD)
        raw_scores = (
            jnp.einsum("qhd,khd->hqk", query_part, key_part, preferred_element_type=jnp.float32)
            * score_scale
        )
        return jnp.where(key_mask[None], raw_scores, masked_score)

    def scores_for(remote_block, key_mask):
        return scores_with(queries, remote_block, key_mask)

    running_max = jnp.full((local_heads, block_rows), masked_score, jnp.float32)
    running_sum = jnp.zeros((local_heads, block_rows), jnp.float32)
    for remote_block, key_mask in zip(remote, masks):
        block_scores = scores_for(remote_block, key_mask)
        new_max = jnp.maximum(running_max, jnp.max(block_scores, axis=-1))
        running_sum = running_sum * jnp.exp(running_max - new_max) + jnp.sum(
            jnp.exp(block_scores - new_max[:, :, None]), axis=-1
        )
        running_max = new_max
    log_total = running_max + jnp.log(running_sum)
    attended = jnp.zeros((block_rows, local_heads, HD), jnp.float32)
    for remote_block, key_mask in zip(remote, masks):
        block_scores = scores_for(remote_block, key_mask)
        probs = jnp.exp(block_scores - log_total[:, :, None]).astype(jnp.bfloat16)
        value_part = remote_block[:, 1].reshape(block_rows, local_heads, HD)
        attended = attended + jnp.einsum(
            "hqk,khd->qhd", probs, value_part, preferred_element_type=jnp.float32
        )
    attended_send = attended.reshape(block_rows, 1, local_width).astype(jnp.bfloat16)
    attended_low = lax.all_to_all(
        attended_send, "hd", split_axis=0, concat_axis=1, tiled=True
    ).reshape(rows_here, model_width)
    gain_one = gain_first.astype(jnp.float32)
    gain_two = gain_second.astype(jnp.float32)
    attn_out = product(attended_low, out_full)
    first, scaled_one, inv_one = normalize(
        tokens.astype(jnp.float32) + attn_out, gain_one, bias_first.astype(jnp.float32)
    )
    first_low = first.astype(jnp.bfloat16)
    gate_proj = product(first_low, gate_full)
    up_proj = product(first_low, up_full)
    sigmoid_gate = jax.nn.sigmoid(gate_proj)
    silu_gate = gate_proj * sigmoid_gate
    hidden = (silu_gate * up_proj).astype(jnp.bfloat16)
    branch = product(hidden, down_full)
    second, scaled_two, inv_two = normalize(
        first + branch, gain_two, bias_second.astype(jnp.float32)
    )
    layer_out = second.astype(jnp.bfloat16)
    weights = (
        lax.all_gather(shards[0], ("cp", "hd"), axis=0, tiled=True),
        lax.all_gather(shards[1], ("cp", "hd"), axis=0, tiled=True),
        lax.all_gather(shards[2], ("cp", "hd"), axis=0, tiled=True),
        lax.all_gather(shards[3], ("cp", "hd"), axis=0, tiled=True),
        lax.all_gather(shards[4], ("cp", "hd"), axis=0, tiled=True),
        lax.all_gather(shards[5], ("cp", "hd"), axis=0, tiled=True),
        lax.all_gather(shards[6], ("cp", "hd"), axis=0, tiled=True),
        lax.all_gather(shards[7], ("cp", "hd"), axis=0, tiled=True),
        lax.all_gather(shards[8], ("cp", "hd"), axis=0, tiled=True),
    )
    (
        qkv_full,
        out_full,
        gate_full,
        up_full,
        down_full,
        gain_first,
        bias_first,
        gain_second,
        bias_second,
    ) = weights
    upstream = cotangent.astype(jnp.float32)
    dz_two, gain_two_grad, bias_two_grad = normalize_back(upstream, scaled_two, inv_two, gain_two)
    dz_two_low = dz_two.astype(jnp.bfloat16)
    down_sum = product(hidden.T, dz_two_low)
    hidden_grad = product(dz_two_low, down_full.T)
    gate_back = (
        hidden_grad * up_proj * sigmoid_gate * (1.0 + gate_proj * (1.0 - sigmoid_gate))
    ).astype(jnp.bfloat16)
    up_back = (hidden_grad * silu_gate).astype(jnp.bfloat16)
    gate_sum = product(first_low.T, gate_back)
    up_sum = product(first_low.T, up_back)
    first_back = dz_two + product(gate_back, gate_full.T) + product(up_back, up_full.T)
    dz_one, gain_one_grad, bias_one_grad = normalize_back(first_back, scaled_one, inv_one, gain_one)
    dz_one_low = dz_one.astype(jnp.bfloat16)
    out_sum = product(attended_low.T, dz_one_low)
    attended_back = product(dz_one_low, out_full.T).astype(jnp.bfloat16)
    heads_back = lax.all_to_all(
        attended_back.reshape(rows_here, hd_count, local_width),
        "hd",
        split_axis=1,
        concat_axis=0,
        tiled=True,
    )
    heads_back = heads_back.reshape(block_rows, local_heads, HD)
    delta = jnp.transpose(jnp.sum(heads_back.astype(jnp.float32) * attended, axis=-1))
    query_grad = jnp.zeros((block_rows, local_heads, HD), jnp.float32)
    pair_total = jnp.zeros((block_rows, 2, local_width), jnp.float32)
    remote = [own_block] + [shifted(own_block, "cp", distance) for distance in shifts[1:]]
    for distance, remote_block, key_mask in zip(shifts, remote, masks):
        pair_block_scores = scores_with(queries, remote_block, key_mask)
        pair_probs = jnp.exp(pair_block_scores - log_total[:, :, None])
        pair_key_part = remote_block[:, 0].reshape(block_rows, local_heads, HD)
        pair_value_part = remote_block[:, 1].reshape(block_rows, local_heads, HD)
        value_grad = jnp.einsum(
            "hqk,qhd->khd",
            pair_probs.astype(jnp.bfloat16),
            heads_back,
            preferred_element_type=jnp.float32,
        )
        prob_grad = jnp.einsum(
            "qhd,khd->hqk", heads_back, pair_value_part, preferred_element_type=jnp.float32
        )
        score_grad = (pair_probs * (prob_grad - delta[:, :, None])).astype(jnp.bfloat16)
        query_term = (
            jnp.einsum(
                "hqk,khd->qhd", score_grad, pair_key_part, preferred_element_type=jnp.float32
            )
            * score_scale
        )
        key_grad = (
            jnp.einsum("hqk,qhd->khd", score_grad, queries, preferred_element_type=jnp.float32)
            * score_scale
        )
        grad_pair = jnp.stack(
            [
                key_grad.reshape(block_rows, local_width),
                value_grad.reshape(block_rows, local_width),
            ],
            axis=1,
        )
        query_term, grad_pair = (query_term, grad_pair)
        query_grad = query_grad + query_term
        if distance == 0:
            pair_total = grad_pair
        else:
            pair_total = pair_total + shifted(
                grad_pair.astype(jnp.bfloat16), "cp", -distance
            ).astype(grad_pair.dtype)
    query_back = rotate_back(query_grad, cosine, sine).reshape(block_rows, local_width)
    key_back = rotate_back(
        pair_total[:, 0].reshape(block_rows, local_heads, HD), cosine, sine
    ).reshape(block_rows, local_width)
    raw_back = jnp.stack([query_back, key_back, pair_total[:, 1]], axis=1).astype(jnp.bfloat16)
    raw_back = lax.all_to_all(
        raw_back.reshape(block_rows, 3, 1, local_width),
        "hd",
        split_axis=0,
        concat_axis=2,
        tiled=True,
    )
    raw_back = raw_back.reshape(rows_here, 3 * model_width)
    qkv_sum = product(tokens.T, raw_back)
    tokens_grad = (dz_one + product(raw_back, qkv_full.T)).astype(jnp.bfloat16)
    summed = (
        lax.psum_scatter(qkv_sum, ("cp", "hd"), scatter_dimension=0, tiled=True),
        lax.psum_scatter(out_sum, ("cp", "hd"), scatter_dimension=0, tiled=True),
        lax.psum_scatter(gate_sum, ("cp", "hd"), scatter_dimension=0, tiled=True),
        lax.psum_scatter(up_sum, ("cp", "hd"), scatter_dimension=0, tiled=True),
        lax.psum_scatter(down_sum, ("cp", "hd"), scatter_dimension=0, tiled=True),
        lax.psum_scatter(gain_one_grad, ("cp", "hd"), scatter_dimension=0, tiled=True),
        lax.psum_scatter(bias_one_grad, ("cp", "hd"), scatter_dimension=0, tiled=True),
        lax.psum_scatter(gain_two_grad, ("cp", "hd"), scatter_dimension=0, tiled=True),
        lax.psum_scatter(bias_two_grad, ("cp", "hd"), scatter_dimension=0, tiled=True),
    )
    return (
        layer_out,
        tokens_grad,
        summed[0],
        summed[1],
        summed[2],
        summed[3],
        summed[4],
        summed[5],
        summed[6],
        summed[7],
        summed[8],
    )


MESH = pl.DeviceIdType.MESH
ZN, YN, CN, XN = 4, 2, 2, 2
BLOCKS = ZN * YN * CN * XN


def place():
    cp = lax.axis_index("cp")
    x = lax.axis_index("hd")
    return x, lax.rem(cp // CN, YN), cp // (YN * CN), lax.rem(cp, CN)


def device(x, y, z, c):
    return ((z * YN + y) * CN + c, x)


def block(x, y, z, c):
    return ((z * YN + y) * CN + c) * XN + x


def when(cond, fn):
    if cond is None:
        fn()
    else:
        pl.when(cond)(fn)


def both(a, b):
    if a is None:
        return b
    if b is None:
        return a
    return jnp.logical_and(a, b)


def halves(ref):
    rows, cols = ref.shape[-2:]
    if rows % 32 == 0:
        return ref.at[pl.ds(0, rows // 2)], ref.at[pl.ds(rows // 2, rows // 2)]
    if cols % 256 == 0:
        return ref.at[:, pl.ds(0, cols // 2)], ref.at[:, pl.ds(cols // 2, cols // 2)]
    return ref, None


def greet(x, y, z, c, far):
    barrier = pltpu.get_barrier_semaphore()
    for peer in (device(1 - x, y, z, c), device(x, 1 - y, z, c), device(x, y, z, 1 - c)):
        pl.semaphore_signal(barrier, inc=1, device_id=peer, device_id_type=MESH)
    count = 3
    if far:
        for k in range(1, ZN):
            peer = device(x, y, lax.rem(z + k, ZN), c)
            pl.semaphore_signal(barrier, inc=1, device_id=peer, device_id_type=MESH)
        count = count + ZN - 1
    else:
        pl.when(z > 0)(lambda: pl.semaphore_signal(barrier, inc=1, device_id=device(x, y, z - 1, c), device_id_type=MESH))
        pl.when(z < ZN - 1)(lambda: pl.semaphore_signal(barrier, inc=1, device_id=device(x, y, z + 1, c), device_id_type=MESH))
        count = count + (z > 0).astype(jnp.int32) + (z < ZN - 1).astype(jnp.int32)
    pl.semaphore_wait(barrier, count)


SENDS = 40
RECVS = 36


def gather_kernel(modes, *refs):
    n = len(modes)
    ins, outs, (lsem, ssem, rsem) = refs[:n], refs[n : 2 * n], refs[2 * n :]
    x, y, z, c = place()
    ox, oy, oc = 1 - x, 1 - y, 1 - c
    greet(x, y, z, c, any(m != "bcast" for m in modes))
    sent = []

    def copy(k, src, dst, s, r, peer):
        return pltpu.make_async_remote_copy(
            src_ref=src,
            dst_ref=dst,
            send_sem=ssem.at[k, s],
            recv_sem=rsem.at[k, r],
            device_id=peer,
            device_id_type=MESH,
        )

    def send(cond, *args):
        when(cond, lambda: copy(*args).start())
        sent.append((cond, args))

    def arrived(cond, k, ref, r):
        when(cond, lambda: copy(k, ref, ref, 0, r, device(ox, y, z, c)).wait_recv())

    for k, mode in enumerate(modes):
        if mode == "bcast":
            mine, spot = ins[k], outs[k].at[block(x, y, z, c)]
        elif mode == "swap":
            mine, spot = ins[k].at[z], outs[k].at[z]
        else:
            mine, spot = ins[k].at[z], outs[k].at[block(x, y, z, c)]
        pltpu.make_async_copy(mine, spot, lsem.at[k]).start()

    def spread(k, cond, b, src, up, down):
        here = outs[k].at[block(x, y, b, c)]
        if modes[k] == "bcast":
            if up is not False:
                send(both(cond, up), k, src, here, b, b, device(x, y, lax.rem(z + 1, ZN), c))
            if down is not False:
                send(both(cond, down), k, src, here, 4 + b, b, device(x, y, lax.rem(z + ZN - 1, ZN), c))
        send(cond, k, src, here, 8 + b, 4 + b, device(ox, y, z, c))
        send(cond, k, src, here, 16 + b, 12 + b, device(x, oy, z, c))
        send(cond, k, src, here, 24 + b, 20 + b, device(x, y, z, oc))

    def sides(k, cond, b):
        fx = outs[k].at[block(ox, y, b, c)]
        fy = outs[k].at[block(x, oy, b, c)]
        arrived(cond, k, fx, 4 + b)
        first, _ = halves(fx)
        send(cond, k, first, first, 20 + b, 16 + b, device(x, oy, z, c))
        send(cond, k, fx, fx, 28 + b, 24 + b, device(x, y, z, oc))
        arrived(cond, k, fy, 12 + b)
        _, second = halves(fy)
        if second is not None:
            send(cond, k, second, second, 12 + b, 8 + b, device(ox, y, z, c))
        send(cond, k, fy, fy, 32 + b, 28 + b, device(x, y, z, oc))

    def corner(k, cond, b):
        far = outs[k].at[block(ox, oy, b, c)]
        first, second = halves(far)
        arrived(cond, k, first, 16 + b)
        if second is not None:
            arrived(cond, k, second, 8 + b)
        send(cond, k, far, far, 36 + b, 32 + b, device(x, y, z, oc))

    def steps(distance):
        if distance == 0:
            return [(None, z)]
        return [(z >= distance, jnp.maximum(z - distance, 0)), (z + distance < ZN, jnp.minimum(z + distance, ZN - 1))]

    for k, mode in enumerate(modes):
        if mode == "bcast":
            spread(k, None, z, ins[k], z < ZN - 1, z > 0)
        else:
            for d in range(1, ZN):
                to = lax.rem(z + d, ZN)
                spot = outs[k].at[z] if mode == "swap" else outs[k].at[block(x, y, z, c)]
                send(None, k, ins[k].at[to], spot, to, z, device(x, y, to, c))
            if mode == "cross":
                spread(k, None, z, ins[k].at[z], False, False)

    active = [k for k, mode in enumerate(modes) if mode != "swap"]
    for distance in range(1, ZN + 2):
        if distance < ZN:
            for side, (cond, b) in enumerate(steps(distance)):
                for k in active:
                    arrived(cond, k, outs[k].at[block(x, y, b, c)], b)
                    here = outs[k].at[block(x, y, b, c)]
                    spread(k, cond, b, here, z < ZN - 1 if side == 0 else False, z > 0 if side == 1 else False)
        if 0 <= distance - 1 < ZN:
            for cond, b in steps(distance - 1):
                for k in active:
                    sides(k, cond, b)
        if 0 <= distance - 2 < ZN:
            for cond, b in steps(distance - 2):
                for k in active:
                    corner(k, cond, b)
    for k, mode in enumerate(modes):
        if mode == "swap":
            for d in range(1, ZN):
                frm = lax.rem(z + d, ZN)
                arrived(None, k, outs[k].at[frm], frm)
            pltpu.make_async_copy(ins[k].at[z], outs[k].at[z], lsem.at[k]).wait()
        else:
            for b in range(ZN):
                for j, (px, py) in enumerate(((x, y), (ox, y), (x, oy), (ox, oy))):
                    arrived(None, k, outs[k].at[block(px, py, b, oc)], 20 + 4 * j + b)
            spot = outs[k].at[block(x, y, z, c)]
            pltpu.make_async_copy(ins[k] if mode == "bcast" else ins[k].at[z], spot, lsem.at[k]).wait()
    for cond, args in sent:
        when(cond, lambda args=args: copy(*args).wait_send())


def gather(arrays, modes, collective_id):
    shapes = []
    for a, mode in zip(arrays, modes):
        if mode == "bcast":
            shapes.append((BLOCKS,) + a.shape)
        elif mode == "swap":
            shapes.append(a.shape)
        else:
            shapes.append((BLOCKS,) + a.shape[1:])
    n = len(arrays)
    return pl.pallas_call(
        functools.partial(gather_kernel, tuple(modes)),
        out_shape=[jax.ShapeDtypeStruct(s, a.dtype) for s, a in zip(shapes, arrays)],
        in_specs=[pl.BlockSpec(memory_space=pl.ANY)] * n,
        out_specs=[pl.BlockSpec(memory_space=pl.ANY)] * n,
        scratch_shapes=[
            pltpu.SemaphoreType.DMA((n,)),
            pltpu.SemaphoreType.DMA((n, SENDS)),
            pltpu.SemaphoreType.DMA((n, RECVS)),
        ],
        compiler_params=pltpu.CompilerParams(collective_id=collective_id, has_side_effects=True),
    )(*arrays)


def chunk_of(cols):
    for size in (768, 640, 512, 384, 256, 128):
        if cols % size == 0:
            return size
    return cols


def add_up(dst, sources):
    rows, cols = dst.shape[-2:]
    size = chunk_of(cols)

    def step(i, carry):
        span = pl.ds(pl.multiple_of(i * size, size), size)
        total = sources[0][:, span].astype(jnp.float32)
        for source in sources[1:]:
            total = total + source[:, span].astype(jnp.float32)
        dst[:, span] = total.astype(dst.dtype)
        return carry

    if cols == size:
        total = sources[0][...].astype(jnp.float32)
        for source in sources[1:]:
            total = total + source[...].astype(jnp.float32)
        dst[...] = total.astype(dst.dtype)
    else:
        lax.fori_loop(0, cols // size, step, 0)


def reduce_kernel(modes, *refs):
    n = len(modes)
    ins, outs = refs[:n], refs[n : 2 * n]
    lsem, ssem, rsem = refs[2 * n : 2 * n + 3]
    scratch = refs[2 * n + 3 :]
    bufs = []
    for mode in modes:
        count = 0 if mode == "swap" else (4 if mode == "reduce" else 3)
        bufs.append(scratch[:count])
        scratch = scratch[count:]
    x, y, z, c = place()
    ox, oy, oc = 1 - x, 1 - y, 1 - c
    greet(x, y, z, c, any(m != "reduce" for m in modes))
    sent = []

    def copy(k, src, dst, s, r, peer):
        return pltpu.make_async_remote_copy(
            src_ref=src,
            dst_ref=dst,
            send_sem=ssem.at[k, s],
            recv_sem=rsem.at[k, r],
            device_id=peer,
            device_id_type=MESH,
        )

    def send(cond, *args):
        when(cond, lambda: copy(*args).start())
        sent.append((cond, args))

    def arrived(cond, k, ref, r):
        when(cond, lambda: copy(k, ref, ref, 0, r, device(ox, y, z, c)).wait_recv())

    half = z // 2
    order = [3 - 3 * half, 2 - half, 1 - z + 4 * half, z]
    quads = ((ox, oy), (ox, y), (x, oy), (x, y))
    active = [k for k, mode in enumerate(modes) if mode != "swap"]

    for i, b in enumerate(order):
        for k in active:
            acc, cor = bufs[k][:2]
            for j, (px, py) in enumerate(quads):
                send(None, k, ins[k].at[block(px, py, b, oc)], cor.at[4 * i + j], 4 * i + j, 4 * i + j, device(x, y, z, oc))
                pltpu.make_async_copy(ins[k].at[block(px, py, b, c)], acc.at[4 * i + j], lsem.at[k, 4 * i + j]).start()
    for k, mode in enumerate(modes):
        if mode == "swap":
            for d in range(1, ZN):
                to = lax.rem(z + d, ZN)
                send(None, k, ins[k].at[to], outs[k].at[z], d, z, device(x, y, to, c))
            pltpu.make_async_copy(ins[k].at[z], outs[k].at[z], lsem.at[k, 0]).start()

    def loaded(k, i, j):
        acc, cor = bufs[k][:2]
        pltpu.make_async_copy(ins[k].at[0], acc.at[4 * i + j], lsem.at[k, 4 * i + j]).wait()
        arrived(None, k, cor.at[4 * i + j], 4 * i + j)

    for i, b in enumerate(order):
        for k in active:
            acc, cor, side = bufs[k][:3]
            loaded(k, i, 0)
            add_up(acc.at[4 * i], (acc.at[4 * i], cor.at[4 * i]))
            first, second = halves(acc.at[4 * i])
            send(None, k, first, halves(side.at[i])[0], 16 + i, 16 + i, device(x, oy, z, c))
            if second is not None:
                send(None, k, second, halves(side.at[4 + i])[1], 20 + i, 20 + i, device(ox, y, z, c))
    for i, b in enumerate(order):
        for k in active:
            acc, cor, side = bufs[k][:3]
            loaded(k, i, 1)
            add_up(acc.at[4 * i + 1], (acc.at[4 * i + 1], cor.at[4 * i + 1]))
            part = halves(side.at[i])[0]
            arrived(None, k, part, 16 + i)
            mine = halves(acc.at[4 * i + 1])[0]
            add_up(mine, (mine, part))
            send(None, k, acc.at[4 * i + 1], side.at[8 + i], 24 + i, 24 + i, device(ox, y, z, c))
            loaded(k, i, 2)
            add_up(acc.at[4 * i + 2], (acc.at[4 * i + 2], cor.at[4 * i + 2]))
            part = halves(side.at[4 + i])[1]
            if part is not None:
                arrived(None, k, part, 20 + i)
                mine = halves(acc.at[4 * i + 2])[1]
                add_up(mine, (mine, part))
            send(None, k, acc.at[4 * i + 2], side.at[12 + i], 28 + i, 28 + i, device(x, oy, z, c))
    for i, b in enumerate(order):
        for k in active:
            acc, cor, side = bufs[k][:3]
            loaded(k, i, 3)
            own = acc.at[4 * i + 3]
            arrived(None, k, side.at[8 + i], 24 + i)
            arrived(None, k, side.at[12 + i], 28 + i)
            terms = (own, cor.at[4 * i + 3], side.at[8 + i], side.at[12 + i])
            if modes[k] == "cross":
                add_up(own, terms)
                if i < ZN - 1:
                    send(None, k, own, outs[k].at[z], 32 + i, 32 + z, device(x, y, b, c))
                else:
                    pltpu.make_async_copy(own, outs[k].at[z], lsem.at[k, 16]).start()
                continue
            chain = bufs[k][3]
            if i == ZN - 1:
                add_up(outs[k], terms)

                def lower(k=k, chain=chain):
                    arrived(None, k, chain.at[z], 32 + z)
                    add_up(outs[k], (outs[k], chain.at[z]))

                def upper(k=k, chain=chain):
                    arrived(None, k, chain.at[4 + z], 36 + z)
                    add_up(outs[k], (outs[k], chain.at[4 + z]))

                pl.when(z > 0)(lower)
                pl.when(z < ZN - 1)(upper)
            else:
                add_up(own, terms)
                below = both(b > z, z > 0)
                above = both(b < z, z < ZN - 1)

                def lower(k=k, chain=chain, own=own, b=b):
                    arrived(None, k, chain.at[b], 32 + b)
                    add_up(own, (own, chain.at[b]))

                def upper(k=k, chain=chain, own=own, b=b):
                    arrived(None, k, chain.at[4 + b], 36 + b)
                    add_up(own, (own, chain.at[4 + b]))

                pl.when(below)(lower)
                pl.when(above)(upper)
                send(b > z, k, own, chain.at[b], 32 + i, 32 + b, device(x, y, lax.rem(z + 1, ZN), c))
                send(b < z, k, own, chain.at[4 + b], 32 + i, 36 + b, device(x, y, lax.rem(z + ZN - 1, ZN), c))
    for k, mode in enumerate(modes):
        if mode == "reduce":
            continue
        for d in range(1, ZN):
            frm = lax.rem(z + d, ZN)
            arrived(None, k, outs[k].at[frm], frm if mode == "swap" else 32 + frm)
        if mode == "swap":
            pltpu.make_async_copy(ins[k].at[z], outs[k].at[z], lsem.at[k, 0]).wait()
        else:
            pltpu.make_async_copy(bufs[k][0].at[15], outs[k].at[z], lsem.at[k, 16]).wait()
    for cond, args in sent:
        when(cond, lambda args=args: copy(*args).wait_send())


def reduce(arrays, modes, collective_id):
    shapes, specs, scratch = [], [], []
    for a, mode in zip(arrays, modes):
        if mode == "swap":
            shapes.append(jax.ShapeDtypeStruct(a.shape, a.dtype))
            specs.append(pl.BlockSpec(memory_space=pl.ANY))
            continue
        rows, cols = a.shape[1:]
        scratch = scratch + [pltpu.VMEM((16, rows, cols), a.dtype)] * 3
        if mode == "cross":
            shapes.append(jax.ShapeDtypeStruct((ZN, rows, cols), a.dtype))
            specs.append(pl.BlockSpec(memory_space=pl.ANY))
        else:
            scratch = scratch + [pltpu.VMEM((8, rows, cols), a.dtype)]
            shapes.append(jax.ShapeDtypeStruct((rows, cols), jnp.float32))
            specs.append(pl.BlockSpec(memory_space=pltpu.VMEM))
    n = len(arrays)
    return pl.pallas_call(
        functools.partial(reduce_kernel, tuple(modes)),
        out_shape=shapes,
        in_specs=[pl.BlockSpec(memory_space=pl.ANY)] * n,
        out_specs=specs,
        scratch_shapes=[
            pltpu.SemaphoreType.DMA((n, 17)),
            pltpu.SemaphoreType.DMA((n, SENDS)),
            pltpu.SemaphoreType.DMA((n, SENDS)),
        ]
        + scratch,
        compiler_params=pltpu.CompilerParams(
            collective_id=collective_id, has_side_effects=True, vmem_limit_bytes=67043328
        ),
    )(*arrays)


HEAD = 64
GROUP = 3
TILE = 512
WIDE = 1024
EDGE = 128
SPAN = 4096
FAR = 1 << 30


def longest(lengths):
    begin, best, at = jnp.int32(0), lengths[0], jnp.int32(0)
    for j in range(lengths.shape[0]):
        length = lengths[j]
        at = jnp.where(length > best, begin, at)
        best = jnp.maximum(best, length)
        begin = begin + length
    return at, at + best


def lane_slots(lengths, count):
    x, y, z, c = place()
    lane = lax.broadcasted_iota(jnp.int32, (1, count), 1)
    begin, end = longest(lengths)
    spots = [block(x, y, b, c) * count + lane for b in range(ZN)]
    slots, before = [], jnp.zeros((1, count), jnp.int32)
    for b in range(ZN):
        big = jnp.logical_and(spots[b] >= begin, spots[b] < end)
        slots.append(jnp.where(big, before, ZN // 2 + b - before))
        before = before + big.astype(jnp.int32)
    return begin, end, spots, slots


def pick(slots, slot, parts):
    chosen = parts[-1]
    for b in range(len(parts) - 2, -1, -1):
        chosen = jnp.where(slots[b] == slot, parts[b], chosen)
    return chosen


def bounds_of(lengths, spot):
    low, high = jnp.zeros_like(spot), jnp.full_like(spot, FAR)
    begin = jnp.int32(0)
    for j in range(lengths.shape[0]):
        end = begin + lengths[j]
        low = jnp.where(spot >= begin, begin, low)
        high = jnp.where(spot < end, jnp.minimum(high, end), high)
        begin = end
    return low, high


def walk(big, begin, end, low, high, step, init):
    if big:
        base = begin // EDGE * EDGE

        def body(i, carry):
            at = pl.multiple_of(base + i * WIDE, EDGE)
            return step(at, WIDE, False, carry)

        carry = step(pl.multiple_of(base, EDGE), WIDE, True, init)
        carry = lax.fori_loop(1, SPAN // WIDE, body, carry)
        return lax.cond(
            begin > base,
            lambda c: step(pl.multiple_of(base + SPAN, EDGE), EDGE, True, c),
            lambda c: c,
            carry,
        )
    first = jnp.min(low) // TILE
    stop = (jnp.max(high) + TILE - 1) // TILE
    hole_first = jnp.maximum((begin + TILE - 1) // TILE, first)
    hole = jnp.maximum(jnp.minimum(end // TILE, stop) - hole_first, 0)

    def body(i, carry):
        tile = first + i
        tile = jnp.where(jnp.logical_and(hole > 0, tile >= hole_first), tile + hole, tile)
        return step(pl.multiple_of(tile * TILE, TILE), TILE, True, carry)

    return lax.fori_loop(0, stop - first - hole, body, init)


def keys_in(first, size, low, high):
    at = first + lax.broadcasted_iota(jnp.int32, (size, low.shape[1]), 0)
    return jnp.logical_and(at >= low, at < high)


def dot(a, b):
    return jnp.dot(a, b, preferred_element_type=jnp.float32)


def pad_heads(rows, h, slots):
    part = rows[h * HEAD : (h + 1) * HEAD]
    zero = jnp.zeros_like(part)
    return jnp.concatenate([part if s == h else zero for s in slots], axis=0)


Q_SLOTS = (0, 1, 2, -1)
V_SLOTS = (-1, 2, 0, 1)


def forward_kernel(lengths, qt, kv, low_out, out, lse_out, qm, acc, qs, os, ls):
    count = qt.shape[2]
    begin, end, spots, slots = lane_slots(lengths, count)
    for s in range(ZN):
        qs[s] = pick(slots, s, [qt[b] for b in range(ZN)])

    def one_block(big, s, carry):
        low, high = bounds_of(lengths, pick(slots, s, spots))
        rows = qs[s] * jnp.bfloat16(0.125)
        for h in range(GROUP):
            qm[h] = pad_heads(rows, h, Q_SLOTS)
        acc[...] = jnp.zeros_like(acc)

        def step(at, size, masked, stats):
            span = pl.ds(at, size)
            keys = kv[span, 0:256]
            values = kv[span, 128:384].T
            mask = keys_in(at, size, low, high) if masked else None
            fresh = []
            for h in range(GROUP):
                top, total = stats[2 * h], stats[2 * h + 1]
                scores = dot(keys, qm[h])
                if masked:
                    scores = jnp.where(mask, scores, -1e9)
                new_top = jnp.maximum(top, jnp.max(scores, axis=0, keepdims=True))
                shrink = jnp.exp(top - new_top)
                weights = jnp.exp(scores - new_top)
                total = total * shrink + jnp.sum(weights, axis=0, keepdims=True)
                row = V_SLOTS.index(h) * HEAD
                acc[h] = acc[h] * shrink + dot(values[row : row + HEAD], weights.astype(jnp.bfloat16))
                fresh = fresh + [new_top, total]
            return tuple(fresh)

        init = (jnp.full((1, count), -1e9, jnp.float32), jnp.zeros((1, count), jnp.float32)) * GROUP
        stats = walk(big, begin, end, low, high, step, init)
        for h in range(GROUP):
            top, total = stats[2 * h], stats[2 * h + 1]
            os[s, h * HEAD : (h + 1) * HEAD] = acc[h] / total
            ls[s, h : h + 1] = top + jnp.log(total)
        return carry

    lax.fori_loop(0, ZN // 2, functools.partial(one_block, True), 0)
    lax.fori_loop(ZN // 2, ZN, functools.partial(one_block, False), 0)
    for b in range(ZN):
        value = pick([jnp.full_like(slots[b], s) for s in range(ZN)], slots[b], [os[s] for s in range(ZN)])
        out[b] = value
        low_out[b] = value.astype(low_out.dtype)
        lse_out[b] = pick([jnp.full_like(slots[b], s) for s in range(ZN)], slots[b], [ls[s] for s in range(ZN)])


def attend(lengths, qt, kv):
    blocks, rows, count = qt.shape
    whole = pl.BlockSpec(memory_space=pltpu.VMEM)
    return pl.pallas_call(
        forward_kernel,
        out_shape=[
            jax.ShapeDtypeStruct(qt.shape, jnp.bfloat16),
            jax.ShapeDtypeStruct(qt.shape, jnp.float32),
            jax.ShapeDtypeStruct((blocks, 8, count), jnp.float32),
        ],
        in_specs=[pl.BlockSpec(memory_space=pltpu.SMEM), whole, whole],
        out_specs=[whole] * 3,
        scratch_shapes=[
            pltpu.VMEM((GROUP, 256, count), jnp.bfloat16),
            pltpu.VMEM((GROUP, HEAD, count), jnp.float32),
            pltpu.VMEM(qt.shape, jnp.bfloat16),
            pltpu.VMEM(qt.shape, jnp.float32),
            pltpu.VMEM((blocks, 8, count), jnp.float32),
        ],
        compiler_params=pltpu.CompilerParams(vmem_limit_bytes=67043328),
    )(lengths, qt, kv)


def backward_kernel(lengths, qt, kv, out, lse, dot_in, cosine, sine, dq_out, dkv_out, qmt, qm, dmt, dm, dq, acc, qs, ds, es, ls, dqs):
    count = qt.shape[2]
    tiles = kv.shape[0] // TILE

    def clear(tile, carry):
        acc[pl.ds(pl.multiple_of(tile * TILE, TILE), TILE), :] = jnp.zeros((TILE, acc.shape[1]), jnp.float32)
        return carry

    lax.fori_loop(0, tiles, clear, 0)

    begin, end, spots, slots = lane_slots(lengths, count)
    for b in range(ZN):
        product_rows = dot_in[b].astype(jnp.float32) * out[b]
        for h in range(GROUP):
            es[b, h : h + 1] = jnp.sum(product_rows[h * HEAD : (h + 1) * HEAD], axis=0, keepdims=True)
    for s in range(ZN):
        qs[s] = pick(slots, s, [qt[b] for b in range(ZN)])
        ds[s] = pick(slots, s, [dot_in[b] for b in range(ZN)])
        ls[s] = pick(slots, s, [lse[b] for b in range(ZN)])
    picked = [pick(slots, s, [es[b] for b in range(ZN)]) for s in range(ZN)]
    for s in range(ZN):
        es[s] = picked[s]

    def one_block(big, s, carry):
        low, high = bounds_of(lengths, pick(slots, s, spots))
        rows = qs[s] * jnp.bfloat16(0.125)
        grads = ds[s]
        deltas = [es[s, h : h + 1] for h in range(GROUP)]
        levels = [ls[s, h : h + 1] for h in range(GROUP)]
        for h in range(GROUP):
            padded = pad_heads(rows, h, Q_SLOTS)
            qmt[h] = padded
            qm[h * count : (h + 1) * count] = padded.T
            padded = pad_heads(grads, h, V_SLOTS)
            dmt[h] = padded
            dm[h * count : (h + 1) * count] = padded.T
        dq[...] = jnp.zeros_like(dq)

        def step(at, size, masked, inner):
            span = pl.ds(at, size)
            keys = kv[span, 0:256]
            values = kv[span, 128:384]
            turned = keys.T
            mask = keys_in(at, size, low, high) if masked else None
            probs, slopes = [], []
            for h in range(GROUP):
                weights = jnp.exp(dot(keys, qmt[h]) - levels[h])
                if masked:
                    weights = jnp.where(mask, weights, 0.0)
                slope = (weights * (dot(values, dmt[h]) - deltas[h])).astype(jnp.bfloat16)
                dq[h] += dot(turned[h * HEAD : (h + 1) * HEAD], slope)
                probs.append(weights.astype(jnp.bfloat16))
                slopes.append(slope)
            dv = dot(jnp.concatenate(probs, axis=1), dm[...])
            dk = dot(jnp.concatenate(slopes, axis=1), qm[...])
            acc[span, 0:128] += dk[:, :128]
            acc[span, 128:256] += dk[:, 128:] + dv[:, :128]
            acc[span, 256:384] += dv[:, 128:]
            return inner

        walk(big, begin, end, low, high, step, 0)
        for h in range(GROUP):
            dqs[s, h * HEAD : (h + 1) * HEAD] = dq[h] * 0.125
        return carry

    lax.fori_loop(0, ZN // 2, functools.partial(one_block, True), 0)
    lax.fori_loop(ZN // 2, ZN, functools.partial(one_block, False), 0)
    half = HEAD // 2
    for b in range(ZN):
        back = pick([jnp.full_like(slots[b], s) for s in range(ZN)], slots[b], [dqs[s] for s in range(ZN)])
        for h in range(GROUP):
            at = h * HEAD
            w1, w2 = back[at : at + half], back[at + half : at + HEAD]
            dq_out[b, at : at + half] = (w1 * cosine[b] + w2 * sine[b]).astype(dq_out.dtype)
            dq_out[b, at + half : at + HEAD] = (w2 * cosine[b] - w1 * sine[b]).astype(dq_out.dtype)

    def finish(tile, carry):
        span = pl.ds(pl.multiple_of(tile * TILE, TILE), TILE)
        dkv_out[span, :] = acc[span, :].astype(dkv_out.dtype)
        return carry

    lax.fori_loop(0, tiles, finish, 0)


def attend_back(lengths, qt, kv, out, lse, dots, cosine, sine):
    blocks, rows, count = qt.shape
    whole = pl.BlockSpec(memory_space=pltpu.VMEM)
    return pl.pallas_call(
        backward_kernel,
        out_shape=[
            jax.ShapeDtypeStruct(qt.shape, jnp.bfloat16),
            jax.ShapeDtypeStruct(kv.shape, jnp.bfloat16),
        ],
        in_specs=[pl.BlockSpec(memory_space=pltpu.SMEM)] + [whole] * 7,
        out_specs=[whole] * 2,
        scratch_shapes=[
            pltpu.VMEM((GROUP, 256, count), jnp.bfloat16),
            pltpu.VMEM((GROUP * count, 256), jnp.bfloat16),
            pltpu.VMEM((GROUP, 256, count), jnp.bfloat16),
            pltpu.VMEM((GROUP * count, 256), jnp.bfloat16),
            pltpu.VMEM((GROUP, HEAD, count), jnp.float32),
            pltpu.VMEM(kv.shape, jnp.float32),
            pltpu.VMEM(qt.shape, jnp.bfloat16),
            pltpu.VMEM(qt.shape, jnp.bfloat16),
            pltpu.VMEM((blocks, 8, count), jnp.float32),
            pltpu.VMEM((blocks, 8, count), jnp.float32),
            pltpu.VMEM(qt.shape, jnp.float32),
        ],
        compiler_params=pltpu.CompilerParams(vmem_limit_bytes=67043328),
    )(lengths, qt, kv, out, lse, dots, cosine, sine)


KV_SLOTS = (0, 1, 2, 5, 3, 4)


def turn(rows, cosine, sine):
    first, second = rows[:, 0], rows[:, 1]
    return jnp.stack([first * cosine - second * sine, second * cosine + first * sine], axis=1)


def turn_back(rows, cosine, sine):
    first, second = rows[:, 0], rows[:, 1]
    return jnp.stack([first * cosine + second * sine, second * cosine - first * sine], axis=1)


def tables(lengths, first, count):
    starts = jnp.cumsum(lengths) - lengths
    position = first[:, None] + jnp.arange(count, dtype=jnp.int32)[None, :]
    begun = position[..., None] >= starts
    offsets = position - jnp.max(jnp.where(begun, starts, 0), axis=-1)
    half = HEAD // 2
    frequency = rope_base ** (-(jnp.arange(half, dtype=jnp.float32) * 2.0) / HEAD)
    angles = offsets.astype(jnp.float32)[:, None, :] * frequency[None, :, None]
    return jnp.cos(angles), jnp.sin(angles)


def contract(left, right, dims):
    return lax.dot_general(left, right, (dims, ((), ())), preferred_element_type=jnp.float32)


def local_grid(
    tokens,
    qkv_weight,
    out_weight,
    gate_weight,
    up_weight,
    down_weight,
    first_gain,
    first_bias,
    second_gain,
    second_bias,
    lengths,
    cotangent,
):
    bf16 = jnp.bfloat16
    rows, width = tokens.shape
    share = first_gain.shape[0]
    heads = width // HEAD
    half = HEAD // 2
    x, y, z, c = place()
    small = jnp.stack([first_gain, first_bias, second_gain, second_bias])
    small = jnp.pad(small, ((0, 4), (0, 128 - share)))
    hidden_width = gate_weight.shape[1]

    (qkv_blocks,) = gather([qkv_weight], ["bcast"], 1)
    qkv_full = qkv_blocks.reshape(width, 3 * width)
    turned = jnp.stack([block(x, y, b, c) for b in range(ZN)]) * rows
    cos_all, sin_all = tables(lengths, turned, rows)
    cosine = lax.dynamic_index_in_dim(cos_all, z, 0, keepdims=False)
    sine = lax.dynamic_index_in_dim(sin_all, z, 0, keepdims=False)

    raw = contract(qkv_full, tokens, ((0,), (1,))).astype(bf16)
    raw = raw.reshape(3, heads, 2, half, rows)
    queries = turn(raw[0].astype(jnp.float32), cosine, sine).astype(bf16)
    keys = turn(raw[1].astype(jnp.float32), cosine, sine).astype(bf16)
    queries = queries.reshape(ZN, GROUP * HEAD, rows)
    pairs = jnp.concatenate(
        [keys.reshape(ZN, GROUP, HEAD, rows), raw[2].reshape(ZN, GROUP, HEAD, rows)], axis=1
    )
    pairs = jnp.concatenate([pairs[:, s : s + 1] for s in KV_SLOTS], axis=1)
    pairs = jnp.swapaxes(pairs.reshape(ZN, 2 * GROUP * HEAD, rows), 1, 2)

    wide = jnp.concatenate([out_weight, gate_weight, up_weight], axis=1)
    pairs_all, queries, wide, down_full, small = gather(
        [pairs, queries, wide, down_weight, small], ["cross", "swap", "bcast", "bcast", "bcast"], 2
    )
    wide = wide.reshape(width, -1)
    out_full = wide[:, :width]
    both_full = wide[:, width:]
    down_full = down_full.reshape(hidden_width, width)
    gain_one, bias_one, gain_two, bias_two = [
        small[:, i, :share].reshape(width).astype(jnp.float32) for i in range(4)
    ]
    pairs_all = pairs_all.reshape(-1, 2 * GROUP * HEAD)
    low, attended, lse = attend(lengths, queries, pairs_all)
    (low,) = gather([low], ["swap"], 3)
    low = low.reshape(width, rows)

    attn_out = contract(low, out_full, ((0,), (0,)))
    first, scaled_one, inv_one = normalize(tokens.astype(jnp.float32) + attn_out, gain_one, bias_one)
    first_low = first.astype(bf16)
    both = product(first_low, both_full)
    gate_proj, up_proj = both[:, :hidden_width], both[:, hidden_width:]
    sigmoid_gate = jax.nn.sigmoid(gate_proj)
    silu_gate = gate_proj * sigmoid_gate
    hidden = (silu_gate * up_proj).astype(bf16)
    branch = product(hidden, down_full)
    second, scaled_two, inv_two = normalize(first + branch, gain_two, bias_two)
    layer_out = second.astype(bf16)

    upstream = cotangent.astype(jnp.float32)
    dz_two, gain_two_grad, bias_two_grad = normalize_back(upstream, scaled_two, inv_two, gain_two)
    dz_two_low = dz_two.astype(bf16)
    down_sum = contract(hidden, dz_two_low, ((0,), (0,))).astype(bf16)
    hidden_grad = contract(dz_two_low, down_full, ((1,), (1,)))
    gate_back = (
        hidden_grad * up_proj * sigmoid_gate * (1.0 + gate_proj * (1.0 - sigmoid_gate))
    ).astype(bf16)
    up_back = (hidden_grad * silu_gate).astype(bf16)
    both_back = jnp.concatenate([gate_back, up_back], axis=1)
    both_sum = contract(first_low, both_back, ((0,), (0,))).astype(bf16)
    first_back = dz_two + contract(both_back, both_full, ((1,), (1,)))
    dz_one, gain_one_grad, bias_one_grad = normalize_back(first_back, scaled_one, inv_one, gain_one)
    dz_one_low = dz_one.astype(bf16)
    out_sum = product(low, dz_one_low).astype(bf16)
    attended_back = contract(out_full, dz_one_low, ((1,), (1,))).astype(bf16)
    (attended_back,) = gather([attended_back.reshape(ZN, GROUP * HEAD, rows)], ["swap"], 4)

    query_back, pair_back = attend_back(
        lengths, queries, pairs_all, attended, lse, attended_back, cos_all, sin_all
    )
    small_sum = jnp.stack([gain_one_grad, bias_one_grad, gain_two_grad, bias_two_grad])
    small_sum = jnp.swapaxes(small_sum.reshape(4, BLOCKS, share), 0, 1)
    small_sum = jnp.pad(small_sum, ((0, 0), (0, 4), (0, 128 - share)))
    pair_back, query_back, out_grad, both_grad, down_grad, small_grad = reduce(
        [
            pair_back.reshape(BLOCKS, rows, 2 * GROUP * HEAD),
            query_back,
            out_sum.reshape(BLOCKS, share, width),
            both_sum.reshape(BLOCKS, share, 2 * hidden_width),
            down_sum.reshape(BLOCKS, -1, width),
            small_sum,
        ],
        ["cross", "swap", "reduce", "reduce", "reduce", "reduce"],
        5,
    )
    pair_back = jnp.swapaxes(pair_back, 1, 2).reshape(ZN, 2 * GROUP, HEAD, rows)
    pair_back = [pair_back[:, KV_SLOTS.index(s)] for s in range(2 * GROUP)]
    key_back = jnp.stack(pair_back[:GROUP], axis=1).reshape(heads, 2, half, rows)
    key_back = turn_back(key_back.astype(jnp.float32), cosine, sine).astype(bf16)
    value_back = jnp.stack(pair_back[GROUP:], axis=1)
    raw_back = jnp.concatenate(
        [
            query_back.reshape(width, rows),
            key_back.reshape(width, rows),
            value_back.reshape(width, rows),
        ],
        axis=0,
    )
    qkv_sum = contract(tokens, raw_back, ((0,), (1,))).astype(bf16)
    tokens_grad = (dz_one + contract(raw_back, qkv_full, ((0,), (1,)))).astype(bf16)
    (qkv_grad,) = reduce([qkv_sum.reshape(BLOCKS, share, 3 * width)], ["reduce"], 6)
    return (
        layer_out,
        tokens_grad,
        qkv_grad,
        out_grad,
        both_grad[:, :hidden_width],
        both_grad[:, hidden_width:],
        down_grad,
        small_grad[0, :share],
        small_grad[1, :share],
        small_grad[2, :share],
        small_grad[3, :share],
    )


def solution(mesh):
    rows = P(("cp", "hd"), None)
    line = P(("cp", "hd"))
    local = local_grid if (mesh.shape["cp"], mesh.shape["hd"]) == (ZN * YN * CN, XN) else local_any
    return jax.shard_map(
        local,
        mesh=mesh,
        in_specs=(rows,) * 6 + (line,) * 4 + (P(), rows),
        out_specs=(rows,) * 7 + (line,) * 4,
        check_vma=False,
    )
```

```python
import functools

import jax
import jax.numpy as jnp
from jax import lax
from jax.experimental import pallas as pl
from jax.experimental.pallas import tpu as pltpu
from jax.sharding import PartitionSpec as P

HD = 64
REACH = 8


rope_base = 1000.0
norm_eps = 1e-12
score_scale = 0.125
masked_score = -1000000000.0


def shifted(block, axis, distance):
    devices = range(lax.axis_size(axis))
    route = [(i - distance, i) for i in devices if i - distance in devices]
    return lax.ppermute(block, axis, route)


def doc_layout(lengths, first_row, row_count):
    starts = jnp.cumsum(lengths) - lengths
    position = first_row + jnp.arange(row_count, dtype=jnp.int32)
    at_or_after = position[:, None] >= starts[None, :]
    doc_ids = jnp.sum(at_or_after.astype(jnp.int32), axis=1) - 1
    doc_begin = jnp.max(jnp.where(at_or_after, starts[None, :], 0), axis=1)
    return (doc_ids, position - doc_begin)


def rope_tables(offsets, head_size):
    half_size = head_size // 2
    frequency = rope_base ** (-(jnp.arange(half_size, dtype=jnp.float32) * 2.0) / head_size)
    angles = offsets.astype(jnp.float32)[:, None] * frequency[None, :]
    return (jnp.cos(angles), jnp.sin(angles))


def rotate(values, cosine, sine):
    half_size = values.shape[-1] // 2
    first_half = values[..., :half_size]
    second_half = values[..., half_size:]
    cos_rows = cosine[:, None, :]
    sin_rows = sine[:, None, :]
    return jnp.concatenate(
        [
            first_half * cos_rows - second_half * sin_rows,
            second_half * cos_rows + first_half * sin_rows,
        ],
        axis=-1,
    )


def rotate_back(grads, cosine, sine):
    half_size = grads.shape[-1] // 2
    first_half = grads[..., :half_size]
    second_half = grads[..., half_size:]
    cos_rows = cosine[:, None, :]
    sin_rows = sine[:, None, :]
    return jnp.concatenate(
        [
            first_half * cos_rows + second_half * sin_rows,
            second_half * cos_rows - first_half * sin_rows,
        ],
        axis=-1,
    )


def normalize(hidden_in, gain_vec, bias_vec):
    average = jnp.mean(hidden_in, axis=-1, keepdims=True)
    centered = hidden_in - average
    variance = jnp.mean(centered * centered, axis=-1, keepdims=True)
    inv_std = lax.rsqrt(variance + norm_eps)
    scaled = centered * inv_std
    return (scaled * gain_vec + bias_vec, scaled, inv_std)


def normalize_back(upstream, scaled, inv_std, gain_vec):
    weighted = upstream * gain_vec
    inner = (
        weighted
        - jnp.mean(weighted, axis=-1, keepdims=True)
        - scaled * jnp.mean(weighted * scaled, axis=-1, keepdims=True)
    )
    return (inv_std * inner, jnp.sum(upstream * scaled, axis=0), jnp.sum(upstream, axis=0))


def product(left, right):
    return jnp.dot(left, right, preferred_element_type=jnp.float32)


def local_any(
    tokens,
    qkv_weight,
    out_weight,
    gate_weight,
    up_weight,
    down_weight,
    first_gain,
    first_bias,
    second_gain,
    second_bias,
    doc_lengths,
    cotangent,
):
    rows_here = tokens.shape[0]
    model_width = tokens.shape[1]
    hd_count = lax.axis_size("hd")
    cp_count = lax.axis_size("cp")
    cp_index = lax.axis_index("cp")
    block_rows = rows_here * hd_count
    local_width = model_width // hd_count
    local_heads = local_width // HD
    shifts = [0]
    for distance in range(1, REACH + 1):
        shifts = shifts + [-distance, distance]
    shards = (
        qkv_weight,
        out_weight,
        gate_weight,
        up_weight,
        down_weight,
        first_gain,
        first_bias,
        second_gain,
        second_bias,
    )
    weights = (
        lax.all_gather(shards[0], ("cp", "hd"), axis=0, tiled=True),
        lax.all_gather(shards[1], ("cp", "hd"), axis=0, tiled=True),
        lax.all_gather(shards[2], ("cp", "hd"), axis=0, tiled=True),
        lax.all_gather(shards[3], ("cp", "hd"), axis=0, tiled=True),
        lax.all_gather(shards[4], ("cp", "hd"), axis=0, tiled=True),
        lax.all_gather(shards[5], ("cp", "hd"), axis=0, tiled=True),
        lax.all_gather(shards[6], ("cp", "hd"), axis=0, tiled=True),
        lax.all_gather(shards[7], ("cp", "hd"), axis=0, tiled=True),
        lax.all_gather(shards[8], ("cp", "hd"), axis=0, tiled=True),
    )
    (
        qkv_full,
        out_full,
        gate_full,
        up_full,
        down_full,
        gain_first,
        bias_first,
        gain_second,
        bias_second,
    ) = weights
    raw_rows = product(tokens, qkv_full).astype(jnp.bfloat16)
    grouped = lax.all_to_all(
        raw_rows.reshape(rows_here, 3, hd_count, local_width),
        "hd",
        split_axis=2,
        concat_axis=0,
        tiled=True,
    )
    grouped = grouped.reshape(block_rows, 3, local_width)
    query_docs, offsets = doc_layout(doc_lengths, cp_index * block_rows, block_rows)
    cosine, sine = rope_tables(offsets, HD)
    queries = rotate(
        grouped[:, 0].astype(jnp.float32).reshape(block_rows, local_heads, HD), cosine, sine
    ).astype(jnp.bfloat16)
    key_rows = rotate(
        grouped[:, 1].astype(jnp.float32).reshape(block_rows, local_heads, HD), cosine, sine
    ).astype(jnp.bfloat16)
    own_block = jnp.stack([key_rows.reshape(block_rows, local_width), grouped[:, 2]], axis=1)

    def key_docs(distance):
        source = cp_index - distance
        doc_ids, unused_offsets = doc_layout(doc_lengths, source * block_rows, block_rows)
        inside = jnp.logical_and(source >= 0, source < cp_count)
        return jnp.where(inside, doc_ids, -2)

    remote = [own_block] + [shifted(own_block, "cp", distance) for distance in shifts[1:]]
    masks = [query_docs[:, None] == key_docs(distance)[None, :] for distance in shifts]

    def scores_with(query_part, remote_block, key_mask):
        key_part = remote_block[:, 0].reshape(block_rows, local_heads, HD)
        raw_scores = (
            jnp.einsum("qhd,khd->hqk", query_part, key_part, preferred_element_type=jnp.float32)
            * score_scale
        )
        return jnp.where(key_mask[None], raw_scores, masked_score)

    def scores_for(remote_block, key_mask):
        return scores_with(queries, remote_block, key_mask)

    running_max = jnp.full((local_heads, block_rows), masked_score, jnp.float32)
    running_sum = jnp.zeros((local_heads, block_rows), jnp.float32)
    for remote_block, key_mask in zip(remote, masks):
        block_scores = scores_for(remote_block, key_mask)
        new_max = jnp.maximum(running_max, jnp.max(block_scores, axis=-1))
        running_sum = running_sum * jnp.exp(running_max - new_max) + jnp.sum(
            jnp.exp(block_scores - new_max[:, :, None]), axis=-1
        )
        running_max = new_max
    log_total = running_max + jnp.log(running_sum)
    attended = jnp.zeros((block_rows, local_heads, HD), jnp.float32)
    for remote_block, key_mask in zip(remote, masks):
        block_scores = scores_for(remote_block, key_mask)
        probs = jnp.exp(block_scores - log_total[:, :, None]).astype(jnp.bfloat16)
        value_part = remote_block[:, 1].reshape(block_rows, local_heads, HD)
        attended = attended + jnp.einsum(
            "hqk,khd->qhd", probs, value_part, preferred_element_type=jnp.float32
        )
    attended_send = attended.reshape(block_rows, 1, local_width).astype(jnp.bfloat16)
    attended_low = lax.all_to_all(
        attended_send, "hd", split_axis=0, concat_axis=1, tiled=True
    ).reshape(rows_here, model_width)
    gain_one = gain_first.astype(jnp.float32)
    gain_two = gain_second.astype(jnp.float32)
    attn_out = product(attended_low, out_full)
    first, scaled_one, inv_one = normalize(
        tokens.astype(jnp.float32) + attn_out, gain_one, bias_first.astype(jnp.float32)
    )
    first_low = first.astype(jnp.bfloat16)
    gate_proj = product(first_low, gate_full)
    up_proj = product(first_low, up_full)
    sigmoid_gate = jax.nn.sigmoid(gate_proj)
    silu_gate = gate_proj * sigmoid_gate
    hidden = (silu_gate * up_proj).astype(jnp.bfloat16)
    branch = product(hidden, down_full)
    second, scaled_two, inv_two = normalize(
        first + branch, gain_two, bias_second.astype(jnp.float32)
    )
    layer_out = second.astype(jnp.bfloat16)
    weights = (
        lax.all_gather(shards[0], ("cp", "hd"), axis=0, tiled=True),
        lax.all_gather(shards[1], ("cp", "hd"), axis=0, tiled=True),
        lax.all_gather(shards[2], ("cp", "hd"), axis=0, tiled=True),
        lax.all_gather(shards[3], ("cp", "hd"), axis=0, tiled=True),
        lax.all_gather(shards[4], ("cp", "hd"), axis=0, tiled=True),
        lax.all_gather(shards[5], ("cp", "hd"), axis=0, tiled=True),
        lax.all_gather(shards[6], ("cp", "hd"), axis=0, tiled=True),
        lax.all_gather(shards[7], ("cp", "hd"), axis=0, tiled=True),
        lax.all_gather(shards[8], ("cp", "hd"), axis=0, tiled=True),
    )
    (
        qkv_full,
        out_full,
        gate_full,
        up_full,
        down_full,
        gain_first,
        bias_first,
        gain_second,
        bias_second,
    ) = weights
    upstream = cotangent.astype(jnp.float32)
    dz_two, gain_two_grad, bias_two_grad = normalize_back(upstream, scaled_two, inv_two, gain_two)
    dz_two_low = dz_two.astype(jnp.bfloat16)
    down_sum = product(hidden.T, dz_two_low)
    hidden_grad = product(dz_two_low, down_full.T)
    gate_back = (
        hidden_grad * up_proj * sigmoid_gate * (1.0 + gate_proj * (1.0 - sigmoid_gate))
    ).astype(jnp.bfloat16)
    up_back = (hidden_grad * silu_gate).astype(jnp.bfloat16)
    gate_sum = product(first_low.T, gate_back)
    up_sum = product(first_low.T, up_back)
    first_back = dz_two + product(gate_back, gate_full.T) + product(up_back, up_full.T)
    dz_one, gain_one_grad, bias_one_grad = normalize_back(first_back, scaled_one, inv_one, gain_one)
    dz_one_low = dz_one.astype(jnp.bfloat16)
    out_sum = product(attended_low.T, dz_one_low)
    attended_back = product(dz_one_low, out_full.T).astype(jnp.bfloat16)
    heads_back = lax.all_to_all(
        attended_back.reshape(rows_here, hd_count, local_width),
        "hd",
        split_axis=1,
        concat_axis=0,
        tiled=True,
    )
    heads_back = heads_back.reshape(block_rows, local_heads, HD)
    delta = jnp.transpose(jnp.sum(heads_back.astype(jnp.float32) * attended, axis=-1))
    query_grad = jnp.zeros((block_rows, local_heads, HD), jnp.float32)
    pair_total = jnp.zeros((block_rows, 2, local_width), jnp.float32)
    remote = [own_block] + [shifted(own_block, "cp", distance) for distance in shifts[1:]]
    for distance, remote_block, key_mask in zip(shifts, remote, masks):
        pair_block_scores = scores_with(queries, remote_block, key_mask)
        pair_probs = jnp.exp(pair_block_scores - log_total[:, :, None])
        pair_key_part = remote_block[:, 0].reshape(block_rows, local_heads, HD)
        pair_value_part = remote_block[:, 1].reshape(block_rows, local_heads, HD)
        value_grad = jnp.einsum(
            "hqk,qhd->khd",
            pair_probs.astype(jnp.bfloat16),
            heads_back,
            preferred_element_type=jnp.float32,
        )
        prob_grad = jnp.einsum(
            "qhd,khd->hqk", heads_back, pair_value_part, preferred_element_type=jnp.float32
        )
        score_grad = (pair_probs * (prob_grad - delta[:, :, None])).astype(jnp.bfloat16)
        query_term = (
            jnp.einsum(
                "hqk,khd->qhd", score_grad, pair_key_part, preferred_element_type=jnp.float32
            )
            * score_scale
        )
        key_grad = (
            jnp.einsum("hqk,qhd->khd", score_grad, queries, preferred_element_type=jnp.float32)
            * score_scale
        )
        grad_pair = jnp.stack(
            [
                key_grad.reshape(block_rows, local_width),
                value_grad.reshape(block_rows, local_width),
            ],
            axis=1,
        )
        query_term, grad_pair = (query_term, grad_pair)
        query_grad = query_grad + query_term
        if distance == 0:
            pair_total = grad_pair
        else:
            pair_total = pair_total + shifted(
                grad_pair.astype(jnp.bfloat16), "cp", -distance
            ).astype(grad_pair.dtype)
    query_back = rotate_back(query_grad, cosine, sine).reshape(block_rows, local_width)
    key_back = rotate_back(
        pair_total[:, 0].reshape(block_rows, local_heads, HD), cosine, sine
    ).reshape(block_rows, local_width)
    raw_back = jnp.stack([query_back, key_back, pair_total[:, 1]], axis=1).astype(jnp.bfloat16)
    raw_back = lax.all_to_all(
        raw_back.reshape(block_rows, 3, 1, local_width),
        "hd",
        split_axis=0,
        concat_axis=2,
        tiled=True,
    )
    raw_back = raw_back.reshape(rows_here, 3 * model_width)
    qkv_sum = product(tokens.T, raw_back)
    tokens_grad = (dz_one + product(raw_back, qkv_full.T)).astype(jnp.bfloat16)
    summed = (
        lax.psum_scatter(qkv_sum, ("cp", "hd"), scatter_dimension=0, tiled=True),
        lax.psum_scatter(out_sum, ("cp", "hd"), scatter_dimension=0, tiled=True),
        lax.psum_scatter(gate_sum, ("cp", "hd"), scatter_dimension=0, tiled=True),
        lax.psum_scatter(up_sum, ("cp", "hd"), scatter_dimension=0, tiled=True),
        lax.psum_scatter(down_sum, ("cp", "hd"), scatter_dimension=0, tiled=True),
        lax.psum_scatter(gain_one_grad, ("cp", "hd"), scatter_dimension=0, tiled=True),
        lax.psum_scatter(bias_one_grad, ("cp", "hd"), scatter_dimension=0, tiled=True),
        lax.psum_scatter(gain_two_grad, ("cp", "hd"), scatter_dimension=0, tiled=True),
        lax.psum_scatter(bias_two_grad, ("cp", "hd"), scatter_dimension=0, tiled=True),
    )
    return (
        layer_out,
        tokens_grad,
        summed[0],
        summed[1],
        summed[2],
        summed[3],
        summed[4],
        summed[5],
        summed[6],
        summed[7],
        summed[8],
    )


MESH = pl.DeviceIdType.MESH
ZN, YN, CN, XN = 4, 2, 2, 2
BLOCKS = ZN * YN * CN * XN


def place():
    cp = lax.axis_index("cp")
    x = lax.axis_index("hd")
    return x, lax.rem(cp // CN, YN), cp // (YN * CN), lax.rem(cp, CN)


def device(x, y, z, c):
    return ((z * YN + y) * CN + c, x)


def block(x, y, z, c):
    return ((z * YN + y) * CN + c) * XN + x


def when(cond, fn):
    if cond is None:
        fn()
    else:
        pl.when(cond)(fn)


def both(a, b):
    if a is None:
        return b
    if b is None:
        return a
    return jnp.logical_and(a, b)


def halves(ref):
    rows, cols = ref.shape[-2:]
    if rows % 32 == 0:
        return ref.at[pl.ds(0, rows // 2)], ref.at[pl.ds(rows // 2, rows // 2)]
    if cols % 256 == 0:
        return ref.at[:, pl.ds(0, cols // 2)], ref.at[:, pl.ds(cols // 2, cols // 2)]
    return ref, None


def greet(x, y, z, c, far):
    barrier = pltpu.get_barrier_semaphore()
    for peer in (device(1 - x, y, z, c), device(x, 1 - y, z, c), device(x, y, z, 1 - c)):
        pl.semaphore_signal(barrier, inc=1, device_id=peer, device_id_type=MESH)
    count = 3
    if far:
        for k in range(1, ZN):
            peer = device(x, y, lax.rem(z + k, ZN), c)
            pl.semaphore_signal(barrier, inc=1, device_id=peer, device_id_type=MESH)
        count = count + ZN - 1
    else:
        pl.when(z > 0)(lambda: pl.semaphore_signal(barrier, inc=1, device_id=device(x, y, z - 1, c), device_id_type=MESH))
        pl.when(z < ZN - 1)(lambda: pl.semaphore_signal(barrier, inc=1, device_id=device(x, y, z + 1, c), device_id_type=MESH))
        count = count + (z > 0).astype(jnp.int32) + (z < ZN - 1).astype(jnp.int32)
    pl.semaphore_wait(barrier, count)


SENDS = 40
RECVS = 36


CHAINED = ("bcast", "by_x", "by_y")
REST = ("rest_x", "rest_y")


def gather_kernel(modes, *refs):
    n = len(modes)
    ins, refs = refs[:n], refs[n:]
    refs = refs[sum(mode in REST for mode in modes) :]
    outs, (lsem, ssem, rsem) = refs[:n], refs[n:]
    x, y, z, c = place()
    ox, oy, oc = 1 - x, 1 - y, 1 - c
    greet(x, y, z, c, any(m in ("swap", "cross") for m in modes))
    sent = []

    def copy(k, src, dst, s, r, peer):
        return pltpu.make_async_remote_copy(
            src_ref=src,
            dst_ref=dst,
            send_sem=ssem.at[k, s],
            recv_sem=rsem.at[k, r],
            device_id=peer,
            device_id_type=MESH,
        )

    def send(cond, *args):
        when(cond, lambda: copy(*args).start())
        sent.append((cond, args))

    def arrived(cond, k, ref, r):
        when(cond, lambda: copy(k, ref, ref, 0, r, device(ox, y, z, c)).wait_recv())

    locals_ = []

    def keep(k, i, mine, spot):
        pltpu.make_async_copy(mine, spot, lsem.at[k, i]).start()
        locals_.append((k, i, mine, spot))

    for k, mode in enumerate(modes):
        if mode in CHAINED:
            keep(k, 0, ins[k], outs[k].at[block(x, y, z, c)])
        elif mode == "swap":
            keep(k, 0, ins[k].at[z], outs[k].at[z])
        elif mode == "cross":
            keep(k, 0, ins[k].at[z], outs[k].at[block(x, y, z, c)])

    def spread(k, cond, b, src, up, down):
        here = outs[k].at[block(x, y, b, c)]
        if modes[k] in CHAINED:
            if up is not False:
                send(both(cond, up), k, src, here, b, b, device(x, y, lax.rem(z + 1, ZN), c))
            if down is not False:
                send(both(cond, down), k, src, here, 4 + b, b, device(x, y, lax.rem(z + ZN - 1, ZN), c))
        if modes[k] != "by_y":
            send(cond, k, src, here, 8 + b, 4 + b, device(ox, y, z, c))
        if modes[k] != "by_x":
            send(cond, k, src, here, 16 + b, 12 + b, device(x, oy, z, c))
        send(cond, k, src, here, 24 + b, 20 + b, device(x, y, z, oc))

    def sides(k, cond, b):
        fx = outs[k].at[block(ox, y, b, c)]
        fy = outs[k].at[block(x, oy, b, c)]
        full = modes[k] in ("bcast", "cross")
        if modes[k] != "by_y":
            arrived(cond, k, fx, 4 + b)
            first, _ = halves(fx)
            if full:
                send(cond, k, first, first, 20 + b, 16 + b, device(x, oy, z, c))
            send(cond, k, fx, fx, 28 + b, 24 + b, device(x, y, z, oc))
        if modes[k] != "by_x":
            arrived(cond, k, fy, 12 + b)
            _, second = halves(fy)
            if full and second is not None:
                send(cond, k, second, second, 12 + b, 8 + b, device(ox, y, z, c))
            send(cond, k, fy, fy, 32 + b, 28 + b, device(x, y, z, oc))

    def corner(k, cond, b):
        far = outs[k].at[block(ox, oy, b, c)]
        first, second = halves(far)
        arrived(cond, k, first, 16 + b)
        if second is not None:
            arrived(cond, k, second, 8 + b)
        send(cond, k, far, far, 36 + b, 32 + b, device(x, y, z, oc))

    def steps(distance):
        if distance == 0:
            return [(None, z)]
        return [(z >= distance, jnp.maximum(z - distance, 0)), (z + distance < ZN, jnp.minimum(z + distance, ZN - 1))]

    for k, mode in enumerate(modes):
        if mode in CHAINED:
            spread(k, None, z, ins[k], z < ZN - 1, z > 0)
        elif mode in REST:
            for b in range(ZN):
                for j in range(2):
                    spot = block(j, oy, b, c) if mode == "rest_y" else block(ox, j, b, c)
                    keep(k, 2 * b + j, ins[k].at[2 * b + j], outs[k].at[spot])
                    send(None, k, ins[k].at[2 * b + j], outs[k].at[spot], 2 * b + j, 2 * b + j, device(x, y, z, oc))
        else:
            for d in range(1, ZN):
                to = lax.rem(z + d, ZN)
                spot = outs[k].at[z] if mode == "swap" else outs[k].at[block(x, y, z, c)]
                send(None, k, ins[k].at[to], spot, to, z, device(x, y, to, c))
            if mode == "cross":
                spread(k, None, z, ins[k].at[z], False, False)

    active = [k for k, mode in enumerate(modes) if mode in CHAINED or mode == "cross"]
    full = [k for k in active if modes[k] in ("bcast", "cross")]
    for distance in range(1, ZN + 2 if active else 0):
        if distance < ZN:
            for side, (cond, b) in enumerate(steps(distance)):
                for k in active:
                    arrived(cond, k, outs[k].at[block(x, y, b, c)], b)
                    here = outs[k].at[block(x, y, b, c)]
                    spread(k, cond, b, here, z < ZN - 1 if side == 0 else False, z > 0 if side == 1 else False)
        if 0 <= distance - 1 < ZN:
            for cond, b in steps(distance - 1):
                for k in active:
                    sides(k, cond, b)
        if 0 <= distance - 2 < ZN:
            for cond, b in steps(distance - 2):
                for k in full:
                    corner(k, cond, b)
    for k, mode in enumerate(modes):
        if mode == "swap":
            for d in range(1, ZN):
                frm = lax.rem(z + d, ZN)
                arrived(None, k, outs[k].at[frm], frm)
        elif mode in REST:
            for b in range(ZN):
                for j in range(2):
                    spot = block(j, oy, b, oc) if mode == "rest_y" else block(ox, j, b, oc)
                    arrived(None, k, outs[k].at[spot], 2 * b + j)
        else:
            quads = {"by_x": (0, 1), "by_y": (0, 2)}.get(mode, (0, 1, 2, 3))
            for b in range(ZN):
                for j in quads:
                    px, py = ((x, y), (ox, y), (x, oy), (ox, oy))[j]
                    arrived(None, k, outs[k].at[block(px, py, b, oc)], 20 + 4 * j + b)
    for k, i, mine, spot in locals_:
        pltpu.make_async_copy(mine, spot, lsem.at[k, i]).wait()
    for cond, args in sent:
        when(cond, lambda args=args: copy(*args).wait_send())


def gather(arrays, modes, collective_id, filled=()):
    shapes = []
    rest = [k for k, mode in enumerate(modes) if mode in REST]
    for k, (a, mode) in enumerate(zip(arrays, modes)):
        if mode in CHAINED:
            shapes.append((BLOCKS,) + a.shape)
        elif mode == "swap":
            shapes.append(a.shape)
        else:
            shapes.append((BLOCKS,) + a.shape[1:])
    n = len(arrays)
    return pl.pallas_call(
        functools.partial(gather_kernel, tuple(modes)),
        out_shape=[jax.ShapeDtypeStruct(s, a.dtype) for s, a in zip(shapes, arrays)],
        in_specs=[pl.BlockSpec(memory_space=pl.ANY)] * (n + len(rest)),
        out_specs=[pl.BlockSpec(memory_space=pl.ANY)] * n,
        input_output_aliases={n + i: k for i, k in enumerate(rest)},
        scratch_shapes=[
            pltpu.SemaphoreType.DMA((n, 8)),
            pltpu.SemaphoreType.DMA((n, SENDS)),
            pltpu.SemaphoreType.DMA((n, RECVS)),
        ],
        compiler_params=pltpu.CompilerParams(collective_id=collective_id, has_side_effects=True),
    )(*arrays, *filled)


def chunk_of(cols):
    for size in (768, 640, 512, 384, 256, 128):
        if cols % size == 0:
            return size
    return cols


def add_up(dst, sources):
    rows, cols = dst.shape[-2:]
    size = chunk_of(cols)

    def step(i, carry):
        span = pl.ds(pl.multiple_of(i * size, size), size)
        total = sources[0][:, span].astype(jnp.float32)
        for source in sources[1:]:
            total = total + source[:, span].astype(jnp.float32)
        dst[:, span] = total.astype(dst.dtype)
        return carry

    if cols == size:
        total = sources[0][...].astype(jnp.float32)
        for source in sources[1:]:
            total = total + source[...].astype(jnp.float32)
        dst[...] = total.astype(dst.dtype)
    else:
        lax.fori_loop(0, cols // size, step, 0)


BUFFERS = {"swap": 0, "pair_x": 2, "pair_y": 2, "cross": 3, "reduce": 4, "rest_x": 4, "rest_y": 4}
PAIR = ("pair_x", "pair_y")


def take(refs, counts):
    groups = []
    for count in counts:
        groups.append(refs[:count])
        refs = refs[count:]
    return groups, refs


def reduce_kernel(modes, *refs):
    n = len(modes)
    ins, refs = take(refs, [2 if mode in REST else 1 for mode in modes])
    outs, refs = take(refs, [2 if mode in PAIR else 1 for mode in modes])
    (lsem, ssem, rsem), scratch = refs[:3], refs[3:]
    bufs, _ = take(scratch, [BUFFERS[mode] for mode in modes])
    others, seconds = ins, outs
    ins, outs = [group[0] for group in ins], [group[0] for group in outs]
    x, y, z, c = place()
    ox, oy, oc = 1 - x, 1 - y, 1 - c
    greet(x, y, z, c, any(m in ("swap", "cross") for m in modes))
    sent = []

    def copy(k, src, dst, s, r, peer):
        return pltpu.make_async_remote_copy(
            src_ref=src,
            dst_ref=dst,
            send_sem=ssem.at[k, s],
            recv_sem=rsem.at[k, r],
            device_id=peer,
            device_id_type=MESH,
        )

    def send(cond, *args):
        when(cond, lambda: copy(*args).start())
        sent.append((cond, args))

    def arrived(cond, k, ref, r):
        when(cond, lambda: copy(k, ref, ref, 0, r, device(ox, y, z, c)).wait_recv())

    half = z // 2
    order = [3 - 3 * half, 2 - half, 1 - z + 4 * half, z]
    quads = ((ox, oy), (ox, y), (x, oy), (x, y))
    active = [k for k, mode in enumerate(modes) if mode in ("cross", "reduce")]
    paired = [k for k, mode in enumerate(modes) if mode in PAIR]
    rest = [k for k, mode in enumerate(modes) if mode in REST]

    for i, b in enumerate(order):
        for k in active:
            acc, cor = bufs[k][:2]
            for j, (px, py) in enumerate(quads):
                send(None, k, ins[k].at[block(px, py, b, oc)], cor.at[4 * i + j], 4 * i + j, 4 * i + j, device(x, y, z, oc))
                pltpu.make_async_copy(ins[k].at[block(px, py, b, c)], acc.at[4 * i + j], lsem.at[k, 4 * i + j]).start()
    for k in rest:
        acc, rec = bufs[k][:2]
        for i, b in enumerate(order):
            for j in range(2):
                mine = (x, y)[modes[k] == "rest_x"]
                spot = 2 * b + (mine if j else 1 - mine)
                pltpu.make_async_copy(ins[k].at[spot], acc.at[2 * i + j], lsem.at[k, 2 * i + j]).start()
                pltpu.make_async_copy(others[k][1].at[spot], rec.at[2 * i + j], lsem.at[k, 8 + 2 * i + j]).start()

    def spots(k, i):
        b, j = i // 2, i % 2
        if modes[k] == "pair_y":
            return (j, y, b), (j, oy, b)
        return (x, j, b), (ox, j, b)

    for k in paired:
        acc, cor = bufs[k]
        for i in range(8):
            for s, (px, py, b) in enumerate(spots(k, i)):
                send(None, k, ins[k].at[block(px, py, b, oc)], cor.at[2 * i + s], 2 * i + s, 2 * i + s, device(x, y, z, oc))
                pltpu.make_async_copy(ins[k].at[block(px, py, b, c)], acc.at[2 * i + s], lsem.at[k, 2 * i + s]).start()
    for k, mode in enumerate(modes):
        if mode == "swap":
            for d in range(1, ZN):
                to = lax.rem(z + d, ZN)
                send(None, k, ins[k].at[to], outs[k].at[z], d, z, device(x, y, to, c))
            pltpu.make_async_copy(ins[k].at[z], outs[k].at[z], lsem.at[k, 0]).start()

    def loaded(k, i, j):
        acc, cor = bufs[k][:2]
        pltpu.make_async_copy(ins[k].at[0], acc.at[4 * i + j], lsem.at[k, 4 * i + j]).wait()
        arrived(None, k, cor.at[4 * i + j], 4 * i + j)

    for k in paired:
        acc, cor = bufs[k]

        def join(i, carry, k=k, acc=acc, cor=cor):
            for s in range(2):
                at = 2 * i + s
                pltpu.make_async_copy(ins[k].at[0], acc.at[at], lsem.at[k, at]).wait()
                arrived(None, k, cor.at[at], at)
                add_up(seconds[k][s].at[i], (acc.at[at], cor.at[at]))
            return carry

        lax.fori_loop(0, 8, join, 0)

    def fetched(k, i, j):
        acc, rec = bufs[k][:2]
        pltpu.make_async_copy(ins[k].at[0], acc.at[2 * i + j], lsem.at[k, 2 * i + j]).wait()
        pltpu.make_async_copy(ins[k].at[0], rec.at[2 * i + j], lsem.at[k, 8 + 2 * i + j]).wait()

    for i, b in enumerate(order):
        for k in rest:
            acc, rec, side = bufs[k][:3]
            fetched(k, i, 0)
            add_up(acc.at[2 * i], (acc.at[2 * i], rec.at[2 * i]))
            peer = device(x, oy, z, c) if modes[k] == "rest_x" else device(ox, y, z, c)
            send(None, k, acc.at[2 * i], side.at[i], 16 + i, 16 + i, peer)
        for k in active:
            acc, cor, side = bufs[k][:3]
            loaded(k, i, 0)
            add_up(acc.at[4 * i], (acc.at[4 * i], cor.at[4 * i]))
            first, second = halves(acc.at[4 * i])
            send(None, k, first, halves(side.at[i])[0], 16 + i, 16 + i, device(x, oy, z, c))
            if second is not None:
                send(None, k, second, halves(side.at[4 + i])[1], 20 + i, 20 + i, device(ox, y, z, c))
    for i, b in enumerate(order):
        for k in active:
            acc, cor, side = bufs[k][:3]
            loaded(k, i, 1)
            add_up(acc.at[4 * i + 1], (acc.at[4 * i + 1], cor.at[4 * i + 1]))
            part = halves(side.at[i])[0]
            arrived(None, k, part, 16 + i)
            mine = halves(acc.at[4 * i + 1])[0]
            add_up(mine, (mine, part))
            send(None, k, acc.at[4 * i + 1], side.at[8 + i], 24 + i, 24 + i, device(ox, y, z, c))
            loaded(k, i, 2)
            add_up(acc.at[4 * i + 2], (acc.at[4 * i + 2], cor.at[4 * i + 2]))
            part = halves(side.at[4 + i])[1]
            if part is not None:
                arrived(None, k, part, 20 + i)
                mine = halves(acc.at[4 * i + 2])[1]
                add_up(mine, (mine, part))
            send(None, k, acc.at[4 * i + 2], side.at[12 + i], 28 + i, 28 + i, device(x, oy, z, c))
    for i, b in enumerate(order):
        for k in sorted(active + rest):
            side = bufs[k][2]
            if k in rest:
                acc, rec = bufs[k][:2]
                fetched(k, i, 1)
                arrived(None, k, side.at[i], 16 + i)
                own = acc.at[2 * i + 1]
                terms = (own, rec.at[2 * i + 1], side.at[i])
            else:
                acc, cor = bufs[k][:2]
                loaded(k, i, 3)
                own = acc.at[4 * i + 3]
                arrived(None, k, side.at[8 + i], 24 + i)
                arrived(None, k, side.at[12 + i], 28 + i)
                terms = (own, cor.at[4 * i + 3], side.at[8 + i], side.at[12 + i])
            if modes[k] == "cross":
                add_up(own, terms)
                if i < ZN - 1:
                    send(None, k, own, outs[k].at[z], 32 + i, 32 + z, device(x, y, b, c))
                else:
                    pltpu.make_async_copy(own, outs[k].at[z], lsem.at[k, 16]).start()
                continue
            chain = bufs[k][3]
            if i == ZN - 1:
                add_up(outs[k], terms)

                def lower(k=k, chain=chain):
                    arrived(None, k, chain.at[z], 32 + z)
                    add_up(outs[k], (outs[k], chain.at[z]))

                def upper(k=k, chain=chain):
                    arrived(None, k, chain.at[4 + z], 36 + z)
                    add_up(outs[k], (outs[k], chain.at[4 + z]))

                pl.when(z > 0)(lower)
                pl.when(z < ZN - 1)(upper)
            else:
                add_up(own, terms)
                below = both(b > z, z > 0)
                above = both(b < z, z < ZN - 1)

                def lower(k=k, chain=chain, own=own, b=b):
                    arrived(None, k, chain.at[b], 32 + b)
                    add_up(own, (own, chain.at[b]))

                def upper(k=k, chain=chain, own=own, b=b):
                    arrived(None, k, chain.at[4 + b], 36 + b)
                    add_up(own, (own, chain.at[4 + b]))

                pl.when(below)(lower)
                pl.when(above)(upper)
                send(b > z, k, own, chain.at[b], 32 + i, 32 + b, device(x, y, lax.rem(z + 1, ZN), c))
                send(b < z, k, own, chain.at[4 + b], 32 + i, 36 + b, device(x, y, lax.rem(z + ZN - 1, ZN), c))
    for k, mode in enumerate(modes):
        if mode not in ("swap", "cross"):
            continue
        for d in range(1, ZN):
            frm = lax.rem(z + d, ZN)
            arrived(None, k, outs[k].at[frm], frm if mode == "swap" else 32 + frm)
        if mode == "swap":
            pltpu.make_async_copy(ins[k].at[z], outs[k].at[z], lsem.at[k, 0]).wait()
        else:
            pltpu.make_async_copy(bufs[k][0].at[15], outs[k].at[z], lsem.at[k, 16]).wait()
    for cond, args in sent:
        when(cond, lambda args=args: copy(*args).wait_send())


def reduce(arrays, modes, collective_id):
    shapes, specs, scratch, operands = [], [], [], []
    anywhere, local = pl.BlockSpec(memory_space=pl.ANY), pl.BlockSpec(memory_space=pltpu.VMEM)
    for a, mode in zip(arrays, modes):
        operands = operands + (list(a) if mode in REST else [a])
        a = a[0] if mode in REST else a
        rows, cols = a.shape[1:]
        sizes = {"swap": (), "pair_x": (16, 16), "cross": (16, 16, 16), "reduce": (16, 16, 16, 8), "rest_x": (8, 8, 4, 8)}
        sizes = sizes[mode.replace("_y", "_x")]
        scratch = scratch + [pltpu.VMEM((size, rows, cols), a.dtype) for size in sizes]
        if mode == "swap":
            shapes.append(jax.ShapeDtypeStruct(a.shape, a.dtype))
            specs.append(anywhere)
        elif mode in PAIR:
            shapes = shapes + [jax.ShapeDtypeStruct((8, rows, cols), a.dtype)] * 2
            specs = specs + [local] * 2
        elif mode == "cross":
            shapes.append(jax.ShapeDtypeStruct((ZN, rows, cols), a.dtype))
            specs.append(anywhere)
        else:
            shapes.append(jax.ShapeDtypeStruct((rows, cols), jnp.float32))
            specs.append(local)
    n = len(arrays)
    return pl.pallas_call(
        functools.partial(reduce_kernel, tuple(modes)),
        out_shape=shapes,
        in_specs=[anywhere] * len(operands),
        out_specs=specs,
        scratch_shapes=[
            pltpu.SemaphoreType.DMA((n, 17)),
            pltpu.SemaphoreType.DMA((n, SENDS)),
            pltpu.SemaphoreType.DMA((n, SENDS)),
        ]
        + scratch,
        compiler_params=pltpu.CompilerParams(
            collective_id=collective_id, has_side_effects=True, vmem_limit_bytes=67043328
        ),
    )(*operands)


HEAD = 64
GROUP = 3
TILE = 512
WIDE = 1024
EDGE = 128
SPAN = 4096
FAR = 1 << 30


def longest(lengths):
    begin, best, at = jnp.int32(0), lengths[0], jnp.int32(0)
    for j in range(lengths.shape[0]):
        length = lengths[j]
        at = jnp.where(length > best, begin, at)
        best = jnp.maximum(best, length)
        begin = begin + length
    return at, at + best


def lane_slots(lengths, count):
    x, y, z, c = place()
    lane = lax.broadcasted_iota(jnp.int32, (1, count), 1)
    begin, end = longest(lengths)
    spots = [block(x, y, b, c) * count + lane for b in range(ZN)]
    slots, before = [], jnp.zeros((1, count), jnp.int32)
    for b in range(ZN):
        big = jnp.logical_and(spots[b] >= begin, spots[b] < end)
        slots.append(jnp.where(big, before, ZN // 2 + b - before))
        before = before + big.astype(jnp.int32)
    return begin, end, spots, slots


def pick(slots, slot, parts):
    chosen = parts[-1]
    for b in range(len(parts) - 2, -1, -1):
        chosen = jnp.where(slots[b] == slot, parts[b], chosen)
    return chosen


def bounds_of(lengths, spot):
    low, high = jnp.zeros_like(spot), jnp.full_like(spot, FAR)
    begin = jnp.int32(0)
    for j in range(lengths.shape[0]):
        end = begin + lengths[j]
        low = jnp.where(spot >= begin, begin, low)
        high = jnp.where(spot < end, jnp.minimum(high, end), high)
        begin = end
    return low, high


def walk(big, begin, end, low, high, step, init):
    if big:
        base = begin // EDGE * EDGE

        def body(i, carry):
            at = pl.multiple_of(base + i * WIDE, EDGE)
            return step(at, WIDE, False, carry)

        carry = step(pl.multiple_of(base, EDGE), WIDE, True, init)
        carry = lax.fori_loop(1, SPAN // WIDE, body, carry)
        return lax.cond(
            begin > base,
            lambda c: step(pl.multiple_of(base + SPAN, EDGE), EDGE, True, c),
            lambda c: c,
            carry,
        )
    first = jnp.min(low) // TILE
    stop = (jnp.max(high) + TILE - 1) // TILE
    hole_first = jnp.maximum((begin + TILE - 1) // TILE, first)
    hole = jnp.maximum(jnp.minimum(end // TILE, stop) - hole_first, 0)

    def body(i, carry):
        tile = first + i
        tile = jnp.where(jnp.logical_and(hole > 0, tile >= hole_first), tile + hole, tile)
        return step(pl.multiple_of(tile * TILE, TILE), TILE, True, carry)

    return lax.fori_loop(0, stop - first - hole, body, init)


def keys_in(first, size, low, high):
    at = first + lax.broadcasted_iota(jnp.int32, (size, low.shape[1]), 0)
    return jnp.logical_and(at >= low, at < high)


def dot(a, b):
    return jnp.dot(a, b, preferred_element_type=jnp.float32)


def pad_heads(rows, h, slots):
    part = rows[h * HEAD : (h + 1) * HEAD]
    zero = jnp.zeros_like(part)
    return jnp.concatenate([part if s == h else zero for s in slots], axis=0)


Q_SLOTS = (0, 1, 2, -1)
V_SLOTS = (-1, 2, 0, 1)


def forward_kernel(lengths, qt, kv, low_out, out, lse_out, qm, acc, qs, os, ls):
    count = qt.shape[2]
    begin, end, spots, slots = lane_slots(lengths, count)
    for s in range(ZN):
        qs[s] = pick(slots, s, [qt[b] for b in range(ZN)])

    def one_block(big, s, carry):
        low, high = bounds_of(lengths, pick(slots, s, spots))
        rows = qs[s] * jnp.bfloat16(0.125)
        for h in range(GROUP):
            qm[h] = pad_heads(rows, h, Q_SLOTS)
        acc[...] = jnp.zeros_like(acc)

        def step(at, size, masked, stats):
            span = pl.ds(at, size)
            keys = kv[span, 0:256]
            values = kv[span, 128:384].T
            mask = keys_in(at, size, low, high) if masked else None
            fresh = []
            for h in range(GROUP):
                top, total = stats[2 * h], stats[2 * h + 1]
                scores = dot(keys, qm[h])
                if masked:
                    scores = jnp.where(mask, scores, -1e9)
                new_top = jnp.maximum(top, jnp.max(scores, axis=0, keepdims=True))
                shrink = jnp.exp(top - new_top)
                weights = jnp.exp(scores - new_top)
                total = total * shrink + jnp.sum(weights, axis=0, keepdims=True)
                row = V_SLOTS.index(h) * HEAD
                acc[h] = acc[h] * shrink + dot(values[row : row + HEAD], weights.astype(jnp.bfloat16))
                fresh = fresh + [new_top, total]
            return tuple(fresh)

        init = (jnp.full((1, count), -1e9, jnp.float32), jnp.zeros((1, count), jnp.float32)) * GROUP
        stats = walk(big, begin, end, low, high, step, init)
        for h in range(GROUP):
            top, total = stats[2 * h], stats[2 * h + 1]
            os[s, h * HEAD : (h + 1) * HEAD] = acc[h] / total
            ls[s, h : h + 1] = top + jnp.log(total)
        return carry

    lax.fori_loop(0, ZN // 2, functools.partial(one_block, True), 0)
    lax.fori_loop(ZN // 2, ZN, functools.partial(one_block, False), 0)
    for b in range(ZN):
        value = pick([jnp.full_like(slots[b], s) for s in range(ZN)], slots[b], [os[s] for s in range(ZN)])
        out[b] = value
        low_out[b] = value.astype(low_out.dtype)
        lse_out[b] = pick([jnp.full_like(slots[b], s) for s in range(ZN)], slots[b], [ls[s] for s in range(ZN)])


def attend(lengths, qt, kv):
    blocks, rows, count = qt.shape
    whole = pl.BlockSpec(memory_space=pltpu.VMEM)
    return pl.pallas_call(
        forward_kernel,
        out_shape=[
            jax.ShapeDtypeStruct(qt.shape, jnp.bfloat16),
            jax.ShapeDtypeStruct(qt.shape, jnp.float32),
            jax.ShapeDtypeStruct((blocks, 8, count), jnp.float32),
        ],
        in_specs=[pl.BlockSpec(memory_space=pltpu.SMEM), whole, whole],
        out_specs=[whole] * 3,
        scratch_shapes=[
            pltpu.VMEM((GROUP, 256, count), jnp.bfloat16),
            pltpu.VMEM((GROUP, HEAD, count), jnp.float32),
            pltpu.VMEM(qt.shape, jnp.bfloat16),
            pltpu.VMEM(qt.shape, jnp.float32),
            pltpu.VMEM((blocks, 8, count), jnp.float32),
        ],
        compiler_params=pltpu.CompilerParams(vmem_limit_bytes=67043328),
    )(lengths, qt, kv)


def backward_kernel(lengths, qt, kv, out, lse, dot_in, cosine, sine, dq_out, dkv_out, qmt, qm, dmt, dm, dq, acc, qs, ds, es, ls, dqs):
    count = qt.shape[2]
    tiles = kv.shape[0] // TILE

    def clear(tile, carry):
        acc[pl.ds(pl.multiple_of(tile * TILE, TILE), TILE), :] = jnp.zeros((TILE, acc.shape[1]), jnp.float32)
        return carry

    lax.fori_loop(0, tiles, clear, 0)

    begin, end, spots, slots = lane_slots(lengths, count)
    for b in range(ZN):
        product_rows = dot_in[b].astype(jnp.float32) * out[b]
        for h in range(GROUP):
            es[b, h : h + 1] = jnp.sum(product_rows[h * HEAD : (h + 1) * HEAD], axis=0, keepdims=True)
    for s in range(ZN):
        qs[s] = pick(slots, s, [qt[b] for b in range(ZN)])
        ds[s] = pick(slots, s, [dot_in[b] for b in range(ZN)])
        ls[s] = pick(slots, s, [lse[b] for b in range(ZN)])
    picked = [pick(slots, s, [es[b] for b in range(ZN)]) for s in range(ZN)]
    for s in range(ZN):
        es[s] = picked[s]

    def one_block(big, s, carry):
        low, high = bounds_of(lengths, pick(slots, s, spots))
        rows = qs[s] * jnp.bfloat16(0.125)
        grads = ds[s]
        deltas = [es[s, h : h + 1] for h in range(GROUP)]
        levels = [ls[s, h : h + 1] for h in range(GROUP)]
        for h in range(GROUP):
            padded = pad_heads(rows, h, Q_SLOTS)
            qmt[h] = padded
            qm[h * count : (h + 1) * count] = padded.T
            padded = pad_heads(grads, h, V_SLOTS)
            dmt[h] = padded
            dm[h * count : (h + 1) * count] = padded.T
        dq[...] = jnp.zeros_like(dq)

        def step(at, size, masked, inner):
            span = pl.ds(at, size)
            keys = kv[span, 0:256]
            values = kv[span, 128:384]
            turned = keys.T
            mask = keys_in(at, size, low, high) if masked else None
            probs, slopes = [], []
            for h in range(GROUP):
                weights = jnp.exp(dot(keys, qmt[h]) - levels[h])
                if masked:
                    weights = jnp.where(mask, weights, 0.0)
                slope = (weights * (dot(values, dmt[h]) - deltas[h])).astype(jnp.bfloat16)
                dq[h] += dot(turned[h * HEAD : (h + 1) * HEAD], slope)
                probs.append(weights.astype(jnp.bfloat16))
                slopes.append(slope)
            dv = dot(jnp.concatenate(probs, axis=1), dm[...])
            dk = dot(jnp.concatenate(slopes, axis=1), qm[...])
            acc[span, 0:128] += dk[:, :128]
            acc[span, 128:256] += dk[:, 128:] + dv[:, :128]
            acc[span, 256:384] += dv[:, 128:]
            return inner

        walk(big, begin, end, low, high, step, 0)
        for h in range(GROUP):
            dqs[s, h * HEAD : (h + 1) * HEAD] = dq[h] * 0.125
        return carry

    lax.fori_loop(0, ZN // 2, functools.partial(one_block, True), 0)
    lax.fori_loop(ZN // 2, ZN, functools.partial(one_block, False), 0)
    half = HEAD // 2
    for b in range(ZN):
        back = pick([jnp.full_like(slots[b], s) for s in range(ZN)], slots[b], [dqs[s] for s in range(ZN)])
        for h in range(GROUP):
            at = h * HEAD
            w1, w2 = back[at : at + half], back[at + half : at + HEAD]
            dq_out[b, at : at + half] = (w1 * cosine[b] + w2 * sine[b]).astype(dq_out.dtype)
            dq_out[b, at + half : at + HEAD] = (w2 * cosine[b] - w1 * sine[b]).astype(dq_out.dtype)

    def finish(tile, carry):
        span = pl.ds(pl.multiple_of(tile * TILE, TILE), TILE)
        dkv_out[span, :] = acc[span, :].astype(dkv_out.dtype)
        return carry

    lax.fori_loop(0, tiles, finish, 0)


def attend_back(lengths, qt, kv, out, lse, dots, cosine, sine):
    blocks, rows, count = qt.shape
    whole = pl.BlockSpec(memory_space=pltpu.VMEM)
    return pl.pallas_call(
        backward_kernel,
        out_shape=[
            jax.ShapeDtypeStruct(qt.shape, jnp.bfloat16),
            jax.ShapeDtypeStruct(kv.shape, jnp.bfloat16),
        ],
        in_specs=[pl.BlockSpec(memory_space=pltpu.SMEM)] + [whole] * 7,
        out_specs=[whole] * 2,
        scratch_shapes=[
            pltpu.VMEM((GROUP, 256, count), jnp.bfloat16),
            pltpu.VMEM((GROUP * count, 256), jnp.bfloat16),
            pltpu.VMEM((GROUP, 256, count), jnp.bfloat16),
            pltpu.VMEM((GROUP * count, 256), jnp.bfloat16),
            pltpu.VMEM((GROUP, HEAD, count), jnp.float32),
            pltpu.VMEM(kv.shape, jnp.float32),
            pltpu.VMEM(qt.shape, jnp.bfloat16),
            pltpu.VMEM(qt.shape, jnp.bfloat16),
            pltpu.VMEM((blocks, 8, count), jnp.float32),
            pltpu.VMEM((blocks, 8, count), jnp.float32),
            pltpu.VMEM(qt.shape, jnp.float32),
        ],
        compiler_params=pltpu.CompilerParams(vmem_limit_bytes=67043328),
    )(lengths, qt, kv, out, lse, dots, cosine, sine)


KV_SLOTS = (0, 1, 2, 5, 3, 4)


def turn(rows, cosine, sine):
    first, second = rows[:, 0], rows[:, 1]
    return jnp.stack([first * cosine - second * sine, second * cosine + first * sine], axis=1)


def turn_back(rows, cosine, sine):
    first, second = rows[:, 0], rows[:, 1]
    return jnp.stack([first * cosine + second * sine, second * cosine - first * sine], axis=1)


def tables(lengths, first, count):
    starts = jnp.cumsum(lengths) - lengths
    position = first[:, None] + jnp.arange(count, dtype=jnp.int32)[None, :]
    begun = position[..., None] >= starts
    offsets = position - jnp.max(jnp.where(begun, starts, 0), axis=-1)
    half = HEAD // 2
    frequency = rope_base ** (-(jnp.arange(half, dtype=jnp.float32) * 2.0) / HEAD)
    angles = offsets.astype(jnp.float32)[:, None, :] * frequency[None, :, None]
    return jnp.cos(angles), jnp.sin(angles)


def contract(left, right, dims):
    return lax.dot_general(left, right, (dims, ((), ())), preferred_element_type=jnp.float32)


def local_grid(
    tokens,
    qkv_weight,
    out_weight,
    gate_weight,
    up_weight,
    down_weight,
    first_gain,
    first_bias,
    second_gain,
    second_bias,
    lengths,
    cotangent,
):
    bf16 = jnp.bfloat16
    rows, width = tokens.shape
    share = first_gain.shape[0]
    heads = width // HEAD
    half = HEAD // 2
    x, y, z, c = place()
    spots = [(px, py, pz, pc) for pz in range(ZN) for py in range(YN) for pc in range(CN) for px in range(XN)]
    over_x = [(block(*p), block(1 - p[0], *p[1:])) for p in spots]
    over_y = [(block(*p), block(p[0], 1 - p[1], *p[2:])) for p in spots]
    small = jnp.stack([first_gain, first_bias, second_gain, second_bias])
    small = jnp.pad(small, ((0, 4), (0, 128 - share)))
    hidden_width = gate_weight.shape[1]

    (qkv_blocks,) = gather([qkv_weight], ["bcast"], 1)
    qkv_full = qkv_blocks.reshape(width, 3 * width)
    turned = jnp.stack([block(x, y, b, c) for b in range(ZN)]) * rows
    cos_all, sin_all = tables(lengths, turned, rows)
    cosine = lax.dynamic_index_in_dim(cos_all, z, 0, keepdims=False)
    sine = lax.dynamic_index_in_dim(sin_all, z, 0, keepdims=False)

    raw = contract(qkv_full, tokens, ((0,), (1,))).astype(bf16)
    raw = raw.reshape(3, heads, 2, half, rows)
    queries = turn(raw[0].astype(jnp.float32), cosine, sine).astype(bf16)
    keys = turn(raw[1].astype(jnp.float32), cosine, sine).astype(bf16)
    queries = queries.reshape(ZN, GROUP * HEAD, rows)
    pairs = jnp.concatenate(
        [keys.reshape(ZN, GROUP, HEAD, rows), raw[2].reshape(ZN, GROUP, HEAD, rows)], axis=1
    )
    pairs = jnp.concatenate([pairs[:, s : s + 1] for s in KV_SLOTS], axis=1)
    pairs = jnp.swapaxes(pairs.reshape(ZN, 2 * GROUP * HEAD, rows), 1, 2)

    pairs_all, queries, out_full, down_full, small, gate_part, up_part = gather(
        [pairs, queries, out_weight, down_weight, small, gate_weight, up_weight],
        ["cross", "swap", "bcast", "bcast", "bcast", "by_x", "by_y"],
        2,
    )
    out_full = out_full.reshape(width, width)
    grid = (ZN, YN, CN, XN) + gate_weight.shape
    gate_send = gate_part.reshape(grid)[:, y, c].reshape((2 * ZN,) + gate_weight.shape)
    up_send = up_part.reshape(grid)[:, :, c, x].reshape((2 * ZN,) + up_weight.shape)
    gate_rest = lax.ppermute(gate_send, ("cp", "hd"), over_y)
    up_rest = lax.ppermute(up_send, ("cp", "hd"), over_x)
    down_full = down_full.reshape(hidden_width, width)
    gain_one, bias_one, gain_two, bias_two = [
        small[:, i, :share].reshape(width).astype(jnp.float32) for i in range(4)
    ]
    pairs_all = pairs_all.reshape(-1, 2 * GROUP * HEAD)
    low, attended, lse = attend(lengths, queries, pairs_all)
    low, gate_full, up_full = gather(
        [low, gate_rest, up_rest], ["swap", "rest_y", "rest_x"], 3, (gate_part, up_part)
    )
    gate_full = gate_full.reshape(width, hidden_width)
    up_full = up_full.reshape(width, hidden_width)
    low = low.reshape(width, rows)

    attn_out = contract(low, out_full, ((0,), (0,)))
    first, scaled_one, inv_one = normalize(tokens.astype(jnp.float32) + attn_out, gain_one, bias_one)
    first_low = first.astype(bf16)
    gate_proj = product(first_low, gate_full)
    up_proj = product(first_low, up_full)
    sigmoid_gate = jax.nn.sigmoid(gate_proj)
    silu_gate = gate_proj * sigmoid_gate
    hidden = (silu_gate * up_proj).astype(bf16)
    branch = product(hidden, down_full)
    second, scaled_two, inv_two = normalize(first + branch, gain_two, bias_two)
    layer_out = second.astype(bf16)

    upstream = cotangent.astype(jnp.float32)
    dz_two, gain_two_grad, bias_two_grad = normalize_back(upstream, scaled_two, inv_two, gain_two)
    dz_two_low = dz_two.astype(bf16)
    down_sum = contract(hidden, dz_two_low, ((0,), (0,))).astype(bf16)
    hidden_grad = contract(dz_two_low, down_full, ((1,), (1,)))
    gate_back = (
        hidden_grad * up_proj * sigmoid_gate * (1.0 + gate_proj * (1.0 - sigmoid_gate))
    ).astype(bf16)
    up_back = (hidden_grad * silu_gate).astype(bf16)
    gate_sum = contract(first_low, gate_back, ((0,), (0,))).astype(bf16)
    up_sum = contract(first_low, up_back, ((0,), (0,))).astype(bf16)
    first_back = (
        dz_two + contract(gate_back, gate_full, ((1,), (1,))) + contract(up_back, up_full, ((1,), (1,)))
    )
    dz_one, gain_one_grad, bias_one_grad = normalize_back(first_back, scaled_one, inv_one, gain_one)
    dz_one_low = dz_one.astype(bf16)
    out_sum = product(low, dz_one_low).astype(bf16)
    attended_back = contract(out_full, dz_one_low, ((1,), (1,))).astype(bf16)
    attended_back, gate_keep, gate_send, up_keep, up_send = reduce(
        [
            attended_back.reshape(ZN, GROUP * HEAD, rows),
            gate_sum.reshape((BLOCKS,) + gate_weight.shape),
            up_sum.reshape((BLOCKS,) + up_weight.shape),
        ],
        ["swap", "pair_y", "pair_x"],
        4,
    )
    gate_rest = lax.ppermute(gate_send, ("cp", "hd"), over_y)
    up_rest = lax.ppermute(up_send, ("cp", "hd"), over_x)

    query_back, pair_back = attend_back(
        lengths, queries, pairs_all, attended, lse, attended_back, cos_all, sin_all
    )
    small_sum = jnp.stack([gain_one_grad, bias_one_grad, gain_two_grad, bias_two_grad])
    small_sum = jnp.swapaxes(small_sum.reshape(4, BLOCKS, share), 0, 1)
    small_sum = jnp.pad(small_sum, ((0, 0), (0, 4), (0, 128 - share)))
    pair_back, query_back, out_grad, down_grad, small_grad, gate_grad, up_grad = reduce(
        [
            pair_back.reshape(BLOCKS, rows, 2 * GROUP * HEAD),
            query_back,
            out_sum.reshape(BLOCKS, share, width),
            down_sum.reshape(BLOCKS, -1, width),
            small_sum,
            (gate_keep, gate_rest),
            (up_keep, up_rest),
        ],
        ["cross", "swap", "reduce", "reduce", "reduce", "rest_y", "rest_x"],
        5,
    )
    pair_back = jnp.swapaxes(pair_back, 1, 2).reshape(ZN, 2 * GROUP, HEAD, rows)
    pair_back = [pair_back[:, KV_SLOTS.index(s)] for s in range(2 * GROUP)]
    key_back = jnp.stack(pair_back[:GROUP], axis=1).reshape(heads, 2, half, rows)
    key_back = turn_back(key_back.astype(jnp.float32), cosine, sine).astype(bf16)
    value_back = jnp.stack(pair_back[GROUP:], axis=1)
    raw_back = jnp.concatenate(
        [
            query_back.reshape(width, rows),
            key_back.reshape(width, rows),
            value_back.reshape(width, rows),
        ],
        axis=0,
    )
    qkv_sum = contract(tokens, raw_back, ((0,), (1,))).astype(bf16)
    tokens_grad = (dz_one + contract(raw_back, qkv_full, ((0,), (1,)))).astype(bf16)
    (qkv_grad,) = reduce([qkv_sum.reshape(BLOCKS, share, 3 * width)], ["reduce"], 6)
    return (
        layer_out,
        tokens_grad,
        qkv_grad,
        out_grad,
        gate_grad,
        up_grad,
        down_grad,
        small_grad[0, :share],
        small_grad[1, :share],
        small_grad[2, :share],
        small_grad[3, :share],
    )


def solution(mesh):
    rows = P(("cp", "hd"), None)
    line = P(("cp", "hd"))
    local = local_grid if (mesh.shape["cp"], mesh.shape["hd"]) == (ZN * YN * CN, XN) else local_any
    return jax.shard_map(
        local,
        mesh=mesh,
        in_specs=(rows,) * 6 + (line,) * 4 + (P(), rows),
        out_specs=(rows,) * 7 + (line,) * 4,
        check_vma=False,
    )
```

```python
import functools

import jax
import jax.numpy as jnp
from jax import lax
from jax.experimental import pallas as pl
from jax.experimental.pallas import tpu as pltpu
from jax.sharding import PartitionSpec as P

HD = 64
REACH = 8


rope_base = 1000.0
norm_eps = 1e-12
score_scale = 0.125
masked_score = -1000000000.0


def shifted(block, axis, distance):
    devices = range(lax.axis_size(axis))
    route = [(i - distance, i) for i in devices if i - distance in devices]
    return lax.ppermute(block, axis, route)


def doc_layout(lengths, first_row, row_count):
    starts = jnp.cumsum(lengths) - lengths
    position = first_row + jnp.arange(row_count, dtype=jnp.int32)
    at_or_after = position[:, None] >= starts[None, :]
    doc_ids = jnp.sum(at_or_after.astype(jnp.int32), axis=1) - 1
    doc_begin = jnp.max(jnp.where(at_or_after, starts[None, :], 0), axis=1)
    return (doc_ids, position - doc_begin)


def rope_tables(offsets, head_size):
    half_size = head_size // 2
    frequency = rope_base ** (-(jnp.arange(half_size, dtype=jnp.float32) * 2.0) / head_size)
    angles = offsets.astype(jnp.float32)[:, None] * frequency[None, :]
    return (jnp.cos(angles), jnp.sin(angles))


def rotate(values, cosine, sine):
    half_size = values.shape[-1] // 2
    first_half = values[..., :half_size]
    second_half = values[..., half_size:]
    cos_rows = cosine[:, None, :]
    sin_rows = sine[:, None, :]
    return jnp.concatenate(
        [
            first_half * cos_rows - second_half * sin_rows,
            second_half * cos_rows + first_half * sin_rows,
        ],
        axis=-1,
    )


def rotate_back(grads, cosine, sine):
    half_size = grads.shape[-1] // 2
    first_half = grads[..., :half_size]
    second_half = grads[..., half_size:]
    cos_rows = cosine[:, None, :]
    sin_rows = sine[:, None, :]
    return jnp.concatenate(
        [
            first_half * cos_rows + second_half * sin_rows,
            second_half * cos_rows - first_half * sin_rows,
        ],
        axis=-1,
    )


def normalize(hidden_in, gain_vec, bias_vec):
    average = jnp.mean(hidden_in, axis=-1, keepdims=True)
    centered = hidden_in - average
    variance = jnp.mean(centered * centered, axis=-1, keepdims=True)
    inv_std = lax.rsqrt(variance + norm_eps)
    scaled = centered * inv_std
    return (scaled * gain_vec + bias_vec, scaled, inv_std)


def normalize_back(upstream, scaled, inv_std, gain_vec):
    weighted = upstream * gain_vec
    inner = (
        weighted
        - jnp.mean(weighted, axis=-1, keepdims=True)
        - scaled * jnp.mean(weighted * scaled, axis=-1, keepdims=True)
    )
    return (inv_std * inner, jnp.sum(upstream * scaled, axis=0), jnp.sum(upstream, axis=0))


def product(left, right):
    return jnp.dot(left, right, preferred_element_type=jnp.float32)


def local_any(
    tokens,
    qkv_weight,
    out_weight,
    gate_weight,
    up_weight,
    down_weight,
    first_gain,
    first_bias,
    second_gain,
    second_bias,
    doc_lengths,
    cotangent,
):
    rows_here = tokens.shape[0]
    model_width = tokens.shape[1]
    hd_count = lax.axis_size("hd")
    cp_count = lax.axis_size("cp")
    cp_index = lax.axis_index("cp")
    block_rows = rows_here * hd_count
    local_width = model_width // hd_count
    local_heads = local_width // HD
    shifts = [0]
    for distance in range(1, REACH + 1):
        shifts = shifts + [-distance, distance]
    shards = (
        qkv_weight,
        out_weight,
        gate_weight,
        up_weight,
        down_weight,
        first_gain,
        first_bias,
        second_gain,
        second_bias,
    )
    weights = (
        lax.all_gather(shards[0], ("cp", "hd"), axis=0, tiled=True),
        lax.all_gather(shards[1], ("cp", "hd"), axis=0, tiled=True),
        lax.all_gather(shards[2], ("cp", "hd"), axis=0, tiled=True),
        lax.all_gather(shards[3], ("cp", "hd"), axis=0, tiled=True),
        lax.all_gather(shards[4], ("cp", "hd"), axis=0, tiled=True),
        lax.all_gather(shards[5], ("cp", "hd"), axis=0, tiled=True),
        lax.all_gather(shards[6], ("cp", "hd"), axis=0, tiled=True),
        lax.all_gather(shards[7], ("cp", "hd"), axis=0, tiled=True),
        lax.all_gather(shards[8], ("cp", "hd"), axis=0, tiled=True),
    )
    (
        qkv_full,
        out_full,
        gate_full,
        up_full,
        down_full,
        gain_first,
        bias_first,
        gain_second,
        bias_second,
    ) = weights
    raw_rows = product(tokens, qkv_full).astype(jnp.bfloat16)
    grouped = lax.all_to_all(
        raw_rows.reshape(rows_here, 3, hd_count, local_width),
        "hd",
        split_axis=2,
        concat_axis=0,
        tiled=True,
    )
    grouped = grouped.reshape(block_rows, 3, local_width)
    query_docs, offsets = doc_layout(doc_lengths, cp_index * block_rows, block_rows)
    cosine, sine = rope_tables(offsets, HD)
    queries = rotate(
        grouped[:, 0].astype(jnp.float32).reshape(block_rows, local_heads, HD), cosine, sine
    ).astype(jnp.bfloat16)
    key_rows = rotate(
        grouped[:, 1].astype(jnp.float32).reshape(block_rows, local_heads, HD), cosine, sine
    ).astype(jnp.bfloat16)
    own_block = jnp.stack([key_rows.reshape(block_rows, local_width), grouped[:, 2]], axis=1)

    def key_docs(distance):
        source = cp_index - distance
        doc_ids, unused_offsets = doc_layout(doc_lengths, source * block_rows, block_rows)
        inside = jnp.logical_and(source >= 0, source < cp_count)
        return jnp.where(inside, doc_ids, -2)

    remote = [own_block] + [shifted(own_block, "cp", distance) for distance in shifts[1:]]
    masks = [query_docs[:, None] == key_docs(distance)[None, :] for distance in shifts]

    def scores_with(query_part, remote_block, key_mask):
        key_part = remote_block[:, 0].reshape(block_rows, local_heads, HD)
        raw_scores = (
            jnp.einsum("qhd,khd->hqk", query_part, key_part, preferred_element_type=jnp.float32)
            * score_scale
        )
        return jnp.where(key_mask[None], raw_scores, masked_score)

    def scores_for(remote_block, key_mask):
        return scores_with(queries, remote_block, key_mask)

    running_max = jnp.full((local_heads, block_rows), masked_score, jnp.float32)
    running_sum = jnp.zeros((local_heads, block_rows), jnp.float32)
    for remote_block, key_mask in zip(remote, masks):
        block_scores = scores_for(remote_block, key_mask)
        new_max = jnp.maximum(running_max, jnp.max(block_scores, axis=-1))
        running_sum = running_sum * jnp.exp(running_max - new_max) + jnp.sum(
            jnp.exp(block_scores - new_max[:, :, None]), axis=-1
        )
        running_max = new_max
    log_total = running_max + jnp.log(running_sum)
    attended = jnp.zeros((block_rows, local_heads, HD), jnp.float32)
    for remote_block, key_mask in zip(remote, masks):
        block_scores = scores_for(remote_block, key_mask)
        probs = jnp.exp(block_scores - log_total[:, :, None]).astype(jnp.bfloat16)
        value_part = remote_block[:, 1].reshape(block_rows, local_heads, HD)
        attended = attended + jnp.einsum(
            "hqk,khd->qhd", probs, value_part, preferred_element_type=jnp.float32
        )
    attended_send = attended.reshape(block_rows, 1, local_width).astype(jnp.bfloat16)
    attended_low = lax.all_to_all(
        attended_send, "hd", split_axis=0, concat_axis=1, tiled=True
    ).reshape(rows_here, model_width)
    gain_one = gain_first.astype(jnp.float32)
    gain_two = gain_second.astype(jnp.float32)
    attn_out = product(attended_low, out_full)
    first, scaled_one, inv_one = normalize(
        tokens.astype(jnp.float32) + attn_out, gain_one, bias_first.astype(jnp.float32)
    )
    first_low = first.astype(jnp.bfloat16)
    gate_proj = product(first_low, gate_full)
    up_proj = product(first_low, up_full)
    sigmoid_gate = jax.nn.sigmoid(gate_proj)
    silu_gate = gate_proj * sigmoid_gate
    hidden = (silu_gate * up_proj).astype(jnp.bfloat16)
    branch = product(hidden, down_full)
    second, scaled_two, inv_two = normalize(
        first + branch, gain_two, bias_second.astype(jnp.float32)
    )
    layer_out = second.astype(jnp.bfloat16)
    weights = (
        lax.all_gather(shards[0], ("cp", "hd"), axis=0, tiled=True),
        lax.all_gather(shards[1], ("cp", "hd"), axis=0, tiled=True),
        lax.all_gather(shards[2], ("cp", "hd"), axis=0, tiled=True),
        lax.all_gather(shards[3], ("cp", "hd"), axis=0, tiled=True),
        lax.all_gather(shards[4], ("cp", "hd"), axis=0, tiled=True),
        lax.all_gather(shards[5], ("cp", "hd"), axis=0, tiled=True),
        lax.all_gather(shards[6], ("cp", "hd"), axis=0, tiled=True),
        lax.all_gather(shards[7], ("cp", "hd"), axis=0, tiled=True),
        lax.all_gather(shards[8], ("cp", "hd"), axis=0, tiled=True),
    )
    (
        qkv_full,
        out_full,
        gate_full,
        up_full,
        down_full,
        gain_first,
        bias_first,
        gain_second,
        bias_second,
    ) = weights
    upstream = cotangent.astype(jnp.float32)
    dz_two, gain_two_grad, bias_two_grad = normalize_back(upstream, scaled_two, inv_two, gain_two)
    dz_two_low = dz_two.astype(jnp.bfloat16)
    down_sum = product(hidden.T, dz_two_low)
    hidden_grad = product(dz_two_low, down_full.T)
    gate_back = (
        hidden_grad * up_proj * sigmoid_gate * (1.0 + gate_proj * (1.0 - sigmoid_gate))
    ).astype(jnp.bfloat16)
    up_back = (hidden_grad * silu_gate).astype(jnp.bfloat16)
    gate_sum = product(first_low.T, gate_back)
    up_sum = product(first_low.T, up_back)
    first_back = dz_two + product(gate_back, gate_full.T) + product(up_back, up_full.T)
    dz_one, gain_one_grad, bias_one_grad = normalize_back(first_back, scaled_one, inv_one, gain_one)
    dz_one_low = dz_one.astype(jnp.bfloat16)
    out_sum = product(attended_low.T, dz_one_low)
    attended_back = product(dz_one_low, out_full.T).astype(jnp.bfloat16)
    heads_back = lax.all_to_all(
        attended_back.reshape(rows_here, hd_count, local_width),
        "hd",
        split_axis=1,
        concat_axis=0,
        tiled=True,
    )
    heads_back = heads_back.reshape(block_rows, local_heads, HD)
    delta = jnp.transpose(jnp.sum(heads_back.astype(jnp.float32) * attended, axis=-1))
    query_grad = jnp.zeros((block_rows, local_heads, HD), jnp.float32)
    pair_total = jnp.zeros((block_rows, 2, local_width), jnp.float32)
    remote = [own_block] + [shifted(own_block, "cp", distance) for distance in shifts[1:]]
    for distance, remote_block, key_mask in zip(shifts, remote, masks):
        pair_block_scores = scores_with(queries, remote_block, key_mask)
        pair_probs = jnp.exp(pair_block_scores - log_total[:, :, None])
        pair_key_part = remote_block[:, 0].reshape(block_rows, local_heads, HD)
        pair_value_part = remote_block[:, 1].reshape(block_rows, local_heads, HD)
        value_grad = jnp.einsum(
            "hqk,qhd->khd",
            pair_probs.astype(jnp.bfloat16),
            heads_back,
            preferred_element_type=jnp.float32,
        )
        prob_grad = jnp.einsum(
            "qhd,khd->hqk", heads_back, pair_value_part, preferred_element_type=jnp.float32
        )
        score_grad = (pair_probs * (prob_grad - delta[:, :, None])).astype(jnp.bfloat16)
        query_term = (
            jnp.einsum(
                "hqk,khd->qhd", score_grad, pair_key_part, preferred_element_type=jnp.float32
            )
            * score_scale
        )
        key_grad = (
            jnp.einsum("hqk,qhd->khd", score_grad, queries, preferred_element_type=jnp.float32)
            * score_scale
        )
        grad_pair = jnp.stack(
            [
                key_grad.reshape(block_rows, local_width),
                value_grad.reshape(block_rows, local_width),
            ],
            axis=1,
        )
        query_term, grad_pair = (query_term, grad_pair)
        query_grad = query_grad + query_term
        if distance == 0:
            pair_total = grad_pair
        else:
            pair_total = pair_total + shifted(
                grad_pair.astype(jnp.bfloat16), "cp", -distance
            ).astype(grad_pair.dtype)
    query_back = rotate_back(query_grad, cosine, sine).reshape(block_rows, local_width)
    key_back = rotate_back(
        pair_total[:, 0].reshape(block_rows, local_heads, HD), cosine, sine
    ).reshape(block_rows, local_width)
    raw_back = jnp.stack([query_back, key_back, pair_total[:, 1]], axis=1).astype(jnp.bfloat16)
    raw_back = lax.all_to_all(
        raw_back.reshape(block_rows, 3, 1, local_width),
        "hd",
        split_axis=0,
        concat_axis=2,
        tiled=True,
    )
    raw_back = raw_back.reshape(rows_here, 3 * model_width)
    qkv_sum = product(tokens.T, raw_back)
    tokens_grad = (dz_one + product(raw_back, qkv_full.T)).astype(jnp.bfloat16)
    summed = (
        lax.psum_scatter(qkv_sum, ("cp", "hd"), scatter_dimension=0, tiled=True),
        lax.psum_scatter(out_sum, ("cp", "hd"), scatter_dimension=0, tiled=True),
        lax.psum_scatter(gate_sum, ("cp", "hd"), scatter_dimension=0, tiled=True),
        lax.psum_scatter(up_sum, ("cp", "hd"), scatter_dimension=0, tiled=True),
        lax.psum_scatter(down_sum, ("cp", "hd"), scatter_dimension=0, tiled=True),
        lax.psum_scatter(gain_one_grad, ("cp", "hd"), scatter_dimension=0, tiled=True),
        lax.psum_scatter(bias_one_grad, ("cp", "hd"), scatter_dimension=0, tiled=True),
        lax.psum_scatter(gain_two_grad, ("cp", "hd"), scatter_dimension=0, tiled=True),
        lax.psum_scatter(bias_two_grad, ("cp", "hd"), scatter_dimension=0, tiled=True),
    )
    return (
        layer_out,
        tokens_grad,
        summed[0],
        summed[1],
        summed[2],
        summed[3],
        summed[4],
        summed[5],
        summed[6],
        summed[7],
        summed[8],
    )


MESH = pl.DeviceIdType.MESH
ZN, YN, CN, XN = 4, 2, 2, 2
BLOCKS = ZN * YN * CN * XN


def place():
    cp = lax.axis_index("cp")
    x = lax.axis_index("hd")
    return x, lax.rem(cp // CN, YN), cp // (YN * CN), lax.rem(cp, CN)


def device(x, y, z, c):
    return ((z * YN + y) * CN + c, x)


def block(x, y, z, c):
    return ((z * YN + y) * CN + c) * XN + x


def when(cond, fn):
    if cond is None:
        fn()
    else:
        pl.when(cond)(fn)


def both(a, b):
    if a is None:
        return b
    if b is None:
        return a
    return jnp.logical_and(a, b)


def halves(ref):
    rows, cols = ref.shape[-2:]
    if rows % 32 == 0:
        return ref.at[pl.ds(0, rows // 2)], ref.at[pl.ds(rows // 2, rows // 2)]
    if cols % 256 == 0:
        return ref.at[:, pl.ds(0, cols // 2)], ref.at[:, pl.ds(cols // 2, cols // 2)]
    return ref, None


def greet(x, y, z, c, far):
    barrier = pltpu.get_barrier_semaphore()
    for peer in (device(1 - x, y, z, c), device(x, 1 - y, z, c), device(x, y, z, 1 - c)):
        pl.semaphore_signal(barrier, inc=1, device_id=peer, device_id_type=MESH)
    count = 3
    if far:
        for k in range(1, ZN):
            peer = device(x, y, lax.rem(z + k, ZN), c)
            pl.semaphore_signal(barrier, inc=1, device_id=peer, device_id_type=MESH)
        count = count + ZN - 1
    else:
        pl.when(z > 0)(lambda: pl.semaphore_signal(barrier, inc=1, device_id=device(x, y, z - 1, c), device_id_type=MESH))
        pl.when(z < ZN - 1)(lambda: pl.semaphore_signal(barrier, inc=1, device_id=device(x, y, z + 1, c), device_id_type=MESH))
        count = count + (z > 0).astype(jnp.int32) + (z < ZN - 1).astype(jnp.int32)
    pl.semaphore_wait(barrier, count)


SENDS = 40
RECVS = 36


CHAINED = ("bcast", "by_x", "by_y")
REST = ("rest_x", "rest_y")


SHORT_PLAN = [
    (fn, "chained", d - lag)
    for d in range(1, ZN + 2)
    for lag, fn in enumerate(("onward", "beside", "across"))
    if (d > 0 if lag else d < ZN) and 0 <= d - lag < ZN
]
PLAN = [
    ("onward", "chained", 1),
    ("beside", "chained", 0),
    ("beside", "crossed", 0),
    ("across", "chained", 0),
    ("beside", "chained", 1),
    ("onward", "crossed", 1),
    ("across", "crossed", 0),
    ("across", "chained", 1),
    ("onward", "crossed", 2),
    ("onward", "crossed", 3),
    ("beside", "crossed", 1),
    ("onward", "chained", 2),
    ("beside", "crossed", 2),
    ("beside", "crossed", 3),
    ("beside", "chained", 2),
    ("across", "crossed", 1),
    ("onward", "chained", 3),
    ("across", "crossed", 2),
    ("across", "crossed", 3),
    ("across", "chained", 2),
    ("beside", "chained", 3),
    ("across", "chained", 3),
]


def gather_kernel(modes, *refs):
    n = len(modes)
    ins, refs = refs[:n], refs[n:]
    refs = refs[sum(mode in REST for mode in modes) :]
    outs, (lsem, ssem, rsem) = refs[:n], refs[n:]
    x, y, z, c = place()
    ox, oy, oc = 1 - x, 1 - y, 1 - c
    greet(x, y, z, c, any(m in ("swap", "cross") for m in modes))
    sent = []

    def copy(k, src, dst, s, r, peer):
        return pltpu.make_async_remote_copy(
            src_ref=src,
            dst_ref=dst,
            send_sem=ssem.at[k, s],
            recv_sem=rsem.at[k, r],
            device_id=peer,
            device_id_type=MESH,
        )

    def send(cond, *args):
        when(cond, lambda: copy(*args).start())
        sent.append((cond, args))

    def arrived(cond, k, ref, r):
        when(cond, lambda: copy(k, ref, ref, 0, r, device(ox, y, z, c)).wait_recv())

    locals_ = []

    def keep(k, i, mine, spot):
        pltpu.make_async_copy(mine, spot, lsem.at[k, i]).start()
        locals_.append((k, i, mine, spot))

    for k, mode in enumerate(modes):
        if mode in CHAINED:
            keep(k, 0, ins[k], outs[k].at[block(x, y, z, c)])
        elif mode == "swap":
            keep(k, 0, ins[k].at[z], outs[k].at[z])
        elif mode == "cross":
            keep(k, 0, ins[k].at[z], outs[k].at[block(x, y, z, c)])

    def spread(k, cond, b, src, up, down):
        here = outs[k].at[block(x, y, b, c)]
        if modes[k] in CHAINED:
            if up is not False:
                send(both(cond, up), k, src, here, b, b, device(x, y, lax.rem(z + 1, ZN), c))
            if down is not False:
                send(both(cond, down), k, src, here, 4 + b, b, device(x, y, lax.rem(z + ZN - 1, ZN), c))
        if modes[k] != "by_y":
            send(cond, k, src, here, 8 + b, 4 + b, device(ox, y, z, c))
        if modes[k] != "by_x":
            send(cond, k, src, here, 16 + b, 12 + b, device(x, oy, z, c))
        send(cond, k, src, here, 24 + b, 20 + b, device(x, y, z, oc))

    def sides(k, cond, b):
        fx = outs[k].at[block(ox, y, b, c)]
        fy = outs[k].at[block(x, oy, b, c)]
        full = modes[k] in ("bcast", "cross")
        if modes[k] != "by_y":
            arrived(cond, k, fx, 4 + b)
            first, _ = halves(fx)
            if full:
                send(cond, k, first, first, 20 + b, 16 + b, device(x, oy, z, c))
            send(cond, k, fx, fx, 28 + b, 24 + b, device(x, y, z, oc))
        if modes[k] != "by_x":
            arrived(cond, k, fy, 12 + b)
            _, second = halves(fy)
            if full and second is not None:
                send(cond, k, second, second, 12 + b, 8 + b, device(ox, y, z, c))
            send(cond, k, fy, fy, 32 + b, 28 + b, device(x, y, z, oc))

    def corner(k, cond, b):
        far = outs[k].at[block(ox, oy, b, c)]
        first, second = halves(far)
        arrived(cond, k, first, 16 + b)
        if second is not None:
            arrived(cond, k, second, 8 + b)
        send(cond, k, far, far, 36 + b, 32 + b, device(x, y, z, oc))

    def steps(distance):
        if distance == 0:
            return [(None, z)]
        return [(z >= distance, jnp.maximum(z - distance, 0)), (z + distance < ZN, jnp.minimum(z + distance, ZN - 1))]

    chained = [k for k, mode in enumerate(modes) if mode in CHAINED]
    crossed = [k for k, mode in enumerate(modes) if mode == "cross"]
    swapped = [k for k, mode in enumerate(modes) if mode == "swap"]

    def exchange(ks):
        for k in ks:
            for d in range(1, ZN):
                to = lax.rem(z + d, ZN)
                spot = outs[k].at[z] if modes[k] == "swap" else outs[k].at[block(x, y, z, c)]
                send(None, k, ins[k].at[to], spot, to, z, device(x, y, to, c))

    for k in chained:
        spread(k, None, z, ins[k], z < ZN - 1, z > 0)
    for k, mode in enumerate(modes):
        if mode in REST:
            for b in range(ZN):
                for j in range(2):
                    spot = block(j, oy, b, c) if mode == "rest_y" else block(ox, j, b, c)
                    keep(k, 2 * b + j, ins[k].at[2 * b + j], outs[k].at[spot])
                    send(None, k, ins[k].at[2 * b + j], outs[k].at[spot], 2 * b + j, 2 * b + j, device(x, y, z, oc))
    for k in crossed:
        spread(k, None, z, ins[k].at[z], False, False)
    exchange(crossed)

    def onward(ks, distance):
        for side, (cond, b) in enumerate(steps(distance)):
            for k in ks:
                here = outs[k].at[block(x, y, b, c)]
                arrived(cond, k, here, b)
                spread(k, cond, b, here, z < ZN - 1 if side == 0 else False, z > 0 if side == 1 else False)

    def beside(ks, distance):
        for cond, b in steps(distance):
            for k in ks:
                sides(k, cond, b)

    def across(ks, distance):
        for cond, b in steps(distance):
            for k in ks:
                if modes[k] in ("bcast", "cross"):
                    corner(k, cond, b)

    plan = PLAN if crossed else SHORT_PLAN
    for fn, ks, distance in plan if chained else ():
        fn = {"onward": onward, "beside": beside, "across": across}[fn]
        fn(chained if ks == "chained" else crossed, distance)
        if fn is onward and distance == 2 and ks == "chained":
            exchange(swapped)
            swapped = []
    exchange(swapped)
    for k, mode in enumerate(modes):
        if mode == "swap":
            for d in range(1, ZN):
                frm = lax.rem(z + d, ZN)
                arrived(None, k, outs[k].at[frm], frm)
        elif mode in REST:
            for b in range(ZN):
                for j in range(2):
                    spot = block(j, oy, b, oc) if mode == "rest_y" else block(ox, j, b, oc)
                    arrived(None, k, outs[k].at[spot], 2 * b + j)
        else:
            quads = {"by_x": (0, 1), "by_y": (0, 2)}.get(mode, (0, 1, 2, 3))
            for b in range(ZN):
                for j in quads:
                    px, py = ((x, y), (ox, y), (x, oy), (ox, oy))[j]
                    arrived(None, k, outs[k].at[block(px, py, b, oc)], 20 + 4 * j + b)
    for k, i, mine, spot in locals_:
        pltpu.make_async_copy(mine, spot, lsem.at[k, i]).wait()
    for cond, args in sent:
        when(cond, lambda args=args: copy(*args).wait_send())


def gather(arrays, modes, collective_id, filled=()):
    shapes = []
    rest = [k for k, mode in enumerate(modes) if mode in REST]
    for k, (a, mode) in enumerate(zip(arrays, modes)):
        if mode in CHAINED:
            shapes.append((BLOCKS,) + a.shape)
        elif mode == "swap":
            shapes.append(a.shape)
        else:
            shapes.append((BLOCKS,) + a.shape[1:])
    n = len(arrays)
    return pl.pallas_call(
        functools.partial(gather_kernel, tuple(modes)),
        out_shape=[jax.ShapeDtypeStruct(s, a.dtype) for s, a in zip(shapes, arrays)],
        in_specs=[pl.BlockSpec(memory_space=pltpu.VMEM)] * n + [pl.BlockSpec(memory_space=pl.ANY)] * len(rest),
        out_specs=[pl.BlockSpec(memory_space=pl.ANY)] * n,
        input_output_aliases={n + i: k for i, k in enumerate(rest)},
        scratch_shapes=[
            pltpu.SemaphoreType.DMA((n, 8)),
            pltpu.SemaphoreType.DMA((n, SENDS)),
            pltpu.SemaphoreType.DMA((n, RECVS)),
        ],
        compiler_params=pltpu.CompilerParams(collective_id=collective_id, has_side_effects=True),
    )(*arrays, *filled)


def chunk_of(cols):
    for size in (768, 640, 512, 384, 256, 128):
        if cols % size == 0:
            return size
    return cols


def add_up(dst, sources):
    rows, cols = dst.shape[-2:]
    size = chunk_of(cols)

    def step(i, carry):
        span = pl.ds(pl.multiple_of(i * size, size), size)
        total = sources[0][:, span].astype(jnp.float32)
        for source in sources[1:]:
            total = total + source[:, span].astype(jnp.float32)
        dst[:, span] = total.astype(dst.dtype)
        return carry

    if cols == size:
        total = sources[0][...].astype(jnp.float32)
        for source in sources[1:]:
            total = total + source[...].astype(jnp.float32)
        dst[...] = total.astype(dst.dtype)
    else:
        lax.fori_loop(0, cols // size, step, 0)


BUFFERS = {"swap": 0, "pair_x": 2, "pair_y": 2, "cross": 3, "reduce": 4, "rest_x": 4, "rest_y": 4}
PAIR = ("pair_x", "pair_y")


def take(refs, counts):
    groups = []
    for count in counts:
        groups.append(refs[:count])
        refs = refs[count:]
    return groups, refs


def reduce_kernel(modes, *refs):
    n = len(modes)
    ins, refs = take(refs, [2 if mode in REST else 1 for mode in modes])
    outs, refs = take(refs, [2 if mode in PAIR else 1 for mode in modes])
    (lsem, ssem, rsem), scratch = refs[:3], refs[3:]
    bufs, _ = take(scratch, [BUFFERS[mode] for mode in modes])
    others, seconds = ins, outs
    ins, outs = [group[0] for group in ins], [group[0] for group in outs]
    x, y, z, c = place()
    ox, oy, oc = 1 - x, 1 - y, 1 - c
    greet(x, y, z, c, any(m in ("swap", "cross") for m in modes))
    sent = []

    def copy(k, src, dst, s, r, peer):
        return pltpu.make_async_remote_copy(
            src_ref=src,
            dst_ref=dst,
            send_sem=ssem.at[k, s],
            recv_sem=rsem.at[k, r],
            device_id=peer,
            device_id_type=MESH,
        )

    def send(cond, *args):
        when(cond, lambda: copy(*args).start())
        sent.append((cond, args))

    def arrived(cond, k, ref, r):
        when(cond, lambda: copy(k, ref, ref, 0, r, device(ox, y, z, c)).wait_recv())

    half = z // 2
    order = [3 - 3 * half, 2 - half, 1 - z + 4 * half, z]
    quads = ((ox, oy), (ox, y), (x, oy), (x, y))
    active = [k for k, mode in enumerate(modes) if mode in ("cross", "reduce")]
    paired = [k for k, mode in enumerate(modes) if mode in PAIR]
    rest = [k for k, mode in enumerate(modes) if mode in REST]

    for k in rest:
        acc, rec = bufs[k][:2]
        for i, b in enumerate(order):
            for j in range(2):
                mine = (x, y)[modes[k] == "rest_x"]
                spot = 2 * b + (mine if j else 1 - mine)
                pltpu.make_async_copy(ins[k].at[spot], acc.at[2 * i + j], lsem.at[k, 2 * i + j]).start()
                pltpu.make_async_copy(others[k][1].at[spot], rec.at[2 * i + j], lsem.at[k, 8 + 2 * i + j]).start()
    for k in active:
        for i, b in enumerate(order):
            acc, cor = bufs[k][:2]
            for j, (px, py) in enumerate(quads):
                send(None, k, ins[k].at[block(px, py, b, oc)], cor.at[4 * i + j], 4 * i + j, 4 * i + j, device(x, y, z, oc))
                pltpu.make_async_copy(ins[k].at[block(px, py, b, c)], acc.at[4 * i + j], lsem.at[k, 4 * i + j]).start()

    def spots(k, i):
        b, j = i // 2, i % 2
        if modes[k] == "pair_y":
            return (j, y, b), (j, oy, b)
        return (x, j, b), (ox, j, b)

    for k in paired:
        acc, cor = bufs[k]
        for i in range(8):
            for s, (px, py, b) in enumerate(spots(k, i)):
                send(None, k, ins[k].at[block(px, py, b, oc)], cor.at[2 * i + s], 2 * i + s, 2 * i + s, device(x, y, z, oc))
                pltpu.make_async_copy(ins[k].at[block(px, py, b, c)], acc.at[2 * i + s], lsem.at[k, 2 * i + s]).start()
    for k, mode in enumerate(modes):
        if mode == "swap":
            for d in range(1, ZN):
                to = lax.rem(z + d, ZN)
                send(None, k, ins[k].at[to], outs[k].at[z], d, z, device(x, y, to, c))
            pltpu.make_async_copy(ins[k].at[z], outs[k].at[z], lsem.at[k, 0]).start()

    def loaded(k, i, j):
        acc, cor = bufs[k][:2]
        pltpu.make_async_copy(ins[k].at[0], acc.at[4 * i + j], lsem.at[k, 4 * i + j]).wait()
        arrived(None, k, cor.at[4 * i + j], 4 * i + j)

    for k in paired:
        acc, cor = bufs[k]

        def join(i, carry, k=k, acc=acc, cor=cor):
            for s in range(2):
                at = 2 * i + s
                pltpu.make_async_copy(ins[k].at[0], acc.at[at], lsem.at[k, at]).wait()
                arrived(None, k, cor.at[at], at)
                add_up(seconds[k][s].at[i], (acc.at[at], cor.at[at]))
            return carry

        lax.fori_loop(0, 8, join, 0)

    def fetched(k, i, j):
        acc, rec = bufs[k][:2]
        pltpu.make_async_copy(ins[k].at[0], acc.at[2 * i + j], lsem.at[k, 2 * i + j]).wait()
        pltpu.make_async_copy(ins[k].at[0], rec.at[2 * i + j], lsem.at[k, 8 + 2 * i + j]).wait()

    def ahead(k, i, b):
        acc, rec, side = bufs[k][:3]
        fetched(k, i, 0)
        add_up(acc.at[2 * i], (acc.at[2 * i], rec.at[2 * i]))
        peer = device(x, oy, z, c) if modes[k] == "rest_x" else device(ox, y, z, c)
        send(None, k, acc.at[2 * i], side.at[i], 16 + i, 16 + i, peer)

    def corner(k, i, b):
        acc, cor, side = bufs[k][:3]
        loaded(k, i, 0)
        add_up(acc.at[4 * i], (acc.at[4 * i], cor.at[4 * i]))
        first, second = halves(acc.at[4 * i])
        send(None, k, first, halves(side.at[i])[0], 16 + i, 16 + i, device(x, oy, z, c))
        if second is not None:
            send(None, k, second, halves(side.at[4 + i])[1], 20 + i, 20 + i, device(ox, y, z, c))

    def beside(k, i, b):
        acc, cor, side = bufs[k][:3]
        loaded(k, i, 1)
        add_up(acc.at[4 * i + 1], (acc.at[4 * i + 1], cor.at[4 * i + 1]))
        part = halves(side.at[i])[0]
        arrived(None, k, part, 16 + i)
        mine = halves(acc.at[4 * i + 1])[0]
        add_up(mine, (mine, part))
        send(None, k, acc.at[4 * i + 1], side.at[8 + i], 24 + i, 24 + i, device(ox, y, z, c))
        loaded(k, i, 2)
        add_up(acc.at[4 * i + 2], (acc.at[4 * i + 2], cor.at[4 * i + 2]))
        part = halves(side.at[4 + i])[1]
        if part is not None:
            arrived(None, k, part, 20 + i)
            mine = halves(acc.at[4 * i + 2])[1]
            add_up(mine, (mine, part))
        send(None, k, acc.at[4 * i + 2], side.at[12 + i], 28 + i, 28 + i, device(x, oy, z, c))

    def settle(k, i, b):
        side = bufs[k][2]
        if k in rest:
            acc, rec = bufs[k][:2]
            fetched(k, i, 1)
            arrived(None, k, side.at[i], 16 + i)
            own = acc.at[2 * i + 1]
            terms = (own, rec.at[2 * i + 1], side.at[i])
        else:
            acc, cor = bufs[k][:2]
            loaded(k, i, 3)
            own = acc.at[4 * i + 3]
            arrived(None, k, side.at[8 + i], 24 + i)
            arrived(None, k, side.at[12 + i], 28 + i)
            terms = (own, cor.at[4 * i + 3], side.at[8 + i], side.at[12 + i])
        if modes[k] == "cross":
            add_up(own, terms)
            if i < ZN - 1:
                send(None, k, own, outs[k].at[z], 32 + i, 32 + z, device(x, y, b, c))
            else:
                pltpu.make_async_copy(own, outs[k].at[z], lsem.at[k, 16]).start()
            return
        chain = bufs[k][3]
        if i == ZN - 1:
            add_up(outs[k], terms)

            def lower(k=k, chain=chain):
                arrived(None, k, chain.at[z], 32 + z)
                add_up(outs[k], (outs[k], chain.at[z]))

            def upper(k=k, chain=chain):
                arrived(None, k, chain.at[4 + z], 36 + z)
                add_up(outs[k], (outs[k], chain.at[4 + z]))

            pl.when(z > 0)(lower)
            pl.when(z < ZN - 1)(upper)
        else:
            add_up(own, terms)
            below = both(b > z, z > 0)
            above = both(b < z, z < ZN - 1)

            def lower(k=k, chain=chain, own=own, b=b):
                arrived(None, k, chain.at[b], 32 + b)
                add_up(own, (own, chain.at[b]))

            def upper(k=k, chain=chain, own=own, b=b):
                arrived(None, k, chain.at[4 + b], 36 + b)
                add_up(own, (own, chain.at[4 + b]))

            pl.when(below)(lower)
            pl.when(above)(upper)
            send(b > z, k, own, chain.at[b], 32 + i, 32 + b, device(x, y, lax.rem(z + 1, ZN), c))
            send(b < z, k, own, chain.at[4 + b], 32 + i, 36 + b, device(x, y, lax.rem(z + ZN - 1, ZN), c))

    crossed = [k for k in active if modes[k] == "cross"]
    plain = [k for k in active if modes[k] == "reduce"]
    stages = [[(ahead, rest)], [(corner, crossed)], [(corner, plain)]]
    stages = stages + [[(settle, rest), (beside, crossed)], [(settle, crossed), (beside, plain)], [(settle, plain)]]
    for stage in stages:
        for i, b in enumerate(order):
            for fn, ks in stage:
                for k in ks:
                    fn(k, i, b)
    for k, mode in enumerate(modes):
        if mode not in ("swap", "cross"):
            continue
        for d in range(1, ZN):
            frm = lax.rem(z + d, ZN)
            arrived(None, k, outs[k].at[frm], frm if mode == "swap" else 32 + frm)
        if mode == "swap":
            pltpu.make_async_copy(ins[k].at[z], outs[k].at[z], lsem.at[k, 0]).wait()
        else:
            pltpu.make_async_copy(bufs[k][0].at[15], outs[k].at[z], lsem.at[k, 16]).wait()
    for cond, args in sent:
        when(cond, lambda args=args: copy(*args).wait_send())


def reduce(arrays, modes, collective_id):
    shapes, specs, scratch, operands, inputs = [], [], [], [], []
    anywhere, local = pl.BlockSpec(memory_space=pl.ANY), pl.BlockSpec(memory_space=pltpu.VMEM)
    for a, mode in zip(arrays, modes):
        operands = operands + (list(a) if mode in REST else [a])
        inputs = inputs + [local if mode == "swap" else anywhere] * (2 if mode in REST else 1)
        a = a[0] if mode in REST else a
        rows, cols = a.shape[1:]
        sizes = {"swap": (), "pair_x": (16, 16), "cross": (16, 16, 16), "reduce": (16, 16, 16, 8), "rest_x": (8, 8, 4, 8)}
        sizes = sizes[mode.replace("_y", "_x")]
        scratch = scratch + [pltpu.VMEM((size, rows, cols), a.dtype) for size in sizes]
        if mode == "swap":
            shapes.append(jax.ShapeDtypeStruct(a.shape, a.dtype))
            specs.append(anywhere)
        elif mode in PAIR:
            shapes = shapes + [jax.ShapeDtypeStruct((8, rows, cols), a.dtype)] * 2
            specs = specs + [local] * 2
        elif mode == "cross":
            shapes.append(jax.ShapeDtypeStruct((ZN, rows, cols), a.dtype))
            specs.append(anywhere)
        else:
            shapes.append(jax.ShapeDtypeStruct((rows, cols), jnp.float32))
            specs.append(local)
    n = len(arrays)
    return pl.pallas_call(
        functools.partial(reduce_kernel, tuple(modes)),
        out_shape=shapes,
        in_specs=inputs,
        out_specs=specs,
        scratch_shapes=[
            pltpu.SemaphoreType.DMA((n, 17)),
            pltpu.SemaphoreType.DMA((n, SENDS)),
            pltpu.SemaphoreType.DMA((n, SENDS)),
        ]
        + scratch,
        compiler_params=pltpu.CompilerParams(
            collective_id=collective_id, has_side_effects=True, vmem_limit_bytes=67043328
        ),
    )(*operands)


HEAD = 64
GROUP = 3
TILE = 512
WIDE = 1024
EDGE = 128
SPAN = 4096
FAR = 1 << 30


def longest(lengths):
    begin, best, at = jnp.int32(0), lengths[0], jnp.int32(0)
    for j in range(lengths.shape[0]):
        length = lengths[j]
        at = jnp.where(length > best, begin, at)
        best = jnp.maximum(best, length)
        begin = begin + length
    return at, at + best


def lane_slots(lengths, count):
    x, y, z, c = place()
    lane = lax.broadcasted_iota(jnp.int32, (1, count), 1)
    begin, end = longest(lengths)
    spots = [block(x, y, b, c) * count + lane for b in range(ZN)]
    slots, before = [], jnp.zeros((1, count), jnp.int32)
    for b in range(ZN):
        big = jnp.logical_and(spots[b] >= begin, spots[b] < end)
        slots.append(jnp.where(big, before, ZN // 2 + b - before))
        before = before + big.astype(jnp.int32)
    return begin, end, spots, slots


def pick(slots, slot, parts):
    chosen = parts[-1]
    for b in range(len(parts) - 2, -1, -1):
        chosen = jnp.where(slots[b] == slot, parts[b], chosen)
    return chosen


def bounds_of(lengths, spot):
    low, high = jnp.zeros_like(spot), jnp.full_like(spot, FAR)
    begin = jnp.int32(0)
    for j in range(lengths.shape[0]):
        end = begin + lengths[j]
        low = jnp.where(spot >= begin, begin, low)
        high = jnp.where(spot < end, jnp.minimum(high, end), high)
        begin = end
    return low, high


def walk(big, begin, end, low, high, step, init):
    if big:
        base = begin // EDGE * EDGE

        def body(i, carry):
            at = pl.multiple_of(base + i * WIDE, EDGE)
            return step(at, WIDE, False, carry)

        carry = step(pl.multiple_of(base, EDGE), WIDE, True, init)
        carry = lax.fori_loop(1, SPAN // WIDE, body, carry)
        return lax.cond(
            begin > base,
            lambda c: step(pl.multiple_of(base + SPAN, EDGE), EDGE, True, c),
            lambda c: c,
            carry,
        )
    first = jnp.min(low) // TILE
    stop = (jnp.max(high) + TILE - 1) // TILE
    hole_first = jnp.maximum((begin + TILE - 1) // TILE, first)
    hole = jnp.maximum(jnp.minimum(end // TILE, stop) - hole_first, 0)

    def body(i, carry):
        tile = first + i
        tile = jnp.where(jnp.logical_and(hole > 0, tile >= hole_first), tile + hole, tile)
        return step(pl.multiple_of(tile * TILE, TILE), TILE, True, carry)

    return lax.fori_loop(0, stop - first - hole, body, init)


def keys_in(first, size, low, high):
    at = first + lax.broadcasted_iota(jnp.int32, (size, low.shape[1]), 0)
    return jnp.logical_and(at >= low, at < high)


def dot(a, b):
    return jnp.dot(a, b, preferred_element_type=jnp.float32)


def pad_heads(rows, h, slots):
    part = rows[h * HEAD : (h + 1) * HEAD]
    zero = jnp.zeros_like(part)
    return jnp.concatenate([part if s == h else zero for s in slots], axis=0)


Q_SLOTS = (0, 1, 2, -1)
V_SLOTS = (-1, 2, 0, 1)


def forward_kernel(lengths, qt, kv, low_out, out, lse_out, qm, acc, qs, os, ls):
    count = qt.shape[2]
    begin, end, spots, slots = lane_slots(lengths, count)
    for s in range(ZN):
        qs[s] = pick(slots, s, [qt[b] for b in range(ZN)])

    def one_block(big, s, carry):
        low, high = bounds_of(lengths, pick(slots, s, spots))
        rows = qs[s] * jnp.bfloat16(0.125)
        for h in range(GROUP):
            qm[h] = pad_heads(rows, h, Q_SLOTS)
        acc[...] = jnp.zeros_like(acc)

        def step(at, size, masked, stats):
            span = pl.ds(at, size)
            keys = kv[span, 0:256]
            values = kv[span, 128:384].T
            mask = keys_in(at, size, low, high) if masked else None
            fresh = []
            for h in range(GROUP):
                top, total = stats[2 * h], stats[2 * h + 1]
                scores = dot(keys, qm[h])
                if masked:
                    scores = jnp.where(mask, scores, -1e9)
                new_top = jnp.maximum(top, jnp.max(scores, axis=0, keepdims=True))
                shrink = jnp.exp(top - new_top)
                weights = jnp.exp(scores - new_top)
                total = total * shrink + jnp.sum(weights, axis=0, keepdims=True)
                row = V_SLOTS.index(h) * HEAD
                acc[h] = acc[h] * shrink + dot(values[row : row + HEAD], weights.astype(jnp.bfloat16))
                fresh = fresh + [new_top, total]
            return tuple(fresh)

        init = (jnp.full((1, count), -1e9, jnp.float32), jnp.zeros((1, count), jnp.float32)) * GROUP
        stats = walk(big, begin, end, low, high, step, init)
        for h in range(GROUP):
            top, total = stats[2 * h], stats[2 * h + 1]
            os[s, h * HEAD : (h + 1) * HEAD] = acc[h] / total
            ls[s, h : h + 1] = top + jnp.log(total)
        return carry

    lax.fori_loop(0, ZN // 2, functools.partial(one_block, True), 0)
    lax.fori_loop(ZN // 2, ZN, functools.partial(one_block, False), 0)
    for b in range(ZN):
        value = pick([jnp.full_like(slots[b], s) for s in range(ZN)], slots[b], [os[s] for s in range(ZN)])
        out[b] = value
        low_out[b] = value.astype(low_out.dtype)
        lse_out[b] = pick([jnp.full_like(slots[b], s) for s in range(ZN)], slots[b], [ls[s] for s in range(ZN)])


def attend(lengths, qt, kv):
    blocks, rows, count = qt.shape
    whole = pl.BlockSpec(memory_space=pltpu.VMEM)
    return pl.pallas_call(
        forward_kernel,
        out_shape=[
            jax.ShapeDtypeStruct(qt.shape, jnp.bfloat16),
            jax.ShapeDtypeStruct(qt.shape, jnp.float32),
            jax.ShapeDtypeStruct((blocks, 8, count), jnp.float32),
        ],
        in_specs=[pl.BlockSpec(memory_space=pltpu.SMEM), whole, whole],
        out_specs=[whole] * 3,
        scratch_shapes=[
            pltpu.VMEM((GROUP, 256, count), jnp.bfloat16),
            pltpu.VMEM((GROUP, HEAD, count), jnp.float32),
            pltpu.VMEM(qt.shape, jnp.bfloat16),
            pltpu.VMEM(qt.shape, jnp.float32),
            pltpu.VMEM((blocks, 8, count), jnp.float32),
        ],
        compiler_params=pltpu.CompilerParams(vmem_limit_bytes=67043328),
    )(lengths, qt, kv)


def backward_kernel(lengths, qt, kv, out, lse, dot_in, cosine, sine, dq_out, dkv_out, qmt, qm, dmt, dm, dq, acc, qs, ds, es, ls, dqs):
    count = qt.shape[2]
    tiles = kv.shape[0] // TILE

    def clear(tile, carry):
        acc[pl.ds(pl.multiple_of(tile * TILE, TILE), TILE), :] = jnp.zeros((TILE, acc.shape[1]), jnp.float32)
        return carry

    lax.fori_loop(0, tiles, clear, 0)

    begin, end, spots, slots = lane_slots(lengths, count)
    for b in range(ZN):
        product_rows = dot_in[b].astype(jnp.float32) * out[b]
        for h in range(GROUP):
            es[b, h : h + 1] = jnp.sum(product_rows[h * HEAD : (h + 1) * HEAD], axis=0, keepdims=True)
    for s in range(ZN):
        qs[s] = pick(slots, s, [qt[b] for b in range(ZN)])
        ds[s] = pick(slots, s, [dot_in[b] for b in range(ZN)])
        ls[s] = pick(slots, s, [lse[b] for b in range(ZN)])
    picked = [pick(slots, s, [es[b] for b in range(ZN)]) for s in range(ZN)]
    for s in range(ZN):
        es[s] = picked[s]

    def one_block(big, s, carry):
        low, high = bounds_of(lengths, pick(slots, s, spots))
        rows = qs[s] * jnp.bfloat16(0.125)
        grads = ds[s]
        deltas = [es[s, h : h + 1] for h in range(GROUP)]
        levels = [ls[s, h : h + 1] for h in range(GROUP)]
        for h in range(GROUP):
            padded = pad_heads(rows, h, Q_SLOTS)
            qmt[h] = padded
            qm[h * count : (h + 1) * count] = padded.T
            padded = pad_heads(grads, h, V_SLOTS)
            dmt[h] = padded
            dm[h * count : (h + 1) * count] = padded.T
        dq[...] = jnp.zeros_like(dq)

        def step(at, size, masked, inner):
            span = pl.ds(at, size)
            keys = kv[span, 0:256]
            values = kv[span, 128:384]
            turned = keys.T
            mask = keys_in(at, size, low, high) if masked else None
            probs, slopes = [], []
            for h in range(GROUP):
                weights = jnp.exp(dot(keys, qmt[h]) - levels[h])
                if masked:
                    weights = jnp.where(mask, weights, 0.0)
                slope = (weights * (dot(values, dmt[h]) - deltas[h])).astype(jnp.bfloat16)
                dq[h] += dot(turned[h * HEAD : (h + 1) * HEAD], slope)
                probs.append(weights.astype(jnp.bfloat16))
                slopes.append(slope)
            dv = dot(jnp.concatenate(probs, axis=1), dm[...])
            dk = dot(jnp.concatenate(slopes, axis=1), qm[...])
            acc[span, 0:128] += dk[:, :128]
            acc[span, 128:256] += dk[:, 128:] + dv[:, :128]
            acc[span, 256:384] += dv[:, 128:]
            return inner

        walk(big, begin, end, low, high, step, 0)
        for h in range(GROUP):
            dqs[s, h * HEAD : (h + 1) * HEAD] = dq[h] * 0.125
        return carry

    lax.fori_loop(0, ZN // 2, functools.partial(one_block, True), 0)
    lax.fori_loop(ZN // 2, ZN, functools.partial(one_block, False), 0)
    half = HEAD // 2
    for b in range(ZN):
        back = pick([jnp.full_like(slots[b], s) for s in range(ZN)], slots[b], [dqs[s] for s in range(ZN)])
        for h in range(GROUP):
            at = h * HEAD
            w1, w2 = back[at : at + half], back[at + half : at + HEAD]
            dq_out[b, at : at + half] = (w1 * cosine[b] + w2 * sine[b]).astype(dq_out.dtype)
            dq_out[b, at + half : at + HEAD] = (w2 * cosine[b] - w1 * sine[b]).astype(dq_out.dtype)

    def finish(tile, carry):
        span = pl.ds(pl.multiple_of(tile * TILE, TILE), TILE)
        dkv_out[span, :] = acc[span, :].astype(dkv_out.dtype)
        return carry

    lax.fori_loop(0, tiles, finish, 0)


def attend_back(lengths, qt, kv, out, lse, dots, cosine, sine):
    blocks, rows, count = qt.shape
    whole = pl.BlockSpec(memory_space=pltpu.VMEM)
    return pl.pallas_call(
        backward_kernel,
        out_shape=[
            jax.ShapeDtypeStruct(qt.shape, jnp.bfloat16),
            jax.ShapeDtypeStruct(kv.shape, jnp.bfloat16),
        ],
        in_specs=[pl.BlockSpec(memory_space=pltpu.SMEM)] + [whole] * 7,
        out_specs=[whole] * 2,
        scratch_shapes=[
            pltpu.VMEM((GROUP, 256, count), jnp.bfloat16),
            pltpu.VMEM((GROUP * count, 256), jnp.bfloat16),
            pltpu.VMEM((GROUP, 256, count), jnp.bfloat16),
            pltpu.VMEM((GROUP * count, 256), jnp.bfloat16),
            pltpu.VMEM((GROUP, HEAD, count), jnp.float32),
            pltpu.VMEM(kv.shape, jnp.float32),
            pltpu.VMEM(qt.shape, jnp.bfloat16),
            pltpu.VMEM(qt.shape, jnp.bfloat16),
            pltpu.VMEM((blocks, 8, count), jnp.float32),
            pltpu.VMEM((blocks, 8, count), jnp.float32),
            pltpu.VMEM(qt.shape, jnp.float32),
        ],
        compiler_params=pltpu.CompilerParams(vmem_limit_bytes=67043328),
    )(lengths, qt, kv, out, lse, dots, cosine, sine)


KV_SLOTS = (0, 1, 2, 5, 3, 4)


def turn(rows, cosine, sine):
    first, second = rows[:, 0], rows[:, 1]
    return jnp.stack([first * cosine - second * sine, second * cosine + first * sine], axis=1)


def turn_back(rows, cosine, sine):
    first, second = rows[:, 0], rows[:, 1]
    return jnp.stack([first * cosine + second * sine, second * cosine - first * sine], axis=1)


def tables(lengths, first, count):
    starts = jnp.cumsum(lengths) - lengths
    position = first[:, None] + jnp.arange(count, dtype=jnp.int32)[None, :]
    begun = position[..., None] >= starts
    offsets = position - jnp.max(jnp.where(begun, starts, 0), axis=-1)
    half = HEAD // 2
    frequency = rope_base ** (-(jnp.arange(half, dtype=jnp.float32) * 2.0) / HEAD)
    angles = offsets.astype(jnp.float32)[:, None, :] * frequency[None, :, None]
    return jnp.cos(angles), jnp.sin(angles)


def contract(left, right, dims):
    return lax.dot_general(left, right, (dims, ((), ())), preferred_element_type=jnp.float32)


def local_grid(
    tokens,
    qkv_weight,
    out_weight,
    gate_weight,
    up_weight,
    down_weight,
    first_gain,
    first_bias,
    second_gain,
    second_bias,
    lengths,
    cotangent,
):
    bf16 = jnp.bfloat16
    rows, width = tokens.shape
    share = first_gain.shape[0]
    heads = width // HEAD
    half = HEAD // 2
    x, y, z, c = place()
    spots = [(px, py, pz, pc) for pz in range(ZN) for py in range(YN) for pc in range(CN) for px in range(XN)]
    over_x = [(block(*p), block(1 - p[0], *p[1:])) for p in spots]
    over_y = [(block(*p), block(p[0], 1 - p[1], *p[2:])) for p in spots]
    small = jnp.stack([first_gain, first_bias, second_gain, second_bias])
    small = jnp.pad(small, ((0, 4), (0, 128 - share)))
    hidden_width = gate_weight.shape[1]

    (qkv_blocks,) = gather([qkv_weight], ["bcast"], 1)
    qkv_full = qkv_blocks.reshape(width, 3 * width)
    turned = jnp.stack([block(x, y, b, c) for b in range(ZN)]) * rows
    cos_all, sin_all = tables(lengths, turned, rows)
    cosine = lax.dynamic_index_in_dim(cos_all, z, 0, keepdims=False)
    sine = lax.dynamic_index_in_dim(sin_all, z, 0, keepdims=False)

    raw = contract(qkv_full, tokens, ((0,), (1,))).astype(bf16)
    raw = raw.reshape(3, heads, 2, half, rows)
    queries = turn(raw[0].astype(jnp.float32), cosine, sine).astype(bf16)
    keys = turn(raw[1].astype(jnp.float32), cosine, sine).astype(bf16)
    queries = queries.reshape(ZN, GROUP * HEAD, rows)
    pairs = jnp.concatenate(
        [keys.reshape(ZN, GROUP, HEAD, rows), raw[2].reshape(ZN, GROUP, HEAD, rows)], axis=1
    )
    pairs = jnp.concatenate([pairs[:, s : s + 1] for s in KV_SLOTS], axis=1)
    pairs = jnp.swapaxes(pairs.reshape(ZN, 2 * GROUP * HEAD, rows), 1, 2)

    pairs_all, queries, out_full, down_full, small, gate_part, up_part = gather(
        [pairs, queries, out_weight, down_weight, small, gate_weight, up_weight],
        ["cross", "swap", "bcast", "bcast", "bcast", "by_x", "by_y"],
        2,
    )
    out_full = out_full.reshape(width, width)
    grid = (ZN, YN, CN, XN) + gate_weight.shape
    gate_send = gate_part.reshape(grid)[:, y, c].reshape((2 * ZN,) + gate_weight.shape)
    up_send = up_part.reshape(grid)[:, :, c, x].reshape((2 * ZN,) + up_weight.shape)
    gate_rest = lax.ppermute(gate_send, ("cp", "hd"), over_y)
    up_rest = lax.ppermute(up_send, ("cp", "hd"), over_x)
    down_full = down_full.reshape(hidden_width, width)
    gain_one, bias_one, gain_two, bias_two = [
        small[:, i, :share].reshape(width).astype(jnp.float32) for i in range(4)
    ]
    pairs_all = pairs_all.reshape(-1, 2 * GROUP * HEAD)
    low, attended, lse = attend(lengths, queries, pairs_all)
    low, gate_full, up_full = gather(
        [low, gate_rest, up_rest], ["swap", "rest_y", "rest_x"], 3, (gate_part, up_part)
    )
    gate_full = gate_full.reshape(width, hidden_width)
    up_full = up_full.reshape(width, hidden_width)
    low = low.reshape(width, rows)

    attn_out = contract(low, out_full, ((0,), (0,)))
    first, scaled_one, inv_one = normalize(tokens.astype(jnp.float32) + attn_out, gain_one, bias_one)
    first_low = first.astype(bf16)
    gate_proj = product(first_low, gate_full)
    up_proj = product(first_low, up_full)
    sigmoid_gate = jax.nn.sigmoid(gate_proj)
    silu_gate = gate_proj * sigmoid_gate
    hidden = (silu_gate * up_proj).astype(bf16)
    branch = product(hidden, down_full)
    second, scaled_two, inv_two = normalize(first + branch, gain_two, bias_two)
    layer_out = second.astype(bf16)

    upstream = cotangent.astype(jnp.float32)
    dz_two, gain_two_grad, bias_two_grad = normalize_back(upstream, scaled_two, inv_two, gain_two)
    dz_two_low = dz_two.astype(bf16)
    down_sum = contract(hidden, dz_two_low, ((0,), (0,))).astype(bf16)
    hidden_grad = contract(dz_two_low, down_full, ((1,), (1,)))
    gate_back = (
        hidden_grad * up_proj * sigmoid_gate * (1.0 + gate_proj * (1.0 - sigmoid_gate))
    ).astype(bf16)
    up_back = (hidden_grad * silu_gate).astype(bf16)
    gate_sum = contract(first_low, gate_back, ((0,), (0,))).astype(bf16)
    up_sum = contract(first_low, up_back, ((0,), (0,))).astype(bf16)
    first_back = (
        dz_two + contract(gate_back, gate_full, ((1,), (1,))) + contract(up_back, up_full, ((1,), (1,)))
    )
    dz_one, gain_one_grad, bias_one_grad = normalize_back(first_back, scaled_one, inv_one, gain_one)
    dz_one_low = dz_one.astype(bf16)
    out_sum = product(low, dz_one_low).astype(bf16)
    attended_back = contract(out_full, dz_one_low, ((1,), (1,))).astype(bf16)
    attended_back, gate_keep, gate_send, up_keep, up_send = reduce(
        [
            attended_back.reshape(ZN, GROUP * HEAD, rows),
            gate_sum.reshape((BLOCKS,) + gate_weight.shape),
            up_sum.reshape((BLOCKS,) + up_weight.shape),
        ],
        ["swap", "pair_y", "pair_x"],
        4,
    )
    gate_rest = lax.ppermute(gate_send, ("cp", "hd"), over_y)
    up_rest = lax.ppermute(up_send, ("cp", "hd"), over_x)

    query_back, pair_back = attend_back(
        lengths, queries, pairs_all, attended, lse, attended_back, cos_all, sin_all
    )
    small_sum = jnp.stack([gain_one_grad, bias_one_grad, gain_two_grad, bias_two_grad])
    small_sum = jnp.swapaxes(small_sum.reshape(4, BLOCKS, share), 0, 1)
    small_sum = jnp.pad(small_sum, ((0, 0), (0, 4), (0, 128 - share)))
    pair_back, query_back, out_grad, down_grad, small_grad, gate_grad, up_grad = reduce(
        [
            pair_back.reshape(BLOCKS, rows, 2 * GROUP * HEAD),
            query_back,
            out_sum.reshape(BLOCKS, share, width),
            down_sum.reshape(BLOCKS, -1, width),
            small_sum,
            (gate_keep, gate_rest),
            (up_keep, up_rest),
        ],
        ["cross", "swap", "reduce", "reduce", "reduce", "rest_y", "rest_x"],
        5,
    )
    pair_back = jnp.swapaxes(pair_back, 1, 2).reshape(ZN, 2 * GROUP, HEAD, rows)
    pair_back = [pair_back[:, KV_SLOTS.index(s)] for s in range(2 * GROUP)]
    key_back = jnp.stack(pair_back[:GROUP], axis=1).reshape(heads, 2, half, rows)
    key_back = turn_back(key_back.astype(jnp.float32), cosine, sine).astype(bf16)
    value_back = jnp.stack(pair_back[GROUP:], axis=1)
    raw_back = jnp.concatenate(
        [
            query_back.reshape(width, rows),
            key_back.reshape(width, rows),
            value_back.reshape(width, rows),
        ],
        axis=0,
    )
    qkv_sum = contract(tokens, raw_back, ((0,), (1,))).astype(bf16)
    tokens_grad = (dz_one + contract(raw_back, qkv_full, ((0,), (1,)))).astype(bf16)
    (qkv_grad,) = reduce([qkv_sum.reshape(BLOCKS, share, 3 * width)], ["reduce"], 6)
    return (
        layer_out,
        tokens_grad,
        qkv_grad,
        out_grad,
        gate_grad,
        up_grad,
        down_grad,
        small_grad[0, :share],
        small_grad[1, :share],
        small_grad[2, :share],
        small_grad[3, :share],
    )


def solution(mesh):
    rows = P(("cp", "hd"), None)
    line = P(("cp", "hd"))
    local = local_grid if (mesh.shape["cp"], mesh.shape["hd"]) == (ZN * YN * CN, XN) else local_any
    return jax.shard_map(
        local,
        mesh=mesh,
        in_specs=(rows,) * 6 + (line,) * 4 + (P(), rows),
        out_specs=(rows,) * 7 + (line,) * 4,
        check_vma=False,
    )
```

```python
import functools

import jax
import jax.numpy as jnp
from jax import lax
from jax.experimental import pallas as pl
from jax.experimental.pallas import tpu as pltpu
from jax.sharding import PartitionSpec as P

HD = 64
REACH = 8


rope_base = 1000.0
norm_eps = 1e-12
score_scale = 0.125
masked_score = -1000000000.0


def shifted(block, axis, distance):
    devices = range(lax.axis_size(axis))
    route = [(i - distance, i) for i in devices if i - distance in devices]
    return lax.ppermute(block, axis, route)


def doc_layout(lengths, first_row, row_count):
    starts = jnp.cumsum(lengths) - lengths
    position = first_row + jnp.arange(row_count, dtype=jnp.int32)
    at_or_after = position[:, None] >= starts[None, :]
    doc_ids = jnp.sum(at_or_after.astype(jnp.int32), axis=1) - 1
    doc_begin = jnp.max(jnp.where(at_or_after, starts[None, :], 0), axis=1)
    return (doc_ids, position - doc_begin)


def rope_tables(offsets, head_size):
    half_size = head_size // 2
    frequency = rope_base ** (-(jnp.arange(half_size, dtype=jnp.float32) * 2.0) / head_size)
    angles = offsets.astype(jnp.float32)[:, None] * frequency[None, :]
    return (jnp.cos(angles), jnp.sin(angles))


def rotate(values, cosine, sine):
    half_size = values.shape[-1] // 2
    first_half = values[..., :half_size]
    second_half = values[..., half_size:]
    cos_rows = cosine[:, None, :]
    sin_rows = sine[:, None, :]
    return jnp.concatenate(
        [
            first_half * cos_rows - second_half * sin_rows,
            second_half * cos_rows + first_half * sin_rows,
        ],
        axis=-1,
    )


def rotate_back(grads, cosine, sine):
    half_size = grads.shape[-1] // 2
    first_half = grads[..., :half_size]
    second_half = grads[..., half_size:]
    cos_rows = cosine[:, None, :]
    sin_rows = sine[:, None, :]
    return jnp.concatenate(
        [
            first_half * cos_rows + second_half * sin_rows,
            second_half * cos_rows - first_half * sin_rows,
        ],
        axis=-1,
    )


def normalize(hidden_in, gain_vec, bias_vec):
    average = jnp.mean(hidden_in, axis=-1, keepdims=True)
    centered = hidden_in - average
    variance = jnp.mean(centered * centered, axis=-1, keepdims=True)
    inv_std = lax.rsqrt(variance + norm_eps)
    scaled = centered * inv_std
    return (scaled * gain_vec + bias_vec, scaled, inv_std)


def normalize_back(upstream, scaled, inv_std, gain_vec):
    weighted = upstream * gain_vec
    inner = (
        weighted
        - jnp.mean(weighted, axis=-1, keepdims=True)
        - scaled * jnp.mean(weighted * scaled, axis=-1, keepdims=True)
    )
    return (inv_std * inner, jnp.sum(upstream * scaled, axis=0), jnp.sum(upstream, axis=0))


def product(left, right):
    return jnp.dot(left, right, preferred_element_type=jnp.float32)


def local_any(
    tokens,
    qkv_weight,
    out_weight,
    gate_weight,
    up_weight,
    down_weight,
    first_gain,
    first_bias,
    second_gain,
    second_bias,
    doc_lengths,
    cotangent,
):
    rows_here = tokens.shape[0]
    model_width = tokens.shape[1]
    hd_count = lax.axis_size("hd")
    cp_count = lax.axis_size("cp")
    cp_index = lax.axis_index("cp")
    block_rows = rows_here * hd_count
    local_width = model_width // hd_count
    local_heads = local_width // HD
    shifts = [0]
    for distance in range(1, REACH + 1):
        shifts = shifts + [-distance, distance]
    shards = (
        qkv_weight,
        out_weight,
        gate_weight,
        up_weight,
        down_weight,
        first_gain,
        first_bias,
        second_gain,
        second_bias,
    )
    weights = (
        lax.all_gather(shards[0], ("cp", "hd"), axis=0, tiled=True),
        lax.all_gather(shards[1], ("cp", "hd"), axis=0, tiled=True),
        lax.all_gather(shards[2], ("cp", "hd"), axis=0, tiled=True),
        lax.all_gather(shards[3], ("cp", "hd"), axis=0, tiled=True),
        lax.all_gather(shards[4], ("cp", "hd"), axis=0, tiled=True),
        lax.all_gather(shards[5], ("cp", "hd"), axis=0, tiled=True),
        lax.all_gather(shards[6], ("cp", "hd"), axis=0, tiled=True),
        lax.all_gather(shards[7], ("cp", "hd"), axis=0, tiled=True),
        lax.all_gather(shards[8], ("cp", "hd"), axis=0, tiled=True),
    )
    (
        qkv_full,
        out_full,
        gate_full,
        up_full,
        down_full,
        gain_first,
        bias_first,
        gain_second,
        bias_second,
    ) = weights
    raw_rows = product(tokens, qkv_full).astype(jnp.bfloat16)
    grouped = lax.all_to_all(
        raw_rows.reshape(rows_here, 3, hd_count, local_width),
        "hd",
        split_axis=2,
        concat_axis=0,
        tiled=True,
    )
    grouped = grouped.reshape(block_rows, 3, local_width)
    query_docs, offsets = doc_layout(doc_lengths, cp_index * block_rows, block_rows)
    cosine, sine = rope_tables(offsets, HD)
    queries = rotate(
        grouped[:, 0].astype(jnp.float32).reshape(block_rows, local_heads, HD), cosine, sine
    ).astype(jnp.bfloat16)
    key_rows = rotate(
        grouped[:, 1].astype(jnp.float32).reshape(block_rows, local_heads, HD), cosine, sine
    ).astype(jnp.bfloat16)
    own_block = jnp.stack([key_rows.reshape(block_rows, local_width), grouped[:, 2]], axis=1)

    def key_docs(distance):
        source = cp_index - distance
        doc_ids, unused_offsets = doc_layout(doc_lengths, source * block_rows, block_rows)
        inside = jnp.logical_and(source >= 0, source < cp_count)
        return jnp.where(inside, doc_ids, -2)

    remote = [own_block] + [shifted(own_block, "cp", distance) for distance in shifts[1:]]
    masks = [query_docs[:, None] == key_docs(distance)[None, :] for distance in shifts]

    def scores_with(query_part, remote_block, key_mask):
        key_part = remote_block[:, 0].reshape(block_rows, local_heads, HD)
        raw_scores = (
            jnp.einsum("qhd,khd->hqk", query_part, key_part, preferred_element_type=jnp.float32)
            * score_scale
        )
        return jnp.where(key_mask[None], raw_scores, masked_score)

    def scores_for(remote_block, key_mask):
        return scores_with(queries, remote_block, key_mask)

    running_max = jnp.full((local_heads, block_rows), masked_score, jnp.float32)
    running_sum = jnp.zeros((local_heads, block_rows), jnp.float32)
    for remote_block, key_mask in zip(remote, masks):
        block_scores = scores_for(remote_block, key_mask)
        new_max = jnp.maximum(running_max, jnp.max(block_scores, axis=-1))
        running_sum = running_sum * jnp.exp(running_max - new_max) + jnp.sum(
            jnp.exp(block_scores - new_max[:, :, None]), axis=-1
        )
        running_max = new_max
    log_total = running_max + jnp.log(running_sum)
    attended = jnp.zeros((block_rows, local_heads, HD), jnp.float32)
    for remote_block, key_mask in zip(remote, masks):
        block_scores = scores_for(remote_block, key_mask)
        probs = jnp.exp(block_scores - log_total[:, :, None]).astype(jnp.bfloat16)
        value_part = remote_block[:, 1].reshape(block_rows, local_heads, HD)
        attended = attended + jnp.einsum(
            "hqk,khd->qhd", probs, value_part, preferred_element_type=jnp.float32
        )
    attended_send = attended.reshape(block_rows, 1, local_width).astype(jnp.bfloat16)
    attended_low = lax.all_to_all(
        attended_send, "hd", split_axis=0, concat_axis=1, tiled=True
    ).reshape(rows_here, model_width)
    gain_one = gain_first.astype(jnp.float32)
    gain_two = gain_second.astype(jnp.float32)
    attn_out = product(attended_low, out_full)
    first, scaled_one, inv_one = normalize(
        tokens.astype(jnp.float32) + attn_out, gain_one, bias_first.astype(jnp.float32)
    )
    first_low = first.astype(jnp.bfloat16)
    gate_proj = product(first_low, gate_full)
    up_proj = product(first_low, up_full)
    sigmoid_gate = jax.nn.sigmoid(gate_proj)
    silu_gate = gate_proj * sigmoid_gate
    hidden = (silu_gate * up_proj).astype(jnp.bfloat16)
    branch = product(hidden, down_full)
    second, scaled_two, inv_two = normalize(
        first + branch, gain_two, bias_second.astype(jnp.float32)
    )
    layer_out = second.astype(jnp.bfloat16)
    weights = (
        lax.all_gather(shards[0], ("cp", "hd"), axis=0, tiled=True),
        lax.all_gather(shards[1], ("cp", "hd"), axis=0, tiled=True),
        lax.all_gather(shards[2], ("cp", "hd"), axis=0, tiled=True),
        lax.all_gather(shards[3], ("cp", "hd"), axis=0, tiled=True),
        lax.all_gather(shards[4], ("cp", "hd"), axis=0, tiled=True),
        lax.all_gather(shards[5], ("cp", "hd"), axis=0, tiled=True),
        lax.all_gather(shards[6], ("cp", "hd"), axis=0, tiled=True),
        lax.all_gather(shards[7], ("cp", "hd"), axis=0, tiled=True),
        lax.all_gather(shards[8], ("cp", "hd"), axis=0, tiled=True),
    )
    (
        qkv_full,
        out_full,
        gate_full,
        up_full,
        down_full,
        gain_first,
        bias_first,
        gain_second,
        bias_second,
    ) = weights
    upstream = cotangent.astype(jnp.float32)
    dz_two, gain_two_grad, bias_two_grad = normalize_back(upstream, scaled_two, inv_two, gain_two)
    dz_two_low = dz_two.astype(jnp.bfloat16)
    down_sum = product(hidden.T, dz_two_low)
    hidden_grad = product(dz_two_low, down_full.T)
    gate_back = (
        hidden_grad * up_proj * sigmoid_gate * (1.0 + gate_proj * (1.0 - sigmoid_gate))
    ).astype(jnp.bfloat16)
    up_back = (hidden_grad * silu_gate).astype(jnp.bfloat16)
    gate_sum = product(first_low.T, gate_back)
    up_sum = product(first_low.T, up_back)
    first_back = dz_two + product(gate_back, gate_full.T) + product(up_back, up_full.T)
    dz_one, gain_one_grad, bias_one_grad = normalize_back(first_back, scaled_one, inv_one, gain_one)
    dz_one_low = dz_one.astype(jnp.bfloat16)
    out_sum = product(attended_low.T, dz_one_low)
    attended_back = product(dz_one_low, out_full.T).astype(jnp.bfloat16)
    heads_back = lax.all_to_all(
        attended_back.reshape(rows_here, hd_count, local_width),
        "hd",
        split_axis=1,
        concat_axis=0,
        tiled=True,
    )
    heads_back = heads_back.reshape(block_rows, local_heads, HD)
    delta = jnp.transpose(jnp.sum(heads_back.astype(jnp.float32) * attended, axis=-1))
    query_grad = jnp.zeros((block_rows, local_heads, HD), jnp.float32)
    pair_total = jnp.zeros((block_rows, 2, local_width), jnp.float32)
    remote = [own_block] + [shifted(own_block, "cp", distance) for distance in shifts[1:]]
    for distance, remote_block, key_mask in zip(shifts, remote, masks):
        pair_block_scores = scores_with(queries, remote_block, key_mask)
        pair_probs = jnp.exp(pair_block_scores - log_total[:, :, None])
        pair_key_part = remote_block[:, 0].reshape(block_rows, local_heads, HD)
        pair_value_part = remote_block[:, 1].reshape(block_rows, local_heads, HD)
        value_grad = jnp.einsum(
            "hqk,qhd->khd",
            pair_probs.astype(jnp.bfloat16),
            heads_back,
            preferred_element_type=jnp.float32,
        )
        prob_grad = jnp.einsum(
            "qhd,khd->hqk", heads_back, pair_value_part, preferred_element_type=jnp.float32
        )
        score_grad = (pair_probs * (prob_grad - delta[:, :, None])).astype(jnp.bfloat16)
        query_term = (
            jnp.einsum(
                "hqk,khd->qhd", score_grad, pair_key_part, preferred_element_type=jnp.float32
            )
            * score_scale
        )
        key_grad = (
            jnp.einsum("hqk,qhd->khd", score_grad, queries, preferred_element_type=jnp.float32)
            * score_scale
        )
        grad_pair = jnp.stack(
            [
                key_grad.reshape(block_rows, local_width),
                value_grad.reshape(block_rows, local_width),
            ],
            axis=1,
        )
        query_term, grad_pair = (query_term, grad_pair)
        query_grad = query_grad + query_term
        if distance == 0:
            pair_total = grad_pair
        else:
            pair_total = pair_total + shifted(
                grad_pair.astype(jnp.bfloat16), "cp", -distance
            ).astype(grad_pair.dtype)
    query_back = rotate_back(query_grad, cosine, sine).reshape(block_rows, local_width)
    key_back = rotate_back(
        pair_total[:, 0].reshape(block_rows, local_heads, HD), cosine, sine
    ).reshape(block_rows, local_width)
    raw_back = jnp.stack([query_back, key_back, pair_total[:, 1]], axis=1).astype(jnp.bfloat16)
    raw_back = lax.all_to_all(
        raw_back.reshape(block_rows, 3, 1, local_width),
        "hd",
        split_axis=0,
        concat_axis=2,
        tiled=True,
    )
    raw_back = raw_back.reshape(rows_here, 3 * model_width)
    qkv_sum = product(tokens.T, raw_back)
    tokens_grad = (dz_one + product(raw_back, qkv_full.T)).astype(jnp.bfloat16)
    summed = (
        lax.psum_scatter(qkv_sum, ("cp", "hd"), scatter_dimension=0, tiled=True),
        lax.psum_scatter(out_sum, ("cp", "hd"), scatter_dimension=0, tiled=True),
        lax.psum_scatter(gate_sum, ("cp", "hd"), scatter_dimension=0, tiled=True),
        lax.psum_scatter(up_sum, ("cp", "hd"), scatter_dimension=0, tiled=True),
        lax.psum_scatter(down_sum, ("cp", "hd"), scatter_dimension=0, tiled=True),
        lax.psum_scatter(gain_one_grad, ("cp", "hd"), scatter_dimension=0, tiled=True),
        lax.psum_scatter(bias_one_grad, ("cp", "hd"), scatter_dimension=0, tiled=True),
        lax.psum_scatter(gain_two_grad, ("cp", "hd"), scatter_dimension=0, tiled=True),
        lax.psum_scatter(bias_two_grad, ("cp", "hd"), scatter_dimension=0, tiled=True),
    )
    return (
        layer_out,
        tokens_grad,
        summed[0],
        summed[1],
        summed[2],
        summed[3],
        summed[4],
        summed[5],
        summed[6],
        summed[7],
        summed[8],
    )


MESH = pl.DeviceIdType.MESH
ZN, YN, CN, XN = 4, 2, 2, 2
BLOCKS = ZN * YN * CN * XN


def place():
    cp = lax.axis_index("cp")
    x = lax.axis_index("hd")
    return x, lax.rem(cp // CN, YN), cp // (YN * CN), lax.rem(cp, CN)


def device(x, y, z, c):
    return ((z * YN + y) * CN + c, x)


def block(x, y, z, c):
    return ((z * YN + y) * CN + c) * XN + x


def when(cond, fn):
    if cond is None:
        fn()
    else:
        pl.when(cond)(fn)


def both(a, b):
    if a is None:
        return b
    if b is None:
        return a
    return jnp.logical_and(a, b)


def halves(ref):
    rows, cols = ref.shape[-2:]
    if rows % 32 == 0:
        return ref.at[pl.ds(0, rows // 2)], ref.at[pl.ds(rows // 2, rows // 2)]
    if cols % 256 == 0:
        return ref.at[:, pl.ds(0, cols // 2)], ref.at[:, pl.ds(cols // 2, cols // 2)]
    return ref, None


def greet(x, y, z, c, far):
    barrier = pltpu.get_barrier_semaphore()
    for peer in (device(1 - x, y, z, c), device(x, 1 - y, z, c), device(x, y, z, 1 - c)):
        pl.semaphore_signal(barrier, inc=1, device_id=peer, device_id_type=MESH)
    count = 3
    if far:
        for k in range(1, ZN):
            peer = device(x, y, lax.rem(z + k, ZN), c)
            pl.semaphore_signal(barrier, inc=1, device_id=peer, device_id_type=MESH)
        count = count + ZN - 1
    else:
        pl.when(z > 0)(lambda: pl.semaphore_signal(barrier, inc=1, device_id=device(x, y, z - 1, c), device_id_type=MESH))
        pl.when(z < ZN - 1)(lambda: pl.semaphore_signal(barrier, inc=1, device_id=device(x, y, z + 1, c), device_id_type=MESH))
        count = count + (z > 0).astype(jnp.int32) + (z < ZN - 1).astype(jnp.int32)
    pl.semaphore_wait(barrier, count)


SENDS = 40
RECVS = 36


CHAINED = ("bcast", "by_x", "by_y")
REST = ("rest_x", "rest_y")


SHORT_PLAN = [
    (fn, "chained", d - lag)
    for d in range(1, ZN + 2)
    for lag, fn in enumerate(("onward", "beside", "across"))
    if (d > 0 if lag else d < ZN) and 0 <= d - lag < ZN
]
PLAN = [
    ("onward", "chained", 1),
    ("beside", "chained", 0),
    ("beside", "crossed", 0),
    ("across", "chained", 0),
    ("beside", "chained", 1),
    ("onward", "crossed", 1),
    ("across", "crossed", 0),
    ("across", "chained", 1),
    ("onward", "crossed", 2),
    ("onward", "crossed", 3),
    ("beside", "crossed", 1),
    ("onward", "chained", 2),
    ("beside", "crossed", 2),
    ("beside", "crossed", 3),
    ("beside", "chained", 2),
    ("across", "crossed", 1),
    ("onward", "chained", 3),
    ("across", "crossed", 2),
    ("across", "crossed", 3),
    ("across", "chained", 2),
    ("beside", "chained", 3),
    ("across", "chained", 3),
]


def gather_kernel(modes, *refs):
    n = len(modes)
    ins, refs = refs[:n], refs[n:]
    refs = refs[sum(mode in REST for mode in modes) :]
    outs, (lsem, ssem, rsem) = refs[:n], refs[n:]
    x, y, z, c = place()
    ox, oy, oc = 1 - x, 1 - y, 1 - c
    greet(x, y, z, c, any(m in ("swap", "cross") for m in modes))
    sent = []

    def copy(k, src, dst, s, r, peer):
        return pltpu.make_async_remote_copy(
            src_ref=src,
            dst_ref=dst,
            send_sem=ssem.at[k, s],
            recv_sem=rsem.at[k, r],
            device_id=peer,
            device_id_type=MESH,
        )

    def send(cond, *args):
        when(cond, lambda: copy(*args).start())
        sent.append((cond, args))

    def arrived(cond, k, ref, r):
        when(cond, lambda: copy(k, ref, ref, 0, r, device(ox, y, z, c)).wait_recv())

    locals_ = []

    def keep(k, i, mine, spot):
        pltpu.make_async_copy(mine, spot, lsem.at[k, i]).start()
        locals_.append((k, i, mine, spot))

    for k, mode in enumerate(modes):
        if mode in CHAINED:
            keep(k, 0, ins[k], outs[k].at[block(x, y, z, c)])
        elif mode == "swap":
            keep(k, 0, ins[k].at[z], outs[k].at[z])
        elif mode == "cross":
            keep(k, 0, ins[k].at[z], outs[k].at[block(x, y, z, c)])

    def spread(k, cond, b, src, up, down):
        here = outs[k].at[block(x, y, b, c)]
        if modes[k] in CHAINED:
            if up is not False:
                send(both(cond, up), k, src, here, b, b, device(x, y, lax.rem(z + 1, ZN), c))
            if down is not False:
                send(both(cond, down), k, src, here, 4 + b, b, device(x, y, lax.rem(z + ZN - 1, ZN), c))
        if modes[k] != "by_y":
            send(cond, k, src, here, 8 + b, 4 + b, device(ox, y, z, c))
        if modes[k] != "by_x":
            send(cond, k, src, here, 16 + b, 12 + b, device(x, oy, z, c))
        send(cond, k, src, here, 24 + b, 20 + b, device(x, y, z, oc))

    def sides(k, cond, b):
        fx = outs[k].at[block(ox, y, b, c)]
        fy = outs[k].at[block(x, oy, b, c)]
        full = modes[k] in ("bcast", "cross")
        if modes[k] != "by_y":
            arrived(cond, k, fx, 4 + b)
            first, _ = halves(fx)
            if full:
                send(cond, k, first, first, 20 + b, 16 + b, device(x, oy, z, c))
            send(cond, k, fx, fx, 28 + b, 24 + b, device(x, y, z, oc))
        if modes[k] != "by_x":
            arrived(cond, k, fy, 12 + b)
            _, second = halves(fy)
            if full and second is not None:
                send(cond, k, second, second, 12 + b, 8 + b, device(ox, y, z, c))
            send(cond, k, fy, fy, 32 + b, 28 + b, device(x, y, z, oc))

    def corner(k, cond, b):
        far = outs[k].at[block(ox, oy, b, c)]
        first, second = halves(far)
        arrived(cond, k, first, 16 + b)
        if second is not None:
            arrived(cond, k, second, 8 + b)
        send(cond, k, far, far, 36 + b, 32 + b, device(x, y, z, oc))

    def steps(distance):
        if distance == 0:
            return [(None, z)]
        return [(z >= distance, jnp.maximum(z - distance, 0)), (z + distance < ZN, jnp.minimum(z + distance, ZN - 1))]

    chained = [k for k, mode in enumerate(modes) if mode in CHAINED]
    crossed = [k for k, mode in enumerate(modes) if mode == "cross"]
    swapped = [k for k, mode in enumerate(modes) if mode == "swap"]

    def exchange(ks):
        for k in ks:
            for d in range(1, ZN):
                to = lax.rem(z + d, ZN)
                spot = outs[k].at[z] if modes[k] == "swap" else outs[k].at[block(x, y, z, c)]
                send(None, k, ins[k].at[to], spot, to, z, device(x, y, to, c))

    for k in chained:
        spread(k, None, z, ins[k], z < ZN - 1, z > 0)
    for k, mode in enumerate(modes):
        if mode in REST:
            for b in range(ZN):
                for j in range(2):
                    spot = block(j, oy, b, c) if mode == "rest_y" else block(ox, j, b, c)
                    keep(k, 2 * b + j, ins[k].at[2 * b + j], outs[k].at[spot])
                    send(None, k, ins[k].at[2 * b + j], outs[k].at[spot], 2 * b + j, 2 * b + j, device(x, y, z, oc))
    for k in crossed:
        spread(k, None, z, ins[k].at[z], False, False)
    exchange(crossed)

    def onward(ks, distance):
        for side, (cond, b) in enumerate(steps(distance)):
            for k in ks:
                here = outs[k].at[block(x, y, b, c)]
                arrived(cond, k, here, b)
                spread(k, cond, b, here, z < ZN - 1 if side == 0 else False, z > 0 if side == 1 else False)

    def beside(ks, distance):
        for cond, b in steps(distance):
            for k in ks:
                sides(k, cond, b)

    def across(ks, distance):
        for cond, b in steps(distance):
            for k in ks:
                if modes[k] in ("bcast", "cross"):
                    corner(k, cond, b)

    plan = PLAN if crossed else SHORT_PLAN
    for fn, ks, distance in plan if chained else ():
        fn = {"onward": onward, "beside": beside, "across": across}[fn]
        fn(chained if ks == "chained" else crossed, distance)
        if fn is onward and distance == 2 and ks == "chained":
            exchange(swapped)
            swapped = []
    exchange(swapped)
    for k, mode in enumerate(modes):
        if mode == "swap":
            for d in range(1, ZN):
                frm = lax.rem(z + d, ZN)
                arrived(None, k, outs[k].at[frm], frm)
        elif mode in REST:
            for b in range(ZN):
                for j in range(2):
                    spot = block(j, oy, b, oc) if mode == "rest_y" else block(ox, j, b, oc)
                    arrived(None, k, outs[k].at[spot], 2 * b + j)
        else:
            quads = {"by_x": (0, 1), "by_y": (0, 2)}.get(mode, (0, 1, 2, 3))
            for b in range(ZN):
                for j in quads:
                    px, py = ((x, y), (ox, y), (x, oy), (ox, oy))[j]
                    arrived(None, k, outs[k].at[block(px, py, b, oc)], 20 + 4 * j + b)
    for k, i, mine, spot in locals_:
        pltpu.make_async_copy(mine, spot, lsem.at[k, i]).wait()
    for cond, args in sent:
        when(cond, lambda args=args: copy(*args).wait_send())


def gather(arrays, modes, collective_id, filled=()):
    shapes = []
    rest = [k for k, mode in enumerate(modes) if mode in REST]
    for k, (a, mode) in enumerate(zip(arrays, modes)):
        if mode in CHAINED:
            shapes.append((BLOCKS,) + a.shape)
        elif mode == "swap":
            shapes.append(a.shape)
        else:
            shapes.append((BLOCKS,) + a.shape[1:])
    n = len(arrays)
    return pl.pallas_call(
        functools.partial(gather_kernel, tuple(modes)),
        out_shape=[jax.ShapeDtypeStruct(s, a.dtype) for s, a in zip(shapes, arrays)],
        in_specs=[pl.BlockSpec(memory_space=pltpu.VMEM)] * n + [pl.BlockSpec(memory_space=pl.ANY)] * len(rest),
        out_specs=[pl.BlockSpec(memory_space=pl.ANY)] * n,
        input_output_aliases={n + i: k for i, k in enumerate(rest)},
        scratch_shapes=[
            pltpu.SemaphoreType.DMA((n, 8)),
            pltpu.SemaphoreType.DMA((n, SENDS)),
            pltpu.SemaphoreType.DMA((n, RECVS)),
        ],
        compiler_params=pltpu.CompilerParams(collective_id=collective_id, has_side_effects=True),
    )(*arrays, *filled)


def chunk_of(cols):
    for size in (768, 640, 512, 384, 256, 128):
        if cols % size == 0:
            return size
    return cols


def add_up(dst, sources):
    rows, cols = dst.shape[-2:]
    size = chunk_of(cols)

    def step(i, carry):
        span = pl.ds(pl.multiple_of(i * size, size), size)
        total = sources[0][:, span].astype(jnp.float32)
        for source in sources[1:]:
            total = total + source[:, span].astype(jnp.float32)
        dst[:, span] = total.astype(dst.dtype)
        return carry

    if cols == size:
        total = sources[0][...].astype(jnp.float32)
        for source in sources[1:]:
            total = total + source[...].astype(jnp.float32)
        dst[...] = total.astype(dst.dtype)
    else:
        lax.fori_loop(0, cols // size, step, 0)


BUFFERS = {"swap": 0, "pair_x": 2, "pair_y": 2, "cross": 3, "reduce": 4, "rest_x": 4, "rest_y": 4}
PAIR = ("pair_x", "pair_y")


def take(refs, counts):
    groups = []
    for count in counts:
        groups.append(refs[:count])
        refs = refs[count:]
    return groups, refs


def reduce_kernel(modes, *refs):
    n = len(modes)
    ins, refs = take(refs, [2 if mode in REST else 1 for mode in modes])
    outs, refs = take(refs, [2 if mode in PAIR else 1 for mode in modes])
    (lsem, ssem, rsem), scratch = refs[:3], refs[3:]
    bufs, _ = take(scratch, [BUFFERS[mode] for mode in modes])
    others, seconds = ins, outs
    ins, outs = [group[0] for group in ins], [group[0] for group in outs]
    x, y, z, c = place()
    ox, oy, oc = 1 - x, 1 - y, 1 - c
    greet(x, y, z, c, any(m in ("swap", "cross") for m in modes))
    sent = []

    def copy(k, src, dst, s, r, peer):
        return pltpu.make_async_remote_copy(
            src_ref=src,
            dst_ref=dst,
            send_sem=ssem.at[k, s],
            recv_sem=rsem.at[k, r],
            device_id=peer,
            device_id_type=MESH,
        )

    def send(cond, *args):
        when(cond, lambda: copy(*args).start())
        sent.append((cond, args))

    def arrived(cond, k, ref, r):
        when(cond, lambda: copy(k, ref, ref, 0, r, device(ox, y, z, c)).wait_recv())

    half = z // 2
    order = [3 - 3 * half, 2 - half, 1 - z + 4 * half, z]
    quads = ((ox, oy), (ox, y), (x, oy), (x, y))
    active = [k for k, mode in enumerate(modes) if mode in ("cross", "reduce")]
    paired = [k for k, mode in enumerate(modes) if mode in PAIR]
    rest = [k for k, mode in enumerate(modes) if mode in REST]

    for k in rest:
        acc, rec = bufs[k][:2]
        for i, b in enumerate(order):
            for j in range(2):
                mine = (x, y)[modes[k] == "rest_x"]
                spot = 2 * b + (mine if j else 1 - mine)
                pltpu.make_async_copy(ins[k].at[spot], acc.at[2 * i + j], lsem.at[k, 2 * i + j]).start()
                pltpu.make_async_copy(others[k][1].at[spot], rec.at[2 * i + j], lsem.at[k, 8 + 2 * i + j]).start()
    for k in active:
        for i, b in enumerate(order):
            acc, cor = bufs[k][:2]
            for j, (px, py) in enumerate(quads):
                send(None, k, ins[k].at[block(px, py, b, oc)], cor.at[4 * i + j], 4 * i + j, 4 * i + j, device(x, y, z, oc))
                pltpu.make_async_copy(ins[k].at[block(px, py, b, c)], acc.at[4 * i + j], lsem.at[k, 4 * i + j]).start()

    def spots(k, i):
        b, j = i // 2, i % 2
        if modes[k] == "pair_y":
            return (j, y, b), (j, oy, b)
        return (x, j, b), (ox, j, b)

    for k in paired:
        acc, cor = bufs[k]
        for i in range(8):
            for s, (px, py, b) in enumerate(spots(k, i)):
                send(None, k, ins[k].at[block(px, py, b, oc)], cor.at[2 * i + s], 2 * i + s, 2 * i + s, device(x, y, z, oc))
                pltpu.make_async_copy(ins[k].at[block(px, py, b, c)], acc.at[2 * i + s], lsem.at[k, 2 * i + s]).start()
    for k, mode in enumerate(modes):
        if mode == "swap":
            for d in range(1, ZN):
                to = lax.rem(z + d, ZN)
                send(None, k, ins[k].at[to], outs[k].at[z], d, z, device(x, y, to, c))
            pltpu.make_async_copy(ins[k].at[z], outs[k].at[z], lsem.at[k, 0]).start()

    def loaded(k, i, j):
        acc, cor = bufs[k][:2]
        pltpu.make_async_copy(ins[k].at[0], acc.at[4 * i + j], lsem.at[k, 4 * i + j]).wait()
        arrived(None, k, cor.at[4 * i + j], 4 * i + j)

    for k in paired:
        acc, cor = bufs[k]

        def join(i, carry, k=k, acc=acc, cor=cor):
            for s in range(2):
                at = 2 * i + s
                pltpu.make_async_copy(ins[k].at[0], acc.at[at], lsem.at[k, at]).wait()
                arrived(None, k, cor.at[at], at)
                add_up(seconds[k][s].at[i], (acc.at[at], cor.at[at]))
            return carry

        lax.fori_loop(0, 8, join, 0)

    def fetched(k, i, j):
        acc, rec = bufs[k][:2]
        pltpu.make_async_copy(ins[k].at[0], acc.at[2 * i + j], lsem.at[k, 2 * i + j]).wait()
        pltpu.make_async_copy(ins[k].at[0], rec.at[2 * i + j], lsem.at[k, 8 + 2 * i + j]).wait()

    def ahead(k, i, b):
        acc, rec, side = bufs[k][:3]
        fetched(k, i, 0)
        add_up(acc.at[2 * i], (acc.at[2 * i], rec.at[2 * i]))
        peer = device(x, oy, z, c) if modes[k] == "rest_x" else device(ox, y, z, c)
        send(None, k, acc.at[2 * i], side.at[i], 16 + i, 16 + i, peer)

    def corner(k, i, b):
        acc, cor, side = bufs[k][:3]
        loaded(k, i, 0)
        add_up(acc.at[4 * i], (acc.at[4 * i], cor.at[4 * i]))
        first, second = halves(acc.at[4 * i])
        send(None, k, first, halves(side.at[i])[0], 16 + i, 16 + i, device(x, oy, z, c))
        if second is not None:
            send(None, k, second, halves(side.at[4 + i])[1], 20 + i, 20 + i, device(ox, y, z, c))

    def beside(k, i, b):
        acc, cor, side = bufs[k][:3]
        loaded(k, i, 1)
        add_up(acc.at[4 * i + 1], (acc.at[4 * i + 1], cor.at[4 * i + 1]))
        part = halves(side.at[i])[0]
        arrived(None, k, part, 16 + i)
        mine = halves(acc.at[4 * i + 1])[0]
        add_up(mine, (mine, part))
        send(None, k, acc.at[4 * i + 1], side.at[8 + i], 24 + i, 24 + i, device(ox, y, z, c))
        loaded(k, i, 2)
        add_up(acc.at[4 * i + 2], (acc.at[4 * i + 2], cor.at[4 * i + 2]))
        part = halves(side.at[4 + i])[1]
        if part is not None:
            arrived(None, k, part, 20 + i)
            mine = halves(acc.at[4 * i + 2])[1]
            add_up(mine, (mine, part))
        send(None, k, acc.at[4 * i + 2], side.at[12 + i], 28 + i, 28 + i, device(x, oy, z, c))

    def settle(k, i, b):
        side = bufs[k][2]
        if k in rest:
            acc, rec = bufs[k][:2]
            fetched(k, i, 1)
            arrived(None, k, side.at[i], 16 + i)
            own = acc.at[2 * i + 1]
            terms = (own, rec.at[2 * i + 1], side.at[i])
        else:
            acc, cor = bufs[k][:2]
            loaded(k, i, 3)
            own = acc.at[4 * i + 3]
            arrived(None, k, side.at[8 + i], 24 + i)
            arrived(None, k, side.at[12 + i], 28 + i)
            terms = (own, cor.at[4 * i + 3], side.at[8 + i], side.at[12 + i])
        if modes[k] == "cross":
            add_up(own, terms)
            if i < ZN - 1:
                send(None, k, own, outs[k].at[z], 32 + i, 32 + z, device(x, y, b, c))
            else:
                pltpu.make_async_copy(own, outs[k].at[z], lsem.at[k, 16]).start()
            return
        chain = bufs[k][3]
        if i == ZN - 1:
            add_up(outs[k], terms)

            def lower(k=k, chain=chain):
                arrived(None, k, chain.at[z], 32 + z)
                add_up(outs[k], (outs[k], chain.at[z]))

            def upper(k=k, chain=chain):
                arrived(None, k, chain.at[4 + z], 36 + z)
                add_up(outs[k], (outs[k], chain.at[4 + z]))

            pl.when(z > 0)(lower)
            pl.when(z < ZN - 1)(upper)
        else:
            add_up(own, terms)
            below = both(b > z, z > 0)
            above = both(b < z, z < ZN - 1)

            def lower(k=k, chain=chain, own=own, b=b):
                arrived(None, k, chain.at[b], 32 + b)
                add_up(own, (own, chain.at[b]))

            def upper(k=k, chain=chain, own=own, b=b):
                arrived(None, k, chain.at[4 + b], 36 + b)
                add_up(own, (own, chain.at[4 + b]))

            pl.when(below)(lower)
            pl.when(above)(upper)
            send(b > z, k, own, chain.at[b], 32 + i, 32 + b, device(x, y, lax.rem(z + 1, ZN), c))
            send(b < z, k, own, chain.at[4 + b], 32 + i, 36 + b, device(x, y, lax.rem(z + ZN - 1, ZN), c))

    crossed = [k for k in active if modes[k] == "cross"]
    plain = [k for k in active if modes[k] == "reduce"]
    stages = [[(ahead, rest)], [(corner, crossed)], [(corner, plain)]]
    stages = stages + [[(settle, rest), (beside, crossed)], [(settle, crossed), (beside, plain)], [(settle, plain)]]
    for stage in stages:
        for i, b in enumerate(order):
            for fn, ks in stage:
                for k in ks:
                    fn(k, i, b)
    for k, mode in enumerate(modes):
        if mode not in ("swap", "cross"):
            continue
        for d in range(1, ZN):
            frm = lax.rem(z + d, ZN)
            arrived(None, k, outs[k].at[frm], frm if mode == "swap" else 32 + frm)
        if mode == "swap":
            pltpu.make_async_copy(ins[k].at[z], outs[k].at[z], lsem.at[k, 0]).wait()
        else:
            pltpu.make_async_copy(bufs[k][0].at[15], outs[k].at[z], lsem.at[k, 16]).wait()
    for cond, args in sent:
        when(cond, lambda args=args: copy(*args).wait_send())


def reduce(arrays, modes, collective_id):
    shapes, specs, scratch, operands, inputs = [], [], [], [], []
    anywhere, local = pl.BlockSpec(memory_space=pl.ANY), pl.BlockSpec(memory_space=pltpu.VMEM)
    for a, mode in zip(arrays, modes):
        operands = operands + (list(a) if mode in REST else [a])
        inputs = inputs + [local if mode == "swap" else anywhere] * (2 if mode in REST else 1)
        a = a[0] if mode in REST else a
        rows, cols = a.shape[1:]
        sizes = {"swap": (), "pair_x": (16, 16), "cross": (16, 16, 16), "reduce": (16, 16, 16, 8), "rest_x": (8, 8, 4, 8)}
        sizes = sizes[mode.replace("_y", "_x")]
        scratch = scratch + [pltpu.VMEM((size, rows, cols), a.dtype) for size in sizes]
        if mode == "swap":
            shapes.append(jax.ShapeDtypeStruct(a.shape, a.dtype))
            specs.append(anywhere)
        elif mode in PAIR:
            shapes = shapes + [jax.ShapeDtypeStruct((8, rows, cols), a.dtype)] * 2
            specs = specs + [local] * 2
        elif mode == "cross":
            shapes.append(jax.ShapeDtypeStruct((ZN, rows, cols), a.dtype))
            specs.append(anywhere)
        else:
            shapes.append(jax.ShapeDtypeStruct((rows, cols), jnp.float32))
            specs.append(local)
    n = len(arrays)
    return pl.pallas_call(
        functools.partial(reduce_kernel, tuple(modes)),
        out_shape=shapes,
        in_specs=inputs,
        out_specs=specs,
        scratch_shapes=[
            pltpu.SemaphoreType.DMA((n, 17)),
            pltpu.SemaphoreType.DMA((n, SENDS)),
            pltpu.SemaphoreType.DMA((n, SENDS)),
        ]
        + scratch,
        compiler_params=pltpu.CompilerParams(
            collective_id=collective_id, has_side_effects=True, vmem_limit_bytes=67043328
        ),
    )(*operands)


HEAD = 64
GROUP = 3
TILE = 512
WIDE = 1024
EDGE = 128
SPAN = 4096
FAR = 1 << 30


def longest(lengths):
    begin, best, at = jnp.int32(0), lengths[0], jnp.int32(0)
    for j in range(lengths.shape[0]):
        length = lengths[j]
        at = jnp.where(length > best, begin, at)
        best = jnp.maximum(best, length)
        begin = begin + length
    return at, at + best


def lane_slots(lengths, count):
    x, y, z, c = place()
    lane = lax.broadcasted_iota(jnp.int32, (1, count), 1)
    begin, end = longest(lengths)
    spots = [block(x, y, b, c) * count + lane for b in range(ZN)]
    slots, before = [], jnp.zeros((1, count), jnp.int32)
    for b in range(ZN):
        big = jnp.logical_and(spots[b] >= begin, spots[b] < end)
        slots.append(jnp.where(big, before, ZN // 2 + b - before))
        before = before + big.astype(jnp.int32)
    return begin, end, spots, slots


def pick(slots, slot, parts):
    chosen = parts[-1]
    for b in range(len(parts) - 2, -1, -1):
        chosen = jnp.where(slots[b] == slot, parts[b], chosen)
    return chosen


def bounds_of(lengths, spot):
    low, high = jnp.zeros_like(spot), jnp.full_like(spot, FAR)
    begin = jnp.int32(0)
    for j in range(lengths.shape[0]):
        end = begin + lengths[j]
        low = jnp.where(spot >= begin, begin, low)
        high = jnp.where(spot < end, jnp.minimum(high, end), high)
        begin = end
    return low, high


def walk(big, begin, end, low, high, step, init):
    if big:
        base = begin // EDGE * EDGE

        def body(i, carry):
            at = pl.multiple_of(base + i * WIDE, EDGE)
            return step(at, WIDE, False, carry)

        carry = step(pl.multiple_of(base, EDGE), WIDE, True, init)
        carry = lax.fori_loop(1, SPAN // WIDE, body, carry)
        return lax.cond(
            begin > base,
            lambda c: step(pl.multiple_of(base + SPAN, EDGE), EDGE, True, c),
            lambda c: c,
            carry,
        )
    first = jnp.min(low) // TILE
    stop = (jnp.max(high) + TILE - 1) // TILE
    hole_first = jnp.maximum((begin + TILE - 1) // TILE, first)
    hole = jnp.maximum(jnp.minimum(end // TILE, stop) - hole_first, 0)

    def body(i, carry):
        tile = first + i
        tile = jnp.where(jnp.logical_and(hole > 0, tile >= hole_first), tile + hole, tile)
        return step(pl.multiple_of(tile * TILE, TILE), TILE, True, carry)

    return lax.fori_loop(0, stop - first - hole, body, init)


def keys_in(first, size, low, high):
    at = first + lax.broadcasted_iota(jnp.int32, (size, low.shape[1]), 0)
    return jnp.logical_and(at >= low, at < high)


def dot(a, b):
    return jnp.dot(a, b, preferred_element_type=jnp.float32)


def pad_heads(rows, h, slots):
    part = rows[h * HEAD : (h + 1) * HEAD]
    zero = jnp.zeros_like(part)
    return jnp.concatenate([part if s == h else zero for s in slots], axis=0)


Q_SLOTS = (0, 1, 2, -1)
V_SLOTS = (-1, 2, 0, 1)


def forward_kernel(lengths, qt, kv, low_out, out, lse_out, qm, acc, qs, os, ls):
    count = qt.shape[2]
    begin, end, spots, slots = lane_slots(lengths, count)
    for s in range(ZN):
        qs[s] = pick(slots, s, [qt[b] for b in range(ZN)])

    def one_block(big, s, carry):
        low, high = bounds_of(lengths, pick(slots, s, spots))
        rows = qs[s] * jnp.bfloat16(0.125)
        for h in range(GROUP):
            qm[h] = pad_heads(rows, h, Q_SLOTS)
        acc[...] = jnp.zeros_like(acc)

        def step(at, size, masked, stats):
            span = pl.ds(at, size)
            keys = kv[span, 0:256]
            values = kv[span, 128:384].T
            mask = keys_in(at, size, low, high) if masked else None
            fresh = []
            for h in range(GROUP):
                top, total = stats[2 * h], stats[2 * h + 1]
                scores = dot(keys, qm[h])
                if masked:
                    scores = jnp.where(mask, scores, -1e9)
                new_top = jnp.maximum(top, jnp.max(scores, axis=0, keepdims=True))
                shrink = jnp.exp(top - new_top)
                weights = jnp.exp(scores - new_top)
                total = total * shrink + jnp.sum(weights, axis=0, keepdims=True)
                row = V_SLOTS.index(h) * HEAD
                acc[h] = acc[h] * shrink + dot(values[row : row + HEAD], weights.astype(jnp.bfloat16))
                fresh = fresh + [new_top, total]
            return tuple(fresh)

        init = (jnp.full((1, count), -1e9, jnp.float32), jnp.zeros((1, count), jnp.float32)) * GROUP
        stats = walk(big, begin, end, low, high, step, init)
        for h in range(GROUP):
            top, total = stats[2 * h], stats[2 * h + 1]
            os[s, h * HEAD : (h + 1) * HEAD] = acc[h] / total
            ls[s, h : h + 1] = top + jnp.log(total)
        return carry

    lax.fori_loop(0, ZN // 2, functools.partial(one_block, True), 0)
    lax.fori_loop(ZN // 2, ZN, functools.partial(one_block, False), 0)
    for b in range(ZN):
        value = pick([jnp.full_like(slots[b], s) for s in range(ZN)], slots[b], [os[s] for s in range(ZN)])
        out[b] = value
        low_out[b] = value.astype(low_out.dtype)
        lse_out[b] = pick([jnp.full_like(slots[b], s) for s in range(ZN)], slots[b], [ls[s] for s in range(ZN)])


def attend(lengths, qt, kv):
    blocks, rows, count = qt.shape
    whole = pl.BlockSpec(memory_space=pltpu.VMEM)
    return pl.pallas_call(
        forward_kernel,
        out_shape=[
            jax.ShapeDtypeStruct(qt.shape, jnp.bfloat16),
            jax.ShapeDtypeStruct(qt.shape, jnp.float32),
            jax.ShapeDtypeStruct((blocks, 8, count), jnp.float32),
        ],
        in_specs=[pl.BlockSpec(memory_space=pltpu.SMEM), whole, whole],
        out_specs=[whole] * 3,
        scratch_shapes=[
            pltpu.VMEM((GROUP, 256, count), jnp.bfloat16),
            pltpu.VMEM((GROUP, HEAD, count), jnp.float32),
            pltpu.VMEM(qt.shape, jnp.bfloat16),
            pltpu.VMEM(qt.shape, jnp.float32),
            pltpu.VMEM((blocks, 8, count), jnp.float32),
        ],
        compiler_params=pltpu.CompilerParams(vmem_limit_bytes=67043328),
    )(lengths, qt, kv)


def backward_kernel(lengths, qt, kv, out, lse, dot_in, cosine, sine, dq_out, dkv_out, qmt, qm, dmt, dm, dq, acc, qs, ds, es, ls, dqs):
    count = qt.shape[2]
    tiles = kv.shape[0] // TILE

    def clear(tile, carry):
        acc[pl.ds(pl.multiple_of(tile * TILE, TILE), TILE), :] = jnp.zeros((TILE, acc.shape[1]), jnp.float32)
        return carry

    lax.fori_loop(0, tiles, clear, 0)

    begin, end, spots, slots = lane_slots(lengths, count)
    for b in range(ZN):
        product_rows = dot_in[b].astype(jnp.float32) * out[b]
        for h in range(GROUP):
            es[b, h : h + 1] = jnp.sum(product_rows[h * HEAD : (h + 1) * HEAD], axis=0, keepdims=True)
    for s in range(ZN):
        qs[s] = pick(slots, s, [qt[b] for b in range(ZN)])
        ds[s] = pick(slots, s, [dot_in[b] for b in range(ZN)])
        ls[s] = pick(slots, s, [lse[b] for b in range(ZN)])
    picked = [pick(slots, s, [es[b] for b in range(ZN)]) for s in range(ZN)]
    for s in range(ZN):
        es[s] = picked[s]

    def one_block(big, s, carry):
        low, high = bounds_of(lengths, pick(slots, s, spots))
        rows = qs[s] * jnp.bfloat16(0.125)
        grads = ds[s]
        deltas = [es[s, h : h + 1] for h in range(GROUP)]
        levels = [ls[s, h : h + 1] for h in range(GROUP)]
        for h in range(GROUP):
            padded = pad_heads(rows, h, Q_SLOTS)
            qmt[h] = padded
            qm[h * count : (h + 1) * count] = padded.T
            padded = pad_heads(grads, h, V_SLOTS)
            dmt[h] = padded
            dm[h * count : (h + 1) * count] = padded.T
        dq[...] = jnp.zeros_like(dq)

        def step(at, size, masked, inner):
            span = pl.ds(at, size)
            keys = kv[span, 0:256]
            values = kv[span, 128:384]
            turned = keys.T
            mask = keys_in(at, size, low, high) if masked else None
            probs, slopes = [], []
            for h in range(GROUP):
                weights = jnp.exp(dot(keys, qmt[h]) - levels[h])
                if masked:
                    weights = jnp.where(mask, weights, 0.0)
                slope = (weights * (dot(values, dmt[h]) - deltas[h])).astype(jnp.bfloat16)
                dq[h] += dot(turned[h * HEAD : (h + 1) * HEAD], slope)
                probs.append(weights.astype(jnp.bfloat16))
                slopes.append(slope)
            dv = dot(jnp.concatenate(probs, axis=1), dm[...])
            dk = dot(jnp.concatenate(slopes, axis=1), qm[...])
            acc[span, 0:128] += dk[:, :128]
            acc[span, 128:256] += dk[:, 128:] + dv[:, :128]
            acc[span, 256:384] += dv[:, 128:]
            return inner

        walk(big, begin, end, low, high, step, 0)
        for h in range(GROUP):
            dqs[s, h * HEAD : (h + 1) * HEAD] = dq[h] * 0.125
        return carry

    lax.fori_loop(0, ZN // 2, functools.partial(one_block, True), 0)
    lax.fori_loop(ZN // 2, ZN, functools.partial(one_block, False), 0)
    half = HEAD // 2
    for b in range(ZN):
        back = pick([jnp.full_like(slots[b], s) for s in range(ZN)], slots[b], [dqs[s] for s in range(ZN)])
        for h in range(GROUP):
            at = h * HEAD
            w1, w2 = back[at : at + half], back[at + half : at + HEAD]
            dq_out[b, at : at + half] = (w1 * cosine[b] + w2 * sine[b]).astype(dq_out.dtype)
            dq_out[b, at + half : at + HEAD] = (w2 * cosine[b] - w1 * sine[b]).astype(dq_out.dtype)

    def finish(tile, carry):
        span = pl.ds(pl.multiple_of(tile * TILE, TILE), TILE)
        dkv_out[span, :] = acc[span, :].astype(dkv_out.dtype)
        return carry

    lax.fori_loop(0, tiles, finish, 0)


def attend_back(lengths, qt, kv, out, lse, dots, cosine, sine):
    blocks, rows, count = qt.shape
    whole = pl.BlockSpec(memory_space=pltpu.VMEM)
    return pl.pallas_call(
        backward_kernel,
        out_shape=[
            jax.ShapeDtypeStruct(qt.shape, jnp.bfloat16),
            jax.ShapeDtypeStruct(kv.shape, jnp.bfloat16),
        ],
        in_specs=[pl.BlockSpec(memory_space=pltpu.SMEM)] + [whole] * 7,
        out_specs=[whole] * 2,
        scratch_shapes=[
            pltpu.VMEM((GROUP, 256, count), jnp.bfloat16),
            pltpu.VMEM((GROUP * count, 256), jnp.bfloat16),
            pltpu.VMEM((GROUP, 256, count), jnp.bfloat16),
            pltpu.VMEM((GROUP * count, 256), jnp.bfloat16),
            pltpu.VMEM((GROUP, HEAD, count), jnp.float32),
            pltpu.VMEM(kv.shape, jnp.float32),
            pltpu.VMEM(qt.shape, jnp.bfloat16),
            pltpu.VMEM(qt.shape, jnp.bfloat16),
            pltpu.VMEM((blocks, 8, count), jnp.float32),
            pltpu.VMEM((blocks, 8, count), jnp.float32),
            pltpu.VMEM(qt.shape, jnp.float32),
        ],
        compiler_params=pltpu.CompilerParams(vmem_limit_bytes=67043328),
    )(lengths, qt, kv, out, lse, dots, cosine, sine)


KV_SLOTS = (0, 1, 2, 5, 3, 4)


def turn(rows, cosine, sine):
    first, second = rows[:, 0], rows[:, 1]
    return jnp.stack([first * cosine - second * sine, second * cosine + first * sine], axis=1)


def turn_back(rows, cosine, sine):
    first, second = rows[:, 0], rows[:, 1]
    return jnp.stack([first * cosine + second * sine, second * cosine - first * sine], axis=1)


def tables(lengths, first, count):
    starts = jnp.cumsum(lengths) - lengths
    position = first[:, None] + jnp.arange(count, dtype=jnp.int32)[None, :]
    begun = position[..., None] >= starts
    offsets = position - jnp.max(jnp.where(begun, starts, 0), axis=-1)
    half = HEAD // 2
    frequency = rope_base ** (-(jnp.arange(half, dtype=jnp.float32) * 2.0) / HEAD)
    angles = offsets.astype(jnp.float32)[:, None, :] * frequency[None, :, None]
    return jnp.cos(angles), jnp.sin(angles)


def norm_back(upstream, scaled, inv_std, gain_vec):
    weighted = upstream * gain_vec
    inner = (
        weighted
        - jnp.mean(weighted, axis=-1, keepdims=True)
        - scaled * jnp.mean(weighted * scaled, axis=-1, keepdims=True)
    )
    sums = [jnp.sum(upstream * scaled, axis=0, keepdims=True), jnp.sum(upstream, axis=0, keepdims=True)]
    return inv_std * inner, sums


def contract(left, right, dims):
    return lax.dot_general(left, right, (dims, ((), ())), preferred_element_type=jnp.float32)


def copies_kernel(*refs):
    n = len(refs) // 3
    ins, outs, bufs, sems = refs[:n], refs[n : 2 * n], refs[2 * n : 3 * n], refs[3 * n]
    loads = [pltpu.make_async_copy(ins[k], bufs[k], sems.at[k]) for k in range(n)]
    stores = [pltpu.make_async_copy(bufs[k], outs[k], sems.at[n + k]) for k in range(n)]
    for load in loads:
        load.start()
    for load, store in zip(loads, stores):
        load.wait()
        store.start()
    for store in stores:
        store.wait()


def copies(arrays):
    n = len(arrays)
    anywhere = pl.BlockSpec(memory_space=pl.ANY)
    return pl.pallas_call(
        copies_kernel,
        out_shape=[jax.ShapeDtypeStruct(a.shape, a.dtype) for a in arrays],
        in_specs=[anywhere] * n,
        out_specs=[anywhere] * n,
        scratch_shapes=[pltpu.VMEM(a.shape, a.dtype) for a in arrays] + [pltpu.SemaphoreType.DMA((2 * n,))],
    )(*arrays)


def local_grid(
    tokens,
    qkv_weight,
    out_weight,
    gate_weight,
    up_weight,
    down_weight,
    first_gain,
    first_bias,
    second_gain,
    second_bias,
    lengths,
    cotangent,
):
    bf16 = jnp.bfloat16
    rows, width = tokens.shape
    share = first_gain.shape[0]
    heads = width // HEAD
    half = HEAD // 2
    x, y, z, c = place()
    spots = [(px, py, pz, pc) for pz in range(ZN) for py in range(YN) for pc in range(CN) for px in range(XN)]
    over_x = [(block(*p), block(1 - p[0], *p[1:])) for p in spots]
    over_y = [(block(*p), block(p[0], 1 - p[1], *p[2:])) for p in spots]
    small = jnp.stack([first_gain, first_bias, second_gain, second_bias])
    small = jnp.pad(small, ((0, 4), (0, 128 - share)))
    hidden_width = gate_weight.shape[1]

    qkv_blocks, gate_part, up_part = gather([qkv_weight, gate_weight, up_weight], ["bcast", "by_x", "by_y"], 1)
    qkv_full = qkv_blocks.reshape(width, 3 * width)
    turned = jnp.stack([block(x, y, b, c) for b in range(ZN)]) * rows
    cos_all, sin_all = tables(lengths, turned, rows)
    cosine = lax.dynamic_index_in_dim(cos_all, z, 0, keepdims=False)
    sine = lax.dynamic_index_in_dim(sin_all, z, 0, keepdims=False)

    raw = contract(qkv_full, tokens, ((0,), (1,))).astype(bf16)
    raw = raw.reshape(3, heads, 2, half, rows)
    queries = turn(raw[0].astype(jnp.float32), cosine, sine).astype(bf16)
    keys = turn(raw[1].astype(jnp.float32), cosine, sine).astype(bf16)
    queries = queries.reshape(ZN, GROUP * HEAD, rows)
    pairs = jnp.concatenate(
        [keys.reshape(ZN, GROUP, HEAD, rows), raw[2].reshape(ZN, GROUP, HEAD, rows)], axis=1
    )
    pairs = jnp.concatenate([pairs[:, s : s + 1] for s in KV_SLOTS], axis=1)
    pairs = jnp.swapaxes(pairs.reshape(ZN, 2 * GROUP * HEAD, rows), 1, 2)

    pairs_all, queries, out_full, down_full, small = gather(
        [pairs, queries, out_weight, down_weight, small], ["cross", "swap", "bcast", "bcast", "bcast"], 2
    )
    out_full = out_full.reshape(width, width)
    grid = (ZN, YN, CN, XN) + gate_weight.shape
    gate_send = gate_part.reshape(grid)[:, y, c].reshape((2 * ZN,) + gate_weight.shape)
    up_send = up_part.reshape(grid)[:, :, c, x].reshape((2 * ZN,) + up_weight.shape)
    gate_rest = lax.ppermute(gate_send, ("cp", "hd"), over_y)
    up_rest = lax.ppermute(up_send, ("cp", "hd"), over_x)
    down_full = down_full.reshape(hidden_width, width)
    small = jnp.swapaxes(small[:, :4, :share], 0, 1).astype(jnp.float32).reshape(4, width)
    small = lax.optimization_barrier(small)
    gain_one, bias_one, gain_two, bias_two = [small[i] for i in range(4)]
    pairs_all = pairs_all.reshape(-1, 2 * GROUP * HEAD)
    low, attended, lse = attend(lengths, queries, pairs_all)
    low, gate_full, up_full = gather(
        [low, gate_rest, up_rest], ["swap", "rest_y", "rest_x"], 3, (gate_part, up_part)
    )
    gate_full = gate_full.reshape(width, hidden_width)
    up_full = up_full.reshape(width, hidden_width)
    low = low.reshape(width, rows)

    attn_out = contract(low, out_full, ((0,), (0,)))
    first, scaled_one, inv_one = normalize(tokens.astype(jnp.float32) + attn_out, gain_one, bias_one)
    first_low = first.astype(bf16)
    gate_proj = product(first_low, gate_full)
    up_proj = product(first_low, up_full)
    sigmoid_gate = jax.nn.sigmoid(gate_proj)
    silu_gate = gate_proj * sigmoid_gate
    hidden = (silu_gate * up_proj).astype(bf16)
    branch = product(hidden, down_full)
    second, scaled_two, inv_two = normalize(first + branch, gain_two, bias_two)
    layer_out = second.astype(bf16)

    upstream = cotangent.astype(jnp.float32)
    dz_two, sums_two = norm_back(upstream, scaled_two, inv_two, gain_two)
    dz_two_low = dz_two.astype(bf16)
    down_sum = contract(hidden, dz_two_low, ((0,), (0,))).astype(bf16)
    hidden_grad = contract(dz_two_low, down_full, ((1,), (1,)))
    gate_back = (
        hidden_grad * up_proj * sigmoid_gate * (1.0 + gate_proj * (1.0 - sigmoid_gate))
    ).astype(bf16)
    up_back = (hidden_grad * silu_gate).astype(bf16)
    gate_sum = contract(first_low, gate_back, ((0,), (0,))).astype(bf16)
    up_sum = contract(first_low, up_back, ((0,), (0,))).astype(bf16)
    first_back = (
        dz_two + contract(gate_back, gate_full, ((1,), (1,))) + contract(up_back, up_full, ((1,), (1,)))
    )
    dz_one, sums_one = norm_back(first_back, scaled_one, inv_one, gain_one)
    dz_one_low = dz_one.astype(bf16)
    out_sum = product(low, dz_one_low).astype(bf16)
    attended_back = contract(out_full, dz_one_low, ((1,), (1,))).astype(bf16)
    attended_back, gate_keep, gate_send, up_keep, up_send = reduce(
        [
            attended_back.reshape(ZN, GROUP * HEAD, rows),
            gate_sum.reshape((BLOCKS,) + gate_weight.shape),
            up_sum.reshape((BLOCKS,) + up_weight.shape),
        ],
        ["swap", "pair_y", "pair_x"],
        4,
    )
    gate_rest = lax.ppermute(gate_send, ("cp", "hd"), over_y)
    up_rest = lax.ppermute(up_send, ("cp", "hd"), over_x)

    query_back, pair_back = attend_back(
        lengths, queries, pairs_all, attended, lse, attended_back, cos_all, sin_all
    )
    small_sum = lax.optimization_barrier(jnp.concatenate(sums_one + sums_two, axis=0))
    small_sum = jnp.swapaxes(small_sum.reshape(4, BLOCKS, share), 0, 1)
    small_sum = jnp.pad(small_sum, ((0, 0), (0, 4), (0, 128 - share)))
    pair_back, query_back, out_grad, down_grad, small_grad, gate_grad, up_grad = reduce(
        [
            pair_back.reshape(BLOCKS, rows, 2 * GROUP * HEAD),
            query_back,
            out_sum.reshape(BLOCKS, share, width),
            down_sum.reshape(BLOCKS, -1, width),
            small_sum,
            (gate_keep, gate_rest),
            (up_keep, up_rest),
        ],
        ["cross", "swap", "reduce", "reduce", "reduce", "rest_y", "rest_x"],
        5,
    )
    pair_back = jnp.swapaxes(pair_back, 1, 2).reshape(ZN, 2 * GROUP, HEAD, rows)
    pair_back = [pair_back[:, KV_SLOTS.index(s)] for s in range(2 * GROUP)]
    key_back = jnp.stack(pair_back[:GROUP], axis=1).reshape(heads, 2, half, rows)
    key_back = turn_back(key_back.astype(jnp.float32), cosine, sine).astype(bf16)
    value_back = jnp.stack(pair_back[GROUP:], axis=1)
    raw_back = jnp.concatenate(
        [
            query_back.reshape(width, rows),
            key_back.reshape(width, rows),
            value_back.reshape(width, rows),
        ],
        axis=0,
    )
    qkv_sum = contract(tokens, raw_back, ((0,), (1,))).astype(bf16)
    tokens_grad = (dz_one + contract(raw_back, qkv_full, ((0,), (1,)))).astype(bf16)
    (qkv_grad,) = reduce([qkv_sum.reshape(BLOCKS, share, 3 * width)], ["reduce"], 6)
    qkv_grad, out_grad, gate_grad, up_grad, down_grad = copies([qkv_grad, out_grad, gate_grad, up_grad, down_grad])
    return (
        layer_out,
        tokens_grad,
        qkv_grad,
        out_grad,
        gate_grad,
        up_grad,
        down_grad,
        small_grad[0, :share],
        small_grad[1, :share],
        small_grad[2, :share],
        small_grad[3, :share],
    )


def solution(mesh):
    rows = P(("cp", "hd"), None)
    line = P(("cp", "hd"))
    local = local_grid if (mesh.shape["cp"], mesh.shape["hd"]) == (ZN * YN * CN, XN) else local_any
    return jax.shard_map(
        local,
        mesh=mesh,
        in_specs=(rows,) * 6 + (line,) * 4 + (P(), rows),
        out_specs=(rows,) * 7 + (line,) * 4,
        check_vma=False,
    )
```

```python
import functools

import jax
import jax.numpy as jnp
from jax import lax
from jax.experimental import pallas as pl
from jax.experimental.pallas import tpu as pltpu
from jax.sharding import PartitionSpec as P

HD = 64
REACH = 8


rope_base = 1000.0
norm_eps = 1e-12
score_scale = 0.125
masked_score = -1000000000.0


def shifted(block, axis, distance):
    devices = range(lax.axis_size(axis))
    route = [(i - distance, i) for i in devices if i - distance in devices]
    return lax.ppermute(block, axis, route)


def doc_layout(lengths, first_row, row_count):
    starts = jnp.cumsum(lengths) - lengths
    position = first_row + jnp.arange(row_count, dtype=jnp.int32)
    at_or_after = position[:, None] >= starts[None, :]
    doc_ids = jnp.sum(at_or_after.astype(jnp.int32), axis=1) - 1
    doc_begin = jnp.max(jnp.where(at_or_after, starts[None, :], 0), axis=1)
    return (doc_ids, position - doc_begin)


def rope_tables(offsets, head_size):
    half_size = head_size // 2
    frequency = rope_base ** (-(jnp.arange(half_size, dtype=jnp.float32) * 2.0) / head_size)
    angles = offsets.astype(jnp.float32)[:, None] * frequency[None, :]
    return (jnp.cos(angles), jnp.sin(angles))


def rotate(values, cosine, sine):
    half_size = values.shape[-1] // 2
    first_half = values[..., :half_size]
    second_half = values[..., half_size:]
    cos_rows = cosine[:, None, :]
    sin_rows = sine[:, None, :]
    return jnp.concatenate(
        [
            first_half * cos_rows - second_half * sin_rows,
            second_half * cos_rows + first_half * sin_rows,
        ],
        axis=-1,
    )


def rotate_back(grads, cosine, sine):
    half_size = grads.shape[-1] // 2
    first_half = grads[..., :half_size]
    second_half = grads[..., half_size:]
    cos_rows = cosine[:, None, :]
    sin_rows = sine[:, None, :]
    return jnp.concatenate(
        [
            first_half * cos_rows + second_half * sin_rows,
            second_half * cos_rows - first_half * sin_rows,
        ],
        axis=-1,
    )


def normalize(hidden_in, gain_vec, bias_vec):
    average = jnp.mean(hidden_in, axis=-1, keepdims=True)
    centered = hidden_in - average
    variance = jnp.mean(centered * centered, axis=-1, keepdims=True)
    inv_std = lax.rsqrt(variance + norm_eps)
    scaled = centered * inv_std
    return (scaled * gain_vec + bias_vec, scaled, inv_std)


def normalize_back(upstream, scaled, inv_std, gain_vec):
    weighted = upstream * gain_vec
    inner = (
        weighted
        - jnp.mean(weighted, axis=-1, keepdims=True)
        - scaled * jnp.mean(weighted * scaled, axis=-1, keepdims=True)
    )
    return (inv_std * inner, jnp.sum(upstream * scaled, axis=0), jnp.sum(upstream, axis=0))


def product(left, right):
    return jnp.dot(left, right, preferred_element_type=jnp.float32)


def local_any(
    tokens,
    qkv_weight,
    out_weight,
    gate_weight,
    up_weight,
    down_weight,
    first_gain,
    first_bias,
    second_gain,
    second_bias,
    doc_lengths,
    cotangent,
):
    rows_here = tokens.shape[0]
    model_width = tokens.shape[1]
    hd_count = lax.axis_size("hd")
    cp_count = lax.axis_size("cp")
    cp_index = lax.axis_index("cp")
    block_rows = rows_here * hd_count
    local_width = model_width // hd_count
    local_heads = local_width // HD
    shifts = [0]
    for distance in range(1, REACH + 1):
        shifts = shifts + [-distance, distance]
    shards = (
        qkv_weight,
        out_weight,
        gate_weight,
        up_weight,
        down_weight,
        first_gain,
        first_bias,
        second_gain,
        second_bias,
    )
    weights = (
        lax.all_gather(shards[0], ("cp", "hd"), axis=0, tiled=True),
        lax.all_gather(shards[1], ("cp", "hd"), axis=0, tiled=True),
        lax.all_gather(shards[2], ("cp", "hd"), axis=0, tiled=True),
        lax.all_gather(shards[3], ("cp", "hd"), axis=0, tiled=True),
        lax.all_gather(shards[4], ("cp", "hd"), axis=0, tiled=True),
        lax.all_gather(shards[5], ("cp", "hd"), axis=0, tiled=True),
        lax.all_gather(shards[6], ("cp", "hd"), axis=0, tiled=True),
        lax.all_gather(shards[7], ("cp", "hd"), axis=0, tiled=True),
        lax.all_gather(shards[8], ("cp", "hd"), axis=0, tiled=True),
    )
    (
        qkv_full,
        out_full,
        gate_full,
        up_full,
        down_full,
        gain_first,
        bias_first,
        gain_second,
        bias_second,
    ) = weights
    raw_rows = product(tokens, qkv_full).astype(jnp.bfloat16)
    grouped = lax.all_to_all(
        raw_rows.reshape(rows_here, 3, hd_count, local_width),
        "hd",
        split_axis=2,
        concat_axis=0,
        tiled=True,
    )
    grouped = grouped.reshape(block_rows, 3, local_width)
    query_docs, offsets = doc_layout(doc_lengths, cp_index * block_rows, block_rows)
    cosine, sine = rope_tables(offsets, HD)
    queries = rotate(
        grouped[:, 0].astype(jnp.float32).reshape(block_rows, local_heads, HD), cosine, sine
    ).astype(jnp.bfloat16)
    key_rows = rotate(
        grouped[:, 1].astype(jnp.float32).reshape(block_rows, local_heads, HD), cosine, sine
    ).astype(jnp.bfloat16)
    own_block = jnp.stack([key_rows.reshape(block_rows, local_width), grouped[:, 2]], axis=1)

    def key_docs(distance):
        source = cp_index - distance
        doc_ids, unused_offsets = doc_layout(doc_lengths, source * block_rows, block_rows)
        inside = jnp.logical_and(source >= 0, source < cp_count)
        return jnp.where(inside, doc_ids, -2)

    remote = [own_block] + [shifted(own_block, "cp", distance) for distance in shifts[1:]]
    masks = [query_docs[:, None] == key_docs(distance)[None, :] for distance in shifts]

    def scores_with(query_part, remote_block, key_mask):
        key_part = remote_block[:, 0].reshape(block_rows, local_heads, HD)
        raw_scores = (
            jnp.einsum("qhd,khd->hqk", query_part, key_part, preferred_element_type=jnp.float32)
            * score_scale
        )
        return jnp.where(key_mask[None], raw_scores, masked_score)

    def scores_for(remote_block, key_mask):
        return scores_with(queries, remote_block, key_mask)

    running_max = jnp.full((local_heads, block_rows), masked_score, jnp.float32)
    running_sum = jnp.zeros((local_heads, block_rows), jnp.float32)
    for remote_block, key_mask in zip(remote, masks):
        block_scores = scores_for(remote_block, key_mask)
        new_max = jnp.maximum(running_max, jnp.max(block_scores, axis=-1))
        running_sum = running_sum * jnp.exp(running_max - new_max) + jnp.sum(
            jnp.exp(block_scores - new_max[:, :, None]), axis=-1
        )
        running_max = new_max
    log_total = running_max + jnp.log(running_sum)
    attended = jnp.zeros((block_rows, local_heads, HD), jnp.float32)
    for remote_block, key_mask in zip(remote, masks):
        block_scores = scores_for(remote_block, key_mask)
        probs = jnp.exp(block_scores - log_total[:, :, None]).astype(jnp.bfloat16)
        value_part = remote_block[:, 1].reshape(block_rows, local_heads, HD)
        attended = attended + jnp.einsum(
            "hqk,khd->qhd", probs, value_part, preferred_element_type=jnp.float32
        )
    attended_send = attended.reshape(block_rows, 1, local_width).astype(jnp.bfloat16)
    attended_low = lax.all_to_all(
        attended_send, "hd", split_axis=0, concat_axis=1, tiled=True
    ).reshape(rows_here, model_width)
    gain_one = gain_first.astype(jnp.float32)
    gain_two = gain_second.astype(jnp.float32)
    attn_out = product(attended_low, out_full)
    first, scaled_one, inv_one = normalize(
        tokens.astype(jnp.float32) + attn_out, gain_one, bias_first.astype(jnp.float32)
    )
    first_low = first.astype(jnp.bfloat16)
    gate_proj = product(first_low, gate_full)
    up_proj = product(first_low, up_full)
    sigmoid_gate = jax.nn.sigmoid(gate_proj)
    silu_gate = gate_proj * sigmoid_gate
    hidden = (silu_gate * up_proj).astype(jnp.bfloat16)
    branch = product(hidden, down_full)
    second, scaled_two, inv_two = normalize(
        first + branch, gain_two, bias_second.astype(jnp.float32)
    )
    layer_out = second.astype(jnp.bfloat16)
    weights = (
        lax.all_gather(shards[0], ("cp", "hd"), axis=0, tiled=True),
        lax.all_gather(shards[1], ("cp", "hd"), axis=0, tiled=True),
        lax.all_gather(shards[2], ("cp", "hd"), axis=0, tiled=True),
        lax.all_gather(shards[3], ("cp", "hd"), axis=0, tiled=True),
        lax.all_gather(shards[4], ("cp", "hd"), axis=0, tiled=True),
        lax.all_gather(shards[5], ("cp", "hd"), axis=0, tiled=True),
        lax.all_gather(shards[6], ("cp", "hd"), axis=0, tiled=True),
        lax.all_gather(shards[7], ("cp", "hd"), axis=0, tiled=True),
        lax.all_gather(shards[8], ("cp", "hd"), axis=0, tiled=True),
    )
    (
        qkv_full,
        out_full,
        gate_full,
        up_full,
        down_full,
        gain_first,
        bias_first,
        gain_second,
        bias_second,
    ) = weights
    upstream = cotangent.astype(jnp.float32)
    dz_two, gain_two_grad, bias_two_grad = normalize_back(upstream, scaled_two, inv_two, gain_two)
    dz_two_low = dz_two.astype(jnp.bfloat16)
    down_sum = product(hidden.T, dz_two_low)
    hidden_grad = product(dz_two_low, down_full.T)
    gate_back = (
        hidden_grad * up_proj * sigmoid_gate * (1.0 + gate_proj * (1.0 - sigmoid_gate))
    ).astype(jnp.bfloat16)
    up_back = (hidden_grad * silu_gate).astype(jnp.bfloat16)
    gate_sum = product(first_low.T, gate_back)
    up_sum = product(first_low.T, up_back)
    first_back = dz_two + product(gate_back, gate_full.T) + product(up_back, up_full.T)
    dz_one, gain_one_grad, bias_one_grad = normalize_back(first_back, scaled_one, inv_one, gain_one)
    dz_one_low = dz_one.astype(jnp.bfloat16)
    out_sum = product(attended_low.T, dz_one_low)
    attended_back = product(dz_one_low, out_full.T).astype(jnp.bfloat16)
    heads_back = lax.all_to_all(
        attended_back.reshape(rows_here, hd_count, local_width),
        "hd",
        split_axis=1,
        concat_axis=0,
        tiled=True,
    )
    heads_back = heads_back.reshape(block_rows, local_heads, HD)
    delta = jnp.transpose(jnp.sum(heads_back.astype(jnp.float32) * attended, axis=-1))
    query_grad = jnp.zeros((block_rows, local_heads, HD), jnp.float32)
    pair_total = jnp.zeros((block_rows, 2, local_width), jnp.float32)
    remote = [own_block] + [shifted(own_block, "cp", distance) for distance in shifts[1:]]
    for distance, remote_block, key_mask in zip(shifts, remote, masks):
        pair_block_scores = scores_with(queries, remote_block, key_mask)
        pair_probs = jnp.exp(pair_block_scores - log_total[:, :, None])
        pair_key_part = remote_block[:, 0].reshape(block_rows, local_heads, HD)
        pair_value_part = remote_block[:, 1].reshape(block_rows, local_heads, HD)
        value_grad = jnp.einsum(
            "hqk,qhd->khd",
            pair_probs.astype(jnp.bfloat16),
            heads_back,
            preferred_element_type=jnp.float32,
        )
        prob_grad = jnp.einsum(
            "qhd,khd->hqk", heads_back, pair_value_part, preferred_element_type=jnp.float32
        )
        score_grad = (pair_probs * (prob_grad - delta[:, :, None])).astype(jnp.bfloat16)
        query_term = (
            jnp.einsum(
                "hqk,khd->qhd", score_grad, pair_key_part, preferred_element_type=jnp.float32
            )
            * score_scale
        )
        key_grad = (
            jnp.einsum("hqk,qhd->khd", score_grad, queries, preferred_element_type=jnp.float32)
            * score_scale
        )
        grad_pair = jnp.stack(
            [
                key_grad.reshape(block_rows, local_width),
                value_grad.reshape(block_rows, local_width),
            ],
            axis=1,
        )
        query_term, grad_pair = (query_term, grad_pair)
        query_grad = query_grad + query_term
        if distance == 0:
            pair_total = grad_pair
        else:
            pair_total = pair_total + shifted(
                grad_pair.astype(jnp.bfloat16), "cp", -distance
            ).astype(grad_pair.dtype)
    query_back = rotate_back(query_grad, cosine, sine).reshape(block_rows, local_width)
    key_back = rotate_back(
        pair_total[:, 0].reshape(block_rows, local_heads, HD), cosine, sine
    ).reshape(block_rows, local_width)
    raw_back = jnp.stack([query_back, key_back, pair_total[:, 1]], axis=1).astype(jnp.bfloat16)
    raw_back = lax.all_to_all(
        raw_back.reshape(block_rows, 3, 1, local_width),
        "hd",
        split_axis=0,
        concat_axis=2,
        tiled=True,
    )
    raw_back = raw_back.reshape(rows_here, 3 * model_width)
    qkv_sum = product(tokens.T, raw_back)
    tokens_grad = (dz_one + product(raw_back, qkv_full.T)).astype(jnp.bfloat16)
    summed = (
        lax.psum_scatter(qkv_sum, ("cp", "hd"), scatter_dimension=0, tiled=True),
        lax.psum_scatter(out_sum, ("cp", "hd"), scatter_dimension=0, tiled=True),
        lax.psum_scatter(gate_sum, ("cp", "hd"), scatter_dimension=0, tiled=True),
        lax.psum_scatter(up_sum, ("cp", "hd"), scatter_dimension=0, tiled=True),
        lax.psum_scatter(down_sum, ("cp", "hd"), scatter_dimension=0, tiled=True),
        lax.psum_scatter(gain_one_grad, ("cp", "hd"), scatter_dimension=0, tiled=True),
        lax.psum_scatter(bias_one_grad, ("cp", "hd"), scatter_dimension=0, tiled=True),
        lax.psum_scatter(gain_two_grad, ("cp", "hd"), scatter_dimension=0, tiled=True),
        lax.psum_scatter(bias_two_grad, ("cp", "hd"), scatter_dimension=0, tiled=True),
    )
    return (
        layer_out,
        tokens_grad,
        summed[0],
        summed[1],
        summed[2],
        summed[3],
        summed[4],
        summed[5],
        summed[6],
        summed[7],
        summed[8],
    )


MESH = pl.DeviceIdType.MESH
ZN, YN, CN, XN = 4, 2, 2, 2
BLOCKS = ZN * YN * CN * XN


def place():
    cp = lax.axis_index("cp")
    x = lax.axis_index("hd")
    return x, lax.rem(cp // CN, YN), cp // (YN * CN), lax.rem(cp, CN)


def device(x, y, z, c):
    return ((z * YN + y) * CN + c, x)


def block(x, y, z, c):
    return ((z * YN + y) * CN + c) * XN + x


def when(cond, fn):
    if cond is None:
        fn()
    else:
        pl.when(cond)(fn)


def both(a, b):
    if a is None:
        return b
    if b is None:
        return a
    return jnp.logical_and(a, b)


def halves(ref):
    rows, cols = ref.shape[-2:]
    if rows % 32 == 0:
        return ref.at[pl.ds(0, rows // 2)], ref.at[pl.ds(rows // 2, rows // 2)]
    if cols % 256 == 0:
        return ref.at[:, pl.ds(0, cols // 2)], ref.at[:, pl.ds(cols // 2, cols // 2)]
    return ref, None


def greet(x, y, z, c, far):
    barrier = pltpu.get_barrier_semaphore()
    for peer in (device(1 - x, y, z, c), device(x, 1 - y, z, c), device(x, y, z, 1 - c)):
        pl.semaphore_signal(barrier, inc=1, device_id=peer, device_id_type=MESH)
    count = 3
    if far:
        for k in range(1, ZN):
            peer = device(x, y, lax.rem(z + k, ZN), c)
            pl.semaphore_signal(barrier, inc=1, device_id=peer, device_id_type=MESH)
        count = count + ZN - 1
    else:
        pl.when(z > 0)(lambda: pl.semaphore_signal(barrier, inc=1, device_id=device(x, y, z - 1, c), device_id_type=MESH))
        pl.when(z < ZN - 1)(lambda: pl.semaphore_signal(barrier, inc=1, device_id=device(x, y, z + 1, c), device_id_type=MESH))
        count = count + (z > 0).astype(jnp.int32) + (z < ZN - 1).astype(jnp.int32)
    pl.semaphore_wait(barrier, count)


SENDS = 40
RECVS = 36


CHAINED = ("bcast", "by_x", "by_y")
REST = ("rest_x", "rest_y")


def take(refs, counts):
    groups = []
    for count in counts:
        groups.append(refs[:count])
        refs = refs[count:]
    return groups, refs


SHORT_PLAN = [
    (fn, "chained", d - lag)
    for d in range(1, ZN + 2)
    for lag, fn in enumerate(("onward", "beside", "across"))
    if (d > 0 if lag else d < ZN) and 0 <= d - lag < ZN
]
PLAN = [
    ("onward", "chained", 1),
    ("beside", "chained", 0),
    ("beside", "crossed", 0),
    ("across", "chained", 0),
    ("beside", "chained", 1),
    ("onward", "crossed", 1),
    ("across", "crossed", 0),
    ("across", "chained", 1),
    ("onward", "crossed", 2),
    ("onward", "crossed", 3),
    ("beside", "crossed", 1),
    ("onward", "chained", 2),
    ("beside", "crossed", 2),
    ("beside", "crossed", 3),
    ("beside", "chained", 2),
    ("across", "crossed", 1),
    ("onward", "chained", 3),
    ("across", "crossed", 2),
    ("across", "crossed", 3),
    ("across", "chained", 2),
    ("beside", "chained", 3),
    ("across", "chained", 3),
]


def gather_kernel(modes, *refs):
    n = len(modes)
    ins, refs = take(refs, [2 if mode in REST else 1 for mode in modes])
    outs, (lsem, ssem, rsem), bufs = refs[:n], refs[n : n + 3], list(refs[n + 3 :])
    bufs = {k: bufs.pop(0) for k, mode in enumerate(modes) if mode in REST}
    pairs, ins = ins, [group[0] for group in ins]
    x, y, z, c = place()
    ox, oy, oc = 1 - x, 1 - y, 1 - c
    greet(x, y, z, c, any(m in ("swap", "cross") for m in modes))
    sent = []

    def copy(k, src, dst, s, r, peer):
        return pltpu.make_async_remote_copy(
            src_ref=src,
            dst_ref=dst,
            send_sem=ssem.at[k, s],
            recv_sem=rsem.at[k, r],
            device_id=peer,
            device_id_type=MESH,
        )

    def send(cond, *args):
        when(cond, lambda: copy(*args).start())
        sent.append((cond, args))

    def arrived(cond, k, ref, r):
        when(cond, lambda: copy(k, ref, ref, 0, r, device(ox, y, z, c)).wait_recv())

    locals_ = []

    def keep(k, i, mine, spot):
        pltpu.make_async_copy(mine, spot, lsem.at[k, i]).start()
        locals_.append((k, i, mine, spot))

    def at(k, px, py, b):
        if modes[k] == "by_x":
            return outs[k].at[2 * b + px]
        if modes[k] == "by_y":
            return outs[k].at[2 * b + py]
        return outs[k].at[block(px, py, b, c)]

    for k, mode in enumerate(modes):
        if mode in CHAINED:
            keep(k, 0, ins[k], at(k, x, y, z))
        elif mode == "swap":
            keep(k, 0, ins[k].at[z], outs[k].at[z])
        elif mode == "cross":
            keep(k, 0, ins[k].at[z], outs[k].at[block(x, y, z, c)])

    def share_of(k, i, core):
        b, j = i % 8 // 2, i % 2
        if modes[k] == "rest_y":
            return block(j, oy if i >= 8 else y, b, core)
        return block(ox if i >= 8 else x, j, b, core)

    def spread(k, cond, b, src, up, down):
        here = at(k, x, y, b)
        if modes[k] in CHAINED:
            if up is not False:
                send(both(cond, up), k, src, here, b, b, device(x, y, lax.rem(z + 1, ZN), c))
            if down is not False:
                send(both(cond, down), k, src, here, 4 + b, b, device(x, y, lax.rem(z + ZN - 1, ZN), c))
        if modes[k] != "by_y":
            send(cond, k, src, here, 8 + b, 4 + b, device(ox, y, z, c))
        if modes[k] != "by_x":
            send(cond, k, src, here, 16 + b, 12 + b, device(x, oy, z, c))
        if modes[k] not in ("by_x", "by_y"):
            send(cond, k, src, here, 24 + b, 20 + b, device(x, y, z, oc))

    def sides(k, cond, b):
        fx, fy = at(k, ox, y, b), at(k, x, oy, b)
        full = modes[k] not in ("by_x", "by_y")
        if modes[k] != "by_y":
            arrived(cond, k, fx, 4 + b)
            first, _ = halves(fx)
            if full:
                send(cond, k, first, first, 20 + b, 16 + b, device(x, oy, z, c))
                send(cond, k, fx, fx, 28 + b, 24 + b, device(x, y, z, oc))
        if modes[k] != "by_x":
            arrived(cond, k, fy, 12 + b)
            _, second = halves(fy)
            if full and second is not None:
                send(cond, k, second, second, 12 + b, 8 + b, device(ox, y, z, c))
            if full:
                send(cond, k, fy, fy, 32 + b, 28 + b, device(x, y, z, oc))

    def corner(k, cond, b):
        far = outs[k].at[block(ox, oy, b, c)]
        first, second = halves(far)
        arrived(cond, k, first, 16 + b)
        if second is not None:
            arrived(cond, k, second, 8 + b)
        send(cond, k, far, far, 36 + b, 32 + b, device(x, y, z, oc))

    def steps(distance):
        if distance == 0:
            return [(None, z)]
        return [(z >= distance, jnp.maximum(z - distance, 0)), (z + distance < ZN, jnp.minimum(z + distance, ZN - 1))]

    chained = [k for k, mode in enumerate(modes) if mode in CHAINED]
    crossed = [k for k, mode in enumerate(modes) if mode == "cross"]
    swapped = [k for k, mode in enumerate(modes) if mode == "swap"]

    def exchange(ks):
        for k in ks:
            for d in range(1, ZN):
                to = lax.rem(z + d, ZN)
                spot = outs[k].at[z] if modes[k] == "swap" else outs[k].at[block(x, y, z, c)]
                send(None, k, ins[k].at[to], spot, to, z, device(x, y, to, c))

    for k in chained:
        spread(k, None, z, ins[k], z < ZN - 1, z > 0)
    if not chained:
        exchange(swapped)
        swapped = []
    for k, mode in enumerate(modes):
        if mode in REST:
            for i in range(16):
                src = pairs[k][i // 8].at[i % 8]
                pltpu.make_async_copy(src, bufs[k].at[i], lsem.at[k, i]).start()
                send(None, k, src, outs[k].at[share_of(k, i, c)], i, i, device(x, y, z, oc))
    for k in crossed:
        spread(k, None, z, ins[k].at[z], False, False)
    exchange(crossed)

    def onward(ks, distance):
        for side, (cond, b) in enumerate(steps(distance)):
            for k in ks:
                here = at(k, x, y, b)
                arrived(cond, k, here, b)
                spread(k, cond, b, here, z < ZN - 1 if side == 0 else False, z > 0 if side == 1 else False)

    def beside(ks, distance):
        for cond, b in steps(distance):
            for k in ks:
                sides(k, cond, b)

    def across(ks, distance):
        for cond, b in steps(distance):
            for k in ks:
                if modes[k] in ("bcast", "cross"):
                    corner(k, cond, b)

    plan = PLAN if crossed else SHORT_PLAN
    for fn, ks, distance in plan if chained else ():
        fn = {"onward": onward, "beside": beside, "across": across}[fn]
        fn(chained if ks == "chained" else crossed, distance)
        if fn is onward and distance == 2 and ks == "chained":
            exchange(swapped)
            swapped = []
    exchange(swapped)
    for k in bufs:
        for i in range(16):
            pltpu.make_async_copy(pairs[k][0].at[0], bufs[k].at[i], lsem.at[k, i]).wait()
            keep(k, i, bufs[k].at[i], outs[k].at[share_of(k, i, c)])
    for k, mode in enumerate(modes):
        if mode == "swap":
            for d in range(1, ZN):
                frm = lax.rem(z + d, ZN)
                arrived(None, k, outs[k].at[frm], frm)
        elif mode in REST:
            for i in range(16):
                arrived(None, k, outs[k].at[share_of(k, i, oc)], i)
        elif mode not in ("by_x", "by_y"):
            quads = (0, 1, 2, 3)
            for b in range(ZN):
                for j in quads:
                    px, py = ((x, y), (ox, y), (x, oy), (ox, oy))[j]
                    arrived(None, k, outs[k].at[block(px, py, b, oc)], 20 + 4 * j + b)
    for k, i, mine, spot in locals_:
        pltpu.make_async_copy(mine, spot, lsem.at[k, i]).wait()
    for cond, args in sent:
        when(cond, lambda args=args: copy(*args).wait_send())


def gather(arrays, modes, collective_id):
    shapes, inputs, operands, scratch = [], [], [], []
    anywhere, local = pl.BlockSpec(memory_space=pl.ANY), pl.BlockSpec(memory_space=pltpu.VMEM)
    for a, mode in zip(arrays, modes):
        inputs = inputs + ([anywhere] * 2 if mode in REST else [local])
        operands = operands + (list(a) if mode in REST else [a])
        if mode in REST:
            a = a[0]
            scratch.append(pltpu.VMEM((16,) + a.shape[1:], a.dtype))
        if mode == "bcast":
            shapes.append((BLOCKS,) + a.shape)
        elif mode in CHAINED:
            shapes.append((2 * ZN,) + a.shape)
        elif mode == "swap":
            shapes.append(a.shape)
        else:
            shapes.append((BLOCKS,) + a.shape[1:])
    n = len(arrays)
    dtypes = [(a[0] if mode in REST else a).dtype for a, mode in zip(arrays, modes)]
    return pl.pallas_call(
        functools.partial(gather_kernel, tuple(modes)),
        out_shape=[jax.ShapeDtypeStruct(shape, dtype) for shape, dtype in zip(shapes, dtypes)],
        in_specs=inputs,
        out_specs=[anywhere] * n,
        scratch_shapes=[
            pltpu.SemaphoreType.DMA((n, 16)),
            pltpu.SemaphoreType.DMA((n, SENDS)),
            pltpu.SemaphoreType.DMA((n, RECVS)),
        ]
        + scratch,
        compiler_params=pltpu.CompilerParams(
            collective_id=collective_id, has_side_effects=True, vmem_limit_bytes=67043328
        ),
    )(*operands)


def chunk_of(cols):
    for size in (768, 640, 512, 384, 256, 128):
        if cols % size == 0:
            return size
    return cols


def add_up(dst, sources):
    rows, cols = dst.shape[-2:]
    tall = 32 if rows > 32 and rows % 32 == 0 else (16 if rows > 32 else rows)
    wide = cols if rows > 32 else chunk_of(cols)

    def step(i, carry):
        if rows > 32:
            spot = (pl.ds(pl.multiple_of(i * tall, tall), tall), slice(None))
        elif cols > wide:
            spot = (slice(None), pl.ds(pl.multiple_of(i * wide, wide), wide))
        else:
            spot = (slice(None), slice(None))
        total = sources[0][spot].astype(jnp.float32)
        for source in sources[1:]:
            total = total + source[spot].astype(jnp.float32)
        dst[spot] = total.astype(dst.dtype)
        return carry

    count = (rows // tall) * (cols // wide)
    if count == 1:
        step(0, 0)
    else:
        lax.fori_loop(0, count, step, 0)


BUFFERS = {"swap": 0, "pair_x": 2, "pair_y": 2, "cross": 3, "reduce": 4, "rest_x": 4, "rest_y": 4}
PAIR = ("pair_x", "pair_y")


def reduce_kernel(modes, *refs):
    n = len(modes)
    ins, refs = take(refs, [2 if mode in REST else 1 for mode in modes])
    outs, refs = take(refs, [2 if mode in PAIR else 1 for mode in modes])
    (lsem, ssem, rsem), scratch = refs[:3], refs[3:]
    bufs, _ = take(scratch, [BUFFERS[mode] for mode in modes])
    others, seconds = ins, outs
    ins, outs = [group[0] for group in ins], [group[0] for group in outs]
    x, y, z, c = place()
    ox, oy, oc = 1 - x, 1 - y, 1 - c
    greet(x, y, z, c, any(m in ("swap", "cross") for m in modes))
    sent = []

    def copy(k, src, dst, s, r, peer):
        return pltpu.make_async_remote_copy(
            src_ref=src,
            dst_ref=dst,
            send_sem=ssem.at[k, s],
            recv_sem=rsem.at[k, r],
            device_id=peer,
            device_id_type=MESH,
        )

    def send(cond, *args):
        when(cond, lambda: copy(*args).start())
        sent.append((cond, args))

    def arrived(cond, k, ref, r):
        when(cond, lambda: copy(k, ref, ref, 0, r, device(ox, y, z, c)).wait_recv())

    half = z // 2
    order = [3 - 3 * half, 2 - half, 1 - z + 4 * half, z]
    quads = ((ox, oy), (ox, y), (x, oy), (x, y))
    active = [k for k, mode in enumerate(modes) if mode in ("cross", "reduce")]
    paired = [k for k, mode in enumerate(modes) if mode in PAIR]
    rest = [k for k, mode in enumerate(modes) if mode in REST]

    for k, mode in enumerate(modes):
        if mode == "swap":
            for d in range(1, ZN):
                to = lax.rem(z + d, ZN)
                send(None, k, ins[k].at[to], outs[k].at[z], d, z, device(x, y, to, c))
            pltpu.make_async_copy(ins[k].at[z], outs[k].at[z], lsem.at[k, 0]).start()

    for k in rest:
        acc, rec = bufs[k][:2]
        for i, b in enumerate(order):
            for j in range(2):
                mine = (x, y)[modes[k] == "rest_x"]
                spot = 2 * b + (mine if j else 1 - mine)
                pltpu.make_async_copy(ins[k].at[spot], acc.at[2 * i + j], lsem.at[k, 2 * i + j]).start()
                pltpu.make_async_copy(others[k][1].at[spot], rec.at[2 * i + j], lsem.at[k, 8 + 2 * i + j]).start()
    for k in active:
        for i, b in enumerate(order):
            acc, cor = bufs[k][:2]
            for j, (px, py) in enumerate(quads):
                send(None, k, ins[k].at[block(px, py, b, oc)], cor.at[4 * i + j], 4 * i + j, 4 * i + j, device(x, y, z, oc))
                pltpu.make_async_copy(ins[k].at[block(px, py, b, c)], acc.at[4 * i + j], lsem.at[k, 4 * i + j]).start()

    def spots(k, i):
        b, j = i // 2, i % 2
        if modes[k] == "pair_y":
            return (j, y, b), (j, oy, b)
        return (x, j, b), (ox, j, b)

    for k in paired:
        acc, cor = bufs[k]
        for i in range(8):
            for s, (px, py, b) in enumerate(spots(k, i)):
                send(None, k, ins[k].at[block(px, py, b, oc)], cor.at[2 * i + s], 2 * i + s, 2 * i + s, device(x, y, z, oc))
                pltpu.make_async_copy(ins[k].at[block(px, py, b, c)], acc.at[2 * i + s], lsem.at[k, 2 * i + s]).start()
    def loaded(k, i, j):
        acc, cor = bufs[k][:2]
        pltpu.make_async_copy(ins[k].at[0], acc.at[4 * i + j], lsem.at[k, 4 * i + j]).wait()
        arrived(None, k, cor.at[4 * i + j], 4 * i + j)

    for k in paired:
        acc, cor = bufs[k]

        def join(i, carry, k=k, acc=acc, cor=cor):
            for s in range(2):
                at = 2 * i + s
                pltpu.make_async_copy(ins[k].at[0], acc.at[at], lsem.at[k, at]).wait()
                arrived(None, k, cor.at[at], at)
                add_up(seconds[k][s].at[i], (acc.at[at], cor.at[at]))
            return carry

        lax.fori_loop(0, 8, join, 0)

    def fetched(k, i, j):
        acc, rec = bufs[k][:2]
        pltpu.make_async_copy(ins[k].at[0], acc.at[2 * i + j], lsem.at[k, 2 * i + j]).wait()
        pltpu.make_async_copy(ins[k].at[0], rec.at[2 * i + j], lsem.at[k, 8 + 2 * i + j]).wait()

    def ahead(k, i, b):
        acc, rec, side = bufs[k][:3]
        fetched(k, i, 0)
        add_up(acc.at[2 * i], (acc.at[2 * i], rec.at[2 * i]))
        peer = device(x, oy, z, c) if modes[k] == "rest_x" else device(ox, y, z, c)
        send(None, k, acc.at[2 * i], side.at[i], 16 + i, 16 + i, peer)

    def corner(k, i, b):
        acc, cor, side = bufs[k][:3]
        loaded(k, i, 0)
        add_up(acc.at[4 * i], (acc.at[4 * i], cor.at[4 * i]))
        first, second = halves(acc.at[4 * i])
        send(None, k, first, halves(side.at[i])[0], 16 + i, 16 + i, device(x, oy, z, c))
        if second is not None:
            send(None, k, second, halves(side.at[4 + i])[1], 20 + i, 20 + i, device(ox, y, z, c))

    def beside(k, i, b):
        acc, cor, side = bufs[k][:3]
        loaded(k, i, 1)
        add_up(acc.at[4 * i + 1], (acc.at[4 * i + 1], cor.at[4 * i + 1]))
        part = halves(side.at[i])[0]
        arrived(None, k, part, 16 + i)
        mine = halves(acc.at[4 * i + 1])[0]
        add_up(mine, (mine, part))
        send(None, k, acc.at[4 * i + 1], side.at[8 + i], 24 + i, 24 + i, device(ox, y, z, c))
        loaded(k, i, 2)
        add_up(acc.at[4 * i + 2], (acc.at[4 * i + 2], cor.at[4 * i + 2]))
        part = halves(side.at[4 + i])[1]
        if part is not None:
            arrived(None, k, part, 20 + i)
            mine = halves(acc.at[4 * i + 2])[1]
            add_up(mine, (mine, part))
        send(None, k, acc.at[4 * i + 2], side.at[12 + i], 28 + i, 28 + i, device(x, oy, z, c))

    def settle(k, i, b):
        side = bufs[k][2]
        if k in rest:
            acc, rec = bufs[k][:2]
            fetched(k, i, 1)
            arrived(None, k, side.at[i], 16 + i)
            own = acc.at[2 * i + 1]
            terms = (own, rec.at[2 * i + 1], side.at[i])
        else:
            acc, cor = bufs[k][:2]
            loaded(k, i, 3)
            own = acc.at[4 * i + 3]
            arrived(None, k, side.at[8 + i], 24 + i)
            arrived(None, k, side.at[12 + i], 28 + i)
            terms = (own, cor.at[4 * i + 3], side.at[8 + i], side.at[12 + i])
        if modes[k] == "cross":
            add_up(own, terms)
            if i < ZN - 1:
                send(None, k, own, outs[k].at[z], 32 + i, 32 + z, device(x, y, b, c))
            else:
                pltpu.make_async_copy(own, outs[k].at[z], lsem.at[k, 16]).start()
            return
        chain = bufs[k][3]
        if i == ZN - 1:
            add_up(outs[k], terms)

            def lower(k=k, chain=chain):
                arrived(None, k, chain.at[z], 32 + z)
                add_up(outs[k], (outs[k], chain.at[z]))

            def upper(k=k, chain=chain):
                arrived(None, k, chain.at[4 + z], 36 + z)
                add_up(outs[k], (outs[k], chain.at[4 + z]))

            pl.when(z > 0)(lower)
            pl.when(z < ZN - 1)(upper)
        else:
            add_up(own, terms)
            below = both(b > z, z > 0)
            above = both(b < z, z < ZN - 1)

            def lower(k=k, chain=chain, own=own, b=b):
                arrived(None, k, chain.at[b], 32 + b)
                add_up(own, (own, chain.at[b]))

            def upper(k=k, chain=chain, own=own, b=b):
                arrived(None, k, chain.at[4 + b], 36 + b)
                add_up(own, (own, chain.at[4 + b]))

            pl.when(below)(lower)
            pl.when(above)(upper)
            send(b > z, k, own, chain.at[b], 32 + i, 32 + b, device(x, y, lax.rem(z + 1, ZN), c))
            send(b < z, k, own, chain.at[4 + b], 32 + i, 36 + b, device(x, y, lax.rem(z + ZN - 1, ZN), c))

    crossed = [k for k in active if modes[k] == "cross"]
    plain = [k for k in active if modes[k] == "reduce"]
    stages = [[(ahead, rest)], [(corner, crossed)], [(corner, plain)]]
    stages = stages + [[(settle, rest), (beside, crossed)], [(settle, crossed), (beside, plain)], [(settle, plain)]]
    for stage in stages:
        for i, b in enumerate(order):
            for fn, ks in stage:
                for k in ks:
                    fn(k, i, b)
    for k, mode in enumerate(modes):
        if mode not in ("swap", "cross"):
            continue
        for d in range(1, ZN):
            frm = lax.rem(z + d, ZN)
            arrived(None, k, outs[k].at[frm], frm if mode == "swap" else 32 + frm)
        if mode == "swap":
            pltpu.make_async_copy(ins[k].at[z], outs[k].at[z], lsem.at[k, 0]).wait()
        else:
            pltpu.make_async_copy(bufs[k][0].at[15], outs[k].at[z], lsem.at[k, 16]).wait()
    for cond, args in sent:
        when(cond, lambda args=args: copy(*args).wait_send())


def reduce(arrays, modes, collective_id):
    shapes, specs, scratch, operands, inputs = [], [], [], [], []
    anywhere, local = pl.BlockSpec(memory_space=pl.ANY), pl.BlockSpec(memory_space=pltpu.VMEM)
    for a, mode in zip(arrays, modes):
        operands = operands + (list(a) if mode in REST else [a])
        inputs = inputs + [local if mode == "swap" else anywhere] * (2 if mode in REST else 1)
        a = a[0] if mode in REST else a
        rows, cols = a.shape[1:]
        sizes = {"swap": (), "pair_x": (16, 16), "cross": (16, 16, 16), "reduce": (16, 16, 16, 8), "rest_x": (8, 8, 4, 8)}
        sizes = sizes[mode.replace("_y", "_x")]
        scratch = scratch + [pltpu.VMEM((size, rows, cols), a.dtype) for size in sizes]
        if mode == "swap":
            shapes.append(jax.ShapeDtypeStruct(a.shape, a.dtype))
            specs.append(anywhere)
        elif mode in PAIR:
            shapes = shapes + [jax.ShapeDtypeStruct((8, rows, cols), a.dtype)] * 2
            specs = specs + [local] * 2
        elif mode == "cross":
            shapes.append(jax.ShapeDtypeStruct((ZN, rows, cols), a.dtype))
            specs.append(anywhere)
        else:
            shapes.append(jax.ShapeDtypeStruct((rows, cols), jnp.float32))
            specs.append(local)
    n = len(arrays)
    return pl.pallas_call(
        functools.partial(reduce_kernel, tuple(modes)),
        out_shape=shapes,
        in_specs=inputs,
        out_specs=specs,
        scratch_shapes=[
            pltpu.SemaphoreType.DMA((n, 17)),
            pltpu.SemaphoreType.DMA((n, SENDS)),
            pltpu.SemaphoreType.DMA((n, SENDS)),
        ]
        + scratch,
        compiler_params=pltpu.CompilerParams(
            collective_id=collective_id, has_side_effects=True, vmem_limit_bytes=67043328
        ),
    )(*operands)


HEAD = 64
GROUP = 3
TILE = 512
WIDE = 1024
EDGE = 128
SPAN = 4096
FAR = 1 << 30


def longest(lengths):
    begin, best, at = jnp.int32(0), lengths[0], jnp.int32(0)
    for j in range(lengths.shape[0]):
        length = lengths[j]
        at = jnp.where(length > best, begin, at)
        best = jnp.maximum(best, length)
        begin = begin + length
    return at, at + best


def lane_slots(lengths, count):
    x, y, z, c = place()
    lane = lax.broadcasted_iota(jnp.int32, (1, count), 1)
    begin, end = longest(lengths)
    spots = [block(x, y, b, c) * count + lane for b in range(ZN)]
    slots, before = [], jnp.zeros((1, count), jnp.int32)
    for b in range(ZN):
        big = jnp.logical_and(spots[b] >= begin, spots[b] < end)
        slots.append(jnp.where(big, before, ZN // 2 + b - before))
        before = before + big.astype(jnp.int32)
    return begin, end, spots, slots


def pick(slots, slot, parts):
    chosen = parts[-1]
    for b in range(len(parts) - 2, -1, -1):
        chosen = jnp.where(slots[b] == slot, parts[b], chosen)
    return chosen


def bounds_of(lengths, spot):
    low, high = jnp.zeros_like(spot), jnp.full_like(spot, FAR)
    begin = jnp.int32(0)
    for j in range(lengths.shape[0]):
        end = begin + lengths[j]
        low = jnp.where(spot >= begin, begin, low)
        high = jnp.where(spot < end, jnp.minimum(high, end), high)
        begin = end
    return low, high


def walk(big, begin, end, low, high, step, init):
    if big:
        base = begin // EDGE * EDGE

        def body(i, carry):
            at = pl.multiple_of(base + i * WIDE, EDGE)
            return step(at, WIDE, False, carry)

        carry = step(pl.multiple_of(base, EDGE), WIDE, True, init)
        carry = lax.fori_loop(1, SPAN // WIDE, body, carry)
        return lax.cond(
            begin > base,
            lambda c: step(pl.multiple_of(base + SPAN, EDGE), EDGE, True, c),
            lambda c: c,
            carry,
        )
    first = jnp.min(low) // TILE
    stop = (jnp.max(high) + TILE - 1) // TILE
    hole_first = jnp.maximum((begin + TILE - 1) // TILE, first)
    hole = jnp.maximum(jnp.minimum(end // TILE, stop) - hole_first, 0)

    def body(i, carry):
        tile = first + i
        tile = jnp.where(jnp.logical_and(hole > 0, tile >= hole_first), tile + hole, tile)
        return step(pl.multiple_of(tile * TILE, TILE), TILE, True, carry)

    return lax.fori_loop(0, stop - first - hole, body, init)


def keys_in(first, size, low, high):
    at = first + lax.broadcasted_iota(jnp.int32, (size, low.shape[1]), 0)
    return jnp.logical_and(at >= low, at < high)


def dot(a, b):
    return jnp.dot(a, b, preferred_element_type=jnp.float32)


def pad_heads(rows, h, slots):
    part = rows[h * HEAD : (h + 1) * HEAD]
    zero = jnp.zeros_like(part)
    return jnp.concatenate([part if s == h else zero for s in slots], axis=0)


Q_SLOTS = (0, 1, 2, -1)
V_SLOTS = (-1, 2, 0, 1)


def forward_kernel(lengths, qt, kv, low_out, out, lse_out, qm, acc, qs, os, ls):
    count = qt.shape[2]
    begin, end, spots, slots = lane_slots(lengths, count)
    for s in range(ZN):
        qs[s] = pick(slots, s, [qt[b] for b in range(ZN)])

    def one_block(big, s, carry):
        low, high = bounds_of(lengths, pick(slots, s, spots))
        rows = qs[s] * jnp.bfloat16(0.125)
        for h in range(GROUP):
            qm[h] = pad_heads(rows, h, Q_SLOTS)
        acc[...] = jnp.zeros_like(acc)

        def step(at, size, masked, stats):
            span = pl.ds(at, size)
            keys = kv[span, 0:256]
            values = kv[span, 128:384].T
            mask = keys_in(at, size, low, high) if masked else None
            fresh = []
            for h in range(GROUP):
                top, total = stats[2 * h], stats[2 * h + 1]
                scores = dot(keys, qm[h])
                if masked:
                    scores = jnp.where(mask, scores, -1e9)
                new_top = jnp.maximum(top, jnp.max(scores, axis=0, keepdims=True))
                shrink = jnp.exp(top - new_top)
                weights = jnp.exp(scores - new_top)
                total = total * shrink + jnp.sum(weights, axis=0, keepdims=True)
                row = V_SLOTS.index(h) * HEAD
                acc[h] = acc[h] * shrink + dot(values[row : row + HEAD], weights.astype(jnp.bfloat16))
                fresh = fresh + [new_top, total]
            return tuple(fresh)

        init = (jnp.full((1, count), -1e9, jnp.float32), jnp.zeros((1, count), jnp.float32)) * GROUP
        stats = walk(big, begin, end, low, high, step, init)
        for h in range(GROUP):
            top, total = stats[2 * h], stats[2 * h + 1]
            os[s, h * HEAD : (h + 1) * HEAD] = acc[h] / total
            ls[s, h : h + 1] = top + jnp.log(total)
        return carry

    lax.fori_loop(0, ZN // 2, functools.partial(one_block, True), 0)
    lax.fori_loop(ZN // 2, ZN, functools.partial(one_block, False), 0)
    for b in range(ZN):
        value = pick([jnp.full_like(slots[b], s) for s in range(ZN)], slots[b], [os[s] for s in range(ZN)])
        out[b] = value
        low_out[b] = value.astype(low_out.dtype)
        lse_out[b] = pick([jnp.full_like(slots[b], s) for s in range(ZN)], slots[b], [ls[s] for s in range(ZN)])


def attend(lengths, qt, kv):
    blocks, rows, count = qt.shape
    whole = pl.BlockSpec(memory_space=pltpu.VMEM)
    return pl.pallas_call(
        forward_kernel,
        out_shape=[
            jax.ShapeDtypeStruct(qt.shape, jnp.bfloat16),
            jax.ShapeDtypeStruct(qt.shape, jnp.float32),
            jax.ShapeDtypeStruct((blocks, 8, count), jnp.float32),
        ],
        in_specs=[pl.BlockSpec(memory_space=pltpu.SMEM), whole, whole],
        out_specs=[whole] * 3,
        scratch_shapes=[
            pltpu.VMEM((GROUP, 256, count), jnp.bfloat16),
            pltpu.VMEM((GROUP, HEAD, count), jnp.float32),
            pltpu.VMEM(qt.shape, jnp.bfloat16),
            pltpu.VMEM(qt.shape, jnp.float32),
            pltpu.VMEM((blocks, 8, count), jnp.float32),
        ],
        compiler_params=pltpu.CompilerParams(vmem_limit_bytes=67043328),
    )(lengths, qt, kv)


def backward_kernel(lengths, qt, kv, out, lse, dot_in, cosine, sine, dq_out, dkv_out, qmt, qm, dmt, dm, dq, acc, qs, ds, es, ls, dqs):
    count = qt.shape[2]
    tiles = kv.shape[0] // TILE

    def clear(tile, carry):
        acc[pl.ds(pl.multiple_of(tile * TILE, TILE), TILE), :] = jnp.zeros((TILE, acc.shape[1]), jnp.float32)
        return carry

    lax.fori_loop(0, tiles, clear, 0)

    begin, end, spots, slots = lane_slots(lengths, count)
    for b in range(ZN):
        product_rows = dot_in[b].astype(jnp.float32) * out[b]
        for h in range(GROUP):
            es[b, h : h + 1] = jnp.sum(product_rows[h * HEAD : (h + 1) * HEAD], axis=0, keepdims=True)
    for s in range(ZN):
        qs[s] = pick(slots, s, [qt[b] for b in range(ZN)])
        ds[s] = pick(slots, s, [dot_in[b] for b in range(ZN)])
        ls[s] = pick(slots, s, [lse[b] for b in range(ZN)])
    picked = [pick(slots, s, [es[b] for b in range(ZN)]) for s in range(ZN)]
    for s in range(ZN):
        es[s] = picked[s]

    def one_block(big, s, carry):
        low, high = bounds_of(lengths, pick(slots, s, spots))
        rows = qs[s] * jnp.bfloat16(0.125)
        grads = ds[s]
        deltas = [es[s, h : h + 1] for h in range(GROUP)]
        levels = [ls[s, h : h + 1] for h in range(GROUP)]
        for h in range(GROUP):
            padded = pad_heads(rows, h, Q_SLOTS)
            qmt[h] = padded
            qm[h * count : (h + 1) * count] = padded.T
            padded = pad_heads(grads, h, V_SLOTS)
            dmt[h] = padded
            dm[h * count : (h + 1) * count] = padded.T
        dq[...] = jnp.zeros_like(dq)

        def step(at, size, masked, inner):
            span = pl.ds(at, size)
            keys = kv[span, 0:256]
            values = kv[span, 128:384]
            turned = keys.T
            mask = keys_in(at, size, low, high) if masked else None
            probs, slopes = [], []
            for h in range(GROUP):
                weights = jnp.exp(dot(keys, qmt[h]) - levels[h])
                if masked:
                    weights = jnp.where(mask, weights, 0.0)
                slope = (weights * (dot(values, dmt[h]) - deltas[h])).astype(jnp.bfloat16)
                dq[h] += dot(turned[h * HEAD : (h + 1) * HEAD], slope)
                probs.append(weights.astype(jnp.bfloat16))
                slopes.append(slope)
            dv = dot(jnp.concatenate(probs, axis=1), dm[...])
            dk = dot(jnp.concatenate(slopes, axis=1), qm[...])
            acc[span, 0:128] += dk[:, :128]
            acc[span, 128:256] += dk[:, 128:] + dv[:, :128]
            acc[span, 256:384] += dv[:, 128:]
            return inner

        walk(big, begin, end, low, high, step, 0)
        for h in range(GROUP):
            dqs[s, h * HEAD : (h + 1) * HEAD] = dq[h] * 0.125
        return carry

    lax.fori_loop(0, ZN // 2, functools.partial(one_block, True), 0)
    lax.fori_loop(ZN // 2, ZN, functools.partial(one_block, False), 0)
    half = HEAD // 2
    for b in range(ZN):
        back = pick([jnp.full_like(slots[b], s) for s in range(ZN)], slots[b], [dqs[s] for s in range(ZN)])
        for h in range(GROUP):
            at = h * HEAD
            w1, w2 = back[at : at + half], back[at + half : at + HEAD]
            dq_out[b, at : at + half] = (w1 * cosine[b] + w2 * sine[b]).astype(dq_out.dtype)
            dq_out[b, at + half : at + HEAD] = (w2 * cosine[b] - w1 * sine[b]).astype(dq_out.dtype)

    def finish(tile, carry):
        span = pl.ds(pl.multiple_of(tile * TILE, TILE), TILE)
        dkv_out[span, :] = acc[span, :].astype(dkv_out.dtype)
        return carry

    lax.fori_loop(0, tiles, finish, 0)


def attend_back(lengths, qt, kv, out, lse, dots, cosine, sine):
    blocks, rows, count = qt.shape
    whole = pl.BlockSpec(memory_space=pltpu.VMEM)
    return pl.pallas_call(
        backward_kernel,
        out_shape=[
            jax.ShapeDtypeStruct(qt.shape, jnp.bfloat16),
            jax.ShapeDtypeStruct(kv.shape, jnp.bfloat16),
        ],
        in_specs=[pl.BlockSpec(memory_space=pltpu.SMEM)] + [whole] * 7,
        out_specs=[whole] * 2,
        scratch_shapes=[
            pltpu.VMEM((GROUP, 256, count), jnp.bfloat16),
            pltpu.VMEM((GROUP * count, 256), jnp.bfloat16),
            pltpu.VMEM((GROUP, 256, count), jnp.bfloat16),
            pltpu.VMEM((GROUP * count, 256), jnp.bfloat16),
            pltpu.VMEM((GROUP, HEAD, count), jnp.float32),
            pltpu.VMEM(kv.shape, jnp.float32),
            pltpu.VMEM(qt.shape, jnp.bfloat16),
            pltpu.VMEM(qt.shape, jnp.bfloat16),
            pltpu.VMEM((blocks, 8, count), jnp.float32),
            pltpu.VMEM((blocks, 8, count), jnp.float32),
            pltpu.VMEM(qt.shape, jnp.float32),
        ],
        compiler_params=pltpu.CompilerParams(vmem_limit_bytes=67043328),
    )(lengths, qt, kv, out, lse, dots, cosine, sine)


KV_SLOTS = (0, 1, 2, 5, 3, 4)


def turn(rows, cosine, sine):
    first, second = rows[:, 0], rows[:, 1]
    return jnp.stack([first * cosine - second * sine, second * cosine + first * sine], axis=1)


def turn_back(rows, cosine, sine):
    first, second = rows[:, 0], rows[:, 1]
    return jnp.stack([first * cosine + second * sine, second * cosine - first * sine], axis=1)


def tables(lengths, first, count):
    starts = jnp.cumsum(lengths) - lengths
    position = first[:, None] + jnp.arange(count, dtype=jnp.int32)[None, :]
    begun = position[..., None] >= starts
    offsets = position - jnp.max(jnp.where(begun, starts, 0), axis=-1)
    half = HEAD // 2
    frequency = rope_base ** (-(jnp.arange(half, dtype=jnp.float32) * 2.0) / HEAD)
    angles = offsets.astype(jnp.float32)[:, None, :] * frequency[None, :, None]
    return jnp.cos(angles), jnp.sin(angles)


def norm_back(upstream, scaled, inv_std, gain_vec):
    weighted = upstream * gain_vec
    inner = (
        weighted
        - jnp.mean(weighted, axis=-1, keepdims=True)
        - scaled * jnp.mean(weighted * scaled, axis=-1, keepdims=True)
    )
    sums = [jnp.sum(upstream * scaled, axis=0, keepdims=True), jnp.sum(upstream, axis=0, keepdims=True)]
    return inv_std * inner, sums


def contract(left, right, dims):
    return lax.dot_general(left, right, (dims, ((), ())), preferred_element_type=jnp.float32)


def copies_kernel(*refs):
    n = len(refs) // 3
    ins, outs, bufs, sems = refs[:n], refs[n : 2 * n], refs[2 * n : 3 * n], refs[3 * n]
    loads = [pltpu.make_async_copy(ins[k], bufs[k], sems.at[k]) for k in range(n)]
    stores = [pltpu.make_async_copy(bufs[k], outs[k], sems.at[n + k]) for k in range(n)]
    for load in loads:
        load.start()
    for load, store in zip(loads, stores):
        load.wait()
        store.start()
    for store in stores:
        store.wait()


def copies(arrays):
    n = len(arrays)
    anywhere = pl.BlockSpec(memory_space=pl.ANY)
    return pl.pallas_call(
        copies_kernel,
        out_shape=[jax.ShapeDtypeStruct(a.shape, a.dtype) for a in arrays],
        in_specs=[anywhere] * n,
        out_specs=[anywhere] * n,
        scratch_shapes=[pltpu.VMEM(a.shape, a.dtype) for a in arrays] + [pltpu.SemaphoreType.DMA((2 * n,))],
    )(*arrays)


def local_grid(
    tokens,
    qkv_weight,
    out_weight,
    gate_weight,
    up_weight,
    down_weight,
    first_gain,
    first_bias,
    second_gain,
    second_bias,
    lengths,
    cotangent,
):
    bf16 = jnp.bfloat16
    rows, width = tokens.shape
    share = first_gain.shape[0]
    heads = width // HEAD
    half = HEAD // 2
    x, y, z, c = place()
    spots = [(px, py, pz, pc) for pz in range(ZN) for py in range(YN) for pc in range(CN) for px in range(XN)]
    over_x = [(block(*p), block(1 - p[0], *p[1:])) for p in spots]
    over_y = [(block(*p), block(p[0], 1 - p[1], *p[2:])) for p in spots]
    small = jnp.stack([first_gain, first_bias, second_gain, second_bias])
    small = jnp.pad(small, ((0, 4), (0, 128 - share)))
    hidden_width = gate_weight.shape[1]

    qkv_blocks, gate_part, up_part = gather([qkv_weight, gate_weight, up_weight], ["bcast", "by_x", "by_y"], 1)
    qkv_full = qkv_blocks.reshape(width, 3 * width)
    turned = jnp.stack([block(x, y, b, c) for b in range(ZN)]) * rows
    cos_all, sin_all = tables(lengths, turned, rows)
    cosine = lax.dynamic_index_in_dim(cos_all, z, 0, keepdims=False)
    sine = lax.dynamic_index_in_dim(sin_all, z, 0, keepdims=False)

    raw = contract(qkv_full, tokens, ((0,), (1,))).astype(bf16)
    raw = raw.reshape(3, heads, 2, half, rows)
    queries = turn(raw[0].astype(jnp.float32), cosine, sine).astype(bf16)
    keys = turn(raw[1].astype(jnp.float32), cosine, sine).astype(bf16)
    queries = queries.reshape(ZN, GROUP * HEAD, rows)
    pairs = jnp.concatenate(
        [keys.reshape(ZN, GROUP, HEAD, rows), raw[2].reshape(ZN, GROUP, HEAD, rows)], axis=1
    )
    pairs = jnp.concatenate([pairs[:, s : s + 1] for s in KV_SLOTS], axis=1)
    pairs = jnp.swapaxes(pairs.reshape(ZN, 2 * GROUP * HEAD, rows), 1, 2)

    pairs_all, queries, out_full, down_full, small = gather(
        [pairs, queries, out_weight, down_weight, small], ["cross", "swap", "bcast", "bcast", "bcast"], 2
    )
    out_full = out_full.reshape(width, width)
    gate_part, up_part, queries = lax.optimization_barrier((gate_part, up_part, queries))
    gate_rest = lax.ppermute(gate_part, ("cp", "hd"), over_y)
    up_rest = lax.ppermute(up_part, ("cp", "hd"), over_x)
    down_full = down_full.reshape(hidden_width, width)
    small = jnp.swapaxes(small[:, :4, :share], 0, 1).astype(jnp.float32).reshape(4, width)
    small = lax.optimization_barrier(small)
    gain_one, bias_one, gain_two, bias_two = [small[i] for i in range(4)]
    pairs_all = pairs_all.reshape(-1, 2 * GROUP * HEAD)
    low, attended, lse = attend(lengths, queries, pairs_all)
    low, gate_full, up_full = gather(
        [low, (gate_part, gate_rest), (up_part, up_rest)], ["swap", "rest_y", "rest_x"], 3
    )
    gate_full = gate_full.reshape(width, hidden_width)
    up_full = up_full.reshape(width, hidden_width)
    low = low.reshape(width, rows)

    attn_out = contract(low, out_full, ((0,), (0,)))
    first, scaled_one, inv_one = normalize(tokens.astype(jnp.float32) + attn_out, gain_one, bias_one)
    first_low = first.astype(bf16)
    gate_proj = product(first_low, gate_full)
    up_proj = product(first_low, up_full)
    sigmoid_gate = jax.nn.sigmoid(gate_proj)
    silu_gate = gate_proj * sigmoid_gate
    hidden = (silu_gate * up_proj).astype(bf16)
    branch = product(hidden, down_full)
    second, scaled_two, inv_two = normalize(first + branch, gain_two, bias_two)
    layer_out = second.astype(bf16)

    upstream = cotangent.astype(jnp.float32)
    dz_two, sums_two = norm_back(upstream, scaled_two, inv_two, gain_two)
    dz_two_low = dz_two.astype(bf16)
    down_sum = contract(hidden, dz_two_low, ((0,), (0,))).astype(bf16)
    hidden_grad = contract(dz_two_low, down_full, ((1,), (1,)))
    gate_back = (
        hidden_grad * up_proj * sigmoid_gate * (1.0 + gate_proj * (1.0 - sigmoid_gate))
    ).astype(bf16)
    up_back = (hidden_grad * silu_gate).astype(bf16)
    gate_sum = contract(first_low, gate_back, ((0,), (0,))).astype(bf16)
    up_sum = contract(first_low, up_back, ((0,), (0,))).astype(bf16)
    first_back = (
        dz_two + contract(gate_back, gate_full, ((1,), (1,))) + contract(up_back, up_full, ((1,), (1,)))
    )
    dz_one, sums_one = norm_back(first_back, scaled_one, inv_one, gain_one)
    dz_one_low = dz_one.astype(bf16)
    out_sum = product(low, dz_one_low).astype(bf16)
    attended_back = contract(out_full, dz_one_low, ((1,), (1,))).astype(bf16)
    attended_back, gate_keep, gate_send, up_keep, up_send = reduce(
        [
            attended_back.reshape(ZN, GROUP * HEAD, rows),
            gate_sum.reshape((BLOCKS,) + gate_weight.shape),
            up_sum.reshape((BLOCKS,) + up_weight.shape),
        ],
        ["swap", "pair_y", "pair_x"],
        4,
    )
    gate_rest = lax.ppermute(gate_send, ("cp", "hd"), over_y)
    up_rest = lax.ppermute(up_send, ("cp", "hd"), over_x)

    query_back, pair_back = attend_back(
        lengths, queries, pairs_all, attended, lse, attended_back, cos_all, sin_all
    )
    small_sum = lax.optimization_barrier(jnp.concatenate(sums_one + sums_two, axis=0))
    small_sum = jnp.swapaxes(small_sum.reshape(4, BLOCKS, share), 0, 1)
    small_sum = jnp.pad(small_sum, ((0, 0), (0, 4), (0, 128 - share)))
    pair_back, query_back, out_grad, down_grad, small_grad, gate_grad, up_grad = reduce(
        [
            pair_back.reshape(BLOCKS, rows, 2 * GROUP * HEAD),
            query_back,
            out_sum.reshape(BLOCKS, share, width),
            down_sum.reshape(BLOCKS, -1, width),
            small_sum,
            (gate_keep, gate_rest),
            (up_keep, up_rest),
        ],
        ["cross", "swap", "reduce", "reduce", "reduce", "rest_y", "rest_x"],
        5,
    )
    pair_back = jnp.swapaxes(pair_back, 1, 2).reshape(ZN, 2 * GROUP, HEAD, rows)
    pair_back = [pair_back[:, KV_SLOTS.index(s)] for s in range(2 * GROUP)]
    key_back = jnp.stack(pair_back[:GROUP], axis=1).reshape(heads, 2, half, rows)
    key_back = turn_back(key_back.astype(jnp.float32), cosine, sine).astype(bf16)
    value_back = jnp.stack(pair_back[GROUP:], axis=1)
    raw_back = jnp.concatenate(
        [
            query_back.reshape(width, rows),
            key_back.reshape(width, rows),
            value_back.reshape(width, rows),
        ],
        axis=0,
    )
    qkv_sum = contract(tokens, raw_back, ((0,), (1,))).astype(bf16)
    tokens_grad = (dz_one + contract(raw_back, qkv_full, ((0,), (1,)))).astype(bf16)
    (qkv_grad,) = reduce([qkv_sum.reshape(BLOCKS, share, 3 * width)], ["reduce"], 6)
    qkv_grad, out_grad, gate_grad, up_grad, down_grad = copies([qkv_grad, out_grad, gate_grad, up_grad, down_grad])
    return (
        layer_out,
        tokens_grad,
        qkv_grad,
        out_grad,
        gate_grad,
        up_grad,
        down_grad,
        small_grad[0, :share],
        small_grad[1, :share],
        small_grad[2, :share],
        small_grad[3, :share],
    )


def solution(mesh):
    rows = P(("cp", "hd"), None)
    line = P(("cp", "hd"))
    local = local_grid if (mesh.shape["cp"], mesh.shape["hd"]) == (ZN * YN * CN, XN) else local_any
    return jax.shard_map(
        local,
        mesh=mesh,
        in_specs=(rows,) * 6 + (line,) * 4 + (P(), rows),
        out_specs=(rows,) * 7 + (line,) * 4,
        check_vma=False,
    )
```

```python
import functools

import jax
import jax.numpy as jnp
from jax import lax
from jax.experimental import pallas as pl
from jax.experimental.pallas import tpu as pltpu
from jax.sharding import PartitionSpec as P

HD = 64
REACH = 8


rope_base = 1000.0
norm_eps = 1e-12
score_scale = 0.125
masked_score = -1000000000.0


def shifted(block, axis, distance):
    devices = range(lax.axis_size(axis))
    route = [(i - distance, i) for i in devices if i - distance in devices]
    return lax.ppermute(block, axis, route)


def doc_layout(lengths, first_row, row_count):
    starts = jnp.cumsum(lengths) - lengths
    position = first_row + jnp.arange(row_count, dtype=jnp.int32)
    at_or_after = position[:, None] >= starts[None, :]
    doc_ids = jnp.sum(at_or_after.astype(jnp.int32), axis=1) - 1
    doc_begin = jnp.max(jnp.where(at_or_after, starts[None, :], 0), axis=1)
    return (doc_ids, position - doc_begin)


def rope_tables(offsets, head_size):
    half_size = head_size // 2
    frequency = rope_base ** (-(jnp.arange(half_size, dtype=jnp.float32) * 2.0) / head_size)
    angles = offsets.astype(jnp.float32)[:, None] * frequency[None, :]
    return (jnp.cos(angles), jnp.sin(angles))


def rotate(values, cosine, sine):
    half_size = values.shape[-1] // 2
    first_half = values[..., :half_size]
    second_half = values[..., half_size:]
    cos_rows = cosine[:, None, :]
    sin_rows = sine[:, None, :]
    return jnp.concatenate(
        [
            first_half * cos_rows - second_half * sin_rows,
            second_half * cos_rows + first_half * sin_rows,
        ],
        axis=-1,
    )


def rotate_back(grads, cosine, sine):
    half_size = grads.shape[-1] // 2
    first_half = grads[..., :half_size]
    second_half = grads[..., half_size:]
    cos_rows = cosine[:, None, :]
    sin_rows = sine[:, None, :]
    return jnp.concatenate(
        [
            first_half * cos_rows + second_half * sin_rows,
            second_half * cos_rows - first_half * sin_rows,
        ],
        axis=-1,
    )


def normalize(hidden_in, gain_vec, bias_vec):
    average = jnp.mean(hidden_in, axis=-1, keepdims=True)
    centered = hidden_in - average
    variance = jnp.mean(centered * centered, axis=-1, keepdims=True)
    inv_std = lax.rsqrt(variance + norm_eps)
    scaled = centered * inv_std
    return (scaled * gain_vec + bias_vec, scaled, inv_std)


def normalize_back(upstream, scaled, inv_std, gain_vec):
    weighted = upstream * gain_vec
    inner = (
        weighted
        - jnp.mean(weighted, axis=-1, keepdims=True)
        - scaled * jnp.mean(weighted * scaled, axis=-1, keepdims=True)
    )
    return (inv_std * inner, jnp.sum(upstream * scaled, axis=0), jnp.sum(upstream, axis=0))


def product(left, right):
    return jnp.dot(left, right, preferred_element_type=jnp.float32)


def local_any(
    tokens,
    qkv_weight,
    out_weight,
    gate_weight,
    up_weight,
    down_weight,
    first_gain,
    first_bias,
    second_gain,
    second_bias,
    doc_lengths,
    cotangent,
):
    rows_here = tokens.shape[0]
    model_width = tokens.shape[1]
    hd_count = lax.axis_size("hd")
    cp_count = lax.axis_size("cp")
    cp_index = lax.axis_index("cp")
    block_rows = rows_here * hd_count
    local_width = model_width // hd_count
    local_heads = local_width // HD
    shifts = [0]
    for distance in range(1, REACH + 1):
        shifts = shifts + [-distance, distance]
    shards = (
        qkv_weight,
        out_weight,
        gate_weight,
        up_weight,
        down_weight,
        first_gain,
        first_bias,
        second_gain,
        second_bias,
    )
    weights = (
        lax.all_gather(shards[0], ("cp", "hd"), axis=0, tiled=True),
        lax.all_gather(shards[1], ("cp", "hd"), axis=0, tiled=True),
        lax.all_gather(shards[2], ("cp", "hd"), axis=0, tiled=True),
        lax.all_gather(shards[3], ("cp", "hd"), axis=0, tiled=True),
        lax.all_gather(shards[4], ("cp", "hd"), axis=0, tiled=True),
        lax.all_gather(shards[5], ("cp", "hd"), axis=0, tiled=True),
        lax.all_gather(shards[6], ("cp", "hd"), axis=0, tiled=True),
        lax.all_gather(shards[7], ("cp", "hd"), axis=0, tiled=True),
        lax.all_gather(shards[8], ("cp", "hd"), axis=0, tiled=True),
    )
    (
        qkv_full,
        out_full,
        gate_full,
        up_full,
        down_full,
        gain_first,
        bias_first,
        gain_second,
        bias_second,
    ) = weights
    raw_rows = product(tokens, qkv_full).astype(jnp.bfloat16)
    grouped = lax.all_to_all(
        raw_rows.reshape(rows_here, 3, hd_count, local_width),
        "hd",
        split_axis=2,
        concat_axis=0,
        tiled=True,
    )
    grouped = grouped.reshape(block_rows, 3, local_width)
    query_docs, offsets = doc_layout(doc_lengths, cp_index * block_rows, block_rows)
    cosine, sine = rope_tables(offsets, HD)
    queries = rotate(
        grouped[:, 0].astype(jnp.float32).reshape(block_rows, local_heads, HD), cosine, sine
    ).astype(jnp.bfloat16)
    key_rows = rotate(
        grouped[:, 1].astype(jnp.float32).reshape(block_rows, local_heads, HD), cosine, sine
    ).astype(jnp.bfloat16)
    own_block = jnp.stack([key_rows.reshape(block_rows, local_width), grouped[:, 2]], axis=1)

    def key_docs(distance):
        source = cp_index - distance
        doc_ids, unused_offsets = doc_layout(doc_lengths, source * block_rows, block_rows)
        inside = jnp.logical_and(source >= 0, source < cp_count)
        return jnp.where(inside, doc_ids, -2)

    remote = [own_block] + [shifted(own_block, "cp", distance) for distance in shifts[1:]]
    masks = [query_docs[:, None] == key_docs(distance)[None, :] for distance in shifts]

    def scores_with(query_part, remote_block, key_mask):
        key_part = remote_block[:, 0].reshape(block_rows, local_heads, HD)
        raw_scores = (
            jnp.einsum("qhd,khd->hqk", query_part, key_part, preferred_element_type=jnp.float32)
            * score_scale
        )
        return jnp.where(key_mask[None], raw_scores, masked_score)

    def scores_for(remote_block, key_mask):
        return scores_with(queries, remote_block, key_mask)

    running_max = jnp.full((local_heads, block_rows), masked_score, jnp.float32)
    running_sum = jnp.zeros((local_heads, block_rows), jnp.float32)
    for remote_block, key_mask in zip(remote, masks):
        block_scores = scores_for(remote_block, key_mask)
        new_max = jnp.maximum(running_max, jnp.max(block_scores, axis=-1))
        running_sum = running_sum * jnp.exp(running_max - new_max) + jnp.sum(
            jnp.exp(block_scores - new_max[:, :, None]), axis=-1
        )
        running_max = new_max
    log_total = running_max + jnp.log(running_sum)
    attended = jnp.zeros((block_rows, local_heads, HD), jnp.float32)
    for remote_block, key_mask in zip(remote, masks):
        block_scores = scores_for(remote_block, key_mask)
        probs = jnp.exp(block_scores - log_total[:, :, None]).astype(jnp.bfloat16)
        value_part = remote_block[:, 1].reshape(block_rows, local_heads, HD)
        attended = attended + jnp.einsum(
            "hqk,khd->qhd", probs, value_part, preferred_element_type=jnp.float32
        )
    attended_send = attended.reshape(block_rows, 1, local_width).astype(jnp.bfloat16)
    attended_low = lax.all_to_all(
        attended_send, "hd", split_axis=0, concat_axis=1, tiled=True
    ).reshape(rows_here, model_width)
    gain_one = gain_first.astype(jnp.float32)
    gain_two = gain_second.astype(jnp.float32)
    attn_out = product(attended_low, out_full)
    first, scaled_one, inv_one = normalize(
        tokens.astype(jnp.float32) + attn_out, gain_one, bias_first.astype(jnp.float32)
    )
    first_low = first.astype(jnp.bfloat16)
    gate_proj = product(first_low, gate_full)
    up_proj = product(first_low, up_full)
    sigmoid_gate = jax.nn.sigmoid(gate_proj)
    silu_gate = gate_proj * sigmoid_gate
    hidden = (silu_gate * up_proj).astype(jnp.bfloat16)
    branch = product(hidden, down_full)
    second, scaled_two, inv_two = normalize(
        first + branch, gain_two, bias_second.astype(jnp.float32)
    )
    layer_out = second.astype(jnp.bfloat16)
    weights = (
        lax.all_gather(shards[0], ("cp", "hd"), axis=0, tiled=True),
        lax.all_gather(shards[1], ("cp", "hd"), axis=0, tiled=True),
        lax.all_gather(shards[2], ("cp", "hd"), axis=0, tiled=True),
        lax.all_gather(shards[3], ("cp", "hd"), axis=0, tiled=True),
        lax.all_gather(shards[4], ("cp", "hd"), axis=0, tiled=True),
        lax.all_gather(shards[5], ("cp", "hd"), axis=0, tiled=True),
        lax.all_gather(shards[6], ("cp", "hd"), axis=0, tiled=True),
        lax.all_gather(shards[7], ("cp", "hd"), axis=0, tiled=True),
        lax.all_gather(shards[8], ("cp", "hd"), axis=0, tiled=True),
    )
    (
        qkv_full,
        out_full,
        gate_full,
        up_full,
        down_full,
        gain_first,
        bias_first,
        gain_second,
        bias_second,
    ) = weights
    upstream = cotangent.astype(jnp.float32)
    dz_two, gain_two_grad, bias_two_grad = normalize_back(upstream, scaled_two, inv_two, gain_two)
    dz_two_low = dz_two.astype(jnp.bfloat16)
    down_sum = product(hidden.T, dz_two_low)
    hidden_grad = product(dz_two_low, down_full.T)
    gate_back = (
        hidden_grad * up_proj * sigmoid_gate * (1.0 + gate_proj * (1.0 - sigmoid_gate))
    ).astype(jnp.bfloat16)
    up_back = (hidden_grad * silu_gate).astype(jnp.bfloat16)
    gate_sum = product(first_low.T, gate_back)
    up_sum = product(first_low.T, up_back)
    first_back = dz_two + product(gate_back, gate_full.T) + product(up_back, up_full.T)
    dz_one, gain_one_grad, bias_one_grad = normalize_back(first_back, scaled_one, inv_one, gain_one)
    dz_one_low = dz_one.astype(jnp.bfloat16)
    out_sum = product(attended_low.T, dz_one_low)
    attended_back = product(dz_one_low, out_full.T).astype(jnp.bfloat16)
    heads_back = lax.all_to_all(
        attended_back.reshape(rows_here, hd_count, local_width),
        "hd",
        split_axis=1,
        concat_axis=0,
        tiled=True,
    )
    heads_back = heads_back.reshape(block_rows, local_heads, HD)
    delta = jnp.transpose(jnp.sum(heads_back.astype(jnp.float32) * attended, axis=-1))
    query_grad = jnp.zeros((block_rows, local_heads, HD), jnp.float32)
    pair_total = jnp.zeros((block_rows, 2, local_width), jnp.float32)
    remote = [own_block] + [shifted(own_block, "cp", distance) for distance in shifts[1:]]
    for distance, remote_block, key_mask in zip(shifts, remote, masks):
        pair_block_scores = scores_with(queries, remote_block, key_mask)
        pair_probs = jnp.exp(pair_block_scores - log_total[:, :, None])
        pair_key_part = remote_block[:, 0].reshape(block_rows, local_heads, HD)
        pair_value_part = remote_block[:, 1].reshape(block_rows, local_heads, HD)
        value_grad = jnp.einsum(
            "hqk,qhd->khd",
            pair_probs.astype(jnp.bfloat16),
            heads_back,
            preferred_element_type=jnp.float32,
        )
        prob_grad = jnp.einsum(
            "qhd,khd->hqk", heads_back, pair_value_part, preferred_element_type=jnp.float32
        )
        score_grad = (pair_probs * (prob_grad - delta[:, :, None])).astype(jnp.bfloat16)
        query_term = (
            jnp.einsum(
                "hqk,khd->qhd", score_grad, pair_key_part, preferred_element_type=jnp.float32
            )
            * score_scale
        )
        key_grad = (
            jnp.einsum("hqk,qhd->khd", score_grad, queries, preferred_element_type=jnp.float32)
            * score_scale
        )
        grad_pair = jnp.stack(
            [
                key_grad.reshape(block_rows, local_width),
                value_grad.reshape(block_rows, local_width),
            ],
            axis=1,
        )
        query_term, grad_pair = (query_term, grad_pair)
        query_grad = query_grad + query_term
        if distance == 0:
            pair_total = grad_pair
        else:
            pair_total = pair_total + shifted(
                grad_pair.astype(jnp.bfloat16), "cp", -distance
            ).astype(grad_pair.dtype)
    query_back = rotate_back(query_grad, cosine, sine).reshape(block_rows, local_width)
    key_back = rotate_back(
        pair_total[:, 0].reshape(block_rows, local_heads, HD), cosine, sine
    ).reshape(block_rows, local_width)
    raw_back = jnp.stack([query_back, key_back, pair_total[:, 1]], axis=1).astype(jnp.bfloat16)
    raw_back = lax.all_to_all(
        raw_back.reshape(block_rows, 3, 1, local_width),
        "hd",
        split_axis=0,
        concat_axis=2,
        tiled=True,
    )
    raw_back = raw_back.reshape(rows_here, 3 * model_width)
    qkv_sum = product(tokens.T, raw_back)
    tokens_grad = (dz_one + product(raw_back, qkv_full.T)).astype(jnp.bfloat16)
    summed = (
        lax.psum_scatter(qkv_sum, ("cp", "hd"), scatter_dimension=0, tiled=True),
        lax.psum_scatter(out_sum, ("cp", "hd"), scatter_dimension=0, tiled=True),
        lax.psum_scatter(gate_sum, ("cp", "hd"), scatter_dimension=0, tiled=True),
        lax.psum_scatter(up_sum, ("cp", "hd"), scatter_dimension=0, tiled=True),
        lax.psum_scatter(down_sum, ("cp", "hd"), scatter_dimension=0, tiled=True),
        lax.psum_scatter(gain_one_grad, ("cp", "hd"), scatter_dimension=0, tiled=True),
        lax.psum_scatter(bias_one_grad, ("cp", "hd"), scatter_dimension=0, tiled=True),
        lax.psum_scatter(gain_two_grad, ("cp", "hd"), scatter_dimension=0, tiled=True),
        lax.psum_scatter(bias_two_grad, ("cp", "hd"), scatter_dimension=0, tiled=True),
    )
    return (
        layer_out,
        tokens_grad,
        summed[0],
        summed[1],
        summed[2],
        summed[3],
        summed[4],
        summed[5],
        summed[6],
        summed[7],
        summed[8],
    )


MESH = pl.DeviceIdType.MESH
ZN, YN, CN, XN = 4, 2, 2, 2
BLOCKS = ZN * YN * CN * XN


def place():
    cp = lax.axis_index("cp")
    x = lax.axis_index("hd")
    return x, lax.rem(cp // CN, YN), cp // (YN * CN), lax.rem(cp, CN)


def device(x, y, z, c):
    return ((z * YN + y) * CN + c, x)


def block(x, y, z, c):
    return ((z * YN + y) * CN + c) * XN + x


def when(cond, fn):
    if cond is None:
        fn()
    else:
        pl.when(cond)(fn)


def both(a, b):
    if a is None:
        return b
    if b is None:
        return a
    return jnp.logical_and(a, b)


def halves(ref):
    rows, cols = ref.shape[-2:]
    if rows % 32 == 0:
        return ref.at[pl.ds(0, rows // 2)], ref.at[pl.ds(rows // 2, rows // 2)]
    if cols % 256 == 0:
        return ref.at[:, pl.ds(0, cols // 2)], ref.at[:, pl.ds(cols // 2, cols // 2)]
    return ref, None


def greet(x, y, z, c, far):
    barrier = pltpu.get_barrier_semaphore()
    for peer in (device(1 - x, y, z, c), device(x, 1 - y, z, c), device(x, y, z, 1 - c)):
        pl.semaphore_signal(barrier, inc=1, device_id=peer, device_id_type=MESH)
    count = 3
    if far:
        for k in range(1, ZN):
            peer = device(x, y, lax.rem(z + k, ZN), c)
            pl.semaphore_signal(barrier, inc=1, device_id=peer, device_id_type=MESH)
        count = count + ZN - 1
    else:
        pl.when(z > 0)(lambda: pl.semaphore_signal(barrier, inc=1, device_id=device(x, y, z - 1, c), device_id_type=MESH))
        pl.when(z < ZN - 1)(lambda: pl.semaphore_signal(barrier, inc=1, device_id=device(x, y, z + 1, c), device_id_type=MESH))
        count = count + (z > 0).astype(jnp.int32) + (z < ZN - 1).astype(jnp.int32)
    pl.semaphore_wait(barrier, count)


SENDS = 40
RECVS = 36


CHAINED = ("bcast", "by_x", "by_y")
REST = ("rest_x", "rest_y")


def take(refs, counts):
    groups = []
    for count in counts:
        groups.append(refs[:count])
        refs = refs[count:]
    return groups, refs


SHORT_PLAN = [
    (fn, "chained", d - lag)
    for d in range(1, ZN + 2)
    for lag, fn in enumerate(("onward", "beside", "across"))
    if (d > 0 if lag else d < ZN) and 0 <= d - lag < ZN
]
PLAN = [
    ("onward", "chained", 1),
    ("beside", "chained", 0),
    ("beside", "crossed", 0),
    ("across", "chained", 0),
    ("beside", "chained", 1),
    ("onward", "crossed", 1),
    ("across", "crossed", 0),
    ("across", "chained", 1),
    ("onward", "crossed", 2),
    ("onward", "crossed", 3),
    ("beside", "crossed", 1),
    ("onward", "chained", 2),
    ("beside", "crossed", 2),
    ("beside", "crossed", 3),
    ("beside", "chained", 2),
    ("across", "crossed", 1),
    ("onward", "chained", 3),
    ("across", "crossed", 2),
    ("across", "crossed", 3),
    ("across", "chained", 2),
    ("beside", "chained", 3),
    ("across", "chained", 3),
]


def gather_kernel(modes, *refs):
    n = len(modes)
    ins, refs = take(refs, [2 if mode in REST else 1 for mode in modes])
    outs, (lsem, ssem, rsem), bufs = refs[:n], refs[n : n + 3], list(refs[n + 3 :])
    bufs = {k: bufs.pop(0) for k, mode in enumerate(modes) if mode in REST}
    pairs, ins = ins, [group[0] for group in ins]
    x, y, z, c = place()
    ox, oy, oc = 1 - x, 1 - y, 1 - c
    greet(x, y, z, c, any(m in ("swap", "cross") for m in modes))
    sent = []

    def copy(k, src, dst, s, r, peer):
        return pltpu.make_async_remote_copy(
            src_ref=src,
            dst_ref=dst,
            send_sem=ssem.at[k, s],
            recv_sem=rsem.at[k, r],
            device_id=peer,
            device_id_type=MESH,
        )

    def send(cond, *args):
        when(cond, lambda: copy(*args).start())
        sent.append((cond, args))

    def arrived(cond, k, ref, r):
        when(cond, lambda: copy(k, ref, ref, 0, r, device(ox, y, z, c)).wait_recv())

    locals_ = []

    def keep(k, i, mine, spot):
        pltpu.make_async_copy(mine, spot, lsem.at[k, i]).start()
        locals_.append((k, i, mine, spot))

    def at(k, px, py, b):
        if modes[k] == "by_x":
            return outs[k].at[2 * b + px]
        if modes[k] == "by_y":
            return outs[k].at[2 * b + py]
        return outs[k].at[block(px, py, b, c)]

    for k, mode in enumerate(modes):
        if mode in CHAINED:
            keep(k, 0, ins[k], at(k, x, y, z))
        elif mode == "swap":
            keep(k, 0, ins[k].at[z], outs[k].at[z])
        elif mode == "cross":
            keep(k, 0, ins[k].at[z], outs[k].at[block(x, y, z, c)])

    def share_of(k, i, core):
        b, j = i % 8 // 2, i % 2
        if modes[k] == "rest_y":
            return block(j, oy if i >= 8 else y, b, core)
        return block(ox if i >= 8 else x, j, b, core)

    def spread(k, cond, b, src, up, down):
        here = at(k, x, y, b)
        if modes[k] in CHAINED:
            if up is not False:
                send(both(cond, up), k, src, here, b, b, device(x, y, lax.rem(z + 1, ZN), c))
            if down is not False:
                send(both(cond, down), k, src, here, 4 + b, b, device(x, y, lax.rem(z + ZN - 1, ZN), c))
        if modes[k] != "by_y":
            send(cond, k, src, here, 8 + b, 4 + b, device(ox, y, z, c))
        if modes[k] != "by_x":
            send(cond, k, src, here, 16 + b, 12 + b, device(x, oy, z, c))
        if modes[k] not in ("by_x", "by_y"):
            send(cond, k, src, here, 24 + b, 20 + b, device(x, y, z, oc))

    def sides(k, cond, b):
        fx, fy = at(k, ox, y, b), at(k, x, oy, b)
        full = modes[k] not in ("by_x", "by_y")
        if modes[k] != "by_y":
            arrived(cond, k, fx, 4 + b)
            first, _ = halves(fx)
            if full:
                send(cond, k, first, first, 20 + b, 16 + b, device(x, oy, z, c))
                send(cond, k, fx, fx, 28 + b, 24 + b, device(x, y, z, oc))
        if modes[k] != "by_x":
            arrived(cond, k, fy, 12 + b)
            _, second = halves(fy)
            if full and second is not None:
                send(cond, k, second, second, 12 + b, 8 + b, device(ox, y, z, c))
            if full:
                send(cond, k, fy, fy, 32 + b, 28 + b, device(x, y, z, oc))

    def corner(k, cond, b):
        far = outs[k].at[block(ox, oy, b, c)]
        first, second = halves(far)
        arrived(cond, k, first, 16 + b)
        if second is not None:
            arrived(cond, k, second, 8 + b)
        send(cond, k, far, far, 36 + b, 32 + b, device(x, y, z, oc))

    def steps(distance):
        if distance == 0:
            return [(None, z)]
        return [(z >= distance, jnp.maximum(z - distance, 0)), (z + distance < ZN, jnp.minimum(z + distance, ZN - 1))]

    chained = [k for k, mode in enumerate(modes) if mode in CHAINED]
    crossed = [k for k, mode in enumerate(modes) if mode == "cross"]
    swapped = [k for k, mode in enumerate(modes) if mode == "swap"]

    def exchange(ks):
        for k in ks:
            for d in range(1, ZN):
                to = lax.rem(z + d, ZN)
                spot = outs[k].at[z] if modes[k] == "swap" else outs[k].at[block(x, y, z, c)]
                send(None, k, ins[k].at[to], spot, to, z, device(x, y, to, c))

    for k in chained:
        spread(k, None, z, ins[k], z < ZN - 1, z > 0)
    if not chained:
        exchange(swapped)
        swapped = []
    for k, mode in enumerate(modes):
        if mode in REST:
            for i in range(16):
                src = pairs[k][i // 8].at[i % 8]
                pltpu.make_async_copy(src, bufs[k].at[i], lsem.at[k, i]).start()
                send(None, k, src, outs[k].at[share_of(k, i, c)], i, i, device(x, y, z, oc))
    for k in crossed:
        spread(k, None, z, ins[k].at[z], False, False)
    exchange(crossed)

    def onward(ks, distance):
        for side, (cond, b) in enumerate(steps(distance)):
            for k in ks:
                here = at(k, x, y, b)
                arrived(cond, k, here, b)
                spread(k, cond, b, here, z < ZN - 1 if side == 0 else False, z > 0 if side == 1 else False)

    def beside(ks, distance):
        for cond, b in steps(distance):
            for k in ks:
                sides(k, cond, b)

    def across(ks, distance):
        for cond, b in steps(distance):
            for k in ks:
                if modes[k] in ("bcast", "cross"):
                    corner(k, cond, b)

    plan = PLAN if crossed else SHORT_PLAN
    for fn, ks, distance in plan if chained else ():
        fn = {"onward": onward, "beside": beside, "across": across}[fn]
        fn(chained if ks == "chained" else crossed, distance)
        if fn is onward and distance == ZN - 1 and ks == "chained":
            exchange(swapped)
            swapped = []
    exchange(swapped)
    for k in bufs:
        for i in range(16):
            pltpu.make_async_copy(pairs[k][0].at[0], bufs[k].at[i], lsem.at[k, i]).wait()
            keep(k, i, bufs[k].at[i], outs[k].at[share_of(k, i, c)])
    for k, mode in enumerate(modes):
        if mode == "swap":
            for d in range(1, ZN):
                frm = lax.rem(z + d, ZN)
                arrived(None, k, outs[k].at[frm], frm)
        elif mode in REST:
            for i in range(16):
                arrived(None, k, outs[k].at[share_of(k, i, oc)], i)
        elif mode not in ("by_x", "by_y"):
            quads = (0, 1, 2, 3)
            for b in range(ZN):
                for j in quads:
                    px, py = ((x, y), (ox, y), (x, oy), (ox, oy))[j]
                    arrived(None, k, outs[k].at[block(px, py, b, oc)], 20 + 4 * j + b)
    for k, i, mine, spot in locals_:
        pltpu.make_async_copy(mine, spot, lsem.at[k, i]).wait()
    for cond, args in sent:
        when(cond, lambda args=args: copy(*args).wait_send())


def gather(arrays, modes, collective_id):
    shapes, inputs, operands, scratch = [], [], [], []
    anywhere, local = pl.BlockSpec(memory_space=pl.ANY), pl.BlockSpec(memory_space=pltpu.VMEM)
    for a, mode in zip(arrays, modes):
        inputs = inputs + ([anywhere] * 2 if mode in REST else [local])
        operands = operands + (list(a) if mode in REST else [a])
        if mode in REST:
            a = a[0]
            scratch.append(pltpu.VMEM((16,) + a.shape[1:], a.dtype))
        if mode == "bcast":
            shapes.append((BLOCKS,) + a.shape)
        elif mode in CHAINED:
            shapes.append((2 * ZN,) + a.shape)
        elif mode == "swap":
            shapes.append(a.shape)
        else:
            shapes.append((BLOCKS,) + a.shape[1:])
    n = len(arrays)
    dtypes = [(a[0] if mode in REST else a).dtype for a, mode in zip(arrays, modes)]
    return pl.pallas_call(
        functools.partial(gather_kernel, tuple(modes)),
        out_shape=[jax.ShapeDtypeStruct(shape, dtype) for shape, dtype in zip(shapes, dtypes)],
        in_specs=inputs,
        out_specs=[anywhere] * n,
        scratch_shapes=[
            pltpu.SemaphoreType.DMA((n, 16)),
            pltpu.SemaphoreType.DMA((n, SENDS)),
            pltpu.SemaphoreType.DMA((n, RECVS)),
        ]
        + scratch,
        compiler_params=pltpu.CompilerParams(
            collective_id=collective_id, has_side_effects=True, vmem_limit_bytes=67043328
        ),
    )(*operands)


def chunk_of(cols):
    for size in (768, 640, 512, 384, 256, 128):
        if cols % size == 0:
            return size
    return cols


def add_up(dst, sources):
    rows, cols = dst.shape[-2:]
    tall = 32 if rows > 32 and rows % 32 == 0 else (16 if rows > 32 else rows)
    wide = cols if rows > 32 else chunk_of(cols)

    def step(i, carry):
        if rows > 32:
            spot = (pl.ds(pl.multiple_of(i * tall, tall), tall), slice(None))
        elif cols > wide:
            spot = (slice(None), pl.ds(pl.multiple_of(i * wide, wide), wide))
        else:
            spot = (slice(None), slice(None))
        total = sources[0][spot].astype(jnp.float32)
        for source in sources[1:]:
            total = total + source[spot].astype(jnp.float32)
        dst[spot] = total.astype(dst.dtype)
        return carry

    count = (rows // tall) * (cols // wide)
    if count == 1:
        step(0, 0)
    else:
        lax.fori_loop(0, count, step, 0)


BUFFERS = {"product": 5, "turned_product": 5, "swap": 0, "pair_x": 2, "pair_y": 2, "cross": 3, "reduce": 4, "rest_x": 4, "rest_y": 4}
PAIR = ("pair_x", "pair_y")
MADE = ("product", "turned_product")


def make(dst, left, right, turned):
    blocks, rows = dst.shape[:2]
    group = blocks // 8

    def step(i, carry):
        span = pl.ds(pl.multiple_of(i * group * rows, 32), group * rows)
        if turned:
            span = pl.ds(pl.multiple_of(i * group * rows, 128), group * rows)
            part = left[:, span].T
        else:
            part = left[span, :]
        total = jnp.dot(part, right[...], preferred_element_type=jnp.float32)
        for j in range(group):
            dst[i * group + j] = total[j * rows : (j + 1) * rows].astype(dst.dtype)
        return carry

    lax.fori_loop(0, blocks // group, step, 0)


def reduce_kernel(modes, *refs):
    n = len(modes)
    ins, refs = take(refs, [2 if mode in REST + MADE else 1 for mode in modes])
    outs, refs = take(refs, [2 if mode in PAIR else 1 for mode in modes])
    (lsem, ssem, rsem), scratch = refs[:3], refs[3:]
    bufs, _ = take(scratch, [BUFFERS[mode] for mode in modes])
    others, seconds = ins, outs
    ins, outs = [group[0] for group in ins], [group[0] for group in outs]
    for k, mode in enumerate(modes):
        if mode in MADE:
            ins[k] = bufs[k][4]
    bufs = [group[:4] for group in bufs]
    x, y, z, c = place()
    ox, oy, oc = 1 - x, 1 - y, 1 - c
    greet(x, y, z, c, any(m in ("swap", "cross") for m in modes))
    sent = []

    def copy(k, src, dst, s, r, peer):
        return pltpu.make_async_remote_copy(
            src_ref=src,
            dst_ref=dst,
            send_sem=ssem.at[k, s],
            recv_sem=rsem.at[k, r],
            device_id=peer,
            device_id_type=MESH,
        )

    def send(cond, *args):
        when(cond, lambda: copy(*args).start())
        sent.append((cond, args))

    def arrived(cond, k, ref, r):
        when(cond, lambda: copy(k, ref, ref, 0, r, device(ox, y, z, c)).wait_recv())

    half = z // 2
    order = [3 - 3 * half, 2 - half, 1 - z + 4 * half, z]
    quads = ((ox, oy), (ox, y), (x, oy), (x, y))
    active = [k for k, mode in enumerate(modes) if mode in ("cross", "reduce") + MADE]
    paired = [k for k, mode in enumerate(modes) if mode in PAIR]
    rest = [k for k, mode in enumerate(modes) if mode in REST]

    for k, mode in enumerate(modes):
        if mode == "swap":
            for d in range(1, ZN):
                to = lax.rem(z + d, ZN)
                send(None, k, ins[k].at[to], outs[k].at[z], d, z, device(x, y, to, c))
            pltpu.make_async_copy(ins[k].at[z], outs[k].at[z], lsem.at[k, 0]).start()

    for k in rest:
        acc, rec = bufs[k][:2]
        for i, b in enumerate(order):
            for j in range(2):
                mine = (x, y)[modes[k] == "rest_x"]
                spot = 2 * b + (mine if j else 1 - mine)
                pltpu.make_async_copy(ins[k].at[spot], acc.at[2 * i + j], lsem.at[k, 2 * i + j]).start()
                pltpu.make_async_copy(others[k][1].at[spot], rec.at[2 * i + j], lsem.at[k, 8 + 2 * i + j]).start()
    for k in active:
        if modes[k] in MADE:
            make(ins[k], *others[k], modes[k] == "turned_product")
        for i, b in enumerate(order):
            acc, cor = bufs[k][:2]
            for j, (px, py) in enumerate(quads):
                send(None, k, ins[k].at[block(px, py, b, oc)], cor.at[4 * i + j], 4 * i + j, 4 * i + j, device(x, y, z, oc))
                pltpu.make_async_copy(ins[k].at[block(px, py, b, c)], acc.at[4 * i + j], lsem.at[k, 4 * i + j]).start()

    def spots(k, i):
        b, j = i // 2, i % 2
        if modes[k] == "pair_y":
            return (j, y, b), (j, oy, b)
        return (x, j, b), (ox, j, b)

    for k in paired:
        acc, cor = bufs[k]
        for i in range(8):
            for s, (px, py, b) in enumerate(spots(k, i)):
                send(None, k, ins[k].at[block(px, py, b, oc)], cor.at[2 * i + s], 2 * i + s, 2 * i + s, device(x, y, z, oc))
                pltpu.make_async_copy(ins[k].at[block(px, py, b, c)], acc.at[2 * i + s], lsem.at[k, 2 * i + s]).start()
    def loaded(k, i, j):
        acc, cor = bufs[k][:2]
        pltpu.make_async_copy(ins[k].at[0], acc.at[4 * i + j], lsem.at[k, 4 * i + j]).wait()
        arrived(None, k, cor.at[4 * i + j], 4 * i + j)

    for k in paired:
        acc, cor = bufs[k]

        def join(i, carry, k=k, acc=acc, cor=cor):
            for s in range(2):
                at = 2 * i + s
                pltpu.make_async_copy(ins[k].at[0], acc.at[at], lsem.at[k, at]).wait()
                arrived(None, k, cor.at[at], at)
                add_up(seconds[k][s].at[i], (acc.at[at], cor.at[at]))
            return carry

        lax.fori_loop(0, 8, join, 0)

    def fetched(k, i, j):
        acc, rec = bufs[k][:2]
        pltpu.make_async_copy(ins[k].at[0], acc.at[2 * i + j], lsem.at[k, 2 * i + j]).wait()
        pltpu.make_async_copy(ins[k].at[0], rec.at[2 * i + j], lsem.at[k, 8 + 2 * i + j]).wait()

    def ahead(k, i, b):
        acc, rec, side = bufs[k][:3]
        fetched(k, i, 0)
        add_up(acc.at[2 * i], (acc.at[2 * i], rec.at[2 * i]))
        peer = device(x, oy, z, c) if modes[k] == "rest_x" else device(ox, y, z, c)
        send(None, k, acc.at[2 * i], side.at[i], 16 + i, 16 + i, peer)

    def corner(k, i, b):
        acc, cor, side = bufs[k][:3]
        loaded(k, i, 0)
        add_up(acc.at[4 * i], (acc.at[4 * i], cor.at[4 * i]))
        first, second = halves(acc.at[4 * i])
        send(None, k, first, halves(side.at[i])[0], 16 + i, 16 + i, device(x, oy, z, c))
        if second is not None:
            send(None, k, second, halves(side.at[4 + i])[1], 20 + i, 20 + i, device(ox, y, z, c))

    def beside(k, i, b):
        acc, cor, side = bufs[k][:3]
        loaded(k, i, 1)
        add_up(acc.at[4 * i + 1], (acc.at[4 * i + 1], cor.at[4 * i + 1]))
        part = halves(side.at[i])[0]
        arrived(None, k, part, 16 + i)
        mine = halves(acc.at[4 * i + 1])[0]
        add_up(mine, (mine, part))
        send(None, k, acc.at[4 * i + 1], side.at[8 + i], 24 + i, 24 + i, device(ox, y, z, c))
        loaded(k, i, 2)
        add_up(acc.at[4 * i + 2], (acc.at[4 * i + 2], cor.at[4 * i + 2]))
        part = halves(side.at[4 + i])[1]
        if part is not None:
            arrived(None, k, part, 20 + i)
            mine = halves(acc.at[4 * i + 2])[1]
            add_up(mine, (mine, part))
        send(None, k, acc.at[4 * i + 2], side.at[12 + i], 28 + i, 28 + i, device(x, oy, z, c))

    def settle(k, i, b):
        side = bufs[k][2]
        if k in rest:
            acc, rec = bufs[k][:2]
            fetched(k, i, 1)
            arrived(None, k, side.at[i], 16 + i)
            own = acc.at[2 * i + 1]
            terms = (own, rec.at[2 * i + 1], side.at[i])
        else:
            acc, cor = bufs[k][:2]
            loaded(k, i, 3)
            own = acc.at[4 * i + 3]
            arrived(None, k, side.at[8 + i], 24 + i)
            arrived(None, k, side.at[12 + i], 28 + i)
            terms = (own, cor.at[4 * i + 3], side.at[8 + i], side.at[12 + i])
        if modes[k] == "cross":
            add_up(own, terms)
            if i < ZN - 1:
                send(None, k, own, outs[k].at[z], 32 + i, 32 + z, device(x, y, b, c))
            else:
                pltpu.make_async_copy(own, outs[k].at[z], lsem.at[k, 16]).start()
            return
        chain = bufs[k][3]
        if i == ZN - 1:
            add_up(outs[k], terms)

            def lower(k=k, chain=chain):
                arrived(None, k, chain.at[z], 32 + z)
                add_up(outs[k], (outs[k], chain.at[z]))

            def upper(k=k, chain=chain):
                arrived(None, k, chain.at[4 + z], 36 + z)
                add_up(outs[k], (outs[k], chain.at[4 + z]))

            pl.when(z > 0)(lower)
            pl.when(z < ZN - 1)(upper)
        else:
            add_up(own, terms)
            below = both(b > z, z > 0)
            above = both(b < z, z < ZN - 1)

            def lower(k=k, chain=chain, own=own, b=b):
                arrived(None, k, chain.at[b], 32 + b)
                add_up(own, (own, chain.at[b]))

            def upper(k=k, chain=chain, own=own, b=b):
                arrived(None, k, chain.at[4 + b], 36 + b)
                add_up(own, (own, chain.at[4 + b]))

            pl.when(below)(lower)
            pl.when(above)(upper)
            send(b > z, k, own, chain.at[b], 32 + i, 32 + b, device(x, y, lax.rem(z + 1, ZN), c))
            send(b < z, k, own, chain.at[4 + b], 32 + i, 36 + b, device(x, y, lax.rem(z + ZN - 1, ZN), c))

    crossed = [k for k in active if modes[k] == "cross"]
    plain = [k for k in active if modes[k] != "cross"]
    stages = [[(ahead, rest)], [(corner, crossed)], [(corner, plain)]]
    stages = stages + [[(settle, rest), (beside, crossed)], [(settle, crossed), (beside, plain)], [(settle, plain)]]
    for stage in stages:
        for i, b in enumerate(order):
            for fn, ks in stage:
                for k in ks:
                    fn(k, i, b)
    for k, mode in enumerate(modes):
        if mode not in ("swap", "cross"):
            continue
        for d in range(1, ZN):
            frm = lax.rem(z + d, ZN)
            arrived(None, k, outs[k].at[frm], frm if mode == "swap" else 32 + frm)
        if mode == "swap":
            pltpu.make_async_copy(ins[k].at[z], outs[k].at[z], lsem.at[k, 0]).wait()
        else:
            pltpu.make_async_copy(bufs[k][0].at[15], outs[k].at[z], lsem.at[k, 16]).wait()
    for cond, args in sent:
        when(cond, lambda args=args: copy(*args).wait_send())


def reduce(arrays, modes, collective_id):
    shapes, specs, scratch, operands, inputs = [], [], [], [], []
    anywhere, local = pl.BlockSpec(memory_space=pl.ANY), pl.BlockSpec(memory_space=pltpu.VMEM)
    for a, mode in zip(arrays, modes):
        operands = operands + (list(a) if mode in REST + MADE else [a])
        inputs = inputs + [local if mode in MADE + ("swap",) else anywhere] * (2 if mode in REST + MADE else 1)
        if mode in MADE:
            tall = a[0].shape[1] if mode == "turned_product" else a[0].shape[0]
            shape = (BLOCKS, tall // BLOCKS, a[1].shape[1])
        else:
            a = a[0] if mode in REST else a
            shape = a.shape
        rows, cols = shape[1:]
        dtype = jnp.bfloat16 if mode in MADE else a.dtype
        sizes = {"swap": (), "pair_x": (16, 16), "cross": (16, 16, 16), "reduce": (16, 16, 16, 8), "rest_x": (8, 8, 4, 8)}
        sizes = sizes["reduce"] + (BLOCKS,) if mode in MADE else sizes[mode.replace("_y", "_x")]
        scratch = scratch + [pltpu.VMEM((size, rows, cols), dtype) for size in sizes]
        if mode == "swap":
            shapes.append(jax.ShapeDtypeStruct(a.shape, a.dtype))
            specs.append(anywhere)
        elif mode in PAIR:
            shapes = shapes + [jax.ShapeDtypeStruct((8, rows, cols), a.dtype)] * 2
            specs = specs + [local] * 2
        elif mode == "cross":
            shapes.append(jax.ShapeDtypeStruct((ZN, rows, cols), a.dtype))
            specs.append(anywhere)
        else:
            shapes.append(jax.ShapeDtypeStruct((rows, cols), jnp.float32))
            specs.append(local)
    n = len(arrays)
    return pl.pallas_call(
        functools.partial(reduce_kernel, tuple(modes)),
        out_shape=shapes,
        in_specs=inputs,
        out_specs=specs,
        scratch_shapes=[
            pltpu.SemaphoreType.DMA((n, 17)),
            pltpu.SemaphoreType.DMA((n, SENDS)),
            pltpu.SemaphoreType.DMA((n, SENDS)),
        ]
        + scratch,
        compiler_params=pltpu.CompilerParams(
            collective_id=collective_id, has_side_effects=True, vmem_limit_bytes=67043328
        ),
    )(*operands)


HEAD = 64
GROUP = 3
TILE = 512
WIDE = 1024
EDGE = 128
SPAN = 4096
FAR = 1 << 30


def longest(lengths):
    begin, best, at = jnp.int32(0), lengths[0], jnp.int32(0)
    for j in range(lengths.shape[0]):
        length = lengths[j]
        at = jnp.where(length > best, begin, at)
        best = jnp.maximum(best, length)
        begin = begin + length
    return at, at + best


def lane_slots(lengths, count):
    x, y, z, c = place()
    lane = lax.broadcasted_iota(jnp.int32, (1, count), 1)
    begin, end = longest(lengths)
    spots = [block(x, y, b, c) * count + lane for b in range(ZN)]
    slots, before = [], jnp.zeros((1, count), jnp.int32)
    for b in range(ZN):
        big = jnp.logical_and(spots[b] >= begin, spots[b] < end)
        slots.append(jnp.where(big, before, ZN // 2 + b - before))
        before = before + big.astype(jnp.int32)
    return begin, end, spots, slots


def pick(slots, slot, parts):
    chosen = parts[-1]
    for b in range(len(parts) - 2, -1, -1):
        chosen = jnp.where(slots[b] == slot, parts[b], chosen)
    return chosen


def bounds_of(lengths, spot):
    low, high = jnp.zeros_like(spot), jnp.full_like(spot, FAR)
    begin = jnp.int32(0)
    for j in range(lengths.shape[0]):
        end = begin + lengths[j]
        low = jnp.where(spot >= begin, begin, low)
        high = jnp.where(spot < end, jnp.minimum(high, end), high)
        begin = end
    return low, high


def walk(big, begin, end, low, high, step, init):
    if big:
        base = begin // EDGE * EDGE

        def body(i, carry):
            at = pl.multiple_of(base + i * WIDE, EDGE)
            return step(at, WIDE, False, carry)

        carry = step(pl.multiple_of(base, EDGE), WIDE, True, init)
        carry = lax.fori_loop(1, SPAN // WIDE, body, carry)
        return lax.cond(
            begin > base,
            lambda c: step(pl.multiple_of(base + SPAN, EDGE), EDGE, True, c),
            lambda c: c,
            carry,
        )
    first = jnp.min(low) // TILE
    stop = (jnp.max(high) + TILE - 1) // TILE
    hole_first = jnp.maximum((begin + TILE - 1) // TILE, first)
    hole = jnp.maximum(jnp.minimum(end // TILE, stop) - hole_first, 0)

    def body(i, carry):
        tile = first + i
        tile = jnp.where(jnp.logical_and(hole > 0, tile >= hole_first), tile + hole, tile)
        return step(pl.multiple_of(tile * TILE, TILE), TILE, True, carry)

    return lax.fori_loop(0, stop - first - hole, body, init)


def keys_in(first, size, low, high):
    at = first + lax.broadcasted_iota(jnp.int32, (size, low.shape[1]), 0)
    return jnp.logical_and(at >= low, at < high)


def dot(a, b):
    return jnp.dot(a, b, preferred_element_type=jnp.float32)


def pad_heads(rows, h, slots):
    part = rows[h * HEAD : (h + 1) * HEAD]
    zero = jnp.zeros_like(part)
    return jnp.concatenate([part if s == h else zero for s in slots], axis=0)


Q_SLOTS = (0, 1, 2, -1)
V_SLOTS = (-1, 2, 0, 1)


def forward_kernel(lengths, qt, kv, low_out, out, lse_out, qm, acc, qs, os, ls):
    count = qt.shape[2]
    begin, end, spots, slots = lane_slots(lengths, count)
    for s in range(ZN):
        qs[s] = pick(slots, s, [qt[b] for b in range(ZN)])

    def one_block(big, s, carry):
        low, high = bounds_of(lengths, pick(slots, s, spots))
        rows = qs[s] * jnp.bfloat16(0.125)
        for h in range(GROUP):
            qm[h] = pad_heads(rows, h, Q_SLOTS)
        acc[...] = jnp.zeros_like(acc)

        def step(at, size, masked, stats):
            span = pl.ds(at, size)
            keys = kv[span, 0:256]
            values = kv[span, 128:384].T
            mask = keys_in(at, size, low, high) if masked else None
            fresh = []
            for h in range(GROUP):
                top, total = stats[2 * h], stats[2 * h + 1]
                scores = dot(keys, qm[h])
                if masked:
                    scores = jnp.where(mask, scores, -1e9)
                new_top = jnp.maximum(top, jnp.max(scores, axis=0, keepdims=True))
                shrink = jnp.exp(top - new_top)
                weights = jnp.exp(scores - new_top)
                total = total * shrink + jnp.sum(weights, axis=0, keepdims=True)
                row = V_SLOTS.index(h) * HEAD
                acc[h] = acc[h] * shrink + dot(values[row : row + HEAD], weights.astype(jnp.bfloat16))
                fresh = fresh + [new_top, total]
            return tuple(fresh)

        init = (jnp.full((1, count), -1e9, jnp.float32), jnp.zeros((1, count), jnp.float32)) * GROUP
        stats = walk(big, begin, end, low, high, step, init)
        for h in range(GROUP):
            top, total = stats[2 * h], stats[2 * h + 1]
            os[s, h * HEAD : (h + 1) * HEAD] = acc[h] / total
            ls[s, h : h + 1] = top + jnp.log(total)
        return carry

    lax.fori_loop(0, ZN // 2, functools.partial(one_block, True), 0)
    lax.fori_loop(ZN // 2, ZN, functools.partial(one_block, False), 0)
    for b in range(ZN):
        value = pick([jnp.full_like(slots[b], s) for s in range(ZN)], slots[b], [os[s] for s in range(ZN)])
        out[b] = value
        low_out[b] = value.astype(low_out.dtype)
        lse_out[b] = pick([jnp.full_like(slots[b], s) for s in range(ZN)], slots[b], [ls[s] for s in range(ZN)])


def attend(lengths, qt, kv):
    blocks, rows, count = qt.shape
    whole = pl.BlockSpec(memory_space=pltpu.VMEM)
    return pl.pallas_call(
        forward_kernel,
        out_shape=[
            jax.ShapeDtypeStruct(qt.shape, jnp.bfloat16),
            jax.ShapeDtypeStruct(qt.shape, jnp.float32),
            jax.ShapeDtypeStruct((blocks, 8, count), jnp.float32),
        ],
        in_specs=[pl.BlockSpec(memory_space=pltpu.SMEM), whole, whole],
        out_specs=[whole] * 3,
        scratch_shapes=[
            pltpu.VMEM((GROUP, 256, count), jnp.bfloat16),
            pltpu.VMEM((GROUP, HEAD, count), jnp.float32),
            pltpu.VMEM(qt.shape, jnp.bfloat16),
            pltpu.VMEM(qt.shape, jnp.float32),
            pltpu.VMEM((blocks, 8, count), jnp.float32),
        ],
        compiler_params=pltpu.CompilerParams(vmem_limit_bytes=67043328),
    )(lengths, qt, kv)


def backward_kernel(lengths, qt, kv, out, lse, dot_in, cosine, sine, dq_out, dkv_out, qmt, qm, dmt, dm, dq, acc, qs, ds, es, ls, dqs):
    count = qt.shape[2]
    tiles = kv.shape[0] // TILE

    def clear(tile, carry):
        acc[pl.ds(pl.multiple_of(tile * TILE, TILE), TILE), :] = jnp.zeros((TILE, acc.shape[1]), jnp.float32)
        return carry

    lax.fori_loop(0, tiles, clear, 0)

    begin, end, spots, slots = lane_slots(lengths, count)
    for b in range(ZN):
        product_rows = dot_in[b].astype(jnp.float32) * out[b]
        for h in range(GROUP):
            es[b, h : h + 1] = jnp.sum(product_rows[h * HEAD : (h + 1) * HEAD], axis=0, keepdims=True)
    for s in range(ZN):
        qs[s] = pick(slots, s, [qt[b] for b in range(ZN)])
        ds[s] = pick(slots, s, [dot_in[b] for b in range(ZN)])
        ls[s] = pick(slots, s, [lse[b] for b in range(ZN)])
    picked = [pick(slots, s, [es[b] for b in range(ZN)]) for s in range(ZN)]
    for s in range(ZN):
        es[s] = picked[s]

    def one_block(big, s, carry):
        low, high = bounds_of(lengths, pick(slots, s, spots))
        rows = qs[s] * jnp.bfloat16(0.125)
        grads = ds[s]
        deltas = [es[s, h : h + 1] for h in range(GROUP)]
        levels = [ls[s, h : h + 1] for h in range(GROUP)]
        for h in range(GROUP):
            padded = pad_heads(rows, h, Q_SLOTS)
            qmt[h] = padded
            qm[h * count : (h + 1) * count] = padded.T
            padded = pad_heads(grads, h, V_SLOTS)
            dmt[h] = padded
            dm[h * count : (h + 1) * count] = padded.T
        dq[...] = jnp.zeros_like(dq)

        def step(at, size, masked, inner):
            span = pl.ds(at, size)
            keys = kv[span, 0:256]
            values = kv[span, 128:384]
            turned = keys.T
            mask = keys_in(at, size, low, high) if masked else None
            probs, slopes = [], []
            for h in range(GROUP):
                weights = jnp.exp(dot(keys, qmt[h]) - levels[h])
                if masked:
                    weights = jnp.where(mask, weights, 0.0)
                slope = (weights * (dot(values, dmt[h]) - deltas[h])).astype(jnp.bfloat16)
                dq[h] += dot(turned[h * HEAD : (h + 1) * HEAD], slope)
                probs.append(weights.astype(jnp.bfloat16))
                slopes.append(slope)
            dv = dot(jnp.concatenate(probs, axis=1), dm[...])
            dk = dot(jnp.concatenate(slopes, axis=1), qm[...])
            acc[span, 0:128] += dk[:, :128]
            acc[span, 128:256] += dk[:, 128:] + dv[:, :128]
            acc[span, 256:384] += dv[:, 128:]
            return inner

        walk(big, begin, end, low, high, step, 0)
        for h in range(GROUP):
            dqs[s, h * HEAD : (h + 1) * HEAD] = dq[h] * 0.125
        return carry

    lax.fori_loop(0, ZN // 2, functools.partial(one_block, True), 0)
    lax.fori_loop(ZN // 2, ZN, functools.partial(one_block, False), 0)
    half = HEAD // 2
    for b in range(ZN):
        back = pick([jnp.full_like(slots[b], s) for s in range(ZN)], slots[b], [dqs[s] for s in range(ZN)])
        for h in range(GROUP):
            at = h * HEAD
            w1, w2 = back[at : at + half], back[at + half : at + HEAD]
            dq_out[b, at : at + half] = (w1 * cosine[b] + w2 * sine[b]).astype(dq_out.dtype)
            dq_out[b, at + half : at + HEAD] = (w2 * cosine[b] - w1 * sine[b]).astype(dq_out.dtype)

    def finish(tile, carry):
        span = pl.ds(pl.multiple_of(tile * TILE, TILE), TILE)
        dkv_out[span, :] = acc[span, :].astype(dkv_out.dtype)
        return carry

    lax.fori_loop(0, tiles, finish, 0)


def attend_back(lengths, qt, kv, out, lse, dots, cosine, sine):
    blocks, rows, count = qt.shape
    whole = pl.BlockSpec(memory_space=pltpu.VMEM)
    return pl.pallas_call(
        backward_kernel,
        out_shape=[
            jax.ShapeDtypeStruct(qt.shape, jnp.bfloat16),
            jax.ShapeDtypeStruct(kv.shape, jnp.bfloat16),
        ],
        in_specs=[pl.BlockSpec(memory_space=pltpu.SMEM)] + [whole] * 7,
        out_specs=[whole] * 2,
        scratch_shapes=[
            pltpu.VMEM((GROUP, 256, count), jnp.bfloat16),
            pltpu.VMEM((GROUP * count, 256), jnp.bfloat16),
            pltpu.VMEM((GROUP, 256, count), jnp.bfloat16),
            pltpu.VMEM((GROUP * count, 256), jnp.bfloat16),
            pltpu.VMEM((GROUP, HEAD, count), jnp.float32),
            pltpu.VMEM(kv.shape, jnp.float32),
            pltpu.VMEM(qt.shape, jnp.bfloat16),
            pltpu.VMEM(qt.shape, jnp.bfloat16),
            pltpu.VMEM((blocks, 8, count), jnp.float32),
            pltpu.VMEM((blocks, 8, count), jnp.float32),
            pltpu.VMEM(qt.shape, jnp.float32),
        ],
        compiler_params=pltpu.CompilerParams(vmem_limit_bytes=67043328),
    )(lengths, qt, kv, out, lse, dots, cosine, sine)


KV_SLOTS = (0, 1, 2, 5, 3, 4)


def turn(rows, cosine, sine):
    first, second = rows[:, 0], rows[:, 1]
    return jnp.stack([first * cosine - second * sine, second * cosine + first * sine], axis=1)


def turn_back(rows, cosine, sine):
    first, second = rows[:, 0], rows[:, 1]
    return jnp.stack([first * cosine + second * sine, second * cosine - first * sine], axis=1)


def tables(lengths, first, count):
    starts = jnp.cumsum(lengths) - lengths
    position = first[:, None] + jnp.arange(count, dtype=jnp.int32)[None, :]
    begun = position[..., None] >= starts
    offsets = position - jnp.max(jnp.where(begun, starts, 0), axis=-1)
    half = HEAD // 2
    frequency = rope_base ** (-(jnp.arange(half, dtype=jnp.float32) * 2.0) / HEAD)
    angles = offsets.astype(jnp.float32)[:, None, :] * frequency[None, :, None]
    return jnp.cos(angles), jnp.sin(angles)


def norm_back(upstream, scaled, inv_std, gain_vec):
    weighted = upstream * gain_vec
    inner = (
        weighted
        - jnp.mean(weighted, axis=-1, keepdims=True)
        - scaled * jnp.mean(weighted * scaled, axis=-1, keepdims=True)
    )
    sums = [jnp.sum(upstream * scaled, axis=0, keepdims=True), jnp.sum(upstream, axis=0, keepdims=True)]
    return inv_std * inner, sums


def contract(left, right, dims):
    return lax.dot_general(left, right, (dims, ((), ())), preferred_element_type=jnp.float32)


def copies_kernel(*refs):
    n = len(refs) // 3
    ins, outs, bufs, sems = refs[:n], refs[n : 2 * n], refs[2 * n : 3 * n], refs[3 * n]
    loads = [pltpu.make_async_copy(ins[k], bufs[k], sems.at[k]) for k in range(n)]
    stores = [pltpu.make_async_copy(bufs[k], outs[k], sems.at[n + k]) for k in range(n)]
    for load in loads:
        load.start()
    for load, store in zip(loads, stores):
        load.wait()
        store.start()
    for store in stores:
        store.wait()


def copies(arrays):
    n = len(arrays)
    anywhere = pl.BlockSpec(memory_space=pl.ANY)
    return pl.pallas_call(
        copies_kernel,
        out_shape=[jax.ShapeDtypeStruct(a.shape, a.dtype) for a in arrays],
        in_specs=[anywhere] * n,
        out_specs=[anywhere] * n,
        scratch_shapes=[pltpu.VMEM(a.shape, a.dtype) for a in arrays] + [pltpu.SemaphoreType.DMA((2 * n,))],
    )(*arrays)


def local_grid(
    tokens,
    qkv_weight,
    out_weight,
    gate_weight,
    up_weight,
    down_weight,
    first_gain,
    first_bias,
    second_gain,
    second_bias,
    lengths,
    cotangent,
):
    bf16 = jnp.bfloat16
    rows, width = tokens.shape
    share = first_gain.shape[0]
    heads = width // HEAD
    half = HEAD // 2
    x, y, z, c = place()
    spots = [(px, py, pz, pc) for pz in range(ZN) for py in range(YN) for pc in range(CN) for px in range(XN)]
    over_x = [(block(*p), block(1 - p[0], *p[1:])) for p in spots]
    over_y = [(block(*p), block(p[0], 1 - p[1], *p[2:])) for p in spots]
    small = jnp.stack([first_gain, first_bias, second_gain, second_bias])
    small = jnp.pad(small, ((0, 4), (0, 128 - share)))
    hidden_width = gate_weight.shape[1]

    (qkv_blocks,) = gather([qkv_weight], ["bcast"], 1)
    qkv_full = qkv_blocks.reshape(width, 3 * width)
    turned = jnp.stack([block(x, y, b, c) for b in range(ZN)]) * rows
    cos_all, sin_all = tables(lengths, turned, rows)
    cosine = lax.dynamic_index_in_dim(cos_all, z, 0, keepdims=False)
    sine = lax.dynamic_index_in_dim(sin_all, z, 0, keepdims=False)

    raw = contract(qkv_full, tokens, ((0,), (1,))).astype(bf16)
    raw = raw.reshape(3, heads, 2, half, rows)
    queries = turn(raw[0].astype(jnp.float32), cosine, sine).astype(bf16)
    keys = turn(raw[1].astype(jnp.float32), cosine, sine).astype(bf16)
    queries = queries.reshape(ZN, GROUP * HEAD, rows)
    pairs = jnp.concatenate(
        [keys.reshape(ZN, GROUP, HEAD, rows), raw[2].reshape(ZN, GROUP, HEAD, rows)], axis=1
    )
    pairs = jnp.concatenate([pairs[:, s : s + 1] for s in KV_SLOTS], axis=1)
    pairs = jnp.swapaxes(pairs.reshape(ZN, 2 * GROUP * HEAD, rows), 1, 2)

    pairs_all, queries, out_full, down_full, small, gate_part, up_part = gather(
        [pairs, queries, out_weight, down_weight, small, gate_weight, up_weight],
        ["cross", "swap", "bcast", "bcast", "bcast", "by_x", "by_y"],
        2,
    )
    out_full = out_full.reshape(width, width)
    gate_rest = lax.ppermute(gate_part, ("cp", "hd"), over_y)
    up_rest = lax.ppermute(up_part, ("cp", "hd"), over_x)
    down_full = down_full.reshape(hidden_width, width)
    small = jnp.swapaxes(small[:, :4, :share], 0, 1).astype(jnp.float32).reshape(4, width)
    small = lax.optimization_barrier(small)
    gain_one, bias_one, gain_two, bias_two = [small[i] for i in range(4)]
    pairs_all = pairs_all.reshape(-1, 2 * GROUP * HEAD)
    low, attended, lse = attend(lengths, queries, pairs_all)
    low, gate_full, up_full = gather(
        [low, (gate_part, gate_rest), (up_part, up_rest)], ["swap", "rest_y", "rest_x"], 3
    )
    gate_full = gate_full.reshape(width, hidden_width)
    up_full = up_full.reshape(width, hidden_width)
    low = low.reshape(width, rows)

    attn_out = contract(low, out_full, ((0,), (0,)))
    first, scaled_one, inv_one = normalize(tokens.astype(jnp.float32) + attn_out, gain_one, bias_one)
    first_low = first.astype(bf16)
    gate_proj = product(first_low, gate_full)
    up_proj = product(first_low, up_full)
    sigmoid_gate = jax.nn.sigmoid(gate_proj)
    silu_gate = gate_proj * sigmoid_gate
    hidden = (silu_gate * up_proj).astype(bf16)
    branch = product(hidden, down_full)
    second, scaled_two, inv_two = normalize(first + branch, gain_two, bias_two)
    layer_out = second.astype(bf16)

    upstream = cotangent.astype(jnp.float32)
    dz_two, sums_two = norm_back(upstream, scaled_two, inv_two, gain_two)
    dz_two_low = dz_two.astype(bf16)
    hidden_grad = contract(dz_two_low, down_full, ((1,), (1,)))
    gate_back = (
        hidden_grad * up_proj * sigmoid_gate * (1.0 + gate_proj * (1.0 - sigmoid_gate))
    ).astype(bf16)
    up_back = (hidden_grad * silu_gate).astype(bf16)
    gate_sum = contract(first_low, gate_back, ((0,), (0,))).astype(bf16)
    up_sum = contract(first_low, up_back, ((0,), (0,))).astype(bf16)
    first_back = (
        dz_two + contract(gate_back, gate_full, ((1,), (1,))) + contract(up_back, up_full, ((1,), (1,)))
    )
    dz_one, sums_one = norm_back(first_back, scaled_one, inv_one, gain_one)
    dz_one_low = dz_one.astype(bf16)
    attended_back = contract(out_full, dz_one_low, ((1,), (1,))).astype(bf16)
    attended_back, gate_keep, gate_send, up_keep, up_send = reduce(
        [
            attended_back.reshape(ZN, GROUP * HEAD, rows),
            gate_sum.reshape((BLOCKS,) + gate_weight.shape),
            up_sum.reshape((BLOCKS,) + up_weight.shape),
        ],
        ["swap", "pair_y", "pair_x"],
        4,
    )
    gate_rest = lax.ppermute(gate_send, ("cp", "hd"), over_y)
    up_rest = lax.ppermute(up_send, ("cp", "hd"), over_x)

    query_back, pair_back = attend_back(
        lengths, queries, pairs_all, attended, lse, attended_back, cos_all, sin_all
    )
    small_sum = lax.optimization_barrier(jnp.concatenate(sums_one + sums_two, axis=0))
    small_sum = jnp.swapaxes(small_sum.reshape(4, BLOCKS, share), 0, 1)
    small_sum = jnp.pad(small_sum, ((0, 0), (0, 4), (0, 128 - share)))
    pair_back, query_back, out_grad, down_grad, small_grad, gate_grad, up_grad = reduce(
        [
            pair_back.reshape(BLOCKS, rows, 2 * GROUP * HEAD),
            query_back,
            (low, dz_one_low),
            (hidden, dz_two_low),
            small_sum,
            (gate_keep, gate_rest),
            (up_keep, up_rest),
        ],
        ["cross", "swap", "product", "turned_product", "reduce", "rest_y", "rest_x"],
        5,
    )
    pair_back = jnp.swapaxes(pair_back, 1, 2).reshape(ZN, 2 * GROUP, HEAD, rows)
    pair_back = [pair_back[:, KV_SLOTS.index(s)] for s in range(2 * GROUP)]
    key_back = jnp.stack(pair_back[:GROUP], axis=1).reshape(heads, 2, half, rows)
    key_back = turn_back(key_back.astype(jnp.float32), cosine, sine).astype(bf16)
    value_back = jnp.stack(pair_back[GROUP:], axis=1)
    raw_back = jnp.concatenate(
        [
            query_back.reshape(width, rows),
            key_back.reshape(width, rows),
            value_back.reshape(width, rows),
        ],
        axis=0,
    )
    qkv_sum = contract(tokens, raw_back, ((0,), (1,))).astype(bf16)
    tokens_grad = (dz_one + contract(raw_back, qkv_full, ((0,), (1,)))).astype(bf16)
    (qkv_grad,) = reduce([qkv_sum.reshape(BLOCKS, share, 3 * width)], ["reduce"], 6)
    qkv_grad, out_grad, gate_grad, up_grad, down_grad = copies([qkv_grad, out_grad, gate_grad, up_grad, down_grad])
    return (
        layer_out,
        tokens_grad,
        qkv_grad,
        out_grad,
        gate_grad,
        up_grad,
        down_grad,
        small_grad[0, :share],
        small_grad[1, :share],
        small_grad[2, :share],
        small_grad[3, :share],
    )


def solution(mesh):
    rows = P(("cp", "hd"), None)
    line = P(("cp", "hd"))
    local = local_grid if (mesh.shape["cp"], mesh.shape["hd"]) == (ZN * YN * CN, XN) else local_any
    return jax.shard_map(
        local,
        mesh=mesh,
        in_specs=(rows,) * 6 + (line,) * 4 + (P(), rows),
        out_specs=(rows,) * 7 + (line,) * 4,
        check_vma=False,
    )
```

```python
import functools

import jax
import jax.numpy as jnp
from jax import lax
from jax.experimental import pallas as pl
from jax.experimental.pallas import tpu as pltpu
from jax.sharding import PartitionSpec as P

HD = 64
REACH = 8


rope_base = 1000.0
norm_eps = 1e-12
score_scale = 0.125
masked_score = -1000000000.0


def shifted(block, axis, distance):
    devices = range(lax.axis_size(axis))
    route = [(i - distance, i) for i in devices if i - distance in devices]
    return lax.ppermute(block, axis, route)


def doc_layout(lengths, first_row, row_count):
    starts = jnp.cumsum(lengths) - lengths
    position = first_row + jnp.arange(row_count, dtype=jnp.int32)
    at_or_after = position[:, None] >= starts[None, :]
    doc_ids = jnp.sum(at_or_after.astype(jnp.int32), axis=1) - 1
    doc_begin = jnp.max(jnp.where(at_or_after, starts[None, :], 0), axis=1)
    return (doc_ids, position - doc_begin)


def rope_tables(offsets, head_size):
    half_size = head_size // 2
    frequency = rope_base ** (-(jnp.arange(half_size, dtype=jnp.float32) * 2.0) / head_size)
    angles = offsets.astype(jnp.float32)[:, None] * frequency[None, :]
    return (jnp.cos(angles), jnp.sin(angles))


def rotate(values, cosine, sine):
    half_size = values.shape[-1] // 2
    first_half = values[..., :half_size]
    second_half = values[..., half_size:]
    cos_rows = cosine[:, None, :]
    sin_rows = sine[:, None, :]
    return jnp.concatenate(
        [
            first_half * cos_rows - second_half * sin_rows,
            second_half * cos_rows + first_half * sin_rows,
        ],
        axis=-1,
    )


def rotate_back(grads, cosine, sine):
    half_size = grads.shape[-1] // 2
    first_half = grads[..., :half_size]
    second_half = grads[..., half_size:]
    cos_rows = cosine[:, None, :]
    sin_rows = sine[:, None, :]
    return jnp.concatenate(
        [
            first_half * cos_rows + second_half * sin_rows,
            second_half * cos_rows - first_half * sin_rows,
        ],
        axis=-1,
    )


def normalize(hidden_in, gain_vec, bias_vec):
    average = jnp.mean(hidden_in, axis=-1, keepdims=True)
    centered = hidden_in - average
    variance = jnp.mean(centered * centered, axis=-1, keepdims=True)
    inv_std = lax.rsqrt(variance + norm_eps)
    scaled = centered * inv_std
    return (scaled * gain_vec + bias_vec, scaled, inv_std)


def normalize_back(upstream, scaled, inv_std, gain_vec):
    weighted = upstream * gain_vec
    inner = (
        weighted
        - jnp.mean(weighted, axis=-1, keepdims=True)
        - scaled * jnp.mean(weighted * scaled, axis=-1, keepdims=True)
    )
    return (inv_std * inner, jnp.sum(upstream * scaled, axis=0), jnp.sum(upstream, axis=0))


def product(left, right):
    return jnp.dot(left, right, preferred_element_type=jnp.float32)


def local_any(
    tokens,
    qkv_weight,
    out_weight,
    gate_weight,
    up_weight,
    down_weight,
    first_gain,
    first_bias,
    second_gain,
    second_bias,
    doc_lengths,
    cotangent,
):
    rows_here = tokens.shape[0]
    model_width = tokens.shape[1]
    hd_count = lax.axis_size("hd")
    cp_count = lax.axis_size("cp")
    cp_index = lax.axis_index("cp")
    block_rows = rows_here * hd_count
    local_width = model_width // hd_count
    local_heads = local_width // HD
    shifts = [0]
    for distance in range(1, REACH + 1):
        shifts = shifts + [-distance, distance]
    shards = (
        qkv_weight,
        out_weight,
        gate_weight,
        up_weight,
        down_weight,
        first_gain,
        first_bias,
        second_gain,
        second_bias,
    )
    weights = (
        lax.all_gather(shards[0], ("cp", "hd"), axis=0, tiled=True),
        lax.all_gather(shards[1], ("cp", "hd"), axis=0, tiled=True),
        lax.all_gather(shards[2], ("cp", "hd"), axis=0, tiled=True),
        lax.all_gather(shards[3], ("cp", "hd"), axis=0, tiled=True),
        lax.all_gather(shards[4], ("cp", "hd"), axis=0, tiled=True),
        lax.all_gather(shards[5], ("cp", "hd"), axis=0, tiled=True),
        lax.all_gather(shards[6], ("cp", "hd"), axis=0, tiled=True),
        lax.all_gather(shards[7], ("cp", "hd"), axis=0, tiled=True),
        lax.all_gather(shards[8], ("cp", "hd"), axis=0, tiled=True),
    )
    (
        qkv_full,
        out_full,
        gate_full,
        up_full,
        down_full,
        gain_first,
        bias_first,
        gain_second,
        bias_second,
    ) = weights
    raw_rows = product(tokens, qkv_full).astype(jnp.bfloat16)
    grouped = lax.all_to_all(
        raw_rows.reshape(rows_here, 3, hd_count, local_width),
        "hd",
        split_axis=2,
        concat_axis=0,
        tiled=True,
    )
    grouped = grouped.reshape(block_rows, 3, local_width)
    query_docs, offsets = doc_layout(doc_lengths, cp_index * block_rows, block_rows)
    cosine, sine = rope_tables(offsets, HD)
    queries = rotate(
        grouped[:, 0].astype(jnp.float32).reshape(block_rows, local_heads, HD), cosine, sine
    ).astype(jnp.bfloat16)
    key_rows = rotate(
        grouped[:, 1].astype(jnp.float32).reshape(block_rows, local_heads, HD), cosine, sine
    ).astype(jnp.bfloat16)
    own_block = jnp.stack([key_rows.reshape(block_rows, local_width), grouped[:, 2]], axis=1)

    def key_docs(distance):
        source = cp_index - distance
        doc_ids, unused_offsets = doc_layout(doc_lengths, source * block_rows, block_rows)
        inside = jnp.logical_and(source >= 0, source < cp_count)
        return jnp.where(inside, doc_ids, -2)

    remote = [own_block] + [shifted(own_block, "cp", distance) for distance in shifts[1:]]
    masks = [query_docs[:, None] == key_docs(distance)[None, :] for distance in shifts]

    def scores_with(query_part, remote_block, key_mask):
        key_part = remote_block[:, 0].reshape(block_rows, local_heads, HD)
        raw_scores = (
            jnp.einsum("qhd,khd->hqk", query_part, key_part, preferred_element_type=jnp.float32)
            * score_scale
        )
        return jnp.where(key_mask[None], raw_scores, masked_score)

    def scores_for(remote_block, key_mask):
        return scores_with(queries, remote_block, key_mask)

    running_max = jnp.full((local_heads, block_rows), masked_score, jnp.float32)
    running_sum = jnp.zeros((local_heads, block_rows), jnp.float32)
    for remote_block, key_mask in zip(remote, masks):
        block_scores = scores_for(remote_block, key_mask)
        new_max = jnp.maximum(running_max, jnp.max(block_scores, axis=-1))
        running_sum = running_sum * jnp.exp(running_max - new_max) + jnp.sum(
            jnp.exp(block_scores - new_max[:, :, None]), axis=-1
        )
        running_max = new_max
    log_total = running_max + jnp.log(running_sum)
    attended = jnp.zeros((block_rows, local_heads, HD), jnp.float32)
    for remote_block, key_mask in zip(remote, masks):
        block_scores = scores_for(remote_block, key_mask)
        probs = jnp.exp(block_scores - log_total[:, :, None]).astype(jnp.bfloat16)
        value_part = remote_block[:, 1].reshape(block_rows, local_heads, HD)
        attended = attended + jnp.einsum(
            "hqk,khd->qhd", probs, value_part, preferred_element_type=jnp.float32
        )
    attended_send = attended.reshape(block_rows, 1, local_width).astype(jnp.bfloat16)
    attended_low = lax.all_to_all(
        attended_send, "hd", split_axis=0, concat_axis=1, tiled=True
    ).reshape(rows_here, model_width)
    gain_one = gain_first.astype(jnp.float32)
    gain_two = gain_second.astype(jnp.float32)
    attn_out = product(attended_low, out_full)
    first, scaled_one, inv_one = normalize(
        tokens.astype(jnp.float32) + attn_out, gain_one, bias_first.astype(jnp.float32)
    )
    first_low = first.astype(jnp.bfloat16)
    gate_proj = product(first_low, gate_full)
    up_proj = product(first_low, up_full)
    sigmoid_gate = jax.nn.sigmoid(gate_proj)
    silu_gate = gate_proj * sigmoid_gate
    hidden = (silu_gate * up_proj).astype(jnp.bfloat16)
    branch = product(hidden, down_full)
    second, scaled_two, inv_two = normalize(
        first + branch, gain_two, bias_second.astype(jnp.float32)
    )
    layer_out = second.astype(jnp.bfloat16)
    weights = (
        lax.all_gather(shards[0], ("cp", "hd"), axis=0, tiled=True),
        lax.all_gather(shards[1], ("cp", "hd"), axis=0, tiled=True),
        lax.all_gather(shards[2], ("cp", "hd"), axis=0, tiled=True),
        lax.all_gather(shards[3], ("cp", "hd"), axis=0, tiled=True),
        lax.all_gather(shards[4], ("cp", "hd"), axis=0, tiled=True),
        lax.all_gather(shards[5], ("cp", "hd"), axis=0, tiled=True),
        lax.all_gather(shards[6], ("cp", "hd"), axis=0, tiled=True),
        lax.all_gather(shards[7], ("cp", "hd"), axis=0, tiled=True),
        lax.all_gather(shards[8], ("cp", "hd"), axis=0, tiled=True),
    )
    (
        qkv_full,
        out_full,
        gate_full,
        up_full,
        down_full,
        gain_first,
        bias_first,
        gain_second,
        bias_second,
    ) = weights
    upstream = cotangent.astype(jnp.float32)
    dz_two, gain_two_grad, bias_two_grad = normalize_back(upstream, scaled_two, inv_two, gain_two)
    dz_two_low = dz_two.astype(jnp.bfloat16)
    down_sum = product(hidden.T, dz_two_low)
    hidden_grad = product(dz_two_low, down_full.T)
    gate_back = (
        hidden_grad * up_proj * sigmoid_gate * (1.0 + gate_proj * (1.0 - sigmoid_gate))
    ).astype(jnp.bfloat16)
    up_back = (hidden_grad * silu_gate).astype(jnp.bfloat16)
    gate_sum = product(first_low.T, gate_back)
    up_sum = product(first_low.T, up_back)
    first_back = dz_two + product(gate_back, gate_full.T) + product(up_back, up_full.T)
    dz_one, gain_one_grad, bias_one_grad = normalize_back(first_back, scaled_one, inv_one, gain_one)
    dz_one_low = dz_one.astype(jnp.bfloat16)
    out_sum = product(attended_low.T, dz_one_low)
    attended_back = product(dz_one_low, out_full.T).astype(jnp.bfloat16)
    heads_back = lax.all_to_all(
        attended_back.reshape(rows_here, hd_count, local_width),
        "hd",
        split_axis=1,
        concat_axis=0,
        tiled=True,
    )
    heads_back = heads_back.reshape(block_rows, local_heads, HD)
    delta = jnp.transpose(jnp.sum(heads_back.astype(jnp.float32) * attended, axis=-1))
    query_grad = jnp.zeros((block_rows, local_heads, HD), jnp.float32)
    pair_total = jnp.zeros((block_rows, 2, local_width), jnp.float32)
    remote = [own_block] + [shifted(own_block, "cp", distance) for distance in shifts[1:]]
    for distance, remote_block, key_mask in zip(shifts, remote, masks):
        pair_block_scores = scores_with(queries, remote_block, key_mask)
        pair_probs = jnp.exp(pair_block_scores - log_total[:, :, None])
        pair_key_part = remote_block[:, 0].reshape(block_rows, local_heads, HD)
        pair_value_part = remote_block[:, 1].reshape(block_rows, local_heads, HD)
        value_grad = jnp.einsum(
            "hqk,qhd->khd",
            pair_probs.astype(jnp.bfloat16),
            heads_back,
            preferred_element_type=jnp.float32,
        )
        prob_grad = jnp.einsum(
            "qhd,khd->hqk", heads_back, pair_value_part, preferred_element_type=jnp.float32
        )
        score_grad = (pair_probs * (prob_grad - delta[:, :, None])).astype(jnp.bfloat16)
        query_term = (
            jnp.einsum(
                "hqk,khd->qhd", score_grad, pair_key_part, preferred_element_type=jnp.float32
            )
            * score_scale
        )
        key_grad = (
            jnp.einsum("hqk,qhd->khd", score_grad, queries, preferred_element_type=jnp.float32)
            * score_scale
        )
        grad_pair = jnp.stack(
            [
                key_grad.reshape(block_rows, local_width),
                value_grad.reshape(block_rows, local_width),
            ],
            axis=1,
        )
        query_term, grad_pair = (query_term, grad_pair)
        query_grad = query_grad + query_term
        if distance == 0:
            pair_total = grad_pair
        else:
            pair_total = pair_total + shifted(
                grad_pair.astype(jnp.bfloat16), "cp", -distance
            ).astype(grad_pair.dtype)
    query_back = rotate_back(query_grad, cosine, sine).reshape(block_rows, local_width)
    key_back = rotate_back(
        pair_total[:, 0].reshape(block_rows, local_heads, HD), cosine, sine
    ).reshape(block_rows, local_width)
    raw_back = jnp.stack([query_back, key_back, pair_total[:, 1]], axis=1).astype(jnp.bfloat16)
    raw_back = lax.all_to_all(
        raw_back.reshape(block_rows, 3, 1, local_width),
        "hd",
        split_axis=0,
        concat_axis=2,
        tiled=True,
    )
    raw_back = raw_back.reshape(rows_here, 3 * model_width)
    qkv_sum = product(tokens.T, raw_back)
    tokens_grad = (dz_one + product(raw_back, qkv_full.T)).astype(jnp.bfloat16)
    summed = (
        lax.psum_scatter(qkv_sum, ("cp", "hd"), scatter_dimension=0, tiled=True),
        lax.psum_scatter(out_sum, ("cp", "hd"), scatter_dimension=0, tiled=True),
        lax.psum_scatter(gate_sum, ("cp", "hd"), scatter_dimension=0, tiled=True),
        lax.psum_scatter(up_sum, ("cp", "hd"), scatter_dimension=0, tiled=True),
        lax.psum_scatter(down_sum, ("cp", "hd"), scatter_dimension=0, tiled=True),
        lax.psum_scatter(gain_one_grad, ("cp", "hd"), scatter_dimension=0, tiled=True),
        lax.psum_scatter(bias_one_grad, ("cp", "hd"), scatter_dimension=0, tiled=True),
        lax.psum_scatter(gain_two_grad, ("cp", "hd"), scatter_dimension=0, tiled=True),
        lax.psum_scatter(bias_two_grad, ("cp", "hd"), scatter_dimension=0, tiled=True),
    )
    return (
        layer_out,
        tokens_grad,
        summed[0],
        summed[1],
        summed[2],
        summed[3],
        summed[4],
        summed[5],
        summed[6],
        summed[7],
        summed[8],
    )


MESH = pl.DeviceIdType.MESH
ZN, YN, CN, XN = 4, 2, 2, 2
BLOCKS = ZN * YN * CN * XN


def place():
    cp = lax.axis_index("cp")
    x = lax.axis_index("hd")
    return x, lax.rem(cp // CN, YN), cp // (YN * CN), lax.rem(cp, CN)


def device(x, y, z, c):
    return ((z * YN + y) * CN + c, x)


def block(x, y, z, c):
    return ((z * YN + y) * CN + c) * XN + x


def when(cond, fn):
    if cond is None:
        fn()
    else:
        pl.when(cond)(fn)


def both(a, b):
    if a is None:
        return b
    if b is None:
        return a
    return jnp.logical_and(a, b)


def halves(ref):
    rows, cols = ref.shape[-2:]
    if rows % 32 == 0:
        return ref.at[pl.ds(0, rows // 2)], ref.at[pl.ds(rows // 2, rows // 2)]
    if cols % 256 == 0:
        return ref.at[:, pl.ds(0, cols // 2)], ref.at[:, pl.ds(cols // 2, cols // 2)]
    return ref, None


def greet(x, y, z, c, far):
    barrier = pltpu.get_barrier_semaphore()
    for peer in (device(1 - x, y, z, c), device(x, 1 - y, z, c), device(x, y, z, 1 - c)):
        pl.semaphore_signal(barrier, inc=1, device_id=peer, device_id_type=MESH)
    count = 3
    if far:
        for k in range(1, ZN):
            peer = device(x, y, lax.rem(z + k, ZN), c)
            pl.semaphore_signal(barrier, inc=1, device_id=peer, device_id_type=MESH)
        count = count + ZN - 1
    else:
        pl.when(z > 0)(lambda: pl.semaphore_signal(barrier, inc=1, device_id=device(x, y, z - 1, c), device_id_type=MESH))
        pl.when(z < ZN - 1)(lambda: pl.semaphore_signal(barrier, inc=1, device_id=device(x, y, z + 1, c), device_id_type=MESH))
        count = count + (z > 0).astype(jnp.int32) + (z < ZN - 1).astype(jnp.int32)
    pl.semaphore_wait(barrier, count)


SENDS = 40
RECVS = 36


BCAST, BY_X, BY_Y, CROSS, SWAP, REST_X, REST_Y, PAIR_X, PAIR_Y, REDUCE, PRODUCT, TURNED_PRODUCT = range(12)
ONWARD, BESIDE, ACROSS = range(3)
CHAINED = (BCAST, BY_X, BY_Y)
REST = (REST_X, REST_Y)


def take(refs, counts):
    groups = []
    for count in counts:
        groups.append(refs[:count])
        refs = refs[count:]
    return groups, refs


SHORT_PLAN = [
    (fn, 0, d - lag)
    for d in range(1, ZN + 2)
    for lag, fn in enumerate((ONWARD, BESIDE, ACROSS))
    if (d > 0 if lag else d < ZN) and 0 <= d - lag < ZN
]
PLAN = [
    (ONWARD, 0, 1),
    (BESIDE, 0, 0),
    (BESIDE, 1, 0),
    (ACROSS, 0, 0),
    (BESIDE, 0, 1),
    (ONWARD, 1, 1),
    (ACROSS, 1, 0),
    (ACROSS, 0, 1),
    (ONWARD, 1, 2),
    (ONWARD, 1, 3),
    (BESIDE, 1, 1),
    (ONWARD, 0, 2),
    (BESIDE, 1, 2),
    (BESIDE, 1, 3),
    (BESIDE, 0, 2),
    (ACROSS, 1, 1),
    (ONWARD, 0, 3),
    (ACROSS, 1, 2),
    (ACROSS, 1, 3),
    (ACROSS, 0, 2),
    (BESIDE, 0, 3),
    (ACROSS, 0, 3),
]


def gather_kernel(modes, *refs):
    n = len(modes)
    ins, refs = take(refs, [2 if mode in REST else 1 for mode in modes])
    outs, (lsem, ssem, rsem), bufs = refs[:n], refs[n : n + 3], list(refs[n + 3 :])
    bufs = {k: bufs.pop(0) for k, mode in enumerate(modes) if mode in REST}
    pairs, ins = ins, [group[0] for group in ins]
    x, y, z, c = place()
    ox, oy, oc = 1 - x, 1 - y, 1 - c
    greet(x, y, z, c, any(m in (SWAP, CROSS) for m in modes))
    sent = []

    def copy(k, src, dst, s, r, peer):
        return pltpu.make_async_remote_copy(
            src_ref=src,
            dst_ref=dst,
            send_sem=ssem.at[k, s],
            recv_sem=rsem.at[k, r],
            device_id=peer,
            device_id_type=MESH,
        )

    def send(cond, *args):
        when(cond, lambda: copy(*args).start())
        sent.append((cond, args))

    def arrived(cond, k, ref, r):
        when(cond, lambda: copy(k, ref, ref, 0, r, device(ox, y, z, c)).wait_recv())

    locals_ = []

    def keep(k, i, mine, spot):
        pltpu.make_async_copy(mine, spot, lsem.at[k, i]).start()
        locals_.append((k, i, mine, spot))

    def at(k, px, py, b):
        if modes[k] == BY_X:
            return outs[k].at[2 * b + px]
        if modes[k] == BY_Y:
            return outs[k].at[2 * b + py]
        return outs[k].at[block(px, py, b, c)]

    for k, mode in enumerate(modes):
        if mode in CHAINED:
            keep(k, 0, ins[k], at(k, x, y, z))
        elif mode == SWAP:
            keep(k, 0, ins[k].at[z], outs[k].at[z])
        elif mode == CROSS:
            keep(k, 0, ins[k].at[z], outs[k].at[block(x, y, z, c)])

    def share_of(k, i, core):
        b, j = i % 8 // 2, i % 2
        if modes[k] == REST_Y:
            return block(j, oy if i >= 8 else y, b, core)
        return block(ox if i >= 8 else x, j, b, core)

    def spread(k, cond, b, src, up, down):
        here = at(k, x, y, b)
        if modes[k] in CHAINED:
            if up is not False:
                send(both(cond, up), k, src, here, b, b, device(x, y, lax.rem(z + 1, ZN), c))
            if down is not False:
                send(both(cond, down), k, src, here, 4 + b, b, device(x, y, lax.rem(z + ZN - 1, ZN), c))
        if modes[k] != BY_Y:
            send(cond, k, src, here, 8 + b, 4 + b, device(ox, y, z, c))
        if modes[k] != BY_X:
            send(cond, k, src, here, 16 + b, 12 + b, device(x, oy, z, c))
        if modes[k] not in (BY_X, BY_Y):
            send(cond, k, src, here, 24 + b, 20 + b, device(x, y, z, oc))

    def sides(k, cond, b):
        fx, fy = at(k, ox, y, b), at(k, x, oy, b)
        full = modes[k] not in (BY_X, BY_Y)
        if modes[k] != BY_Y:
            arrived(cond, k, fx, 4 + b)
            first, _ = halves(fx)
            if full:
                send(cond, k, first, first, 20 + b, 16 + b, device(x, oy, z, c))
                send(cond, k, fx, fx, 28 + b, 24 + b, device(x, y, z, oc))
        if modes[k] != BY_X:
            arrived(cond, k, fy, 12 + b)
            _, second = halves(fy)
            if full and second is not None:
                send(cond, k, second, second, 12 + b, 8 + b, device(ox, y, z, c))
            if full:
                send(cond, k, fy, fy, 32 + b, 28 + b, device(x, y, z, oc))

    def corner(k, cond, b):
        far = outs[k].at[block(ox, oy, b, c)]
        first, second = halves(far)
        arrived(cond, k, first, 16 + b)
        if second is not None:
            arrived(cond, k, second, 8 + b)
        send(cond, k, far, far, 36 + b, 32 + b, device(x, y, z, oc))

    def steps(distance):
        if distance == 0:
            return [(None, z)]
        return [(z >= distance, jnp.maximum(z - distance, 0)), (z + distance < ZN, jnp.minimum(z + distance, ZN - 1))]

    chained = [k for k, mode in enumerate(modes) if mode in CHAINED]
    crossed = [k for k, mode in enumerate(modes) if mode == CROSS]
    swapped = [k for k, mode in enumerate(modes) if mode == SWAP]

    def exchange(ks):
        for k in ks:
            for d in range(1, ZN):
                to = lax.rem(z + d, ZN)
                spot = outs[k].at[z] if modes[k] == SWAP else outs[k].at[block(x, y, z, c)]
                send(None, k, ins[k].at[to], spot, to, z, device(x, y, to, c))

    for k in chained:
        spread(k, None, z, ins[k], z < ZN - 1, z > 0)
    if not chained:
        exchange(swapped)
        swapped = []
    for k, mode in enumerate(modes):
        if mode in REST:
            for i in range(16):
                src = pairs[k][i // 8].at[i % 8]
                pltpu.make_async_copy(src, bufs[k].at[i], lsem.at[k, i]).start()
                send(None, k, src, outs[k].at[share_of(k, i, c)], i, i, device(x, y, z, oc))
    for k in crossed:
        spread(k, None, z, ins[k].at[z], False, False)
    exchange(crossed)

    def onward(ks, distance):
        for side, (cond, b) in enumerate(steps(distance)):
            for k in ks:
                here = at(k, x, y, b)
                arrived(cond, k, here, b)
                spread(k, cond, b, here, z < ZN - 1 if side == 0 else False, z > 0 if side == 1 else False)

    def beside(ks, distance):
        for cond, b in steps(distance):
            for k in ks:
                sides(k, cond, b)

    def across(ks, distance):
        for cond, b in steps(distance):
            for k in ks:
                if modes[k] in (BCAST, CROSS):
                    corner(k, cond, b)

    plan = PLAN if crossed else SHORT_PLAN
    for fn, ks, distance in plan if chained else ():
        fn = {ONWARD: onward, BESIDE: beside, ACROSS: across}[fn]
        fn(chained if ks == 0 else crossed, distance)
        if fn is onward and distance == ZN - 1 and ks == 0:
            exchange(swapped)
            swapped = []
    exchange(swapped)
    for k in bufs:
        for i in range(16):
            pltpu.make_async_copy(pairs[k][0].at[0], bufs[k].at[i], lsem.at[k, i]).wait()
            keep(k, i, bufs[k].at[i], outs[k].at[share_of(k, i, c)])
    for k, mode in enumerate(modes):
        if mode == SWAP:
            for d in range(1, ZN):
                frm = lax.rem(z + d, ZN)
                arrived(None, k, outs[k].at[frm], frm)
        elif mode in REST:
            for i in range(16):
                arrived(None, k, outs[k].at[share_of(k, i, oc)], i)
        elif mode not in (BY_X, BY_Y):
            quads = (0, 1, 2, 3)
            for b in range(ZN):
                for j in quads:
                    px, py = ((x, y), (ox, y), (x, oy), (ox, oy))[j]
                    arrived(None, k, outs[k].at[block(px, py, b, oc)], 20 + 4 * j + b)
    for k, i, mine, spot in locals_:
        pltpu.make_async_copy(mine, spot, lsem.at[k, i]).wait()
    for cond, args in sent:
        when(cond, lambda args=args: copy(*args).wait_send())


def gather(arrays, modes, collective_id):
    shapes, inputs, operands, scratch = [], [], [], []
    anywhere, local = pl.BlockSpec(memory_space=pl.ANY), pl.BlockSpec(memory_space=pltpu.VMEM)
    for a, mode in zip(arrays, modes):
        inputs = inputs + ([anywhere] * 2 if mode in REST else [local])
        operands = operands + (list(a) if mode in REST else [a])
        if mode in REST:
            a = a[0]
            scratch.append(pltpu.VMEM((16,) + a.shape[1:], a.dtype))
        if mode == BCAST:
            shapes.append((BLOCKS,) + a.shape)
        elif mode in CHAINED:
            shapes.append((2 * ZN,) + a.shape)
        elif mode == SWAP:
            shapes.append(a.shape)
        else:
            shapes.append((BLOCKS,) + a.shape[1:])
    n = len(arrays)
    dtypes = [(a[0] if mode in REST else a).dtype for a, mode in zip(arrays, modes)]
    return pl.pallas_call(
        functools.partial(gather_kernel, tuple(modes)),
        out_shape=[jax.ShapeDtypeStruct(shape, dtype) for shape, dtype in zip(shapes, dtypes)],
        in_specs=inputs,
        out_specs=[anywhere] * n,
        scratch_shapes=[
            pltpu.SemaphoreType.DMA((n, 16)),
            pltpu.SemaphoreType.DMA((n, SENDS)),
            pltpu.SemaphoreType.DMA((n, RECVS)),
        ]
        + scratch,
        compiler_params=pltpu.CompilerParams(
            collective_id=collective_id, has_side_effects=True, vmem_limit_bytes=67043328
        ),
    )(*operands)


def chunk_of(cols):
    for size in (768, 640, 512, 384, 256, 128):
        if cols % size == 0:
            return size
    return cols


def add_up(dst, sources):
    rows, cols = dst.shape[-2:]
    tall = 32 if rows > 32 and rows % 32 == 0 else (16 if rows > 32 else rows)
    wide = cols if rows > 32 else chunk_of(cols)

    def step(i, carry):
        if rows > 32:
            spot = (pl.ds(pl.multiple_of(i * tall, tall), tall), slice(None))
        elif cols > wide:
            spot = (slice(None), pl.ds(pl.multiple_of(i * wide, wide), wide))
        else:
            spot = (slice(None), slice(None))
        total = sources[0][spot].astype(jnp.float32)
        for source in sources[1:]:
            total = total + source[spot].astype(jnp.float32)
        dst[spot] = total.astype(dst.dtype)
        return carry

    count = (rows // tall) * (cols // wide)
    if count == 1:
        step(0, 0)
    else:
        lax.fori_loop(0, count, step, 0)


BUFFERS = {PRODUCT: 5, TURNED_PRODUCT: 5, SWAP: 0, PAIR_X: 2, PAIR_Y: 2, CROSS: 3, REDUCE: 4, REST_X: 4, REST_Y: 4}
PAIR = (PAIR_X, PAIR_Y)
MADE = (PRODUCT, TURNED_PRODUCT)


def make(dst, left, right, turned):
    blocks, rows = dst.shape[:2]
    group = blocks // 8

    def step(i, carry):
        span = pl.ds(pl.multiple_of(i * group * rows, 32), group * rows)
        if turned:
            span = pl.ds(pl.multiple_of(i * group * rows, 128), group * rows)
            part = left[:, span].T
        else:
            part = left[span, :]
        total = jnp.dot(part, right[...], preferred_element_type=jnp.float32)
        for j in range(group):
            dst[i * group + j] = total[j * rows : (j + 1) * rows].astype(dst.dtype)
        return carry

    lax.fori_loop(0, blocks // group, step, 0)


def reduce_kernel(modes, *refs):
    n = len(modes)
    ins, refs = take(refs, [2 if mode in REST + MADE else 1 for mode in modes])
    outs, refs = take(refs, [2 if mode in PAIR else 1 for mode in modes])
    (lsem, ssem, rsem), scratch = refs[:3], refs[3:]
    bufs, _ = take(scratch, [BUFFERS[mode] for mode in modes])
    others, seconds = ins, outs
    ins, outs = [group[0] for group in ins], [group[0] for group in outs]
    for k, mode in enumerate(modes):
        if mode in MADE:
            ins[k] = bufs[k][4]
    bufs = [group[:4] for group in bufs]
    x, y, z, c = place()
    ox, oy, oc = 1 - x, 1 - y, 1 - c
    greet(x, y, z, c, any(m in (SWAP, CROSS) for m in modes))
    sent = []

    def copy(k, src, dst, s, r, peer):
        return pltpu.make_async_remote_copy(
            src_ref=src,
            dst_ref=dst,
            send_sem=ssem.at[k, s],
            recv_sem=rsem.at[k, r],
            device_id=peer,
            device_id_type=MESH,
        )

    def send(cond, *args):
        when(cond, lambda: copy(*args).start())
        sent.append((cond, args))

    def arrived(cond, k, ref, r):
        when(cond, lambda: copy(k, ref, ref, 0, r, device(ox, y, z, c)).wait_recv())

    half = z // 2
    order = [3 - 3 * half, 2 - half, 1 - z + 4 * half, z]
    quads = ((ox, oy), (ox, y), (x, oy), (x, y))
    active = [k for k, mode in enumerate(modes) if mode in (CROSS, REDUCE) + MADE]
    paired = [k for k, mode in enumerate(modes) if mode in PAIR]
    rest = [k for k, mode in enumerate(modes) if mode in REST]

    for k, mode in enumerate(modes):
        if mode == SWAP:
            for d in range(1, ZN):
                to = lax.rem(z + d, ZN)
                send(None, k, ins[k].at[to], outs[k].at[z], d, z, device(x, y, to, c))
            pltpu.make_async_copy(ins[k].at[z], outs[k].at[z], lsem.at[k, 0]).start()

    for k in rest:
        acc, rec = bufs[k][:2]
        for i, b in enumerate(order):
            for j in range(2):
                mine = (x, y)[modes[k] == REST_X]
                spot = 2 * b + (mine if j else 1 - mine)
                pltpu.make_async_copy(ins[k].at[spot], acc.at[2 * i + j], lsem.at[k, 2 * i + j]).start()
                pltpu.make_async_copy(others[k][1].at[spot], rec.at[2 * i + j], lsem.at[k, 8 + 2 * i + j]).start()
    def begin(ks):
        for k in ks:
            if modes[k] in MADE:
                make(ins[k], *others[k], modes[k] == TURNED_PRODUCT)
            for i, b in enumerate(order):
                acc, cor = bufs[k][:2]
                for j, (px, py) in enumerate(quads):
                    send(None, k, ins[k].at[block(px, py, b, oc)], cor.at[4 * i + j], 4 * i + j, 4 * i + j, device(x, y, z, oc))
                    pltpu.make_async_copy(ins[k].at[block(px, py, b, c)], acc.at[4 * i + j], lsem.at[k, 4 * i + j]).start()

    begin([k for k in active if modes[k] == CROSS])

    def spots(k, i):
        b, j = i // 2, i % 2
        if modes[k] == PAIR_Y:
            return (j, y, b), (j, oy, b)
        return (x, j, b), (ox, j, b)

    for k in paired:
        acc, cor = bufs[k]
        for i in range(8):
            for s, (px, py, b) in enumerate(spots(k, i)):
                send(None, k, ins[k].at[block(px, py, b, oc)], cor.at[2 * i + s], 2 * i + s, 2 * i + s, device(x, y, z, oc))
                pltpu.make_async_copy(ins[k].at[block(px, py, b, c)], acc.at[2 * i + s], lsem.at[k, 2 * i + s]).start()
    def loaded(k, i, j):
        acc, cor = bufs[k][:2]
        pltpu.make_async_copy(ins[k].at[0], acc.at[4 * i + j], lsem.at[k, 4 * i + j]).wait()
        arrived(None, k, cor.at[4 * i + j], 4 * i + j)

    for k in paired:
        acc, cor = bufs[k]

        def join(i, carry, k=k, acc=acc, cor=cor):
            for s in range(2):
                at = 2 * i + s
                pltpu.make_async_copy(ins[k].at[0], acc.at[at], lsem.at[k, at]).wait()
                arrived(None, k, cor.at[at], at)
                add_up(seconds[k][s].at[i], (acc.at[at], cor.at[at]))
            return carry

        lax.fori_loop(0, 8, join, 0)

    def fetched(k, i, j):
        acc, rec = bufs[k][:2]
        pltpu.make_async_copy(ins[k].at[0], acc.at[2 * i + j], lsem.at[k, 2 * i + j]).wait()
        pltpu.make_async_copy(ins[k].at[0], rec.at[2 * i + j], lsem.at[k, 8 + 2 * i + j]).wait()

    def ahead(k, i, b):
        acc, rec, side = bufs[k][:3]
        fetched(k, i, 0)
        add_up(acc.at[2 * i], (acc.at[2 * i], rec.at[2 * i]))
        peer = device(x, oy, z, c) if modes[k] == REST_X else device(ox, y, z, c)
        send(None, k, acc.at[2 * i], side.at[i], 16 + i, 16 + i, peer)

    def corner(k, i, b):
        acc, cor, side = bufs[k][:3]
        loaded(k, i, 0)
        add_up(acc.at[4 * i], (acc.at[4 * i], cor.at[4 * i]))
        first, second = halves(acc.at[4 * i])
        send(None, k, first, halves(side.at[i])[0], 16 + i, 16 + i, device(x, oy, z, c))
        if second is not None:
            send(None, k, second, halves(side.at[4 + i])[1], 20 + i, 20 + i, device(ox, y, z, c))

    def beside(k, i, b):
        acc, cor, side = bufs[k][:3]
        loaded(k, i, 1)
        add_up(acc.at[4 * i + 1], (acc.at[4 * i + 1], cor.at[4 * i + 1]))
        part = halves(side.at[i])[0]
        arrived(None, k, part, 16 + i)
        mine = halves(acc.at[4 * i + 1])[0]
        add_up(mine, (mine, part))
        send(None, k, acc.at[4 * i + 1], side.at[8 + i], 24 + i, 24 + i, device(ox, y, z, c))
        loaded(k, i, 2)
        add_up(acc.at[4 * i + 2], (acc.at[4 * i + 2], cor.at[4 * i + 2]))
        part = halves(side.at[4 + i])[1]
        if part is not None:
            arrived(None, k, part, 20 + i)
            mine = halves(acc.at[4 * i + 2])[1]
            add_up(mine, (mine, part))
        send(None, k, acc.at[4 * i + 2], side.at[12 + i], 28 + i, 28 + i, device(x, oy, z, c))

    def settle(k, i, b):
        side = bufs[k][2]
        if k in rest:
            acc, rec = bufs[k][:2]
            fetched(k, i, 1)
            arrived(None, k, side.at[i], 16 + i)
            own = acc.at[2 * i + 1]
            terms = (own, rec.at[2 * i + 1], side.at[i])
        else:
            acc, cor = bufs[k][:2]
            loaded(k, i, 3)
            own = acc.at[4 * i + 3]
            arrived(None, k, side.at[8 + i], 24 + i)
            arrived(None, k, side.at[12 + i], 28 + i)
            terms = (own, cor.at[4 * i + 3], side.at[8 + i], side.at[12 + i])
        if modes[k] == CROSS:
            add_up(own, terms)
            if i < ZN - 1:
                send(None, k, own, outs[k].at[z], 32 + i, 32 + z, device(x, y, b, c))
            else:
                pltpu.make_async_copy(own, outs[k].at[z], lsem.at[k, 16]).start()
            return
        chain = bufs[k][3]
        if i == ZN - 1:
            add_up(outs[k], terms)

            def lower(k=k, chain=chain):
                arrived(None, k, chain.at[z], 32 + z)
                add_up(outs[k], (outs[k], chain.at[z]))

            def upper(k=k, chain=chain):
                arrived(None, k, chain.at[4 + z], 36 + z)
                add_up(outs[k], (outs[k], chain.at[4 + z]))

            pl.when(z > 0)(lower)
            pl.when(z < ZN - 1)(upper)
        else:
            add_up(own, terms)
            below = both(b > z, z > 0)
            above = both(b < z, z < ZN - 1)

            def lower(k=k, chain=chain, own=own, b=b):
                arrived(None, k, chain.at[b], 32 + b)
                add_up(own, (own, chain.at[b]))

            def upper(k=k, chain=chain, own=own, b=b):
                arrived(None, k, chain.at[4 + b], 36 + b)
                add_up(own, (own, chain.at[4 + b]))

            pl.when(below)(lower)
            pl.when(above)(upper)
            send(b > z, k, own, chain.at[b], 32 + i, 32 + b, device(x, y, lax.rem(z + 1, ZN), c))
            send(b < z, k, own, chain.at[4 + b], 32 + i, 36 + b, device(x, y, lax.rem(z + ZN - 1, ZN), c))

    crossed = [k for k in active if modes[k] == CROSS]
    plain = [k for k in active if modes[k] != CROSS]
    stages = [[(ahead, rest)], [(corner, crossed)], [(corner, plain)]]
    stages = stages + [[(settle, rest), (beside, crossed)], [(settle, crossed), (beside, plain)], [(settle, plain)]]
    for stage in stages:
        for i, b in enumerate(order):
            for fn, ks in stage:
                for k in ks:
                    fn(k, i, b)
        if stage is stages[0]:
            begin(plain)
    for k, mode in enumerate(modes):
        if mode not in (SWAP, CROSS):
            continue
        for d in range(1, ZN):
            frm = lax.rem(z + d, ZN)
            arrived(None, k, outs[k].at[frm], frm if mode == SWAP else 32 + frm)
        if mode == SWAP:
            pltpu.make_async_copy(ins[k].at[z], outs[k].at[z], lsem.at[k, 0]).wait()
        else:
            pltpu.make_async_copy(bufs[k][0].at[15], outs[k].at[z], lsem.at[k, 16]).wait()
    for cond, args in sent:
        when(cond, lambda args=args: copy(*args).wait_send())


def reduce(arrays, modes, collective_id):
    shapes, specs, scratch, operands, inputs = [], [], [], [], []
    anywhere, local = pl.BlockSpec(memory_space=pl.ANY), pl.BlockSpec(memory_space=pltpu.VMEM)
    for a, mode in zip(arrays, modes):
        operands = operands + (list(a) if mode in REST + MADE else [a])
        inputs = inputs + [local if mode in MADE + (SWAP,) else anywhere] * (2 if mode in REST + MADE else 1)
        if mode in MADE:
            tall = a[0].shape[1] if mode == TURNED_PRODUCT else a[0].shape[0]
            shape = (BLOCKS, tall // BLOCKS, a[1].shape[1])
        else:
            a = a[0] if mode in REST else a
            shape = a.shape
        rows, cols = shape[1:]
        dtype = jnp.bfloat16 if mode in MADE else a.dtype
        sizes = {SWAP: (), CROSS: (16, 16, 16), REDUCE: (16, 16, 16, 8)}
        sizes.update({PAIR_X: (16, 16), PAIR_Y: (16, 16), REST_X: (8, 8, 4, 8), REST_Y: (8, 8, 4, 8)})
        sizes = sizes[REDUCE] + (BLOCKS,) if mode in MADE else sizes[mode]
        scratch = scratch + [pltpu.VMEM((size, rows, cols), dtype) for size in sizes]
        if mode == SWAP:
            shapes.append(jax.ShapeDtypeStruct(a.shape, a.dtype))
            specs.append(anywhere)
        elif mode in PAIR:
            shapes = shapes + [jax.ShapeDtypeStruct((8, rows, cols), a.dtype)] * 2
            specs = specs + [local] * 2
        elif mode == CROSS:
            shapes.append(jax.ShapeDtypeStruct((ZN, rows, cols), a.dtype))
            specs.append(anywhere)
        else:
            shapes.append(jax.ShapeDtypeStruct((rows, cols), jnp.float32))
            specs.append(local)
    n = len(arrays)
    return pl.pallas_call(
        functools.partial(reduce_kernel, tuple(modes)),
        out_shape=shapes,
        in_specs=inputs,
        out_specs=specs,
        scratch_shapes=[
            pltpu.SemaphoreType.DMA((n, 17)),
            pltpu.SemaphoreType.DMA((n, SENDS)),
            pltpu.SemaphoreType.DMA((n, SENDS)),
        ]
        + scratch,
        compiler_params=pltpu.CompilerParams(
            collective_id=collective_id, has_side_effects=True, vmem_limit_bytes=67043328
        ),
    )(*operands)


HEAD = 64
GROUP = 3
TILE = 512
WIDE = 1024
EDGE = 128
SPAN = 4096
FAR = 1 << 30


def longest(lengths):
    begin, best, at = jnp.int32(0), lengths[0], jnp.int32(0)
    for j in range(lengths.shape[0]):
        length = lengths[j]
        at = jnp.where(length > best, begin, at)
        best = jnp.maximum(best, length)
        begin = begin + length
    return at, at + best


def lane_slots(lengths, count):
    x, y, z, c = place()
    lane = lax.broadcasted_iota(jnp.int32, (1, count), 1)
    begin, end = longest(lengths)
    spots = [block(x, y, b, c) * count + lane for b in range(ZN)]
    slots, before = [], jnp.zeros((1, count), jnp.int32)
    for b in range(ZN):
        big = jnp.logical_and(spots[b] >= begin, spots[b] < end)
        slots.append(jnp.where(big, before, ZN // 2 + b - before))
        before = before + big.astype(jnp.int32)
    return begin, end, spots, slots


def pick(slots, slot, parts):
    chosen = parts[-1]
    for b in range(len(parts) - 2, -1, -1):
        chosen = jnp.where(slots[b] == slot, parts[b], chosen)
    return chosen


def bounds_of(lengths, spot):
    low, high = jnp.zeros_like(spot), jnp.full_like(spot, FAR)
    begin = jnp.int32(0)
    for j in range(lengths.shape[0]):
        end = begin + lengths[j]
        low = jnp.where(spot >= begin, begin, low)
        high = jnp.where(spot < end, jnp.minimum(high, end), high)
        begin = end
    return low, high


def walk(big, begin, end, low, high, step, init):
    if big:
        base = begin // EDGE * EDGE

        def body(i, carry):
            at = pl.multiple_of(base + i * WIDE, EDGE)
            return step(at, WIDE, False, carry)

        carry = step(pl.multiple_of(base, EDGE), WIDE, True, init)
        carry = lax.fori_loop(1, SPAN // WIDE, body, carry)
        return lax.cond(
            begin > base,
            lambda c: step(pl.multiple_of(base + SPAN, EDGE), EDGE, True, c),
            lambda c: c,
            carry,
        )
    first = jnp.min(low) // TILE
    stop = (jnp.max(high) + TILE - 1) // TILE
    hole_first = jnp.maximum((begin + TILE - 1) // TILE, first)
    hole = jnp.maximum(jnp.minimum(end // TILE, stop) - hole_first, 0)

    def body(i, carry):
        tile = first + i
        tile = jnp.where(jnp.logical_and(hole > 0, tile >= hole_first), tile + hole, tile)
        return step(pl.multiple_of(tile * TILE, TILE), TILE, True, carry)

    return lax.fori_loop(0, stop - first - hole, body, init)


def keys_in(first, size, low, high):
    at = first + lax.broadcasted_iota(jnp.int32, (size, low.shape[1]), 0)
    return jnp.logical_and(at >= low, at < high)


def dot(a, b):
    return jnp.dot(a, b, preferred_element_type=jnp.float32)


def pad_heads(rows, h, slots):
    part = rows[h * HEAD : (h + 1) * HEAD]
    zero = jnp.zeros_like(part)
    return jnp.concatenate([part if s == h else zero for s in slots], axis=0)


Q_SLOTS = (0, 1, 2, -1)
V_SLOTS = (-1, 2, 0, 1)


def forward_kernel(lengths, qt, kv, low_out, out, lse_out, qm, acc, qs, os, ls):
    count = qt.shape[2]
    begin, end, spots, slots = lane_slots(lengths, count)
    for s in range(ZN):
        qs[s] = pick(slots, s, [qt[b] for b in range(ZN)])

    def one_block(big, s, carry):
        low, high = bounds_of(lengths, pick(slots, s, spots))
        rows = qs[s] * jnp.bfloat16(0.125)
        for h in range(GROUP):
            qm[h] = pad_heads(rows, h, Q_SLOTS)
        acc[...] = jnp.zeros_like(acc)

        def step(at, size, masked, stats):
            span = pl.ds(at, size)
            keys = kv[span, 0:256]
            values = kv[span, 128:384].T
            mask = keys_in(at, size, low, high) if masked else None
            fresh = []
            for h in range(GROUP):
                top, total = stats[2 * h], stats[2 * h + 1]
                scores = dot(keys, qm[h])
                if masked:
                    scores = jnp.where(mask, scores, -1e9)
                new_top = jnp.maximum(top, jnp.max(scores, axis=0, keepdims=True))
                shrink = jnp.exp(top - new_top)
                weights = jnp.exp(scores - new_top)
                total = total * shrink + jnp.sum(weights, axis=0, keepdims=True)
                row = V_SLOTS.index(h) * HEAD
                acc[h] = acc[h] * shrink + dot(values[row : row + HEAD], weights.astype(jnp.bfloat16))
                fresh = fresh + [new_top, total]
            return tuple(fresh)

        init = (jnp.full((1, count), -1e9, jnp.float32), jnp.zeros((1, count), jnp.float32)) * GROUP
        stats = walk(big, begin, end, low, high, step, init)
        for h in range(GROUP):
            top, total = stats[2 * h], stats[2 * h + 1]
            os[s, h * HEAD : (h + 1) * HEAD] = acc[h] / total
            ls[s, h : h + 1] = top + jnp.log(total)
        return carry

    lax.fori_loop(0, ZN // 2, functools.partial(one_block, True), 0)
    lax.fori_loop(ZN // 2, ZN, functools.partial(one_block, False), 0)
    for b in range(ZN):
        value = pick([jnp.full_like(slots[b], s) for s in range(ZN)], slots[b], [os[s] for s in range(ZN)])
        out[b] = value
        low_out[b] = value.astype(low_out.dtype)
        lse_out[b] = pick([jnp.full_like(slots[b], s) for s in range(ZN)], slots[b], [ls[s] for s in range(ZN)])


def attend(lengths, qt, kv):
    blocks, rows, count = qt.shape
    whole = pl.BlockSpec(memory_space=pltpu.VMEM)
    return pl.pallas_call(
        forward_kernel,
        out_shape=[
            jax.ShapeDtypeStruct(qt.shape, jnp.bfloat16),
            jax.ShapeDtypeStruct(qt.shape, jnp.float32),
            jax.ShapeDtypeStruct((blocks, 8, count), jnp.float32),
        ],
        in_specs=[pl.BlockSpec(memory_space=pltpu.SMEM), whole, whole],
        out_specs=[whole] * 3,
        scratch_shapes=[
            pltpu.VMEM((GROUP, 256, count), jnp.bfloat16),
            pltpu.VMEM((GROUP, HEAD, count), jnp.float32),
            pltpu.VMEM(qt.shape, jnp.bfloat16),
            pltpu.VMEM(qt.shape, jnp.float32),
            pltpu.VMEM((blocks, 8, count), jnp.float32),
        ],
        compiler_params=pltpu.CompilerParams(vmem_limit_bytes=67043328),
    )(lengths, qt, kv)


def backward_kernel(lengths, qt, kv, out, lse, dot_in, cosine, sine, dq_out, dkv_out, qmt, qm, dmt, dm, dq, acc, qs, ds, es, ls, dqs):
    count = qt.shape[2]
    tiles = kv.shape[0] // TILE

    def clear(tile, carry):
        acc[pl.ds(pl.multiple_of(tile * TILE, TILE), TILE), :] = jnp.zeros((TILE, acc.shape[1]), jnp.float32)
        return carry

    lax.fori_loop(0, tiles, clear, 0)

    begin, end, spots, slots = lane_slots(lengths, count)
    for b in range(ZN):
        product_rows = dot_in[b].astype(jnp.float32) * out[b]
        for h in range(GROUP):
            es[b, h : h + 1] = jnp.sum(product_rows[h * HEAD : (h + 1) * HEAD], axis=0, keepdims=True)
    for s in range(ZN):
        qs[s] = pick(slots, s, [qt[b] for b in range(ZN)])
        ds[s] = pick(slots, s, [dot_in[b] for b in range(ZN)])
        ls[s] = pick(slots, s, [lse[b] for b in range(ZN)])
    picked = [pick(slots, s, [es[b] for b in range(ZN)]) for s in range(ZN)]
    for s in range(ZN):
        es[s] = picked[s]

    def one_block(big, s, carry):
        low, high = bounds_of(lengths, pick(slots, s, spots))
        rows = qs[s] * jnp.bfloat16(0.125)
        grads = ds[s]
        deltas = [es[s, h : h + 1] for h in range(GROUP)]
        levels = [ls[s, h : h + 1] for h in range(GROUP)]
        for h in range(GROUP):
            padded = pad_heads(rows, h, Q_SLOTS)
            qmt[h] = padded
            qm[h * count : (h + 1) * count] = padded.T
            padded = pad_heads(grads, h, V_SLOTS)
            dmt[h] = padded
            dm[h * count : (h + 1) * count] = padded.T
        dq[...] = jnp.zeros_like(dq)

        def step(at, size, masked, inner):
            span = pl.ds(at, size)
            keys = kv[span, 0:256]
            values = kv[span, 128:384]
            turned = keys.T
            mask = keys_in(at, size, low, high) if masked else None
            probs, slopes = [], []
            for h in range(GROUP):
                weights = jnp.exp(dot(keys, qmt[h]) - levels[h])
                if masked:
                    weights = jnp.where(mask, weights, 0.0)
                slope = (weights * (dot(values, dmt[h]) - deltas[h])).astype(jnp.bfloat16)
                dq[h] += dot(turned[h * HEAD : (h + 1) * HEAD], slope)
                probs.append(weights.astype(jnp.bfloat16))
                slopes.append(slope)
            dv = dot(jnp.concatenate(probs, axis=1), dm[...])
            dk = dot(jnp.concatenate(slopes, axis=1), qm[...])
            acc[span, 0:128] += dk[:, :128]
            acc[span, 128:256] += dk[:, 128:] + dv[:, :128]
            acc[span, 256:384] += dv[:, 128:]
            return inner

        walk(big, begin, end, low, high, step, 0)
        for h in range(GROUP):
            dqs[s, h * HEAD : (h + 1) * HEAD] = dq[h] * 0.125
        return carry

    lax.fori_loop(0, ZN // 2, functools.partial(one_block, True), 0)
    lax.fori_loop(ZN // 2, ZN, functools.partial(one_block, False), 0)
    half = HEAD // 2
    for b in range(ZN):
        back = pick([jnp.full_like(slots[b], s) for s in range(ZN)], slots[b], [dqs[s] for s in range(ZN)])
        for h in range(GROUP):
            at = h * HEAD
            w1, w2 = back[at : at + half], back[at + half : at + HEAD]
            dq_out[b, at : at + half] = (w1 * cosine[b] + w2 * sine[b]).astype(dq_out.dtype)
            dq_out[b, at + half : at + HEAD] = (w2 * cosine[b] - w1 * sine[b]).astype(dq_out.dtype)

    def finish(tile, carry):
        span = pl.ds(pl.multiple_of(tile * TILE, TILE), TILE)
        dkv_out[span, :] = acc[span, :].astype(dkv_out.dtype)
        return carry

    lax.fori_loop(0, tiles, finish, 0)


def attend_back(lengths, qt, kv, out, lse, dots, cosine, sine):
    blocks, rows, count = qt.shape
    whole = pl.BlockSpec(memory_space=pltpu.VMEM)
    return pl.pallas_call(
        backward_kernel,
        out_shape=[
            jax.ShapeDtypeStruct(qt.shape, jnp.bfloat16),
            jax.ShapeDtypeStruct(kv.shape, jnp.bfloat16),
        ],
        in_specs=[pl.BlockSpec(memory_space=pltpu.SMEM)] + [whole] * 7,
        out_specs=[whole] * 2,
        scratch_shapes=[
            pltpu.VMEM((GROUP, 256, count), jnp.bfloat16),
            pltpu.VMEM((GROUP * count, 256), jnp.bfloat16),
            pltpu.VMEM((GROUP, 256, count), jnp.bfloat16),
            pltpu.VMEM((GROUP * count, 256), jnp.bfloat16),
            pltpu.VMEM((GROUP, HEAD, count), jnp.float32),
            pltpu.VMEM(kv.shape, jnp.float32),
            pltpu.VMEM(qt.shape, jnp.bfloat16),
            pltpu.VMEM(qt.shape, jnp.bfloat16),
            pltpu.VMEM((blocks, 8, count), jnp.float32),
            pltpu.VMEM((blocks, 8, count), jnp.float32),
            pltpu.VMEM(qt.shape, jnp.float32),
        ],
        compiler_params=pltpu.CompilerParams(vmem_limit_bytes=67043328),
    )(lengths, qt, kv, out, lse, dots, cosine, sine)


KV_SLOTS = (0, 1, 2, 5, 3, 4)


def turn(rows, cosine, sine):
    first, second = rows[:, 0], rows[:, 1]
    return jnp.stack([first * cosine - second * sine, second * cosine + first * sine], axis=1)


def turn_back(rows, cosine, sine):
    first, second = rows[:, 0], rows[:, 1]
    return jnp.stack([first * cosine + second * sine, second * cosine - first * sine], axis=1)


def tables(lengths, first, count):
    starts = jnp.cumsum(lengths) - lengths
    position = first[:, None] + jnp.arange(count, dtype=jnp.int32)[None, :]
    begun = position[..., None] >= starts
    offsets = position - jnp.max(jnp.where(begun, starts, 0), axis=-1)
    half = HEAD // 2
    frequency = rope_base ** (-(jnp.arange(half, dtype=jnp.float32) * 2.0) / HEAD)
    angles = offsets.astype(jnp.float32)[:, None, :] * frequency[None, :, None]
    return jnp.cos(angles), jnp.sin(angles)


def norm_back(upstream, scaled, inv_std, gain_vec):
    weighted = upstream * gain_vec
    inner = (
        weighted
        - jnp.mean(weighted, axis=-1, keepdims=True)
        - scaled * jnp.mean(weighted * scaled, axis=-1, keepdims=True)
    )
    sums = [jnp.sum(upstream * scaled, axis=0, keepdims=True), jnp.sum(upstream, axis=0, keepdims=True)]
    return inv_std * inner, sums


def contract(left, right, dims):
    return lax.dot_general(left, right, (dims, ((), ())), preferred_element_type=jnp.float32)


def copies_kernel(*refs):
    n = len(refs) // 3
    ins, outs, bufs, sems = refs[:n], refs[n : 2 * n], refs[2 * n : 3 * n], refs[3 * n]
    loads = [pltpu.make_async_copy(ins[k], bufs[k], sems.at[k]) for k in range(n)]
    stores = [pltpu.make_async_copy(bufs[k], outs[k], sems.at[n + k]) for k in range(n)]
    for load in loads:
        load.start()
    for load, store in zip(loads, stores):
        load.wait()
        store.start()
    for store in stores:
        store.wait()


def copies(arrays):
    n = len(arrays)
    anywhere = pl.BlockSpec(memory_space=pl.ANY)
    return pl.pallas_call(
        copies_kernel,
        out_shape=[jax.ShapeDtypeStruct(a.shape, a.dtype) for a in arrays],
        in_specs=[anywhere] * n,
        out_specs=[anywhere] * n,
        scratch_shapes=[pltpu.VMEM(a.shape, a.dtype) for a in arrays] + [pltpu.SemaphoreType.DMA((2 * n,))],
    )(*arrays)


def local_grid(
    tokens,
    qkv_weight,
    out_weight,
    gate_weight,
    up_weight,
    down_weight,
    first_gain,
    first_bias,
    second_gain,
    second_bias,
    lengths,
    cotangent,
):
    bf16 = jnp.bfloat16
    rows, width = tokens.shape
    share = first_gain.shape[0]
    heads = width // HEAD
    half = HEAD // 2
    x, y, z, c = place()
    spots = [(px, py, pz, pc) for pz in range(ZN) for py in range(YN) for pc in range(CN) for px in range(XN)]
    over_x = [(block(*p), block(1 - p[0], *p[1:])) for p in spots]
    over_y = [(block(*p), block(p[0], 1 - p[1], *p[2:])) for p in spots]
    small = jnp.stack([first_gain, first_bias, second_gain, second_bias])
    small = jnp.pad(small, ((0, 4), (0, 128 - share)))
    hidden_width = gate_weight.shape[1]

    (qkv_blocks,) = gather([qkv_weight], [BCAST], 1)
    qkv_full = qkv_blocks.reshape(width, 3 * width)
    turned = jnp.stack([block(x, y, b, c) for b in range(ZN)]) * rows
    cos_all, sin_all = tables(lengths, turned, rows)
    cosine = lax.dynamic_index_in_dim(cos_all, z, 0, keepdims=False)
    sine = lax.dynamic_index_in_dim(sin_all, z, 0, keepdims=False)

    raw = contract(qkv_full, tokens, ((0,), (1,))).astype(bf16)
    raw = raw.reshape(3, heads, 2, half, rows)
    queries = turn(raw[0].astype(jnp.float32), cosine, sine).astype(bf16)
    keys = turn(raw[1].astype(jnp.float32), cosine, sine).astype(bf16)
    queries = queries.reshape(ZN, GROUP * HEAD, rows)
    pairs = jnp.concatenate(
        [keys.reshape(ZN, GROUP, HEAD, rows), raw[2].reshape(ZN, GROUP, HEAD, rows)], axis=1
    )
    pairs = jnp.concatenate([pairs[:, s : s + 1] for s in KV_SLOTS], axis=1)
    pairs = jnp.swapaxes(pairs.reshape(ZN, 2 * GROUP * HEAD, rows), 1, 2)

    pairs_all, queries, out_full, down_full, small, gate_part, up_part = gather(
        [pairs, queries, out_weight, down_weight, small, gate_weight, up_weight],
        [CROSS, SWAP, BCAST, BCAST, BCAST, BY_X, BY_Y],
        2,
    )
    out_full = out_full.reshape(width, width)
    gate_rest = lax.ppermute(gate_part, ("cp", "hd"), over_y)
    up_rest = lax.ppermute(up_part, ("cp", "hd"), over_x)
    down_full = down_full.reshape(hidden_width, width)
    small = jnp.swapaxes(small[:, :4, :share], 0, 1).astype(jnp.float32).reshape(4, width)
    small = lax.optimization_barrier(small)
    gain_one, bias_one, gain_two, bias_two = [small[i] for i in range(4)]
    pairs_all = pairs_all.reshape(-1, 2 * GROUP * HEAD)
    low, attended, lse = attend(lengths, queries, pairs_all)
    low, gate_full, up_full = gather(
        [low, (gate_part, gate_rest), (up_part, up_rest)], [SWAP, REST_Y, REST_X], 3
    )
    gate_full = gate_full.reshape(width, hidden_width)
    up_full = up_full.reshape(width, hidden_width)
    low = low.reshape(width, rows)

    attn_out = contract(low, out_full, ((0,), (0,)))
    first, scaled_one, inv_one = normalize(tokens.astype(jnp.float32) + attn_out, gain_one, bias_one)
    first_low = first.astype(bf16)
    gate_proj = product(first_low, gate_full)
    up_proj = product(first_low, up_full)
    sigmoid_gate = jax.nn.sigmoid(gate_proj)
    silu_gate = gate_proj * sigmoid_gate
    hidden = (silu_gate * up_proj).astype(bf16)
    branch = product(hidden, down_full)
    second, scaled_two, inv_two = normalize(first + branch, gain_two, bias_two)
    layer_out = second.astype(bf16)

    upstream = cotangent.astype(jnp.float32)
    dz_two, sums_two = norm_back(upstream, scaled_two, inv_two, gain_two)
    dz_two_low = dz_two.astype(bf16)
    hidden_grad = contract(dz_two_low, down_full, ((1,), (1,)))
    gate_back = (
        hidden_grad * up_proj * sigmoid_gate * (1.0 + gate_proj * (1.0 - sigmoid_gate))
    ).astype(bf16)
    up_back = (hidden_grad * silu_gate).astype(bf16)
    gate_sum = contract(first_low, gate_back, ((0,), (0,))).astype(bf16)
    up_sum = contract(first_low, up_back, ((0,), (0,))).astype(bf16)
    first_back = (
        dz_two + contract(gate_back, gate_full, ((1,), (1,))) + contract(up_back, up_full, ((1,), (1,)))
    )
    dz_one, sums_one = norm_back(first_back, scaled_one, inv_one, gain_one)
    dz_one_low = dz_one.astype(bf16)
    attended_back = contract(out_full, dz_one_low, ((1,), (1,))).astype(bf16)
    attended_back, gate_keep, gate_send, up_keep, up_send = reduce(
        [
            attended_back.reshape(ZN, GROUP * HEAD, rows),
            gate_sum.reshape((BLOCKS,) + gate_weight.shape),
            up_sum.reshape((BLOCKS,) + up_weight.shape),
        ],
        [SWAP, PAIR_Y, PAIR_X],
        4,
    )
    gate_rest = lax.ppermute(gate_send, ("cp", "hd"), over_y)
    up_rest = lax.ppermute(up_send, ("cp", "hd"), over_x)

    query_back, pair_back = attend_back(
        lengths, queries, pairs_all, attended, lse, attended_back, cos_all, sin_all
    )
    small_sum = lax.optimization_barrier(jnp.concatenate(sums_one + sums_two, axis=0))
    small_sum = jnp.swapaxes(small_sum.reshape(4, BLOCKS, share), 0, 1)
    small_sum = jnp.pad(small_sum, ((0, 0), (0, 4), (0, 128 - share)))
    pair_back, query_back, out_grad, down_grad, small_grad, gate_grad, up_grad = reduce(
        [
            pair_back.reshape(BLOCKS, rows, 2 * GROUP * HEAD),
            query_back,
            (low, dz_one_low),
            (hidden, dz_two_low),
            small_sum,
            (gate_keep, gate_rest),
            (up_keep, up_rest),
        ],
        [CROSS, SWAP, PRODUCT, TURNED_PRODUCT, REDUCE, REST_Y, REST_X],
        5,
    )
    pair_back = jnp.swapaxes(pair_back, 1, 2).reshape(ZN, 2 * GROUP, HEAD, rows)
    pair_back = [pair_back[:, KV_SLOTS.index(s)] for s in range(2 * GROUP)]
    key_back = jnp.stack(pair_back[:GROUP], axis=1).reshape(heads, 2, half, rows)
    key_back = turn_back(key_back.astype(jnp.float32), cosine, sine).astype(bf16)
    value_back = jnp.stack(pair_back[GROUP:], axis=1)
    raw_back = jnp.concatenate(
        [
            query_back.reshape(width, rows),
            key_back.reshape(width, rows),
            value_back.reshape(width, rows),
        ],
        axis=0,
    )
    qkv_sum = contract(tokens, raw_back, ((0,), (1,))).astype(bf16)
    tokens_grad = (dz_one + contract(raw_back, qkv_full, ((0,), (1,)))).astype(bf16)
    (qkv_grad,) = reduce([qkv_sum.reshape(BLOCKS, share, 3 * width)], [REDUCE], 6)
    qkv_grad, out_grad, gate_grad, up_grad, down_grad = copies([qkv_grad, out_grad, gate_grad, up_grad, down_grad])
    return (
        layer_out,
        tokens_grad,
        qkv_grad,
        out_grad,
        gate_grad,
        up_grad,
        down_grad,
        small_grad[0, :share],
        small_grad[1, :share],
        small_grad[2, :share],
        small_grad[3, :share],
    )


def solution(mesh):
    rows = P(("cp", "hd"), None)
    line = P(("cp", "hd"))
    local = local_grid if (mesh.shape["cp"], mesh.shape["hd"]) == (ZN * YN * CN, XN) else local_any
    return jax.shard_map(
        local,
        mesh=mesh,
        in_specs=(rows,) * 6 + (line,) * 4 + (P(), rows),
        out_specs=(rows,) * 7 + (line,) * 4,
        check_vma=False,
    )
```

```python
import functools

import jax
import jax.numpy as jnp
from jax import lax
from jax.experimental import pallas as pl
from jax.experimental.pallas import tpu as pltpu
from jax.sharding import PartitionSpec as P

HD = 64
REACH = 8


rope_base = 1000.0
norm_eps = 1e-12
score_scale = 0.125
masked_score = -1000000000.0


def shifted(block, axis, distance):
    devices = range(lax.axis_size(axis))
    route = [(i - distance, i) for i in devices if i - distance in devices]
    return lax.ppermute(block, axis, route)


def doc_layout(lengths, first_row, row_count):
    starts = jnp.cumsum(lengths) - lengths
    position = first_row + jnp.arange(row_count, dtype=jnp.int32)
    at_or_after = position[:, None] >= starts[None, :]
    doc_ids = jnp.sum(at_or_after.astype(jnp.int32), axis=1) - 1
    doc_begin = jnp.max(jnp.where(at_or_after, starts[None, :], 0), axis=1)
    return (doc_ids, position - doc_begin)


def rope_tables(offsets, head_size):
    half_size = head_size // 2
    frequency = rope_base ** (-(jnp.arange(half_size, dtype=jnp.float32) * 2.0) / head_size)
    angles = offsets.astype(jnp.float32)[:, None] * frequency[None, :]
    return (jnp.cos(angles), jnp.sin(angles))


def rotate(values, cosine, sine):
    half_size = values.shape[-1] // 2
    first_half = values[..., :half_size]
    second_half = values[..., half_size:]
    cos_rows = cosine[:, None, :]
    sin_rows = sine[:, None, :]
    return jnp.concatenate(
        [
            first_half * cos_rows - second_half * sin_rows,
            second_half * cos_rows + first_half * sin_rows,
        ],
        axis=-1,
    )


def rotate_back(grads, cosine, sine):
    half_size = grads.shape[-1] // 2
    first_half = grads[..., :half_size]
    second_half = grads[..., half_size:]
    cos_rows = cosine[:, None, :]
    sin_rows = sine[:, None, :]
    return jnp.concatenate(
        [
            first_half * cos_rows + second_half * sin_rows,
            second_half * cos_rows - first_half * sin_rows,
        ],
        axis=-1,
    )


def normalize(hidden_in, gain_vec, bias_vec):
    average = jnp.mean(hidden_in, axis=-1, keepdims=True)
    centered = hidden_in - average
    variance = jnp.mean(centered * centered, axis=-1, keepdims=True)
    inv_std = lax.rsqrt(variance + norm_eps)
    scaled = centered * inv_std
    return (scaled * gain_vec + bias_vec, scaled, inv_std)


def normalize_back(upstream, scaled, inv_std, gain_vec):
    weighted = upstream * gain_vec
    inner = (
        weighted
        - jnp.mean(weighted, axis=-1, keepdims=True)
        - scaled * jnp.mean(weighted * scaled, axis=-1, keepdims=True)
    )
    return (inv_std * inner, jnp.sum(upstream * scaled, axis=0), jnp.sum(upstream, axis=0))


def product(left, right):
    return jnp.dot(left, right, preferred_element_type=jnp.float32)


def local_any(
    tokens,
    qkv_weight,
    out_weight,
    gate_weight,
    up_weight,
    down_weight,
    first_gain,
    first_bias,
    second_gain,
    second_bias,
    doc_lengths,
    cotangent,
):
    rows_here = tokens.shape[0]
    model_width = tokens.shape[1]
    hd_count = lax.axis_size("hd")
    cp_count = lax.axis_size("cp")
    cp_index = lax.axis_index("cp")
    block_rows = rows_here * hd_count
    local_width = model_width // hd_count
    local_heads = local_width // HD
    shifts = [0]
    for distance in range(1, REACH + 1):
        shifts = shifts + [-distance, distance]
    shards = (
        qkv_weight,
        out_weight,
        gate_weight,
        up_weight,
        down_weight,
        first_gain,
        first_bias,
        second_gain,
        second_bias,
    )
    weights = (
        lax.all_gather(shards[0], ("cp", "hd"), axis=0, tiled=True),
        lax.all_gather(shards[1], ("cp", "hd"), axis=0, tiled=True),
        lax.all_gather(shards[2], ("cp", "hd"), axis=0, tiled=True),
        lax.all_gather(shards[3], ("cp", "hd"), axis=0, tiled=True),
        lax.all_gather(shards[4], ("cp", "hd"), axis=0, tiled=True),
        lax.all_gather(shards[5], ("cp", "hd"), axis=0, tiled=True),
        lax.all_gather(shards[6], ("cp", "hd"), axis=0, tiled=True),
        lax.all_gather(shards[7], ("cp", "hd"), axis=0, tiled=True),
        lax.all_gather(shards[8], ("cp", "hd"), axis=0, tiled=True),
    )
    (
        qkv_full,
        out_full,
        gate_full,
        up_full,
        down_full,
        gain_first,
        bias_first,
        gain_second,
        bias_second,
    ) = weights
    raw_rows = product(tokens, qkv_full).astype(jnp.bfloat16)
    grouped = lax.all_to_all(
        raw_rows.reshape(rows_here, 3, hd_count, local_width),
        "hd",
        split_axis=2,
        concat_axis=0,
        tiled=True,
    )
    grouped = grouped.reshape(block_rows, 3, local_width)
    query_docs, offsets = doc_layout(doc_lengths, cp_index * block_rows, block_rows)
    cosine, sine = rope_tables(offsets, HD)
    queries = rotate(
        grouped[:, 0].astype(jnp.float32).reshape(block_rows, local_heads, HD), cosine, sine
    ).astype(jnp.bfloat16)
    key_rows = rotate(
        grouped[:, 1].astype(jnp.float32).reshape(block_rows, local_heads, HD), cosine, sine
    ).astype(jnp.bfloat16)
    own_block = jnp.stack([key_rows.reshape(block_rows, local_width), grouped[:, 2]], axis=1)

    def key_docs(distance):
        source = cp_index - distance
        doc_ids, unused_offsets = doc_layout(doc_lengths, source * block_rows, block_rows)
        inside = jnp.logical_and(source >= 0, source < cp_count)
        return jnp.where(inside, doc_ids, -2)

    remote = [own_block] + [shifted(own_block, "cp", distance) for distance in shifts[1:]]
    masks = [query_docs[:, None] == key_docs(distance)[None, :] for distance in shifts]

    def scores_with(query_part, remote_block, key_mask):
        key_part = remote_block[:, 0].reshape(block_rows, local_heads, HD)
        raw_scores = (
            jnp.einsum("qhd,khd->hqk", query_part, key_part, preferred_element_type=jnp.float32)
            * score_scale
        )
        return jnp.where(key_mask[None], raw_scores, masked_score)

    def scores_for(remote_block, key_mask):
        return scores_with(queries, remote_block, key_mask)

    running_max = jnp.full((local_heads, block_rows), masked_score, jnp.float32)
    running_sum = jnp.zeros((local_heads, block_rows), jnp.float32)
    for remote_block, key_mask in zip(remote, masks):
        block_scores = scores_for(remote_block, key_mask)
        new_max = jnp.maximum(running_max, jnp.max(block_scores, axis=-1))
        running_sum = running_sum * jnp.exp(running_max - new_max) + jnp.sum(
            jnp.exp(block_scores - new_max[:, :, None]), axis=-1
        )
        running_max = new_max
    log_total = running_max + jnp.log(running_sum)
    attended = jnp.zeros((block_rows, local_heads, HD), jnp.float32)
    for remote_block, key_mask in zip(remote, masks):
        block_scores = scores_for(remote_block, key_mask)
        probs = jnp.exp(block_scores - log_total[:, :, None]).astype(jnp.bfloat16)
        value_part = remote_block[:, 1].reshape(block_rows, local_heads, HD)
        attended = attended + jnp.einsum(
            "hqk,khd->qhd", probs, value_part, preferred_element_type=jnp.float32
        )
    attended_send = attended.reshape(block_rows, 1, local_width).astype(jnp.bfloat16)
    attended_low = lax.all_to_all(
        attended_send, "hd", split_axis=0, concat_axis=1, tiled=True
    ).reshape(rows_here, model_width)
    gain_one = gain_first.astype(jnp.float32)
    gain_two = gain_second.astype(jnp.float32)
    attn_out = product(attended_low, out_full)
    first, scaled_one, inv_one = normalize(
        tokens.astype(jnp.float32) + attn_out, gain_one, bias_first.astype(jnp.float32)
    )
    first_low = first.astype(jnp.bfloat16)
    gate_proj = product(first_low, gate_full)
    up_proj = product(first_low, up_full)
    sigmoid_gate = jax.nn.sigmoid(gate_proj)
    silu_gate = gate_proj * sigmoid_gate
    hidden = (silu_gate * up_proj).astype(jnp.bfloat16)
    branch = product(hidden, down_full)
    second, scaled_two, inv_two = normalize(
        first + branch, gain_two, bias_second.astype(jnp.float32)
    )
    layer_out = second.astype(jnp.bfloat16)
    weights = (
        lax.all_gather(shards[0], ("cp", "hd"), axis=0, tiled=True),
        lax.all_gather(shards[1], ("cp", "hd"), axis=0, tiled=True),
        lax.all_gather(shards[2], ("cp", "hd"), axis=0, tiled=True),
        lax.all_gather(shards[3], ("cp", "hd"), axis=0, tiled=True),
        lax.all_gather(shards[4], ("cp", "hd"), axis=0, tiled=True),
        lax.all_gather(shards[5], ("cp", "hd"), axis=0, tiled=True),
        lax.all_gather(shards[6], ("cp", "hd"), axis=0, tiled=True),
        lax.all_gather(shards[7], ("cp", "hd"), axis=0, tiled=True),
        lax.all_gather(shards[8], ("cp", "hd"), axis=0, tiled=True),
    )
    (
        qkv_full,
        out_full,
        gate_full,
        up_full,
        down_full,
        gain_first,
        bias_first,
        gain_second,
        bias_second,
    ) = weights
    upstream = cotangent.astype(jnp.float32)
    dz_two, gain_two_grad, bias_two_grad = normalize_back(upstream, scaled_two, inv_two, gain_two)
    dz_two_low = dz_two.astype(jnp.bfloat16)
    down_sum = product(hidden.T, dz_two_low)
    hidden_grad = product(dz_two_low, down_full.T)
    gate_back = (
        hidden_grad * up_proj * sigmoid_gate * (1.0 + gate_proj * (1.0 - sigmoid_gate))
    ).astype(jnp.bfloat16)
    up_back = (hidden_grad * silu_gate).astype(jnp.bfloat16)
    gate_sum = product(first_low.T, gate_back)
    up_sum = product(first_low.T, up_back)
    first_back = dz_two + product(gate_back, gate_full.T) + product(up_back, up_full.T)
    dz_one, gain_one_grad, bias_one_grad = normalize_back(first_back, scaled_one, inv_one, gain_one)
    dz_one_low = dz_one.astype(jnp.bfloat16)
    out_sum = product(attended_low.T, dz_one_low)
    attended_back = product(dz_one_low, out_full.T).astype(jnp.bfloat16)
    heads_back = lax.all_to_all(
        attended_back.reshape(rows_here, hd_count, local_width),
        "hd",
        split_axis=1,
        concat_axis=0,
        tiled=True,
    )
    heads_back = heads_back.reshape(block_rows, local_heads, HD)
    delta = jnp.transpose(jnp.sum(heads_back.astype(jnp.float32) * attended, axis=-1))
    query_grad = jnp.zeros((block_rows, local_heads, HD), jnp.float32)
    pair_total = jnp.zeros((block_rows, 2, local_width), jnp.float32)
    remote = [own_block] + [shifted(own_block, "cp", distance) for distance in shifts[1:]]
    for distance, remote_block, key_mask in zip(shifts, remote, masks):
        pair_block_scores = scores_with(queries, remote_block, key_mask)
        pair_probs = jnp.exp(pair_block_scores - log_total[:, :, None])
        pair_key_part = remote_block[:, 0].reshape(block_rows, local_heads, HD)
        pair_value_part = remote_block[:, 1].reshape(block_rows, local_heads, HD)
        value_grad = jnp.einsum(
            "hqk,qhd->khd",
            pair_probs.astype(jnp.bfloat16),
            heads_back,
            preferred_element_type=jnp.float32,
        )
        prob_grad = jnp.einsum(
            "qhd,khd->hqk", heads_back, pair_value_part, preferred_element_type=jnp.float32
        )
        score_grad = (pair_probs * (prob_grad - delta[:, :, None])).astype(jnp.bfloat16)
        query_term = (
            jnp.einsum(
                "hqk,khd->qhd", score_grad, pair_key_part, preferred_element_type=jnp.float32
            )
            * score_scale
        )
        key_grad = (
            jnp.einsum("hqk,qhd->khd", score_grad, queries, preferred_element_type=jnp.float32)
            * score_scale
        )
        grad_pair = jnp.stack(
            [
                key_grad.reshape(block_rows, local_width),
                value_grad.reshape(block_rows, local_width),
            ],
            axis=1,
        )
        query_term, grad_pair = (query_term, grad_pair)
        query_grad = query_grad + query_term
        if distance == 0:
            pair_total = grad_pair
        else:
            pair_total = pair_total + shifted(
                grad_pair.astype(jnp.bfloat16), "cp", -distance
            ).astype(grad_pair.dtype)
    query_back = rotate_back(query_grad, cosine, sine).reshape(block_rows, local_width)
    key_back = rotate_back(
        pair_total[:, 0].reshape(block_rows, local_heads, HD), cosine, sine
    ).reshape(block_rows, local_width)
    raw_back = jnp.stack([query_back, key_back, pair_total[:, 1]], axis=1).astype(jnp.bfloat16)
    raw_back = lax.all_to_all(
        raw_back.reshape(block_rows, 3, 1, local_width),
        "hd",
        split_axis=0,
        concat_axis=2,
        tiled=True,
    )
    raw_back = raw_back.reshape(rows_here, 3 * model_width)
    qkv_sum = product(tokens.T, raw_back)
    tokens_grad = (dz_one + product(raw_back, qkv_full.T)).astype(jnp.bfloat16)
    summed = (
        lax.psum_scatter(qkv_sum, ("cp", "hd"), scatter_dimension=0, tiled=True),
        lax.psum_scatter(out_sum, ("cp", "hd"), scatter_dimension=0, tiled=True),
        lax.psum_scatter(gate_sum, ("cp", "hd"), scatter_dimension=0, tiled=True),
        lax.psum_scatter(up_sum, ("cp", "hd"), scatter_dimension=0, tiled=True),
        lax.psum_scatter(down_sum, ("cp", "hd"), scatter_dimension=0, tiled=True),
        lax.psum_scatter(gain_one_grad, ("cp", "hd"), scatter_dimension=0, tiled=True),
        lax.psum_scatter(bias_one_grad, ("cp", "hd"), scatter_dimension=0, tiled=True),
        lax.psum_scatter(gain_two_grad, ("cp", "hd"), scatter_dimension=0, tiled=True),
        lax.psum_scatter(bias_two_grad, ("cp", "hd"), scatter_dimension=0, tiled=True),
    )
    return (
        layer_out,
        tokens_grad,
        summed[0],
        summed[1],
        summed[2],
        summed[3],
        summed[4],
        summed[5],
        summed[6],
        summed[7],
        summed[8],
    )


MESH = pl.DeviceIdType.MESH
ZN, YN, CN, XN = 4, 2, 2, 2
BLOCKS = ZN * YN * CN * XN


def place():
    cp = lax.axis_index("cp")
    x = lax.axis_index("hd")
    return x, lax.rem(cp // CN, YN), cp // (YN * CN), lax.rem(cp, CN)


def device(x, y, z, c):
    return ((z * YN + y) * CN + c, x)


def block(x, y, z, c):
    return ((z * YN + y) * CN + c) * XN + x


def when(cond, fn):
    if cond is None:
        fn()
    else:
        pl.when(cond)(fn)


def both(a, b):
    if a is None:
        return b
    if b is None:
        return a
    return jnp.logical_and(a, b)


def halves(ref):
    rows, cols = ref.shape[-2:]
    if rows % 32 == 0:
        return ref.at[pl.ds(0, rows // 2)], ref.at[pl.ds(rows // 2, rows // 2)]
    if cols % 256 == 0:
        return ref.at[:, pl.ds(0, cols // 2)], ref.at[:, pl.ds(cols // 2, cols // 2)]
    return ref, None


def greet(x, y, z, c, far):
    barrier = pltpu.get_barrier_semaphore()
    for peer in (device(1 - x, y, z, c), device(x, 1 - y, z, c), device(x, y, z, 1 - c)):
        pl.semaphore_signal(barrier, inc=1, device_id=peer, device_id_type=MESH)
    count = 3
    if far:
        for k in range(1, ZN):
            peer = device(x, y, lax.rem(z + k, ZN), c)
            pl.semaphore_signal(barrier, inc=1, device_id=peer, device_id_type=MESH)
        count = count + ZN - 1
    else:
        pl.when(z > 0)(lambda: pl.semaphore_signal(barrier, inc=1, device_id=device(x, y, z - 1, c), device_id_type=MESH))
        pl.when(z < ZN - 1)(lambda: pl.semaphore_signal(barrier, inc=1, device_id=device(x, y, z + 1, c), device_id_type=MESH))
        count = count + (z > 0).astype(jnp.int32) + (z < ZN - 1).astype(jnp.int32)
    pl.semaphore_wait(barrier, count)


SENDS = 40
RECVS = 36


BCAST, BY_X, BY_Y, CROSS, SWAP, REST_X, REST_Y, PAIR_X, PAIR_Y, REDUCE, PRODUCT, TURNED_PRODUCT = range(12)
ONWARD, BESIDE, ACROSS = range(3)
CHAINED = (BCAST, BY_X, BY_Y)
REST = (REST_X, REST_Y)


def take(refs, counts):
    groups = []
    for count in counts:
        groups.append(refs[:count])
        refs = refs[count:]
    return groups, refs


SHORT_PLAN = [
    (fn, 0, d - lag)
    for d in range(1, ZN + 2)
    for lag, fn in enumerate((ONWARD, BESIDE, ACROSS))
    if (d > 0 if lag else d < ZN) and 0 <= d - lag < ZN
]
PLAN = [
    (ONWARD, 0, 1),
    (BESIDE, 0, 0),
    (BESIDE, 1, 0),
    (ACROSS, 0, 0),
    (BESIDE, 0, 1),
    (ONWARD, 1, 1),
    (ACROSS, 1, 0),
    (ACROSS, 0, 1),
    (ONWARD, 1, 2),
    (ONWARD, 1, 3),
    (BESIDE, 1, 1),
    (ONWARD, 0, 2),
    (BESIDE, 1, 2),
    (BESIDE, 1, 3),
    (BESIDE, 0, 2),
    (ACROSS, 1, 1),
    (ONWARD, 0, 3),
    (ACROSS, 1, 2),
    (ACROSS, 1, 3),
    (ACROSS, 0, 2),
    (BESIDE, 0, 3),
    (ACROSS, 0, 3),
]


def gather_kernel(modes, *refs):
    n = len(modes)
    ins, refs = take(refs, [2 if mode in REST else 1 for mode in modes])
    outs, (lsem, ssem, rsem), bufs = refs[:n], refs[n : n + 3], list(refs[n + 3 :])
    bufs = {k: bufs.pop(0) for k, mode in enumerate(modes) if mode in REST}
    pairs, ins = ins, [group[0] for group in ins]
    x, y, z, c = place()
    ox, oy, oc = 1 - x, 1 - y, 1 - c
    greet(x, y, z, c, any(m in (SWAP, CROSS) for m in modes))
    sent = []

    def copy(k, src, dst, s, r, peer):
        return pltpu.make_async_remote_copy(
            src_ref=src,
            dst_ref=dst,
            send_sem=ssem.at[k, s],
            recv_sem=rsem.at[k, r],
            device_id=peer,
            device_id_type=MESH,
        )

    def send(cond, *args):
        when(cond, lambda: copy(*args).start())
        sent.append((cond, args))

    def arrived(cond, k, ref, r):
        when(cond, lambda: copy(k, ref, ref, 0, r, device(ox, y, z, c)).wait_recv())

    locals_ = []

    def keep(k, i, mine, spot):
        pltpu.make_async_copy(mine, spot, lsem.at[k, i]).start()
        locals_.append((k, i, mine, spot))

    def at(k, px, py, b):
        if modes[k] == BY_X:
            return outs[k].at[2 * b + px]
        if modes[k] == BY_Y:
            return outs[k].at[2 * b + py]
        return outs[k].at[block(px, py, b, c)]

    for k, mode in enumerate(modes):
        if mode in CHAINED:
            keep(k, 0, ins[k], at(k, x, y, z))
        elif mode == SWAP:
            keep(k, 0, ins[k].at[z], outs[k].at[z])
        elif mode == CROSS:
            keep(k, 0, ins[k].at[z], outs[k].at[block(x, y, z, c)])

    def share_of(k, i, core):
        b, j = i % 8 // 2, i % 2
        if modes[k] == REST_Y:
            return block(j, oy if i >= 8 else y, b, core)
        return block(ox if i >= 8 else x, j, b, core)

    def spread(k, cond, b, src, up, down):
        here = at(k, x, y, b)
        if modes[k] in CHAINED:
            if up is not False:
                send(both(cond, up), k, src, here, b, b, device(x, y, lax.rem(z + 1, ZN), c))
            if down is not False:
                send(both(cond, down), k, src, here, 4 + b, b, device(x, y, lax.rem(z + ZN - 1, ZN), c))
        if modes[k] != BY_Y:
            send(cond, k, src, here, 8 + b, 4 + b, device(ox, y, z, c))
        if modes[k] != BY_X:
            send(cond, k, src, here, 16 + b, 12 + b, device(x, oy, z, c))
        if modes[k] not in (BY_X, BY_Y):
            send(cond, k, src, here, 24 + b, 20 + b, device(x, y, z, oc))

    def sides(k, cond, b):
        fx, fy = at(k, ox, y, b), at(k, x, oy, b)
        full = modes[k] not in (BY_X, BY_Y)
        if modes[k] != BY_Y:
            arrived(cond, k, fx, 4 + b)
            first, _ = halves(fx)
            if full:
                send(cond, k, first, first, 20 + b, 16 + b, device(x, oy, z, c))
                send(cond, k, fx, fx, 28 + b, 24 + b, device(x, y, z, oc))
        if modes[k] != BY_X:
            arrived(cond, k, fy, 12 + b)
            _, second = halves(fy)
            if full and second is not None:
                send(cond, k, second, second, 12 + b, 8 + b, device(ox, y, z, c))
            if full:
                send(cond, k, fy, fy, 32 + b, 28 + b, device(x, y, z, oc))

    def corner(k, cond, b):
        far = outs[k].at[block(ox, oy, b, c)]
        first, second = halves(far)
        arrived(cond, k, first, 16 + b)
        if second is not None:
            arrived(cond, k, second, 8 + b)
        send(cond, k, far, far, 36 + b, 32 + b, device(x, y, z, oc))

    def steps(distance):
        if distance == 0:
            return [(None, z)]
        return [(z >= distance, jnp.maximum(z - distance, 0)), (z + distance < ZN, jnp.minimum(z + distance, ZN - 1))]

    chained = [k for k, mode in enumerate(modes) if mode in CHAINED]
    crossed = [k for k, mode in enumerate(modes) if mode == CROSS]
    swapped = [k for k, mode in enumerate(modes) if mode == SWAP]

    def exchange(ks):
        for k in ks:
            for d in range(1, ZN):
                to = lax.rem(z + d, ZN)
                spot = outs[k].at[z] if modes[k] == SWAP else outs[k].at[block(x, y, z, c)]
                send(None, k, ins[k].at[to], spot, to, z, device(x, y, to, c))

    for k in chained:
        spread(k, None, z, ins[k], z < ZN - 1, z > 0)
    if not chained:
        exchange(swapped)
        swapped = []
    for k, mode in enumerate(modes):
        if mode in REST:
            for i in range(16):
                src = pairs[k][i // 8].at[i % 8]
                pltpu.make_async_copy(src, bufs[k].at[i], lsem.at[k, i]).start()
                send(None, k, src, outs[k].at[share_of(k, i, c)], i, i, device(x, y, z, oc))
    for k in crossed:
        spread(k, None, z, ins[k].at[z], False, False)
    exchange(crossed)

    def onward(ks, distance):
        for side, (cond, b) in enumerate(steps(distance)):
            for k in ks:
                here = at(k, x, y, b)
                arrived(cond, k, here, b)
                spread(k, cond, b, here, z < ZN - 1 if side == 0 else False, z > 0 if side == 1 else False)

    def beside(ks, distance):
        for cond, b in steps(distance):
            for k in ks:
                sides(k, cond, b)

    def across(ks, distance):
        for cond, b in steps(distance):
            for k in ks:
                if modes[k] in (BCAST, CROSS):
                    corner(k, cond, b)

    plan = PLAN if crossed else SHORT_PLAN
    for fn, ks, distance in plan if chained else ():
        fn = {ONWARD: onward, BESIDE: beside, ACROSS: across}[fn]
        fn(chained if ks == 0 else crossed, distance)
        if fn is onward and distance == ZN - 1 and ks == 0:
            exchange(swapped)
            swapped = []
    exchange(swapped)
    for k in bufs:
        for i in range(16):
            pltpu.make_async_copy(pairs[k][0].at[0], bufs[k].at[i], lsem.at[k, i]).wait()
            keep(k, i, bufs[k].at[i], outs[k].at[share_of(k, i, c)])
    for k, mode in enumerate(modes):
        if mode == SWAP:
            for d in range(1, ZN):
                frm = lax.rem(z + d, ZN)
                arrived(None, k, outs[k].at[frm], frm)
        elif mode in REST:
            for i in range(16):
                arrived(None, k, outs[k].at[share_of(k, i, oc)], i)
        elif mode not in (BY_X, BY_Y):
            quads = (0, 1, 2, 3)
            for b in range(ZN):
                for j in quads:
                    px, py = ((x, y), (ox, y), (x, oy), (ox, oy))[j]
                    arrived(None, k, outs[k].at[block(px, py, b, oc)], 20 + 4 * j + b)
    for k, i, mine, spot in locals_:
        pltpu.make_async_copy(mine, spot, lsem.at[k, i]).wait()
    for cond, args in sent:
        when(cond, lambda args=args: copy(*args).wait_send())


def gather(arrays, modes, collective_id):
    shapes, inputs, operands, scratch = [], [], [], []
    anywhere, local = pl.BlockSpec(memory_space=pl.ANY), pl.BlockSpec(memory_space=pltpu.VMEM)
    for a, mode in zip(arrays, modes):
        inputs = inputs + ([anywhere] * 2 if mode in REST else [local])
        operands = operands + (list(a) if mode in REST else [a])
        if mode in REST:
            a = a[0]
            scratch.append(pltpu.VMEM((16,) + a.shape[1:], a.dtype))
        if mode == BCAST:
            shapes.append((BLOCKS,) + a.shape)
        elif mode in CHAINED:
            shapes.append((2 * ZN,) + a.shape)
        elif mode == SWAP:
            shapes.append(a.shape)
        else:
            shapes.append((BLOCKS,) + a.shape[1:])
    n = len(arrays)
    dtypes = [(a[0] if mode in REST else a).dtype for a, mode in zip(arrays, modes)]
    return pl.pallas_call(
        functools.partial(gather_kernel, tuple(modes)),
        out_shape=[jax.ShapeDtypeStruct(shape, dtype) for shape, dtype in zip(shapes, dtypes)],
        in_specs=inputs,
        out_specs=[anywhere] * n,
        scratch_shapes=[
            pltpu.SemaphoreType.DMA((n, 16)),
            pltpu.SemaphoreType.DMA((n, SENDS)),
            pltpu.SemaphoreType.DMA((n, RECVS)),
        ]
        + scratch,
        compiler_params=pltpu.CompilerParams(
            collective_id=collective_id, has_side_effects=True, vmem_limit_bytes=67043328
        ),
    )(*operands)


def chunk_of(cols):
    for size in (768, 640, 512, 384, 256, 128):
        if cols % size == 0:
            return size
    return cols


def add_up(dst, sources):
    rows, cols = dst.shape[-2:]
    tall = 32 if rows > 32 and rows % 32 == 0 else (16 if rows > 32 else rows)
    wide = cols if rows > 32 else chunk_of(cols)

    def step(i, carry):
        if rows > 32:
            spot = (pl.ds(pl.multiple_of(i * tall, tall), tall), slice(None))
        elif cols > wide:
            spot = (slice(None), pl.ds(pl.multiple_of(i * wide, wide), wide))
        else:
            spot = (slice(None), slice(None))
        total = sources[0][spot].astype(jnp.float32)
        for source in sources[1:]:
            total = total + source[spot].astype(jnp.float32)
        dst[spot] = total.astype(dst.dtype)
        return carry

    count = (rows // tall) * (cols // wide)
    if count == 1:
        step(0, 0)
    else:
        lax.fori_loop(0, count, step, 0)


BUFFERS = {PRODUCT: 5, TURNED_PRODUCT: 5, SWAP: 0, PAIR_X: 2, PAIR_Y: 2, CROSS: 3, REDUCE: 4, REST_X: 5, REST_Y: 5}
PAIR = (PAIR_X, PAIR_Y)
MADE = (PRODUCT, TURNED_PRODUCT)


def make(dst, left, right, turned):
    blocks, rows = dst.shape[:2]
    group = blocks // 8

    def step(i, carry):
        span = pl.ds(pl.multiple_of(i * group * rows, 32), group * rows)
        if turned:
            span = pl.ds(pl.multiple_of(i * group * rows, 128), group * rows)
            part = left[:, span].T
        else:
            part = left[span, :]
        total = jnp.dot(part, right[...], preferred_element_type=jnp.float32)
        for j in range(group):
            dst[i * group + j] = total[j * rows : (j + 1) * rows].astype(dst.dtype)
        return carry

    lax.fori_loop(0, blocks // group, step, 0)


def reduce_kernel(modes, *refs):
    n = len(modes)
    ins, refs = take(refs, [2 if mode in REST + MADE else 1 for mode in modes])
    outs, refs = refs[:n], refs[n:]
    (lsem, ssem, rsem), scratch = refs[:3], refs[3:]
    bufs, _ = take(scratch, [BUFFERS[mode] for mode in modes])
    others, ins = ins, [group[0] for group in ins]
    for k, mode in enumerate(modes):
        if mode in MADE:
            ins[k] = bufs[k][4]
    x, y, z, c = place()
    ox, oy, oc = 1 - x, 1 - y, 1 - c
    greet(x, y, z, c, any(m in (SWAP, CROSS) for m in modes))
    sent = []

    def copy(k, src, dst, s, r, peer):
        return pltpu.make_async_remote_copy(
            src_ref=src,
            dst_ref=dst,
            send_sem=ssem.at[k, s],
            recv_sem=rsem.at[k, r],
            device_id=peer,
            device_id_type=MESH,
        )

    def send(cond, *args):
        when(cond, lambda: copy(*args).start())
        sent.append((cond, args))

    def arrived(cond, k, ref, r):
        when(cond, lambda: copy(k, ref, ref, 0, r, device(ox, y, z, c)).wait_recv())

    half = z // 2
    order = [3 - 3 * half, 2 - half, 1 - z + 4 * half, z]
    quads = ((ox, oy), (ox, y), (x, oy), (x, y))
    active = [k for k, mode in enumerate(modes) if mode in (CROSS, REDUCE) + MADE]
    paired = [k for k, mode in enumerate(modes) if mode in PAIR]
    rest = [k for k, mode in enumerate(modes) if mode in REST]

    for k, mode in enumerate(modes):
        if mode == SWAP:
            for d in range(1, ZN):
                to = lax.rem(z + d, ZN)
                send(None, k, ins[k].at[to], outs[k].at[z], d, z, device(x, y, to, c))
            pltpu.make_async_copy(ins[k].at[z], outs[k].at[z], lsem.at[k, 0]).start()

    for k in rest:
        acc, rec, _, _, cor = bufs[k]
        for i, b in enumerate(order):
            for j in range(2):
                mine = (x, y)[modes[k] == REST_X]
                other = mine if j else 1 - mine
                px, py = (x, other) if modes[k] == REST_X else (other, y)
                at = 2 * i + j
                send(None, k, ins[k].at[block(px, py, b, oc)], cor.at[at], at, at, device(x, y, z, oc))
                pltpu.make_async_copy(ins[k].at[block(px, py, b, c)], acc.at[at], lsem.at[k, at]).start()
                pltpu.make_async_copy(others[k][1].at[2 * b + other], rec.at[at], lsem.at[k, 8 + at]).start()

    def begin(ks):
        for k in ks:
            if modes[k] in MADE:
                make(ins[k], *others[k], modes[k] == TURNED_PRODUCT)
            for i, b in enumerate(order):
                acc, cor = bufs[k][:2]
                for j, (px, py) in enumerate(quads):
                    send(None, k, ins[k].at[block(px, py, b, oc)], cor.at[4 * i + j], 4 * i + j, 4 * i + j, device(x, y, z, oc))
                    pltpu.make_async_copy(ins[k].at[block(px, py, b, c)], acc.at[4 * i + j], lsem.at[k, 4 * i + j]).start()

    begin([k for k in active if modes[k] == CROSS])

    for k in paired:
        acc, cor = bufs[k]
        for i in range(8):
            b, j = i // 2, i % 2
            px, py = (j, oy) if modes[k] == PAIR_Y else (ox, j)
            send(None, k, ins[k].at[block(px, py, b, oc)], cor.at[i], i, i, device(x, y, z, oc))
            pltpu.make_async_copy(ins[k].at[block(px, py, b, c)], acc.at[i], lsem.at[k, i]).start()

    def loaded(k, i, j):
        acc, cor = bufs[k][:2]
        pltpu.make_async_copy(ins[k].at[0], acc.at[4 * i + j], lsem.at[k, 4 * i + j]).wait()
        arrived(None, k, cor.at[4 * i + j], 4 * i + j)

    for k in paired:
        acc, cor = bufs[k]

        def join(i, carry, k=k, acc=acc, cor=cor):
            pltpu.make_async_copy(ins[k].at[0], acc.at[i], lsem.at[k, i]).wait()
            arrived(None, k, cor.at[i], i)
            add_up(outs[k].at[i], (acc.at[i], cor.at[i]))
            return carry

        lax.fori_loop(0, 8, join, 0)

    def fetched(k, i, j):
        acc, rec, _, _, cor = bufs[k]
        at = 2 * i + j
        pltpu.make_async_copy(ins[k].at[0], acc.at[at], lsem.at[k, at]).wait()
        pltpu.make_async_copy(ins[k].at[0], rec.at[at], lsem.at[k, 8 + at]).wait()
        arrived(None, k, cor.at[at], at)

    def ahead(k, i, b):
        acc, rec, side, _, cor = bufs[k]
        fetched(k, i, 0)
        add_up(acc.at[2 * i], (acc.at[2 * i], rec.at[2 * i], cor.at[2 * i]))
        peer = device(x, oy, z, c) if modes[k] == REST_X else device(ox, y, z, c)
        send(None, k, acc.at[2 * i], side.at[i], 16 + i, 16 + i, peer)

    def corner(k, i, b):
        acc, cor, side = bufs[k][:3]
        loaded(k, i, 0)
        add_up(acc.at[4 * i], (acc.at[4 * i], cor.at[4 * i]))
        first, second = halves(acc.at[4 * i])
        send(None, k, first, halves(side.at[i])[0], 16 + i, 16 + i, device(x, oy, z, c))
        if second is not None:
            send(None, k, second, halves(side.at[4 + i])[1], 20 + i, 20 + i, device(ox, y, z, c))

    def beside(k, i, b):
        acc, cor, side = bufs[k][:3]
        loaded(k, i, 1)
        add_up(acc.at[4 * i + 1], (acc.at[4 * i + 1], cor.at[4 * i + 1]))
        part = halves(side.at[i])[0]
        arrived(None, k, part, 16 + i)
        mine = halves(acc.at[4 * i + 1])[0]
        add_up(mine, (mine, part))
        send(None, k, acc.at[4 * i + 1], side.at[8 + i], 24 + i, 24 + i, device(ox, y, z, c))
        loaded(k, i, 2)
        add_up(acc.at[4 * i + 2], (acc.at[4 * i + 2], cor.at[4 * i + 2]))
        part = halves(side.at[4 + i])[1]
        if part is not None:
            arrived(None, k, part, 20 + i)
            mine = halves(acc.at[4 * i + 2])[1]
            add_up(mine, (mine, part))
        send(None, k, acc.at[4 * i + 2], side.at[12 + i], 28 + i, 28 + i, device(x, oy, z, c))

    def settle(k, i, b):
        side = bufs[k][2]
        if k in rest:
            acc, rec, _, _, cor = bufs[k]
            fetched(k, i, 1)
            arrived(None, k, side.at[i], 16 + i)
            own = acc.at[2 * i + 1]
            terms = (own, rec.at[2 * i + 1], cor.at[2 * i + 1], side.at[i])
        else:
            acc, cor = bufs[k][:2]
            loaded(k, i, 3)
            own = acc.at[4 * i + 3]
            arrived(None, k, side.at[8 + i], 24 + i)
            arrived(None, k, side.at[12 + i], 28 + i)
            terms = (own, cor.at[4 * i + 3], side.at[8 + i], side.at[12 + i])
        if modes[k] == CROSS:
            add_up(own, terms)
            if i < ZN - 1:
                send(None, k, own, outs[k].at[z], 32 + i, 32 + z, device(x, y, b, c))
            else:
                pltpu.make_async_copy(own, outs[k].at[z], lsem.at[k, 16]).start()
            return
        chain = bufs[k][3]
        if i == ZN - 1:
            add_up(outs[k], terms)

            def lower(k=k, chain=chain):
                arrived(None, k, chain.at[z], 32 + z)
                add_up(outs[k], (outs[k], chain.at[z]))

            def upper(k=k, chain=chain):
                arrived(None, k, chain.at[4 + z], 36 + z)
                add_up(outs[k], (outs[k], chain.at[4 + z]))

            pl.when(z > 0)(lower)
            pl.when(z < ZN - 1)(upper)
        else:
            add_up(own, terms)
            below = both(b > z, z > 0)
            above = both(b < z, z < ZN - 1)

            def lower(k=k, chain=chain, own=own, b=b):
                arrived(None, k, chain.at[b], 32 + b)
                add_up(own, (own, chain.at[b]))

            def upper(k=k, chain=chain, own=own, b=b):
                arrived(None, k, chain.at[4 + b], 36 + b)
                add_up(own, (own, chain.at[4 + b]))

            pl.when(below)(lower)
            pl.when(above)(upper)
            send(b > z, k, own, chain.at[b], 32 + i, 32 + b, device(x, y, lax.rem(z + 1, ZN), c))
            send(b < z, k, own, chain.at[4 + b], 32 + i, 36 + b, device(x, y, lax.rem(z + ZN - 1, ZN), c))

    crossed = [k for k in active if modes[k] == CROSS]
    plain = [k for k in active if modes[k] != CROSS]
    stages = [[(ahead, rest)], [(corner, crossed)], [(corner, plain)]]
    stages = stages + [[(settle, rest), (beside, crossed)], [(settle, crossed), (beside, plain)], [(settle, plain)]]
    for stage in stages:
        for i, b in enumerate(order):
            for fn, ks in stage:
                for k in ks:
                    fn(k, i, b)
        if stage is stages[0]:
            begin(plain)
    for k, mode in enumerate(modes):
        if mode not in (SWAP, CROSS):
            continue
        for d in range(1, ZN):
            frm = lax.rem(z + d, ZN)
            arrived(None, k, outs[k].at[frm], frm if mode == SWAP else 32 + frm)
        if mode == SWAP:
            pltpu.make_async_copy(ins[k].at[z], outs[k].at[z], lsem.at[k, 0]).wait()
        else:
            pltpu.make_async_copy(bufs[k][0].at[15], outs[k].at[z], lsem.at[k, 16]).wait()
    for cond, args in sent:
        when(cond, lambda args=args: copy(*args).wait_send())


def reduce(arrays, modes, collective_id):
    shapes, specs, scratch, operands, inputs = [], [], [], [], []
    anywhere, local = pl.BlockSpec(memory_space=pl.ANY), pl.BlockSpec(memory_space=pltpu.VMEM)
    for a, mode in zip(arrays, modes):
        operands = operands + (list(a) if mode in REST + MADE else [a])
        inputs = inputs + [local if mode in MADE + (SWAP,) else anywhere] * (2 if mode in REST + MADE else 1)
        if mode in MADE:
            tall = a[0].shape[1] if mode == TURNED_PRODUCT else a[0].shape[0]
            shape = (BLOCKS, tall // BLOCKS, a[1].shape[1])
        else:
            a = a[0] if mode in REST else a
            shape = a.shape
        rows, cols = shape[1:]
        dtype = jnp.bfloat16 if mode in MADE else a.dtype
        sizes = {SWAP: (), CROSS: (16, 16, 16), REDUCE: (16, 16, 16, 8)}
        sizes.update({PAIR_X: (8, 8), PAIR_Y: (8, 8), REST_X: (8, 8, 4, 8, 8), REST_Y: (8, 8, 4, 8, 8)})
        sizes = sizes[REDUCE] + (BLOCKS,) if mode in MADE else sizes[mode]
        scratch = scratch + [pltpu.VMEM((size, rows, cols), dtype) for size in sizes]
        if mode == SWAP:
            shapes.append(jax.ShapeDtypeStruct(a.shape, a.dtype))
            specs.append(anywhere)
        elif mode in PAIR:
            shapes.append(jax.ShapeDtypeStruct((8, rows, cols), a.dtype))
            specs.append(local)
        elif mode == CROSS:
            shapes.append(jax.ShapeDtypeStruct((ZN, rows, cols), a.dtype))
            specs.append(anywhere)
        else:
            shapes.append(jax.ShapeDtypeStruct((rows, cols), jnp.float32))
            specs.append(local)
    n = len(arrays)
    return pl.pallas_call(
        functools.partial(reduce_kernel, tuple(modes)),
        out_shape=shapes,
        in_specs=inputs,
        out_specs=specs,
        scratch_shapes=[
            pltpu.SemaphoreType.DMA((n, 17)),
            pltpu.SemaphoreType.DMA((n, SENDS)),
            pltpu.SemaphoreType.DMA((n, SENDS)),
        ]
        + scratch,
        compiler_params=pltpu.CompilerParams(
            collective_id=collective_id, has_side_effects=True, vmem_limit_bytes=67043328
        ),
    )(*operands)


HEAD = 64
GROUP = 3
TILE = 512
WIDE = 1024
EDGE = 128
SPAN = 4096
FAR = 1 << 30


def longest(lengths):
    begin, best, at = jnp.int32(0), lengths[0], jnp.int32(0)
    for j in range(lengths.shape[0]):
        length = lengths[j]
        at = jnp.where(length > best, begin, at)
        best = jnp.maximum(best, length)
        begin = begin + length
    return at, at + best


def lane_slots(lengths, count):
    x, y, z, c = place()
    lane = lax.broadcasted_iota(jnp.int32, (1, count), 1)
    begin, end = longest(lengths)
    spots = [block(x, y, b, c) * count + lane for b in range(ZN)]
    slots, before = [], jnp.zeros((1, count), jnp.int32)
    for b in range(ZN):
        big = jnp.logical_and(spots[b] >= begin, spots[b] < end)
        slots.append(jnp.where(big, before, ZN // 2 + b - before))
        before = before + big.astype(jnp.int32)
    return begin, end, spots, slots


def pick(slots, slot, parts):
    chosen = parts[-1]
    for b in range(len(parts) - 2, -1, -1):
        chosen = jnp.where(slots[b] == slot, parts[b], chosen)
    return chosen


def bounds_of(lengths, spot):
    low, high = jnp.zeros_like(spot), jnp.full_like(spot, FAR)
    begin = jnp.int32(0)
    for j in range(lengths.shape[0]):
        end = begin + lengths[j]
        low = jnp.where(spot >= begin, begin, low)
        high = jnp.where(spot < end, jnp.minimum(high, end), high)
        begin = end
    return low, high


def walk(big, begin, end, low, high, step, init):
    if big:
        base = begin // EDGE * EDGE

        def body(i, carry):
            at = pl.multiple_of(base + i * WIDE, EDGE)
            return step(at, WIDE, False, carry)

        carry = step(pl.multiple_of(base, EDGE), WIDE, True, init)
        carry = lax.fori_loop(1, SPAN // WIDE, body, carry)
        return lax.cond(
            begin > base,
            lambda c: step(pl.multiple_of(base + SPAN, EDGE), EDGE, True, c),
            lambda c: c,
            carry,
        )
    first = jnp.min(low) // TILE
    stop = (jnp.max(high) + TILE - 1) // TILE
    hole_first = jnp.maximum((begin + TILE - 1) // TILE, first)
    hole = jnp.maximum(jnp.minimum(end // TILE, stop) - hole_first, 0)

    def body(i, carry):
        tile = first + i
        tile = jnp.where(jnp.logical_and(hole > 0, tile >= hole_first), tile + hole, tile)
        return step(pl.multiple_of(tile * TILE, TILE), TILE, True, carry)

    return lax.fori_loop(0, stop - first - hole, body, init)


def keys_in(first, size, low, high):
    at = first + lax.broadcasted_iota(jnp.int32, (size, low.shape[1]), 0)
    return jnp.logical_and(at >= low, at < high)


def dot(a, b):
    return jnp.dot(a, b, preferred_element_type=jnp.float32)


def pad_heads(rows, h, slots):
    part = rows[h * HEAD : (h + 1) * HEAD]
    zero = jnp.zeros_like(part)
    return jnp.concatenate([part if s == h else zero for s in slots], axis=0)


Q_SLOTS = (0, 1, 2, -1)
V_SLOTS = (-1, 2, 0, 1)


def forward_kernel(lengths, qt, kv, low_out, out, lse_out, qm, acc, qs, os, ls):
    count = qt.shape[2]
    begin, end, spots, slots = lane_slots(lengths, count)
    for s in range(ZN):
        qs[s] = pick(slots, s, [qt[b] for b in range(ZN)])

    def one_block(big, s, carry):
        low, high = bounds_of(lengths, pick(slots, s, spots))
        rows = qs[s] * jnp.bfloat16(0.125)
        for h in range(GROUP):
            qm[h] = pad_heads(rows, h, Q_SLOTS)
        acc[...] = jnp.zeros_like(acc)

        def step(at, size, masked, stats):
            span = pl.ds(at, size)
            keys = kv[span, 0:256]
            values = kv[span, 128:384].T
            mask = keys_in(at, size, low, high) if masked else None
            fresh = []
            for h in range(GROUP):
                top, total = stats[2 * h], stats[2 * h + 1]
                scores = dot(keys, qm[h])
                if masked:
                    scores = jnp.where(mask, scores, -1e9)
                new_top = jnp.maximum(top, jnp.max(scores, axis=0, keepdims=True))
                shrink = jnp.exp(top - new_top)
                weights = jnp.exp(scores - new_top)
                total = total * shrink + jnp.sum(weights, axis=0, keepdims=True)
                row = V_SLOTS.index(h) * HEAD
                acc[h] = acc[h] * shrink + dot(values[row : row + HEAD], weights.astype(jnp.bfloat16))
                fresh = fresh + [new_top, total]
            return tuple(fresh)

        init = (jnp.full((1, count), -1e9, jnp.float32), jnp.zeros((1, count), jnp.float32)) * GROUP
        stats = walk(big, begin, end, low, high, step, init)
        for h in range(GROUP):
            top, total = stats[2 * h], stats[2 * h + 1]
            os[s, h * HEAD : (h + 1) * HEAD] = acc[h] / total
            ls[s, h : h + 1] = top + jnp.log(total)
        return carry

    lax.fori_loop(0, ZN // 2, functools.partial(one_block, True), 0)
    lax.fori_loop(ZN // 2, ZN, functools.partial(one_block, False), 0)
    for b in range(ZN):
        value = pick([jnp.full_like(slots[b], s) for s in range(ZN)], slots[b], [os[s] for s in range(ZN)])
        out[b] = value
        low_out[b] = value.astype(low_out.dtype)
        lse_out[b] = pick([jnp.full_like(slots[b], s) for s in range(ZN)], slots[b], [ls[s] for s in range(ZN)])


def attend(lengths, qt, kv):
    blocks, rows, count = qt.shape
    whole = pl.BlockSpec(memory_space=pltpu.VMEM)
    return pl.pallas_call(
        forward_kernel,
        out_shape=[
            jax.ShapeDtypeStruct(qt.shape, jnp.bfloat16),
            jax.ShapeDtypeStruct(qt.shape, jnp.float32),
            jax.ShapeDtypeStruct((blocks, 8, count), jnp.float32),
        ],
        in_specs=[pl.BlockSpec(memory_space=pltpu.SMEM), whole, whole],
        out_specs=[whole] * 3,
        scratch_shapes=[
            pltpu.VMEM((GROUP, 256, count), jnp.bfloat16),
            pltpu.VMEM((GROUP, HEAD, count), jnp.float32),
            pltpu.VMEM(qt.shape, jnp.bfloat16),
            pltpu.VMEM(qt.shape, jnp.float32),
            pltpu.VMEM((blocks, 8, count), jnp.float32),
        ],
        compiler_params=pltpu.CompilerParams(vmem_limit_bytes=67043328),
    )(lengths, qt, kv)


def backward_kernel(lengths, qt, kv, out, lse, dot_in, cosine, sine, dq_out, dkv_out, qmt, qm, dmt, dm, dq, acc, qs, ds, es, ls, dqs):
    count = qt.shape[2]
    tiles = kv.shape[0] // TILE

    def clear(tile, carry):
        acc[pl.ds(pl.multiple_of(tile * TILE, TILE), TILE), :] = jnp.zeros((TILE, acc.shape[1]), jnp.float32)
        return carry

    lax.fori_loop(0, tiles, clear, 0)

    begin, end, spots, slots = lane_slots(lengths, count)
    for b in range(ZN):
        product_rows = dot_in[b].astype(jnp.float32) * out[b]
        for h in range(GROUP):
            es[b, h : h + 1] = jnp.sum(product_rows[h * HEAD : (h + 1) * HEAD], axis=0, keepdims=True)
    for s in range(ZN):
        qs[s] = pick(slots, s, [qt[b] for b in range(ZN)])
        ds[s] = pick(slots, s, [dot_in[b] for b in range(ZN)])
        ls[s] = pick(slots, s, [lse[b] for b in range(ZN)])
    picked = [pick(slots, s, [es[b] for b in range(ZN)]) for s in range(ZN)]
    for s in range(ZN):
        es[s] = picked[s]

    def one_block(big, s, carry):
        low, high = bounds_of(lengths, pick(slots, s, spots))
        rows = qs[s] * jnp.bfloat16(0.125)
        grads = ds[s]
        deltas = [es[s, h : h + 1] for h in range(GROUP)]
        levels = [ls[s, h : h + 1] for h in range(GROUP)]
        for h in range(GROUP):
            padded = pad_heads(rows, h, Q_SLOTS)
            qmt[h] = padded
            qm[h * count : (h + 1) * count] = padded.T
            padded = pad_heads(grads, h, V_SLOTS)
            dmt[h] = padded
            dm[h * count : (h + 1) * count] = padded.T
        dq[...] = jnp.zeros_like(dq)

        def step(at, size, masked, inner):
            span = pl.ds(at, size)
            keys = kv[span, 0:256]
            values = kv[span, 128:384]
            turned = keys.T
            mask = keys_in(at, size, low, high) if masked else None
            probs, slopes = [], []
            for h in range(GROUP):
                weights = jnp.exp(dot(keys, qmt[h]) - levels[h])
                if masked:
                    weights = jnp.where(mask, weights, 0.0)
                slope = (weights * (dot(values, dmt[h]) - deltas[h])).astype(jnp.bfloat16)
                dq[h] += dot(turned[h * HEAD : (h + 1) * HEAD], slope)
                probs.append(weights.astype(jnp.bfloat16))
                slopes.append(slope)
            dv = dot(jnp.concatenate(probs, axis=1), dm[...])
            dk = dot(jnp.concatenate(slopes, axis=1), qm[...])
            acc[span, 0:128] += dk[:, :128]
            acc[span, 128:256] += dk[:, 128:] + dv[:, :128]
            acc[span, 256:384] += dv[:, 128:]
            return inner

        walk(big, begin, end, low, high, step, 0)
        for h in range(GROUP):
            dqs[s, h * HEAD : (h + 1) * HEAD] = dq[h] * 0.125
        return carry

    lax.fori_loop(0, ZN // 2, functools.partial(one_block, True), 0)
    lax.fori_loop(ZN // 2, ZN, functools.partial(one_block, False), 0)
    half = HEAD // 2
    for b in range(ZN):
        back = pick([jnp.full_like(slots[b], s) for s in range(ZN)], slots[b], [dqs[s] for s in range(ZN)])
        for h in range(GROUP):
            at = h * HEAD
            w1, w2 = back[at : at + half], back[at + half : at + HEAD]
            dq_out[b, at : at + half] = (w1 * cosine[b] + w2 * sine[b]).astype(dq_out.dtype)
            dq_out[b, at + half : at + HEAD] = (w2 * cosine[b] - w1 * sine[b]).astype(dq_out.dtype)

    def finish(tile, carry):
        span = pl.ds(pl.multiple_of(tile * TILE, TILE), TILE)
        dkv_out[span, :] = acc[span, :].astype(dkv_out.dtype)
        return carry

    lax.fori_loop(0, tiles, finish, 0)


def attend_back(lengths, qt, kv, out, lse, dots, cosine, sine):
    blocks, rows, count = qt.shape
    whole = pl.BlockSpec(memory_space=pltpu.VMEM)
    return pl.pallas_call(
        backward_kernel,
        out_shape=[
            jax.ShapeDtypeStruct(qt.shape, jnp.bfloat16),
            jax.ShapeDtypeStruct(kv.shape, jnp.bfloat16),
        ],
        in_specs=[pl.BlockSpec(memory_space=pltpu.SMEM)] + [whole] * 7,
        out_specs=[whole] * 2,
        scratch_shapes=[
            pltpu.VMEM((GROUP, 256, count), jnp.bfloat16),
            pltpu.VMEM((GROUP * count, 256), jnp.bfloat16),
            pltpu.VMEM((GROUP, 256, count), jnp.bfloat16),
            pltpu.VMEM((GROUP * count, 256), jnp.bfloat16),
            pltpu.VMEM((GROUP, HEAD, count), jnp.float32),
            pltpu.VMEM(kv.shape, jnp.float32),
            pltpu.VMEM(qt.shape, jnp.bfloat16),
            pltpu.VMEM(qt.shape, jnp.bfloat16),
            pltpu.VMEM((blocks, 8, count), jnp.float32),
            pltpu.VMEM((blocks, 8, count), jnp.float32),
            pltpu.VMEM(qt.shape, jnp.float32),
        ],
        compiler_params=pltpu.CompilerParams(vmem_limit_bytes=67043328),
    )(lengths, qt, kv, out, lse, dots, cosine, sine)


KV_SLOTS = (0, 1, 2, 5, 3, 4)


def turn(rows, cosine, sine):
    first, second = rows[:, 0], rows[:, 1]
    return jnp.stack([first * cosine - second * sine, second * cosine + first * sine], axis=1)


def turn_back(rows, cosine, sine):
    first, second = rows[:, 0], rows[:, 1]
    return jnp.stack([first * cosine + second * sine, second * cosine - first * sine], axis=1)


def tables(lengths, first, count):
    starts = jnp.cumsum(lengths) - lengths
    position = first[:, None] + jnp.arange(count, dtype=jnp.int32)[None, :]
    begun = position[..., None] >= starts
    offsets = position - jnp.max(jnp.where(begun, starts, 0), axis=-1)
    half = HEAD // 2
    frequency = rope_base ** (-(jnp.arange(half, dtype=jnp.float32) * 2.0) / HEAD)
    angles = offsets.astype(jnp.float32)[:, None, :] * frequency[None, :, None]
    return jnp.cos(angles), jnp.sin(angles)


def norm_back(upstream, scaled, inv_std, gain_vec):
    weighted = upstream * gain_vec
    inner = (
        weighted
        - jnp.mean(weighted, axis=-1, keepdims=True)
        - scaled * jnp.mean(weighted * scaled, axis=-1, keepdims=True)
    )
    sums = [jnp.sum(upstream * scaled, axis=0, keepdims=True), jnp.sum(upstream, axis=0, keepdims=True)]
    return inv_std * inner, sums


def contract(left, right, dims):
    return lax.dot_general(left, right, (dims, ((), ())), preferred_element_type=jnp.float32)


def copies_kernel(*refs):
    n = len(refs) // 3
    ins, outs, bufs, sems = refs[:n], refs[n : 2 * n], refs[2 * n : 3 * n], refs[3 * n]
    loads = [pltpu.make_async_copy(ins[k], bufs[k], sems.at[k]) for k in range(n)]
    stores = [pltpu.make_async_copy(bufs[k], outs[k], sems.at[n + k]) for k in range(n)]
    for load in loads:
        load.start()
    for load, store in zip(loads, stores):
        load.wait()
        store.start()
    for store in stores:
        store.wait()


def copies(arrays):
    n = len(arrays)
    anywhere = pl.BlockSpec(memory_space=pl.ANY)
    return pl.pallas_call(
        copies_kernel,
        out_shape=[jax.ShapeDtypeStruct(a.shape, a.dtype) for a in arrays],
        in_specs=[anywhere] * n,
        out_specs=[anywhere] * n,
        scratch_shapes=[pltpu.VMEM(a.shape, a.dtype) for a in arrays] + [pltpu.SemaphoreType.DMA((2 * n,))],
    )(*arrays)


def local_grid(
    tokens,
    qkv_weight,
    out_weight,
    gate_weight,
    up_weight,
    down_weight,
    first_gain,
    first_bias,
    second_gain,
    second_bias,
    lengths,
    cotangent,
):
    bf16 = jnp.bfloat16
    rows, width = tokens.shape
    share = first_gain.shape[0]
    heads = width // HEAD
    half = HEAD // 2
    x, y, z, c = place()
    spots = [(px, py, pz, pc) for pz in range(ZN) for py in range(YN) for pc in range(CN) for px in range(XN)]
    over_x = [(block(*p), block(1 - p[0], *p[1:])) for p in spots]
    over_y = [(block(*p), block(p[0], 1 - p[1], *p[2:])) for p in spots]
    small = jnp.stack([first_gain, first_bias, second_gain, second_bias])
    small = jnp.pad(small, ((0, 4), (0, 128 - share)))
    hidden_width = gate_weight.shape[1]

    (qkv_blocks,) = gather([qkv_weight], [BCAST], 1)
    qkv_full = qkv_blocks.reshape(width, 3 * width)
    turned = jnp.stack([block(x, y, b, c) for b in range(ZN)]) * rows
    cos_all, sin_all = tables(lengths, turned, rows)
    cosine = lax.dynamic_index_in_dim(cos_all, z, 0, keepdims=False)
    sine = lax.dynamic_index_in_dim(sin_all, z, 0, keepdims=False)

    raw = contract(qkv_full, tokens, ((0,), (1,))).astype(bf16)
    raw = raw.reshape(3, heads, 2, half, rows)
    queries = turn(raw[0].astype(jnp.float32), cosine, sine).astype(bf16)
    keys = turn(raw[1].astype(jnp.float32), cosine, sine).astype(bf16)
    queries = queries.reshape(ZN, GROUP * HEAD, rows)
    pairs = jnp.concatenate(
        [keys.reshape(ZN, GROUP, HEAD, rows), raw[2].reshape(ZN, GROUP, HEAD, rows)], axis=1
    )
    pairs = jnp.concatenate([pairs[:, s : s + 1] for s in KV_SLOTS], axis=1)
    pairs = jnp.swapaxes(pairs.reshape(ZN, 2 * GROUP * HEAD, rows), 1, 2)

    pairs_all, queries, out_full, down_full, small, gate_part, up_part = gather(
        [pairs, queries, out_weight, down_weight, small, gate_weight, up_weight],
        [CROSS, SWAP, BCAST, BCAST, BCAST, BY_X, BY_Y],
        2,
    )
    out_full = out_full.reshape(width, width)
    gate_rest = lax.ppermute(gate_part, ("cp", "hd"), over_y)
    up_rest = lax.ppermute(up_part, ("cp", "hd"), over_x)
    down_full = down_full.reshape(hidden_width, width)
    small = jnp.swapaxes(small[:, :4, :share], 0, 1).astype(jnp.float32).reshape(4, width)
    small = lax.optimization_barrier(small)
    gain_one, bias_one, gain_two, bias_two = [small[i] for i in range(4)]
    pairs_all = pairs_all.reshape(-1, 2 * GROUP * HEAD)
    low, attended, lse = attend(lengths, queries, pairs_all)
    low, gate_full, up_full = gather(
        [low, (gate_part, gate_rest), (up_part, up_rest)], [SWAP, REST_Y, REST_X], 3
    )
    gate_full = gate_full.reshape(width, hidden_width)
    up_full = up_full.reshape(width, hidden_width)
    low = low.reshape(width, rows)

    attn_out = contract(low, out_full, ((0,), (0,)))
    first, scaled_one, inv_one = normalize(tokens.astype(jnp.float32) + attn_out, gain_one, bias_one)
    first_low = first.astype(bf16)
    gate_proj = product(first_low, gate_full)
    up_proj = product(first_low, up_full)
    sigmoid_gate = jax.nn.sigmoid(gate_proj)
    silu_gate = gate_proj * sigmoid_gate
    hidden = (silu_gate * up_proj).astype(bf16)
    branch = product(hidden, down_full)
    second, scaled_two, inv_two = normalize(first + branch, gain_two, bias_two)
    layer_out = second.astype(bf16)

    upstream = cotangent.astype(jnp.float32)
    dz_two, sums_two = norm_back(upstream, scaled_two, inv_two, gain_two)
    dz_two_low = dz_two.astype(bf16)
    hidden_grad = contract(dz_two_low, down_full, ((1,), (1,)))
    gate_back = (
        hidden_grad * up_proj * sigmoid_gate * (1.0 + gate_proj * (1.0 - sigmoid_gate))
    ).astype(bf16)
    up_back = (hidden_grad * silu_gate).astype(bf16)
    gate_sum = contract(first_low, gate_back, ((0,), (0,))).astype(bf16)
    up_sum = contract(first_low, up_back, ((0,), (0,))).astype(bf16)
    first_back = (
        dz_two + contract(gate_back, gate_full, ((1,), (1,))) + contract(up_back, up_full, ((1,), (1,)))
    )
    dz_one, sums_one = norm_back(first_back, scaled_one, inv_one, gain_one)
    dz_one_low = dz_one.astype(bf16)
    attended_back = contract(out_full, dz_one_low, ((1,), (1,))).astype(bf16)
    gate_sum = gate_sum.reshape((BLOCKS,) + gate_weight.shape)
    up_sum = up_sum.reshape((BLOCKS,) + up_weight.shape)
    attended_back, gate_send, up_send = reduce(
        [attended_back.reshape(ZN, GROUP * HEAD, rows), gate_sum, up_sum], [SWAP, PAIR_Y, PAIR_X], 4
    )
    gate_rest = lax.ppermute(gate_send, ("cp", "hd"), over_y)
    up_rest = lax.ppermute(up_send, ("cp", "hd"), over_x)

    query_back, pair_back = attend_back(
        lengths, queries, pairs_all, attended, lse, attended_back, cos_all, sin_all
    )
    small_sum = lax.optimization_barrier(jnp.concatenate(sums_one + sums_two, axis=0))
    small_sum = jnp.swapaxes(small_sum.reshape(4, BLOCKS, share), 0, 1)
    small_sum = jnp.pad(small_sum, ((0, 0), (0, 4), (0, 128 - share)))
    pair_back, query_back, out_grad, down_grad, small_grad, gate_grad, up_grad = reduce(
        [
            pair_back.reshape(BLOCKS, rows, 2 * GROUP * HEAD),
            query_back,
            (low, dz_one_low),
            (hidden, dz_two_low),
            small_sum,
            (gate_sum, gate_rest),
            (up_sum, up_rest),
        ],
        [CROSS, SWAP, PRODUCT, TURNED_PRODUCT, REDUCE, REST_Y, REST_X],
        5,
    )
    pair_back = jnp.swapaxes(pair_back, 1, 2).reshape(ZN, 2 * GROUP, HEAD, rows)
    pair_back = [pair_back[:, KV_SLOTS.index(s)] for s in range(2 * GROUP)]
    key_back = jnp.stack(pair_back[:GROUP], axis=1).reshape(heads, 2, half, rows)
    key_back = turn_back(key_back.astype(jnp.float32), cosine, sine).astype(bf16)
    value_back = jnp.stack(pair_back[GROUP:], axis=1)
    raw_back = jnp.concatenate(
        [
            query_back.reshape(width, rows),
            key_back.reshape(width, rows),
            value_back.reshape(width, rows),
        ],
        axis=0,
    )
    qkv_sum = contract(tokens, raw_back, ((0,), (1,))).astype(bf16)
    tokens_grad = (dz_one + contract(raw_back, qkv_full, ((0,), (1,)))).astype(bf16)
    (qkv_grad,) = reduce([qkv_sum.reshape(BLOCKS, share, 3 * width)], [REDUCE], 6)
    qkv_grad, out_grad, gate_grad, up_grad, down_grad = copies([qkv_grad, out_grad, gate_grad, up_grad, down_grad])
    return (
        layer_out,
        tokens_grad,
        qkv_grad,
        out_grad,
        gate_grad,
        up_grad,
        down_grad,
        small_grad[0, :share],
        small_grad[1, :share],
        small_grad[2, :share],
        small_grad[3, :share],
    )


def solution(mesh):
    rows = P(("cp", "hd"), None)
    line = P(("cp", "hd"))
    local = local_grid if (mesh.shape["cp"], mesh.shape["hd"]) == (ZN * YN * CN, XN) else local_any
    return jax.shard_map(
        local,
        mesh=mesh,
        in_specs=(rows,) * 6 + (line,) * 4 + (P(), rows),
        out_specs=(rows,) * 7 + (line,) * 4,
        check_vma=False,
    )
```

```python
import functools

import jax
import jax.numpy as jnp
from jax import lax
from jax.experimental import pallas as pl
from jax.experimental.pallas import tpu as pltpu
from jax.sharding import PartitionSpec as P

HD = 64
REACH = 8


rope_base = 1000.0
norm_eps = 1e-12
score_scale = 0.125
masked_score = -1000000000.0


def shifted(block, axis, distance):
    devices = range(lax.axis_size(axis))
    route = [(i - distance, i) for i in devices if i - distance in devices]
    return lax.ppermute(block, axis, route)


def doc_layout(lengths, first_row, row_count):
    starts = jnp.cumsum(lengths) - lengths
    position = first_row + jnp.arange(row_count, dtype=jnp.int32)
    at_or_after = position[:, None] >= starts[None, :]
    doc_ids = jnp.sum(at_or_after.astype(jnp.int32), axis=1) - 1
    doc_begin = jnp.max(jnp.where(at_or_after, starts[None, :], 0), axis=1)
    return (doc_ids, position - doc_begin)


def rope_tables(offsets, head_size):
    half_size = head_size // 2
    frequency = rope_base ** (-(jnp.arange(half_size, dtype=jnp.float32) * 2.0) / head_size)
    angles = offsets.astype(jnp.float32)[:, None] * frequency[None, :]
    return (jnp.cos(angles), jnp.sin(angles))


def rotate(values, cosine, sine):
    half_size = values.shape[-1] // 2
    first_half = values[..., :half_size]
    second_half = values[..., half_size:]
    cos_rows = cosine[:, None, :]
    sin_rows = sine[:, None, :]
    return jnp.concatenate(
        [
            first_half * cos_rows - second_half * sin_rows,
            second_half * cos_rows + first_half * sin_rows,
        ],
        axis=-1,
    )


def rotate_back(grads, cosine, sine):
    half_size = grads.shape[-1] // 2
    first_half = grads[..., :half_size]
    second_half = grads[..., half_size:]
    cos_rows = cosine[:, None, :]
    sin_rows = sine[:, None, :]
    return jnp.concatenate(
        [
            first_half * cos_rows + second_half * sin_rows,
            second_half * cos_rows - first_half * sin_rows,
        ],
        axis=-1,
    )


def normalize(hidden_in, gain_vec, bias_vec):
    average = jnp.mean(hidden_in, axis=-1, keepdims=True)
    centered = hidden_in - average
    variance = jnp.mean(centered * centered, axis=-1, keepdims=True)
    inv_std = lax.rsqrt(variance + norm_eps)
    scaled = centered * inv_std
    return (scaled * gain_vec + bias_vec, scaled, inv_std)


def normalize_back(upstream, scaled, inv_std, gain_vec):
    weighted = upstream * gain_vec
    inner = (
        weighted
        - jnp.mean(weighted, axis=-1, keepdims=True)
        - scaled * jnp.mean(weighted * scaled, axis=-1, keepdims=True)
    )
    return (inv_std * inner, jnp.sum(upstream * scaled, axis=0), jnp.sum(upstream, axis=0))


def product(left, right):
    return jnp.dot(left, right, preferred_element_type=jnp.float32)


def local_any(
    tokens,
    qkv_weight,
    out_weight,
    gate_weight,
    up_weight,
    down_weight,
    first_gain,
    first_bias,
    second_gain,
    second_bias,
    doc_lengths,
    cotangent,
):
    rows_here = tokens.shape[0]
    model_width = tokens.shape[1]
    hd_count = lax.axis_size("hd")
    cp_count = lax.axis_size("cp")
    cp_index = lax.axis_index("cp")
    block_rows = rows_here * hd_count
    local_width = model_width // hd_count
    local_heads = local_width // HD
    shifts = [0]
    for distance in range(1, REACH + 1):
        shifts = shifts + [-distance, distance]
    shards = (
        qkv_weight,
        out_weight,
        gate_weight,
        up_weight,
        down_weight,
        first_gain,
        first_bias,
        second_gain,
        second_bias,
    )
    weights = (
        lax.all_gather(shards[0], ("cp", "hd"), axis=0, tiled=True),
        lax.all_gather(shards[1], ("cp", "hd"), axis=0, tiled=True),
        lax.all_gather(shards[2], ("cp", "hd"), axis=0, tiled=True),
        lax.all_gather(shards[3], ("cp", "hd"), axis=0, tiled=True),
        lax.all_gather(shards[4], ("cp", "hd"), axis=0, tiled=True),
        lax.all_gather(shards[5], ("cp", "hd"), axis=0, tiled=True),
        lax.all_gather(shards[6], ("cp", "hd"), axis=0, tiled=True),
        lax.all_gather(shards[7], ("cp", "hd"), axis=0, tiled=True),
        lax.all_gather(shards[8], ("cp", "hd"), axis=0, tiled=True),
    )
    (
        qkv_full,
        out_full,
        gate_full,
        up_full,
        down_full,
        gain_first,
        bias_first,
        gain_second,
        bias_second,
    ) = weights
    raw_rows = product(tokens, qkv_full).astype(jnp.bfloat16)
    grouped = lax.all_to_all(
        raw_rows.reshape(rows_here, 3, hd_count, local_width),
        "hd",
        split_axis=2,
        concat_axis=0,
        tiled=True,
    )
    grouped = grouped.reshape(block_rows, 3, local_width)
    query_docs, offsets = doc_layout(doc_lengths, cp_index * block_rows, block_rows)
    cosine, sine = rope_tables(offsets, HD)
    queries = rotate(
        grouped[:, 0].astype(jnp.float32).reshape(block_rows, local_heads, HD), cosine, sine
    ).astype(jnp.bfloat16)
    key_rows = rotate(
        grouped[:, 1].astype(jnp.float32).reshape(block_rows, local_heads, HD), cosine, sine
    ).astype(jnp.bfloat16)
    own_block = jnp.stack([key_rows.reshape(block_rows, local_width), grouped[:, 2]], axis=1)

    def key_docs(distance):
        source = cp_index - distance
        doc_ids, unused_offsets = doc_layout(doc_lengths, source * block_rows, block_rows)
        inside = jnp.logical_and(source >= 0, source < cp_count)
        return jnp.where(inside, doc_ids, -2)

    remote = [own_block] + [shifted(own_block, "cp", distance) for distance in shifts[1:]]
    masks = [query_docs[:, None] == key_docs(distance)[None, :] for distance in shifts]

    def scores_with(query_part, remote_block, key_mask):
        key_part = remote_block[:, 0].reshape(block_rows, local_heads, HD)
        raw_scores = (
            jnp.einsum("qhd,khd->hqk", query_part, key_part, preferred_element_type=jnp.float32)
            * score_scale
        )
        return jnp.where(key_mask[None], raw_scores, masked_score)

    def scores_for(remote_block, key_mask):
        return scores_with(queries, remote_block, key_mask)

    running_max = jnp.full((local_heads, block_rows), masked_score, jnp.float32)
    running_sum = jnp.zeros((local_heads, block_rows), jnp.float32)
    for remote_block, key_mask in zip(remote, masks):
        block_scores = scores_for(remote_block, key_mask)
        new_max = jnp.maximum(running_max, jnp.max(block_scores, axis=-1))
        running_sum = running_sum * jnp.exp(running_max - new_max) + jnp.sum(
            jnp.exp(block_scores - new_max[:, :, None]), axis=-1
        )
        running_max = new_max
    log_total = running_max + jnp.log(running_sum)
    attended = jnp.zeros((block_rows, local_heads, HD), jnp.float32)
    for remote_block, key_mask in zip(remote, masks):
        block_scores = scores_for(remote_block, key_mask)
        probs = jnp.exp(block_scores - log_total[:, :, None]).astype(jnp.bfloat16)
        value_part = remote_block[:, 1].reshape(block_rows, local_heads, HD)
        attended = attended + jnp.einsum(
            "hqk,khd->qhd", probs, value_part, preferred_element_type=jnp.float32
        )
    attended_send = attended.reshape(block_rows, 1, local_width).astype(jnp.bfloat16)
    attended_low = lax.all_to_all(
        attended_send, "hd", split_axis=0, concat_axis=1, tiled=True
    ).reshape(rows_here, model_width)
    gain_one = gain_first.astype(jnp.float32)
    gain_two = gain_second.astype(jnp.float32)
    attn_out = product(attended_low, out_full)
    first, scaled_one, inv_one = normalize(
        tokens.astype(jnp.float32) + attn_out, gain_one, bias_first.astype(jnp.float32)
    )
    first_low = first.astype(jnp.bfloat16)
    gate_proj = product(first_low, gate_full)
    up_proj = product(first_low, up_full)
    sigmoid_gate = jax.nn.sigmoid(gate_proj)
    silu_gate = gate_proj * sigmoid_gate
    hidden = (silu_gate * up_proj).astype(jnp.bfloat16)
    branch = product(hidden, down_full)
    second, scaled_two, inv_two = normalize(
        first + branch, gain_two, bias_second.astype(jnp.float32)
    )
    layer_out = second.astype(jnp.bfloat16)
    weights = (
        lax.all_gather(shards[0], ("cp", "hd"), axis=0, tiled=True),
        lax.all_gather(shards[1], ("cp", "hd"), axis=0, tiled=True),
        lax.all_gather(shards[2], ("cp", "hd"), axis=0, tiled=True),
        lax.all_gather(shards[3], ("cp", "hd"), axis=0, tiled=True),
        lax.all_gather(shards[4], ("cp", "hd"), axis=0, tiled=True),
        lax.all_gather(shards[5], ("cp", "hd"), axis=0, tiled=True),
        lax.all_gather(shards[6], ("cp", "hd"), axis=0, tiled=True),
        lax.all_gather(shards[7], ("cp", "hd"), axis=0, tiled=True),
        lax.all_gather(shards[8], ("cp", "hd"), axis=0, tiled=True),
    )
    (
        qkv_full,
        out_full,
        gate_full,
        up_full,
        down_full,
        gain_first,
        bias_first,
        gain_second,
        bias_second,
    ) = weights
    upstream = cotangent.astype(jnp.float32)
    dz_two, gain_two_grad, bias_two_grad = normalize_back(upstream, scaled_two, inv_two, gain_two)
    dz_two_low = dz_two.astype(jnp.bfloat16)
    down_sum = product(hidden.T, dz_two_low)
    hidden_grad = product(dz_two_low, down_full.T)
    gate_back = (
        hidden_grad * up_proj * sigmoid_gate * (1.0 + gate_proj * (1.0 - sigmoid_gate))
    ).astype(jnp.bfloat16)
    up_back = (hidden_grad * silu_gate).astype(jnp.bfloat16)
    gate_sum = product(first_low.T, gate_back)
    up_sum = product(first_low.T, up_back)
    first_back = dz_two + product(gate_back, gate_full.T) + product(up_back, up_full.T)
    dz_one, gain_one_grad, bias_one_grad = normalize_back(first_back, scaled_one, inv_one, gain_one)
    dz_one_low = dz_one.astype(jnp.bfloat16)
    out_sum = product(attended_low.T, dz_one_low)
    attended_back = product(dz_one_low, out_full.T).astype(jnp.bfloat16)
    heads_back = lax.all_to_all(
        attended_back.reshape(rows_here, hd_count, local_width),
        "hd",
        split_axis=1,
        concat_axis=0,
        tiled=True,
    )
    heads_back = heads_back.reshape(block_rows, local_heads, HD)
    delta = jnp.transpose(jnp.sum(heads_back.astype(jnp.float32) * attended, axis=-1))
    query_grad = jnp.zeros((block_rows, local_heads, HD), jnp.float32)
    pair_total = jnp.zeros((block_rows, 2, local_width), jnp.float32)
    remote = [own_block] + [shifted(own_block, "cp", distance) for distance in shifts[1:]]
    for distance, remote_block, key_mask in zip(shifts, remote, masks):
        pair_block_scores = scores_with(queries, remote_block, key_mask)
        pair_probs = jnp.exp(pair_block_scores - log_total[:, :, None])
        pair_key_part = remote_block[:, 0].reshape(block_rows, local_heads, HD)
        pair_value_part = remote_block[:, 1].reshape(block_rows, local_heads, HD)
        value_grad = jnp.einsum(
            "hqk,qhd->khd",
            pair_probs.astype(jnp.bfloat16),
            heads_back,
            preferred_element_type=jnp.float32,
        )
        prob_grad = jnp.einsum(
            "qhd,khd->hqk", heads_back, pair_value_part, preferred_element_type=jnp.float32
        )
        score_grad = (pair_probs * (prob_grad - delta[:, :, None])).astype(jnp.bfloat16)
        query_term = (
            jnp.einsum(
                "hqk,khd->qhd", score_grad, pair_key_part, preferred_element_type=jnp.float32
            )
            * score_scale
        )
        key_grad = (
            jnp.einsum("hqk,qhd->khd", score_grad, queries, preferred_element_type=jnp.float32)
            * score_scale
        )
        grad_pair = jnp.stack(
            [
                key_grad.reshape(block_rows, local_width),
                value_grad.reshape(block_rows, local_width),
            ],
            axis=1,
        )
        query_term, grad_pair = (query_term, grad_pair)
        query_grad = query_grad + query_term
        if distance == 0:
            pair_total = grad_pair
        else:
            pair_total = pair_total + shifted(
                grad_pair.astype(jnp.bfloat16), "cp", -distance
            ).astype(grad_pair.dtype)
    query_back = rotate_back(query_grad, cosine, sine).reshape(block_rows, local_width)
    key_back = rotate_back(
        pair_total[:, 0].reshape(block_rows, local_heads, HD), cosine, sine
    ).reshape(block_rows, local_width)
    raw_back = jnp.stack([query_back, key_back, pair_total[:, 1]], axis=1).astype(jnp.bfloat16)
    raw_back = lax.all_to_all(
        raw_back.reshape(block_rows, 3, 1, local_width),
        "hd",
        split_axis=0,
        concat_axis=2,
        tiled=True,
    )
    raw_back = raw_back.reshape(rows_here, 3 * model_width)
    qkv_sum = product(tokens.T, raw_back)
    tokens_grad = (dz_one + product(raw_back, qkv_full.T)).astype(jnp.bfloat16)
    summed = (
        lax.psum_scatter(qkv_sum, ("cp", "hd"), scatter_dimension=0, tiled=True),
        lax.psum_scatter(out_sum, ("cp", "hd"), scatter_dimension=0, tiled=True),
        lax.psum_scatter(gate_sum, ("cp", "hd"), scatter_dimension=0, tiled=True),
        lax.psum_scatter(up_sum, ("cp", "hd"), scatter_dimension=0, tiled=True),
        lax.psum_scatter(down_sum, ("cp", "hd"), scatter_dimension=0, tiled=True),
        lax.psum_scatter(gain_one_grad, ("cp", "hd"), scatter_dimension=0, tiled=True),
        lax.psum_scatter(bias_one_grad, ("cp", "hd"), scatter_dimension=0, tiled=True),
        lax.psum_scatter(gain_two_grad, ("cp", "hd"), scatter_dimension=0, tiled=True),
        lax.psum_scatter(bias_two_grad, ("cp", "hd"), scatter_dimension=0, tiled=True),
    )
    return (
        layer_out,
        tokens_grad,
        summed[0],
        summed[1],
        summed[2],
        summed[3],
        summed[4],
        summed[5],
        summed[6],
        summed[7],
        summed[8],
    )


MESH = pl.DeviceIdType.MESH
ZN, YN, CN, XN = 4, 2, 2, 2
BLOCKS = ZN * YN * CN * XN


def place():
    cp = lax.axis_index("cp")
    x = lax.axis_index("hd")
    return x, lax.rem(cp // CN, YN), cp // (YN * CN), lax.rem(cp, CN)


def device(x, y, z, c):
    return ((z * YN + y) * CN + c, x)


def block(x, y, z, c):
    return ((z * YN + y) * CN + c) * XN + x


def when(cond, fn):
    if cond is None:
        fn()
    else:
        pl.when(cond)(fn)


def both(a, b):
    if a is None:
        return b
    if b is None:
        return a
    return jnp.logical_and(a, b)


def halves(ref):
    rows, cols = ref.shape[-2:]
    if rows % 32 == 0:
        return ref.at[pl.ds(0, rows // 2)], ref.at[pl.ds(rows // 2, rows // 2)]
    if cols % 256 == 0:
        return ref.at[:, pl.ds(0, cols // 2)], ref.at[:, pl.ds(cols // 2, cols // 2)]
    return ref, None


def greet(x, y, z, c, far):
    barrier = pltpu.get_barrier_semaphore()
    for peer in (device(1 - x, y, z, c), device(x, 1 - y, z, c), device(x, y, z, 1 - c)):
        pl.semaphore_signal(barrier, inc=1, device_id=peer, device_id_type=MESH)
    count = 3
    if far:
        for k in range(1, ZN):
            peer = device(x, y, lax.rem(z + k, ZN), c)
            pl.semaphore_signal(barrier, inc=1, device_id=peer, device_id_type=MESH)
        count = count + ZN - 1
    else:
        pl.when(z > 0)(lambda: pl.semaphore_signal(barrier, inc=1, device_id=device(x, y, z - 1, c), device_id_type=MESH))
        pl.when(z < ZN - 1)(lambda: pl.semaphore_signal(barrier, inc=1, device_id=device(x, y, z + 1, c), device_id_type=MESH))
        count = count + (z > 0).astype(jnp.int32) + (z < ZN - 1).astype(jnp.int32)
    pl.semaphore_wait(barrier, count)


SENDS = 40
RECVS = 36


BCAST, BY_X, BY_Y, CROSS, SWAP, REST_X, REST_Y, PAIR_X, PAIR_Y, REDUCE, PRODUCT, TURNED_PRODUCT = range(12)
ONWARD, BESIDE, ACROSS = range(3)
CHAINED = (BCAST, BY_X, BY_Y)
REST = (REST_X, REST_Y)


def take(refs, counts):
    groups = []
    for count in counts:
        groups.append(refs[:count])
        refs = refs[count:]
    return groups, refs


SHORT_PLAN = [
    (fn, 0, d - lag)
    for d in range(1, ZN + 2)
    for lag, fn in enumerate((ONWARD, BESIDE, ACROSS))
    if (d > 0 if lag else d < ZN) and 0 <= d - lag < ZN
]
PLAN = [
    (ONWARD, 0, 1),
    (BESIDE, 0, 0),
    (BESIDE, 1, 0),
    (ACROSS, 0, 0),
    (BESIDE, 0, 1),
    (ONWARD, 1, 1),
    (ACROSS, 1, 0),
    (ACROSS, 0, 1),
    (ONWARD, 1, 2),
    (ONWARD, 1, 3),
    (BESIDE, 1, 1),
    (ONWARD, 0, 2),
    (BESIDE, 1, 2),
    (BESIDE, 1, 3),
    (BESIDE, 0, 2),
    (ACROSS, 1, 1),
    (ONWARD, 0, 3),
    (ACROSS, 1, 2),
    (ACROSS, 1, 3),
    (ACROSS, 0, 2),
    (BESIDE, 0, 3),
    (ACROSS, 0, 3),
]


def gather_kernel(modes, *refs):
    n = len(modes)
    ins, refs = take(refs, [2 if mode in REST else 1 for mode in modes])
    outs, (lsem, ssem, rsem), bufs = refs[:n], refs[n : n + 3], list(refs[n + 3 :])
    bufs = {k: bufs.pop(0) for k, mode in enumerate(modes) if mode in REST}
    pairs, ins = ins, [group[0] for group in ins]
    x, y, z, c = place()
    ox, oy, oc = 1 - x, 1 - y, 1 - c
    greet(x, y, z, c, any(m in (SWAP, CROSS) for m in modes))
    sent = []

    def copy(k, src, dst, s, r, peer):
        return pltpu.make_async_remote_copy(
            src_ref=src,
            dst_ref=dst,
            send_sem=ssem.at[k, s],
            recv_sem=rsem.at[k, r],
            device_id=peer,
            device_id_type=MESH,
        )

    def send(cond, *args):
        when(cond, lambda: copy(*args).start())
        sent.append((cond, args))

    def arrived(cond, k, ref, r):
        when(cond, lambda: copy(k, ref, ref, 0, r, device(ox, y, z, c)).wait_recv())

    locals_ = []

    def keep(k, i, mine, spot):
        pltpu.make_async_copy(mine, spot, lsem.at[k, i]).start()
        locals_.append((k, i, mine, spot))

    def at(k, px, py, b):
        if modes[k] == BY_X:
            return outs[k].at[2 * b + px]
        if modes[k] == BY_Y:
            return outs[k].at[2 * b + py]
        return outs[k].at[block(px, py, b, c)]

    for k, mode in enumerate(modes):
        if mode in CHAINED:
            keep(k, 0, ins[k], at(k, x, y, z))
        elif mode == SWAP:
            keep(k, 0, ins[k].at[z], outs[k].at[z])
        elif mode == CROSS:
            keep(k, 0, ins[k].at[z], outs[k].at[block(x, y, z, c)])

    def share_of(k, i, core):
        b, j = i % 8 // 2, i % 2
        if modes[k] == REST_Y:
            return block(j, oy if i >= 8 else y, b, core)
        return block(ox if i >= 8 else x, j, b, core)

    def spread(k, cond, b, src, up, down):
        here = at(k, x, y, b)
        if modes[k] in CHAINED:
            if up is not False:
                send(both(cond, up), k, src, here, b, b, device(x, y, lax.rem(z + 1, ZN), c))
            if down is not False:
                send(both(cond, down), k, src, here, 4 + b, b, device(x, y, lax.rem(z + ZN - 1, ZN), c))
        if modes[k] != BY_Y:
            send(cond, k, src, here, 8 + b, 4 + b, device(ox, y, z, c))
        if modes[k] != BY_X:
            send(cond, k, src, here, 16 + b, 12 + b, device(x, oy, z, c))
        if modes[k] not in (BY_X, BY_Y):
            send(cond, k, src, here, 24 + b, 20 + b, device(x, y, z, oc))

    def sides(k, cond, b):
        fx, fy = at(k, ox, y, b), at(k, x, oy, b)
        full = modes[k] not in (BY_X, BY_Y)
        if modes[k] != BY_Y:
            arrived(cond, k, fx, 4 + b)
            first, _ = halves(fx)
            if full:
                send(cond, k, first, first, 20 + b, 16 + b, device(x, oy, z, c))
                send(cond, k, fx, fx, 28 + b, 24 + b, device(x, y, z, oc))
        if modes[k] != BY_X:
            arrived(cond, k, fy, 12 + b)
            _, second = halves(fy)
            if full and second is not None:
                send(cond, k, second, second, 12 + b, 8 + b, device(ox, y, z, c))
            if full:
                send(cond, k, fy, fy, 32 + b, 28 + b, device(x, y, z, oc))

    def corner(k, cond, b):
        far = outs[k].at[block(ox, oy, b, c)]
        first, second = halves(far)
        arrived(cond, k, first, 16 + b)
        if second is not None:
            arrived(cond, k, second, 8 + b)
        send(cond, k, far, far, 36 + b, 32 + b, device(x, y, z, oc))

    def steps(distance):
        if distance == 0:
            return [(None, z)]
        return [(z >= distance, jnp.maximum(z - distance, 0)), (z + distance < ZN, jnp.minimum(z + distance, ZN - 1))]

    chained = [k for k, mode in enumerate(modes) if mode in CHAINED]
    crossed = [k for k, mode in enumerate(modes) if mode == CROSS]
    swapped = [k for k, mode in enumerate(modes) if mode == SWAP]

    def exchange(ks):
        for k in ks:
            for d in range(1, ZN):
                to = lax.rem(z + d, ZN)
                spot = outs[k].at[z] if modes[k] == SWAP else outs[k].at[block(x, y, z, c)]
                send(None, k, ins[k].at[to], spot, to, z, device(x, y, to, c))

    for k in chained:
        spread(k, None, z, ins[k], z < ZN - 1, z > 0)
    if not chained:
        exchange(swapped)
        swapped = []
    for k, mode in enumerate(modes):
        if mode in REST:
            for i in range(16):
                src = pairs[k][i // 8].at[i % 8]
                pltpu.make_async_copy(src, bufs[k].at[i], lsem.at[k, i]).start()
                send(None, k, src, outs[k].at[share_of(k, i, c)], i, i, device(x, y, z, oc))
    for k in crossed:
        spread(k, None, z, ins[k].at[z], False, False)
    exchange(crossed)

    def onward(ks, distance):
        for side, (cond, b) in enumerate(steps(distance)):
            for k in ks:
                here = at(k, x, y, b)
                arrived(cond, k, here, b)
                spread(k, cond, b, here, z < ZN - 1 if side == 0 else False, z > 0 if side == 1 else False)

    def beside(ks, distance):
        for cond, b in steps(distance):
            for k in ks:
                sides(k, cond, b)

    def across(ks, distance):
        for cond, b in steps(distance):
            for k in ks:
                if modes[k] in (BCAST, CROSS):
                    corner(k, cond, b)

    plan = PLAN if crossed else SHORT_PLAN
    for fn, ks, distance in plan if chained else ():
        fn = {ONWARD: onward, BESIDE: beside, ACROSS: across}[fn]
        fn(chained if ks == 0 else crossed, distance)
        if fn is onward and distance == ZN - 1 and ks == 0:
            exchange(swapped)
            swapped = []
    exchange(swapped)
    for k in bufs:
        for i in range(16):
            pltpu.make_async_copy(pairs[k][0].at[0], bufs[k].at[i], lsem.at[k, i]).wait()
            keep(k, i, bufs[k].at[i], outs[k].at[share_of(k, i, c)])
    for k, mode in enumerate(modes):
        if mode == SWAP:
            for d in range(1, ZN):
                frm = lax.rem(z + d, ZN)
                arrived(None, k, outs[k].at[frm], frm)
        elif mode in REST:
            for i in range(16):
                arrived(None, k, outs[k].at[share_of(k, i, oc)], i)
        elif mode not in (BY_X, BY_Y):
            quads = (0, 1, 2, 3)
            for b in range(ZN):
                for j in quads:
                    px, py = ((x, y), (ox, y), (x, oy), (ox, oy))[j]
                    arrived(None, k, outs[k].at[block(px, py, b, oc)], 20 + 4 * j + b)
    for k, i, mine, spot in locals_:
        pltpu.make_async_copy(mine, spot, lsem.at[k, i]).wait()
    for cond, args in sent:
        when(cond, lambda args=args: copy(*args).wait_send())


def gather(arrays, modes, collective_id):
    shapes, inputs, operands, scratch = [], [], [], []
    anywhere, local = pl.BlockSpec(memory_space=pltpu.HBM), pl.BlockSpec(memory_space=pltpu.VMEM)
    for a, mode in zip(arrays, modes):
        inputs = inputs + ([anywhere] * 2 if mode in REST else [local])
        operands = operands + (list(a) if mode in REST else [a])
        if mode in REST:
            a = a[0]
            scratch.append(pltpu.VMEM((16,) + a.shape[1:], a.dtype))
        if mode == BCAST:
            shapes.append((BLOCKS,) + a.shape)
        elif mode in CHAINED:
            shapes.append((2 * ZN,) + a.shape)
        elif mode == SWAP:
            shapes.append(a.shape)
        else:
            shapes.append((BLOCKS,) + a.shape[1:])
    n = len(arrays)
    dtypes = [(a[0] if mode in REST else a).dtype for a, mode in zip(arrays, modes)]
    return pl.pallas_call(
        functools.partial(gather_kernel, tuple(modes)),
        out_shape=[jax.ShapeDtypeStruct(shape, dtype) for shape, dtype in zip(shapes, dtypes)],
        in_specs=inputs,
        out_specs=[anywhere] * n,
        scratch_shapes=[
            pltpu.SemaphoreType.DMA((n, 16)),
            pltpu.SemaphoreType.DMA((n, SENDS)),
            pltpu.SemaphoreType.DMA((n, RECVS)),
        ]
        + scratch,
        compiler_params=pltpu.CompilerParams(
            collective_id=collective_id, has_side_effects=True, vmem_limit_bytes=16 << 20
        ),
    )(*operands)


def chunk_of(cols):
    for size in (768, 640, 512, 384, 256, 128):
        if cols % size == 0:
            return size
    return cols


def add_up(dst, sources):
    rows, cols = dst.shape[-2:]
    tall = 32 if rows > 32 and rows % 32 == 0 else (16 if rows > 32 else rows)
    wide = cols if rows > 32 else chunk_of(cols)

    def step(i, carry):
        if rows > 32:
            spot = (pl.ds(pl.multiple_of(i * tall, tall), tall), slice(None))
        elif cols > wide:
            spot = (slice(None), pl.ds(pl.multiple_of(i * wide, wide), wide))
        else:
            spot = (slice(None), slice(None))
        total = sources[0][spot].astype(jnp.float32)
        for source in sources[1:]:
            total = total + source[spot].astype(jnp.float32)
        dst[spot] = total.astype(dst.dtype)
        return carry

    count = (rows // tall) * (cols // wide)
    if count == 1:
        step(0, 0)
    else:
        lax.fori_loop(0, count, step, 0)


BUFFERS = {PRODUCT: 5, TURNED_PRODUCT: 5, SWAP: 0, PAIR_X: 2, PAIR_Y: 2, CROSS: 3, REDUCE: 4, REST_X: 5, REST_Y: 5}
PAIR = (PAIR_X, PAIR_Y)
MADE = (PRODUCT, TURNED_PRODUCT)


def make(dst, left, right, turned):
    blocks, rows = dst.shape[:2]
    group = blocks // 8

    def step(i, carry):
        span = pl.ds(pl.multiple_of(i * group * rows, 32), group * rows)
        if turned:
            span = pl.ds(pl.multiple_of(i * group * rows, 128), group * rows)
            part = left[:, span].T
        else:
            part = left[span, :]
        total = jnp.dot(part, right[...], preferred_element_type=jnp.float32)
        for j in range(group):
            dst[i * group + j] = total[j * rows : (j + 1) * rows].astype(dst.dtype)
        return carry

    lax.fori_loop(0, blocks // group, step, 0)


def reduce_kernel(modes, *refs):
    n = len(modes)
    ins, refs = take(refs, [2 if mode in REST + MADE else 1 for mode in modes])
    outs, refs = refs[:n], refs[n:]
    (lsem, ssem, rsem), scratch = refs[:3], refs[3:]
    bufs, _ = take(scratch, [BUFFERS[mode] for mode in modes])
    others, ins = ins, [group[0] for group in ins]
    for k, mode in enumerate(modes):
        if mode in MADE:
            ins[k] = bufs[k][4]
    x, y, z, c = place()
    ox, oy, oc = 1 - x, 1 - y, 1 - c
    greet(x, y, z, c, any(m in (SWAP, CROSS) for m in modes))
    sent = []

    def copy(k, src, dst, s, r, peer):
        return pltpu.make_async_remote_copy(
            src_ref=src,
            dst_ref=dst,
            send_sem=ssem.at[k, s],
            recv_sem=rsem.at[k, r],
            device_id=peer,
            device_id_type=MESH,
        )

    def send(cond, *args):
        when(cond, lambda: copy(*args).start())
        sent.append((cond, args))

    def arrived(cond, k, ref, r):
        when(cond, lambda: copy(k, ref, ref, 0, r, device(ox, y, z, c)).wait_recv())

    half = z // 2
    order = [3 - 3 * half, 2 - half, 1 - z + 4 * half, z]
    quads = ((ox, oy), (ox, y), (x, oy), (x, y))
    active = [k for k, mode in enumerate(modes) if mode in (CROSS, REDUCE) + MADE]
    paired = [k for k, mode in enumerate(modes) if mode in PAIR]
    rest = [k for k, mode in enumerate(modes) if mode in REST]

    for k, mode in enumerate(modes):
        if mode == SWAP:
            for d in range(1, ZN):
                to = lax.rem(z + d, ZN)
                send(None, k, ins[k].at[to], outs[k].at[z], d, z, device(x, y, to, c))
            pltpu.make_async_copy(ins[k].at[z], outs[k].at[z], lsem.at[k, 0]).start()

    for k in rest:
        acc, rec, _, _, cor = bufs[k]
        for i, b in enumerate(order):
            for j in range(2):
                mine = (x, y)[modes[k] == REST_X]
                other = mine if j else 1 - mine
                px, py = (x, other) if modes[k] == REST_X else (other, y)
                at = 2 * i + j
                send(None, k, ins[k].at[block(px, py, b, oc)], cor.at[at], at, at, device(x, y, z, oc))
                pltpu.make_async_copy(ins[k].at[block(px, py, b, c)], acc.at[at], lsem.at[k, at]).start()
                pltpu.make_async_copy(others[k][1].at[2 * b + other], rec.at[at], lsem.at[k, 8 + at]).start()

    def begin(ks):
        for k in ks:
            if modes[k] in MADE:
                make(ins[k], *others[k], modes[k] == TURNED_PRODUCT)
            for i, b in enumerate(order):
                acc, cor = bufs[k][:2]
                for j, (px, py) in enumerate(quads):
                    send(None, k, ins[k].at[block(px, py, b, oc)], cor.at[4 * i + j], 4 * i + j, 4 * i + j, device(x, y, z, oc))
                    pltpu.make_async_copy(ins[k].at[block(px, py, b, c)], acc.at[4 * i + j], lsem.at[k, 4 * i + j]).start()

    begin([k for k in active if modes[k] == CROSS])

    for k in paired:
        acc, cor = bufs[k]
        for i in range(8):
            b, j = i // 2, i % 2
            px, py = (j, oy) if modes[k] == PAIR_Y else (ox, j)
            send(None, k, ins[k].at[block(px, py, b, oc)], cor.at[i], i, i, device(x, y, z, oc))
            pltpu.make_async_copy(ins[k].at[block(px, py, b, c)], acc.at[i], lsem.at[k, i]).start()

    def loaded(k, i, j):
        acc, cor = bufs[k][:2]
        pltpu.make_async_copy(ins[k].at[0], acc.at[4 * i + j], lsem.at[k, 4 * i + j]).wait()
        arrived(None, k, cor.at[4 * i + j], 4 * i + j)

    for k in paired:
        acc, cor = bufs[k]

        def join(i, carry, k=k, acc=acc, cor=cor):
            pltpu.make_async_copy(ins[k].at[0], acc.at[i], lsem.at[k, i]).wait()
            arrived(None, k, cor.at[i], i)
            add_up(outs[k].at[i], (acc.at[i], cor.at[i]))
            return carry

        lax.fori_loop(0, 8, join, 0)

    def fetched(k, i, j):
        acc, rec, _, _, cor = bufs[k]
        at = 2 * i + j
        pltpu.make_async_copy(ins[k].at[0], acc.at[at], lsem.at[k, at]).wait()
        pltpu.make_async_copy(ins[k].at[0], rec.at[at], lsem.at[k, 8 + at]).wait()
        arrived(None, k, cor.at[at], at)

    def ahead(k, i, b):
        acc, rec, side, _, cor = bufs[k]
        fetched(k, i, 0)
        add_up(acc.at[2 * i], (acc.at[2 * i], rec.at[2 * i], cor.at[2 * i]))
        peer = device(x, oy, z, c) if modes[k] == REST_X else device(ox, y, z, c)
        send(None, k, acc.at[2 * i], side.at[i], 16 + i, 16 + i, peer)

    def corner(k, i, b):
        acc, cor, side = bufs[k][:3]
        loaded(k, i, 0)
        add_up(acc.at[4 * i], (acc.at[4 * i], cor.at[4 * i]))
        first, second = halves(acc.at[4 * i])
        send(None, k, first, halves(side.at[i])[0], 16 + i, 16 + i, device(x, oy, z, c))
        if second is not None:
            send(None, k, second, halves(side.at[4 + i])[1], 20 + i, 20 + i, device(ox, y, z, c))

    def beside(k, i, b):
        acc, cor, side = bufs[k][:3]
        loaded(k, i, 1)
        add_up(acc.at[4 * i + 1], (acc.at[4 * i + 1], cor.at[4 * i + 1]))
        part = halves(side.at[i])[0]
        arrived(None, k, part, 16 + i)
        mine = halves(acc.at[4 * i + 1])[0]
        add_up(mine, (mine, part))
        send(None, k, acc.at[4 * i + 1], side.at[8 + i], 24 + i, 24 + i, device(ox, y, z, c))
        loaded(k, i, 2)
        add_up(acc.at[4 * i + 2], (acc.at[4 * i + 2], cor.at[4 * i + 2]))
        part = halves(side.at[4 + i])[1]
        if part is not None:
            arrived(None, k, part, 20 + i)
            mine = halves(acc.at[4 * i + 2])[1]
            add_up(mine, (mine, part))
        send(None, k, acc.at[4 * i + 2], side.at[12 + i], 28 + i, 28 + i, device(x, oy, z, c))

    def settle(k, i, b):
        side = bufs[k][2]
        if k in rest:
            acc, rec, _, _, cor = bufs[k]
            fetched(k, i, 1)
            arrived(None, k, side.at[i], 16 + i)
            own = acc.at[2 * i + 1]
            terms = (own, rec.at[2 * i + 1], cor.at[2 * i + 1], side.at[i])
        else:
            acc, cor = bufs[k][:2]
            loaded(k, i, 3)
            own = acc.at[4 * i + 3]
            arrived(None, k, side.at[8 + i], 24 + i)
            arrived(None, k, side.at[12 + i], 28 + i)
            terms = (own, cor.at[4 * i + 3], side.at[8 + i], side.at[12 + i])
        if modes[k] == CROSS:
            add_up(own, terms)
            if i < ZN - 1:
                send(None, k, own, outs[k].at[z], 32 + i, 32 + z, device(x, y, b, c))
            else:
                pltpu.make_async_copy(own, outs[k].at[z], lsem.at[k, 16]).start()
            return
        chain = bufs[k][3]
        if i == ZN - 1:
            add_up(outs[k], terms)

            def lower(k=k, chain=chain):
                arrived(None, k, chain.at[z], 32 + z)
                add_up(outs[k], (outs[k], chain.at[z]))

            def upper(k=k, chain=chain):
                arrived(None, k, chain.at[4 + z], 36 + z)
                add_up(outs[k], (outs[k], chain.at[4 + z]))

            pl.when(z > 0)(lower)
            pl.when(z < ZN - 1)(upper)
        else:
            add_up(own, terms)
            below = both(b > z, z > 0)
            above = both(b < z, z < ZN - 1)

            def lower(k=k, chain=chain, own=own, b=b):
                arrived(None, k, chain.at[b], 32 + b)
                add_up(own, (own, chain.at[b]))

            def upper(k=k, chain=chain, own=own, b=b):
                arrived(None, k, chain.at[4 + b], 36 + b)
                add_up(own, (own, chain.at[4 + b]))

            pl.when(below)(lower)
            pl.when(above)(upper)
            send(b > z, k, own, chain.at[b], 32 + i, 32 + b, device(x, y, lax.rem(z + 1, ZN), c))
            send(b < z, k, own, chain.at[4 + b], 32 + i, 36 + b, device(x, y, lax.rem(z + ZN - 1, ZN), c))

    crossed = [k for k in active if modes[k] == CROSS]
    plain = [k for k in active if modes[k] != CROSS]
    stages = [[(ahead, rest)], [(corner, crossed), (settle, rest)], [(corner, plain), (beside, crossed)]]
    stages = stages + [[(settle, crossed), (beside, plain)], [(settle, plain)]]
    for stage in stages:
        for i, b in enumerate(order):
            for fn, ks in stage:
                for k in ks:
                    if fn is not settle or k in crossed or i < ZN - 1:
                        fn(k, i, b)
        if stage is stages[0]:
            begin(plain)
    for k in rest + plain:
        settle(k, ZN - 1, z)
    for k, mode in enumerate(modes):
        if mode not in (SWAP, CROSS):
            continue
        for d in range(1, ZN):
            frm = lax.rem(z + d, ZN)
            arrived(None, k, outs[k].at[frm], frm if mode == SWAP else 32 + frm)
        if mode == SWAP:
            pltpu.make_async_copy(ins[k].at[z], outs[k].at[z], lsem.at[k, 0]).wait()
        else:
            pltpu.make_async_copy(bufs[k][0].at[15], outs[k].at[z], lsem.at[k, 16]).wait()
    for cond, args in sent:
        when(cond, lambda args=args: copy(*args).wait_send())


def reduce(arrays, modes, collective_id):
    shapes, specs, scratch, operands, inputs = [], [], [], [], []
    anywhere, local = pl.BlockSpec(memory_space=pltpu.HBM), pl.BlockSpec(memory_space=pltpu.VMEM)
    for a, mode in zip(arrays, modes):
        operands = operands + (list(a) if mode in REST + MADE else [a])
        inputs = inputs + [local if mode in MADE + (SWAP,) else anywhere] * (2 if mode in REST + MADE else 1)
        if mode in MADE:
            tall = a[0].shape[1] if mode == TURNED_PRODUCT else a[0].shape[0]
            shape = (BLOCKS, tall // BLOCKS, a[1].shape[1])
        else:
            a = a[0] if mode in REST else a
            shape = a.shape
        rows, cols = shape[1:]
        dtype = jnp.bfloat16 if mode in MADE else a.dtype
        sizes = {SWAP: (), CROSS: (16, 16, 16), REDUCE: (16, 16, 16, 8)}
        sizes.update({PAIR_X: (8, 8), PAIR_Y: (8, 8), REST_X: (8, 8, 4, 8, 8), REST_Y: (8, 8, 4, 8, 8)})
        sizes = sizes[REDUCE] + (BLOCKS,) if mode in MADE else sizes[mode]
        scratch = scratch + [pltpu.VMEM((size, rows, cols), dtype) for size in sizes]
        if mode == SWAP:
            shapes.append(jax.ShapeDtypeStruct(a.shape, a.dtype))
            specs.append(anywhere)
        elif mode in PAIR:
            shapes.append(jax.ShapeDtypeStruct((8, rows, cols), a.dtype))
            specs.append(local)
        elif mode == CROSS:
            shapes.append(jax.ShapeDtypeStruct((ZN, rows, cols), a.dtype))
            specs.append(anywhere)
        else:
            shapes.append(jax.ShapeDtypeStruct((rows, cols), jnp.float32))
            specs.append(local)
    n = len(arrays)
    return pl.pallas_call(
        functools.partial(reduce_kernel, tuple(modes)),
        out_shape=shapes,
        in_specs=inputs,
        out_specs=specs,
        scratch_shapes=[
            pltpu.SemaphoreType.DMA((n, 17)),
            pltpu.SemaphoreType.DMA((n, SENDS)),
            pltpu.SemaphoreType.DMA((n, SENDS)),
        ]
        + scratch,
        compiler_params=pltpu.CompilerParams(
            collective_id=collective_id, has_side_effects=True, vmem_limit_bytes=(48 if CROSS in modes else 16) << 20
        ),
    )(*operands)


HEAD = 64
GROUP = 3
TILE = 512
WIDE = 1024
EDGE = 128
SPAN = 4096
FAR = 1 << 30


def longest(lengths):
    begin, best, at = jnp.int32(0), lengths[0], jnp.int32(0)
    for j in range(lengths.shape[0]):
        length = lengths[j]
        at = jnp.where(length > best, begin, at)
        best = jnp.maximum(best, length)
        begin = begin + length
    return at, at + best


def lane_slots(lengths, count):
    x, y, z, c = place()
    lane = lax.broadcasted_iota(jnp.int32, (1, count), 1)
    begin, end = longest(lengths)
    spots = [block(x, y, b, c) * count + lane for b in range(ZN)]
    slots, before = [], jnp.zeros((1, count), jnp.int32)
    for b in range(ZN):
        big = jnp.logical_and(spots[b] >= begin, spots[b] < end)
        slots.append(jnp.where(big, before, ZN // 2 + b - before))
        before = before + big.astype(jnp.int32)
    return begin, end, spots, slots


def pick(slots, slot, parts):
    chosen = parts[-1]
    for b in range(len(parts) - 2, -1, -1):
        chosen = jnp.where(slots[b] == slot, parts[b], chosen)
    return chosen


def bounds_of(lengths, spot):
    low, high = jnp.zeros_like(spot), jnp.full_like(spot, FAR)
    begin = jnp.int32(0)
    for j in range(lengths.shape[0]):
        end = begin + lengths[j]
        low = jnp.where(spot >= begin, begin, low)
        high = jnp.where(spot < end, jnp.minimum(high, end), high)
        begin = end
    return low, high


def walk(big, begin, end, low, high, step, init):
    if big:
        base = begin // EDGE * EDGE

        def body(i, carry):
            at = pl.multiple_of(base + i * WIDE, EDGE)
            return step(at, WIDE, False, carry)

        carry = step(pl.multiple_of(base, EDGE), WIDE, True, init)
        carry = lax.fori_loop(1, SPAN // WIDE, body, carry)
        return lax.cond(
            begin > base,
            lambda c: step(pl.multiple_of(base + SPAN, EDGE), EDGE, True, c),
            lambda c: c,
            carry,
        )
    first = jnp.min(low) // TILE
    stop = (jnp.max(high) + TILE - 1) // TILE
    hole_first = jnp.maximum((begin + TILE - 1) // TILE, first)
    hole = jnp.maximum(jnp.minimum(end // TILE, stop) - hole_first, 0)

    def body(i, carry):
        tile = first + i
        tile = jnp.where(jnp.logical_and(hole > 0, tile >= hole_first), tile + hole, tile)
        return step(pl.multiple_of(tile * TILE, TILE), TILE, True, carry)

    return lax.fori_loop(0, stop - first - hole, body, init)


def keys_in(first, size, low, high):
    at = first + lax.broadcasted_iota(jnp.int32, (size, low.shape[1]), 0)
    return jnp.logical_and(at >= low, at < high)


def dot(a, b):
    return jnp.dot(a, b, preferred_element_type=jnp.float32)


def pad_heads(rows, h, slots):
    part = rows[h * HEAD : (h + 1) * HEAD]
    zero = jnp.zeros_like(part)
    return jnp.concatenate([part if s == h else zero for s in slots], axis=0)


Q_SLOTS = (0, 1, 2, -1)
V_SLOTS = (-1, 2, 0, 1)


def forward_kernel(lengths, qt, kv, low_out, out, lse_out, qm, acc, qs, os, ls):
    count = qt.shape[2]
    begin, end, spots, slots = lane_slots(lengths, count)
    for s in range(ZN):
        qs[s] = pick(slots, s, [qt[b] for b in range(ZN)])

    def one_block(big, s, carry):
        low, high = bounds_of(lengths, pick(slots, s, spots))
        rows = qs[s] * jnp.bfloat16(0.125)
        for h in range(GROUP):
            qm[h] = pad_heads(rows, h, Q_SLOTS)
        acc[...] = jnp.zeros_like(acc)

        def step(at, size, masked, stats):
            span = pl.ds(at, size)
            keys = kv[span, 0:256]
            values = kv[span, 128:384].T
            mask = keys_in(at, size, low, high) if masked else None
            fresh = []
            for h in range(GROUP):
                top, total = stats[2 * h], stats[2 * h + 1]
                scores = dot(keys, qm[h])
                if masked:
                    scores = jnp.where(mask, scores, -1e9)
                new_top = jnp.maximum(top, jnp.max(scores, axis=0, keepdims=True))
                shrink = jnp.exp(top - new_top)
                weights = jnp.exp(scores - new_top)
                total = total * shrink + jnp.sum(weights, axis=0, keepdims=True)
                row = V_SLOTS.index(h) * HEAD
                acc[h] = acc[h] * shrink + dot(values[row : row + HEAD], weights.astype(jnp.bfloat16))
                fresh = fresh + [new_top, total]
            return tuple(fresh)

        init = (jnp.full((1, count), -1e9, jnp.float32), jnp.zeros((1, count), jnp.float32)) * GROUP
        stats = walk(big, begin, end, low, high, step, init)
        for h in range(GROUP):
            top, total = stats[2 * h], stats[2 * h + 1]
            os[s, h * HEAD : (h + 1) * HEAD] = acc[h] / total
            ls[s, h : h + 1] = top + jnp.log(total)
        return carry

    lax.fori_loop(0, ZN // 2, functools.partial(one_block, True), 0)
    lax.fori_loop(ZN // 2, ZN, functools.partial(one_block, False), 0)
    for b in range(ZN):
        value = pick([jnp.full_like(slots[b], s) for s in range(ZN)], slots[b], [os[s] for s in range(ZN)])
        out[b] = value
        low_out[b] = value.astype(low_out.dtype)
        lse_out[b] = pick([jnp.full_like(slots[b], s) for s in range(ZN)], slots[b], [ls[s] for s in range(ZN)])


def attend(lengths, qt, kv):
    blocks, rows, count = qt.shape
    whole = pl.BlockSpec(memory_space=pltpu.VMEM)
    return pl.pallas_call(
        forward_kernel,
        out_shape=[
            jax.ShapeDtypeStruct(qt.shape, jnp.bfloat16),
            jax.ShapeDtypeStruct(qt.shape, jnp.float32),
            jax.ShapeDtypeStruct((blocks, 8, count), jnp.float32),
        ],
        in_specs=[pl.BlockSpec(memory_space=pltpu.SMEM), whole, whole],
        out_specs=[whole] * 3,
        scratch_shapes=[
            pltpu.VMEM((GROUP, 256, count), jnp.bfloat16),
            pltpu.VMEM((GROUP, HEAD, count), jnp.float32),
            pltpu.VMEM(qt.shape, jnp.bfloat16),
            pltpu.VMEM(qt.shape, jnp.float32),
            pltpu.VMEM((blocks, 8, count), jnp.float32),
        ],
        compiler_params=pltpu.CompilerParams(vmem_limit_bytes=32 << 20),
    )(lengths, qt, kv)


def backward_kernel(lengths, qt, kv, out, lse, dot_in, cosine, sine, dq_out, dkv_out, qmt, qm, dmt, dm, dq, acc, qs, ds, es, ls, dqs):
    count = qt.shape[2]
    tiles = kv.shape[0] // TILE

    def clear(tile, carry):
        acc[pl.ds(pl.multiple_of(tile * TILE, TILE), TILE), :] = jnp.zeros((TILE, acc.shape[1]), jnp.float32)
        return carry

    lax.fori_loop(0, tiles, clear, 0)

    begin, end, spots, slots = lane_slots(lengths, count)
    for b in range(ZN):
        product_rows = dot_in[b].astype(jnp.float32) * out[b]
        for h in range(GROUP):
            es[b, h : h + 1] = jnp.sum(product_rows[h * HEAD : (h + 1) * HEAD], axis=0, keepdims=True)
    for s in range(ZN):
        qs[s] = pick(slots, s, [qt[b] for b in range(ZN)])
        ds[s] = pick(slots, s, [dot_in[b] for b in range(ZN)])
        ls[s] = pick(slots, s, [lse[b] for b in range(ZN)])
    picked = [pick(slots, s, [es[b] for b in range(ZN)]) for s in range(ZN)]
    for s in range(ZN):
        es[s] = picked[s]

    def one_block(big, s, carry):
        low, high = bounds_of(lengths, pick(slots, s, spots))
        rows = qs[s] * jnp.bfloat16(0.125)
        grads = ds[s]
        deltas = [es[s, h : h + 1] for h in range(GROUP)]
        levels = [ls[s, h : h + 1] for h in range(GROUP)]
        for h in range(GROUP):
            padded = pad_heads(rows, h, Q_SLOTS)
            qmt[h] = padded
            qm[h * count : (h + 1) * count] = padded.T
            padded = pad_heads(grads, h, V_SLOTS)
            dmt[h] = padded
            dm[h * count : (h + 1) * count] = padded.T
        dq[...] = jnp.zeros_like(dq)

        def step(at, size, masked, inner):
            span = pl.ds(at, size)
            keys = kv[span, 0:256]
            values = kv[span, 128:384]
            turned = keys.T
            mask = keys_in(at, size, low, high) if masked else None
            probs, slopes = [], []
            for h in range(GROUP):
                weights = jnp.exp(dot(keys, qmt[h]) - levels[h])
                if masked:
                    weights = jnp.where(mask, weights, 0.0)
                slope = (weights * (dot(values, dmt[h]) - deltas[h])).astype(jnp.bfloat16)
                dq[h] += dot(turned[h * HEAD : (h + 1) * HEAD], slope)
                probs.append(weights.astype(jnp.bfloat16))
                slopes.append(slope)
            dv = dot(jnp.concatenate(probs, axis=1), dm[...])
            dk = dot(jnp.concatenate(slopes, axis=1), qm[...])
            acc[span, 0:128] += dk[:, :128]
            acc[span, 128:256] += dk[:, 128:] + dv[:, :128]
            acc[span, 256:384] += dv[:, 128:]
            return inner

        walk(big, begin, end, low, high, step, 0)
        for h in range(GROUP):
            dqs[s, h * HEAD : (h + 1) * HEAD] = dq[h] * 0.125
        return carry

    lax.fori_loop(0, ZN // 2, functools.partial(one_block, True), 0)
    lax.fori_loop(ZN // 2, ZN, functools.partial(one_block, False), 0)
    half = HEAD // 2
    for b in range(ZN):
        back = pick([jnp.full_like(slots[b], s) for s in range(ZN)], slots[b], [dqs[s] for s in range(ZN)])
        for h in range(GROUP):
            at = h * HEAD
            w1, w2 = back[at : at + half], back[at + half : at + HEAD]
            dq_out[b, at : at + half] = (w1 * cosine[b] + w2 * sine[b]).astype(dq_out.dtype)
            dq_out[b, at + half : at + HEAD] = (w2 * cosine[b] - w1 * sine[b]).astype(dq_out.dtype)

    def finish(tile, carry):
        span = pl.ds(pl.multiple_of(tile * TILE, TILE), TILE)
        dkv_out[span, :] = acc[span, :].astype(dkv_out.dtype)
        return carry

    lax.fori_loop(0, tiles, finish, 0)


def attend_back(lengths, qt, kv, out, lse, dots, cosine, sine):
    blocks, rows, count = qt.shape
    whole = pl.BlockSpec(memory_space=pltpu.VMEM)
    return pl.pallas_call(
        backward_kernel,
        out_shape=[
            jax.ShapeDtypeStruct(qt.shape, jnp.bfloat16),
            jax.ShapeDtypeStruct(kv.shape, jnp.bfloat16),
        ],
        in_specs=[pl.BlockSpec(memory_space=pltpu.SMEM)] + [whole] * 7,
        out_specs=[whole] * 2,
        scratch_shapes=[
            pltpu.VMEM((GROUP, 256, count), jnp.bfloat16),
            pltpu.VMEM((GROUP * count, 256), jnp.bfloat16),
            pltpu.VMEM((GROUP, 256, count), jnp.bfloat16),
            pltpu.VMEM((GROUP * count, 256), jnp.bfloat16),
            pltpu.VMEM((GROUP, HEAD, count), jnp.float32),
            pltpu.VMEM(kv.shape, jnp.float32),
            pltpu.VMEM(qt.shape, jnp.bfloat16),
            pltpu.VMEM(qt.shape, jnp.bfloat16),
            pltpu.VMEM((blocks, 8, count), jnp.float32),
            pltpu.VMEM((blocks, 8, count), jnp.float32),
            pltpu.VMEM(qt.shape, jnp.float32),
        ],
        compiler_params=pltpu.CompilerParams(vmem_limit_bytes=52 << 20),
    )(lengths, qt, kv, out, lse, dots, cosine, sine)


KV_SLOTS = (0, 1, 2, 5, 3, 4)


def turn(rows, cosine, sine):
    first, second = rows[:, 0], rows[:, 1]
    return jnp.stack([first * cosine - second * sine, second * cosine + first * sine], axis=1)


def turn_back(rows, cosine, sine):
    first, second = rows[:, 0], rows[:, 1]
    return jnp.stack([first * cosine + second * sine, second * cosine - first * sine], axis=1)


def tables(lengths, first, count):
    starts = jnp.cumsum(lengths) - lengths
    position = first[:, None] + jnp.arange(count, dtype=jnp.int32)[None, :]
    begun = position[..., None] >= starts
    offsets = position - jnp.max(jnp.where(begun, starts, 0), axis=-1)
    half = HEAD // 2
    frequency = rope_base ** (-(jnp.arange(half, dtype=jnp.float32) * 2.0) / HEAD)
    angles = offsets.astype(jnp.float32)[:, None, :] * frequency[None, :, None]
    return jnp.cos(angles), jnp.sin(angles)


def norm_back(upstream, scaled, inv_std, gain_vec):
    weighted = upstream * gain_vec
    inner = (
        weighted
        - jnp.mean(weighted, axis=-1, keepdims=True)
        - scaled * jnp.mean(weighted * scaled, axis=-1, keepdims=True)
    )
    sums = [jnp.sum(upstream * scaled, axis=0, keepdims=True), jnp.sum(upstream, axis=0, keepdims=True)]
    return inv_std * inner, sums


def contract(left, right, dims):
    return lax.dot_general(left, right, (dims, ((), ())), preferred_element_type=jnp.float32)


def copies_kernel(*refs):
    n = len(refs) // 3
    ins, outs, bufs, sems = refs[:n], refs[n : 2 * n], refs[2 * n : 3 * n], refs[3 * n]
    loads = [pltpu.make_async_copy(ins[k], bufs[k], sems.at[k]) for k in range(n)]
    stores = [pltpu.make_async_copy(bufs[k], outs[k], sems.at[n + k]) for k in range(n)]
    for load in loads:
        load.start()
    for load, store in zip(loads, stores):
        load.wait()
        store.start()
    for store in stores:
        store.wait()


def copies(arrays):
    n = len(arrays)
    anywhere = pl.BlockSpec(memory_space=pltpu.HBM)
    return pl.pallas_call(
        copies_kernel,
        out_shape=[jax.ShapeDtypeStruct(a.shape, a.dtype) for a in arrays],
        in_specs=[anywhere] * n,
        out_specs=[anywhere] * n,
        scratch_shapes=[pltpu.VMEM(a.shape, a.dtype) for a in arrays] + [pltpu.SemaphoreType.DMA((2 * n,))],
    )(*arrays)


def local_grid(
    tokens,
    qkv_weight,
    out_weight,
    gate_weight,
    up_weight,
    down_weight,
    first_gain,
    first_bias,
    second_gain,
    second_bias,
    lengths,
    cotangent,
):
    bf16 = jnp.bfloat16
    rows, width = tokens.shape
    share = first_gain.shape[0]
    heads = width // HEAD
    half = HEAD // 2
    x, y, z, c = place()
    spots = [(px, py, pz, pc) for pz in range(ZN) for py in range(YN) for pc in range(CN) for px in range(XN)]
    over_x = [(block(*p), block(1 - p[0], *p[1:])) for p in spots]
    over_y = [(block(*p), block(p[0], 1 - p[1], *p[2:])) for p in spots]
    small = jnp.stack([first_gain, first_bias, second_gain, second_bias])
    small = jnp.pad(small, ((0, 4), (0, 128 - share)))
    hidden_width = gate_weight.shape[1]

    (qkv_blocks,) = gather([qkv_weight], [BCAST], 1)
    qkv_full = qkv_blocks.reshape(width, 3 * width)
    turned = jnp.stack([block(x, y, b, c) for b in range(ZN)]) * rows
    cos_all, sin_all = tables(lengths, turned, rows)
    cosine = lax.dynamic_index_in_dim(cos_all, z, 0, keepdims=False)
    sine = lax.dynamic_index_in_dim(sin_all, z, 0, keepdims=False)

    raw = contract(qkv_full, tokens, ((0,), (1,))).astype(bf16)
    raw = raw.reshape(3, heads, 2, half, rows)
    queries = turn(raw[0].astype(jnp.float32), cosine, sine).astype(bf16)
    keys = turn(raw[1].astype(jnp.float32), cosine, sine).astype(bf16)
    queries = queries.reshape(ZN, GROUP * HEAD, rows)
    pairs = jnp.concatenate(
        [keys.reshape(ZN, GROUP, HEAD, rows), raw[2].reshape(ZN, GROUP, HEAD, rows)], axis=1
    )
    pairs = jnp.concatenate([pairs[:, s : s + 1] for s in KV_SLOTS], axis=1)
    pairs = jnp.swapaxes(pairs.reshape(ZN, 2 * GROUP * HEAD, rows), 1, 2)

    pairs_all, queries, out_full, down_full, small, gate_part, up_part = gather(
        [pairs, queries, out_weight, down_weight, small, gate_weight, up_weight],
        [CROSS, SWAP, BCAST, BCAST, BCAST, BY_X, BY_Y],
        2,
    )
    out_full = out_full.reshape(width, width)
    gate_rest = lax.ppermute(gate_part, ("cp", "hd"), over_y)
    up_rest = lax.ppermute(up_part, ("cp", "hd"), over_x)
    down_full = down_full.reshape(hidden_width, width)
    small = jnp.swapaxes(small[:, :4, :share], 0, 1).astype(jnp.float32).reshape(4, width)
    small = lax.optimization_barrier(small)
    gain_one, bias_one, gain_two, bias_two = [small[i] for i in range(4)]
    pairs_all = pairs_all.reshape(-1, 2 * GROUP * HEAD)
    low, attended, lse = attend(lengths, queries, pairs_all)
    low, gate_full, up_full = gather(
        [low, (gate_part, gate_rest), (up_part, up_rest)], [SWAP, REST_Y, REST_X], 3
    )
    gate_full = gate_full.reshape(width, hidden_width)
    up_full = up_full.reshape(width, hidden_width)
    low = low.reshape(width, rows)

    attn_out = contract(low, out_full, ((0,), (0,)))
    first, scaled_one, inv_one = normalize(tokens.astype(jnp.float32) + attn_out, gain_one, bias_one)
    first_low = first.astype(bf16)
    gate_proj = product(first_low, gate_full)
    up_proj = product(first_low, up_full)
    sigmoid_gate = jax.nn.sigmoid(gate_proj)
    silu_gate = gate_proj * sigmoid_gate
    hidden = (silu_gate * up_proj).astype(bf16)
    branch = product(hidden, down_full)
    second, scaled_two, inv_two = normalize(first + branch, gain_two, bias_two)
    layer_out = second.astype(bf16)

    upstream = cotangent.astype(jnp.float32)
    dz_two, sums_two = norm_back(upstream, scaled_two, inv_two, gain_two)
    dz_two_low = dz_two.astype(bf16)
    hidden_grad = contract(dz_two_low, down_full, ((1,), (1,)))
    gate_back = (
        hidden_grad * up_proj * sigmoid_gate * (1.0 + gate_proj * (1.0 - sigmoid_gate))
    ).astype(bf16)
    up_back = (hidden_grad * silu_gate).astype(bf16)
    gate_sum = contract(first_low, gate_back, ((0,), (0,))).astype(bf16)
    up_sum = contract(first_low, up_back, ((0,), (0,))).astype(bf16)
    first_back = (
        dz_two + contract(gate_back, gate_full, ((1,), (1,))) + contract(up_back, up_full, ((1,), (1,)))
    )
    dz_one, sums_one = norm_back(first_back, scaled_one, inv_one, gain_one)
    dz_one_low = dz_one.astype(bf16)
    attended_back = contract(out_full, dz_one_low, ((1,), (1,))).astype(bf16)
    gate_sum = gate_sum.reshape((BLOCKS,) + gate_weight.shape)
    up_sum = up_sum.reshape((BLOCKS,) + up_weight.shape)
    attended_back, gate_send, up_send = reduce(
        [attended_back.reshape(ZN, GROUP * HEAD, rows), gate_sum, up_sum], [SWAP, PAIR_Y, PAIR_X], 4
    )
    gate_rest = lax.ppermute(gate_send, ("cp", "hd"), over_y)
    up_rest = lax.ppermute(up_send, ("cp", "hd"), over_x)

    query_back, pair_back = attend_back(
        lengths, queries, pairs_all, attended, lse, attended_back, cos_all, sin_all
    )
    small_sum = lax.optimization_barrier(jnp.concatenate(sums_one + sums_two, axis=0))
    small_sum = jnp.swapaxes(small_sum.reshape(4, BLOCKS, share), 0, 1)
    small_sum = jnp.pad(small_sum, ((0, 0), (0, 4), (0, 128 - share)))
    pair_back, query_back, out_grad, down_grad, small_grad, gate_grad, up_grad = reduce(
        [
            pair_back.reshape(BLOCKS, rows, 2 * GROUP * HEAD),
            query_back,
            (low, dz_one_low),
            (hidden, dz_two_low),
            small_sum,
            (gate_sum, gate_rest),
            (up_sum, up_rest),
        ],
        [CROSS, SWAP, PRODUCT, TURNED_PRODUCT, REDUCE, REST_Y, REST_X],
        5,
    )
    pair_back = jnp.swapaxes(pair_back, 1, 2).reshape(ZN, 2 * GROUP, HEAD, rows)
    pair_back = [pair_back[:, KV_SLOTS.index(s)] for s in range(2 * GROUP)]
    key_back = jnp.stack(pair_back[:GROUP], axis=1).reshape(heads, 2, half, rows)
    key_back = turn_back(key_back.astype(jnp.float32), cosine, sine).astype(bf16)
    value_back = jnp.stack(pair_back[GROUP:], axis=1)
    raw_back = jnp.concatenate(
        [
            query_back.reshape(width, rows),
            key_back.reshape(width, rows),
            value_back.reshape(width, rows),
        ],
        axis=0,
    )
    qkv_sum = contract(tokens, raw_back, ((0,), (1,))).astype(bf16)
    tokens_grad = (dz_one + contract(raw_back, qkv_full, ((0,), (1,)))).astype(bf16)
    (qkv_grad,) = reduce([qkv_sum.reshape(BLOCKS, share, 3 * width)], [REDUCE], 6)
    qkv_grad, out_grad, gate_grad, up_grad, down_grad = copies([qkv_grad, out_grad, gate_grad, up_grad, down_grad])
    return (
        layer_out,
        tokens_grad,
        qkv_grad,
        out_grad,
        gate_grad,
        up_grad,
        down_grad,
        small_grad[0, :share],
        small_grad[1, :share],
        small_grad[2, :share],
        small_grad[3, :share],
    )


def solution(mesh):
    rows = P(("cp", "hd"), None)
    line = P(("cp", "hd"))
    local = local_grid if (mesh.shape["cp"], mesh.shape["hd"]) == (ZN * YN * CN, XN) else local_any
    return jax.shard_map(
        local,
        mesh=mesh,
        in_specs=(rows,) * 6 + (line,) * 4 + (P(), rows),
        out_specs=(rows,) * 7 + (line,) * 4,
        check_vma=False,
    )
```

```python
import functools

import jax
import jax.numpy as jnp
from jax import lax
from jax.experimental import pallas as pl
from jax.experimental.pallas import tpu as pltpu
from jax.sharding import PartitionSpec as P

HD = 64
REACH = 8


rope_base = 1000.0
norm_eps = 1e-12
score_scale = 0.125
masked_score = -1000000000.0


def shifted(block, axis, distance):
    devices = range(lax.axis_size(axis))
    route = [(i - distance, i) for i in devices if i - distance in devices]
    return lax.ppermute(block, axis, route)


def doc_layout(lengths, first_row, row_count):
    starts = jnp.cumsum(lengths) - lengths
    position = first_row + jnp.arange(row_count, dtype=jnp.int32)
    at_or_after = position[:, None] >= starts[None, :]
    doc_ids = jnp.sum(at_or_after.astype(jnp.int32), axis=1) - 1
    doc_begin = jnp.max(jnp.where(at_or_after, starts[None, :], 0), axis=1)
    return (doc_ids, position - doc_begin)


def rope_tables(offsets, head_size):
    half_size = head_size // 2
    frequency = rope_base ** (-(jnp.arange(half_size, dtype=jnp.float32) * 2.0) / head_size)
    angles = offsets.astype(jnp.float32)[:, None] * frequency[None, :]
    return (jnp.cos(angles), jnp.sin(angles))


def rotate(values, cosine, sine):
    half_size = values.shape[-1] // 2
    first_half = values[..., :half_size]
    second_half = values[..., half_size:]
    cos_rows = cosine[:, None, :]
    sin_rows = sine[:, None, :]
    return jnp.concatenate(
        [
            first_half * cos_rows - second_half * sin_rows,
            second_half * cos_rows + first_half * sin_rows,
        ],
        axis=-1,
    )


def rotate_back(grads, cosine, sine):
    half_size = grads.shape[-1] // 2
    first_half = grads[..., :half_size]
    second_half = grads[..., half_size:]
    cos_rows = cosine[:, None, :]
    sin_rows = sine[:, None, :]
    return jnp.concatenate(
        [
            first_half * cos_rows + second_half * sin_rows,
            second_half * cos_rows - first_half * sin_rows,
        ],
        axis=-1,
    )


def normalize(hidden_in, gain_vec, bias_vec):
    average = jnp.mean(hidden_in, axis=-1, keepdims=True)
    centered = hidden_in - average
    variance = jnp.mean(centered * centered, axis=-1, keepdims=True)
    inv_std = lax.rsqrt(variance + norm_eps)
    scaled = centered * inv_std
    return (scaled * gain_vec + bias_vec, scaled, inv_std)


def normalize_back(upstream, scaled, inv_std, gain_vec):
    weighted = upstream * gain_vec
    inner = (
        weighted
        - jnp.mean(weighted, axis=-1, keepdims=True)
        - scaled * jnp.mean(weighted * scaled, axis=-1, keepdims=True)
    )
    return (inv_std * inner, jnp.sum(upstream * scaled, axis=0), jnp.sum(upstream, axis=0))


def product(left, right):
    return jnp.dot(left, right, preferred_element_type=jnp.float32)


def local_any(
    tokens,
    qkv_weight,
    out_weight,
    gate_weight,
    up_weight,
    down_weight,
    first_gain,
    first_bias,
    second_gain,
    second_bias,
    doc_lengths,
    cotangent,
):
    rows_here = tokens.shape[0]
    model_width = tokens.shape[1]
    hd_count = lax.axis_size("hd")
    cp_count = lax.axis_size("cp")
    cp_index = lax.axis_index("cp")
    block_rows = rows_here * hd_count
    local_width = model_width // hd_count
    local_heads = local_width // HD
    shifts = [0]
    for distance in range(1, REACH + 1):
        shifts = shifts + [-distance, distance]
    shards = (
        qkv_weight,
        out_weight,
        gate_weight,
        up_weight,
        down_weight,
        first_gain,
        first_bias,
        second_gain,
        second_bias,
    )
    weights = (
        lax.all_gather(shards[0], ("cp", "hd"), axis=0, tiled=True),
        lax.all_gather(shards[1], ("cp", "hd"), axis=0, tiled=True),
        lax.all_gather(shards[2], ("cp", "hd"), axis=0, tiled=True),
        lax.all_gather(shards[3], ("cp", "hd"), axis=0, tiled=True),
        lax.all_gather(shards[4], ("cp", "hd"), axis=0, tiled=True),
        lax.all_gather(shards[5], ("cp", "hd"), axis=0, tiled=True),
        lax.all_gather(shards[6], ("cp", "hd"), axis=0, tiled=True),
        lax.all_gather(shards[7], ("cp", "hd"), axis=0, tiled=True),
        lax.all_gather(shards[8], ("cp", "hd"), axis=0, tiled=True),
    )
    (
        qkv_full,
        out_full,
        gate_full,
        up_full,
        down_full,
        gain_first,
        bias_first,
        gain_second,
        bias_second,
    ) = weights
    raw_rows = product(tokens, qkv_full).astype(jnp.bfloat16)
    grouped = lax.all_to_all(
        raw_rows.reshape(rows_here, 3, hd_count, local_width),
        "hd",
        split_axis=2,
        concat_axis=0,
        tiled=True,
    )
    grouped = grouped.reshape(block_rows, 3, local_width)
    query_docs, offsets = doc_layout(doc_lengths, cp_index * block_rows, block_rows)
    cosine, sine = rope_tables(offsets, HD)
    queries = rotate(
        grouped[:, 0].astype(jnp.float32).reshape(block_rows, local_heads, HD), cosine, sine
    ).astype(jnp.bfloat16)
    key_rows = rotate(
        grouped[:, 1].astype(jnp.float32).reshape(block_rows, local_heads, HD), cosine, sine
    ).astype(jnp.bfloat16)
    own_block = jnp.stack([key_rows.reshape(block_rows, local_width), grouped[:, 2]], axis=1)

    def key_docs(distance):
        source = cp_index - distance
        doc_ids, unused_offsets = doc_layout(doc_lengths, source * block_rows, block_rows)
        inside = jnp.logical_and(source >= 0, source < cp_count)
        return jnp.where(inside, doc_ids, -2)

    remote = [own_block] + [shifted(own_block, "cp", distance) for distance in shifts[1:]]
    masks = [query_docs[:, None] == key_docs(distance)[None, :] for distance in shifts]

    def scores_with(query_part, remote_block, key_mask):
        key_part = remote_block[:, 0].reshape(block_rows, local_heads, HD)
        raw_scores = (
            jnp.einsum("qhd,khd->hqk", query_part, key_part, preferred_element_type=jnp.float32)
            * score_scale
        )
        return jnp.where(key_mask[None], raw_scores, masked_score)

    def scores_for(remote_block, key_mask):
        return scores_with(queries, remote_block, key_mask)

    running_max = jnp.full((local_heads, block_rows), masked_score, jnp.float32)
    running_sum = jnp.zeros((local_heads, block_rows), jnp.float32)
    for remote_block, key_mask in zip(remote, masks):
        block_scores = scores_for(remote_block, key_mask)
        new_max = jnp.maximum(running_max, jnp.max(block_scores, axis=-1))
        running_sum = running_sum * jnp.exp(running_max - new_max) + jnp.sum(
            jnp.exp(block_scores - new_max[:, :, None]), axis=-1
        )
        running_max = new_max
    log_total = running_max + jnp.log(running_sum)
    attended = jnp.zeros((block_rows, local_heads, HD), jnp.float32)
    for remote_block, key_mask in zip(remote, masks):
        block_scores = scores_for(remote_block, key_mask)
        probs = jnp.exp(block_scores - log_total[:, :, None]).astype(jnp.bfloat16)
        value_part = remote_block[:, 1].reshape(block_rows, local_heads, HD)
        attended = attended + jnp.einsum(
            "hqk,khd->qhd", probs, value_part, preferred_element_type=jnp.float32
        )
    attended_send = attended.reshape(block_rows, 1, local_width).astype(jnp.bfloat16)
    attended_low = lax.all_to_all(
        attended_send, "hd", split_axis=0, concat_axis=1, tiled=True
    ).reshape(rows_here, model_width)
    gain_one = gain_first.astype(jnp.float32)
    gain_two = gain_second.astype(jnp.float32)
    attn_out = product(attended_low, out_full)
    first, scaled_one, inv_one = normalize(
        tokens.astype(jnp.float32) + attn_out, gain_one, bias_first.astype(jnp.float32)
    )
    first_low = first.astype(jnp.bfloat16)
    gate_proj = product(first_low, gate_full)
    up_proj = product(first_low, up_full)
    sigmoid_gate = jax.nn.sigmoid(gate_proj)
    silu_gate = gate_proj * sigmoid_gate
    hidden = (silu_gate * up_proj).astype(jnp.bfloat16)
    branch = product(hidden, down_full)
    second, scaled_two, inv_two = normalize(
        first + branch, gain_two, bias_second.astype(jnp.float32)
    )
    layer_out = second.astype(jnp.bfloat16)
    weights = (
        lax.all_gather(shards[0], ("cp", "hd"), axis=0, tiled=True),
        lax.all_gather(shards[1], ("cp", "hd"), axis=0, tiled=True),
        lax.all_gather(shards[2], ("cp", "hd"), axis=0, tiled=True),
        lax.all_gather(shards[3], ("cp", "hd"), axis=0, tiled=True),
        lax.all_gather(shards[4], ("cp", "hd"), axis=0, tiled=True),
        lax.all_gather(shards[5], ("cp", "hd"), axis=0, tiled=True),
        lax.all_gather(shards[6], ("cp", "hd"), axis=0, tiled=True),
        lax.all_gather(shards[7], ("cp", "hd"), axis=0, tiled=True),
        lax.all_gather(shards[8], ("cp", "hd"), axis=0, tiled=True),
    )
    (
        qkv_full,
        out_full,
        gate_full,
        up_full,
        down_full,
        gain_first,
        bias_first,
        gain_second,
        bias_second,
    ) = weights
    upstream = cotangent.astype(jnp.float32)
    dz_two, gain_two_grad, bias_two_grad = normalize_back(upstream, scaled_two, inv_two, gain_two)
    dz_two_low = dz_two.astype(jnp.bfloat16)
    down_sum = product(hidden.T, dz_two_low)
    hidden_grad = product(dz_two_low, down_full.T)
    gate_back = (
        hidden_grad * up_proj * sigmoid_gate * (1.0 + gate_proj * (1.0 - sigmoid_gate))
    ).astype(jnp.bfloat16)
    up_back = (hidden_grad * silu_gate).astype(jnp.bfloat16)
    gate_sum = product(first_low.T, gate_back)
    up_sum = product(first_low.T, up_back)
    first_back = dz_two + product(gate_back, gate_full.T) + product(up_back, up_full.T)
    dz_one, gain_one_grad, bias_one_grad = normalize_back(first_back, scaled_one, inv_one, gain_one)
    dz_one_low = dz_one.astype(jnp.bfloat16)
    out_sum = product(attended_low.T, dz_one_low)
    attended_back = product(dz_one_low, out_full.T).astype(jnp.bfloat16)
    heads_back = lax.all_to_all(
        attended_back.reshape(rows_here, hd_count, local_width),
        "hd",
        split_axis=1,
        concat_axis=0,
        tiled=True,
    )
    heads_back = heads_back.reshape(block_rows, local_heads, HD)
    delta = jnp.transpose(jnp.sum(heads_back.astype(jnp.float32) * attended, axis=-1))
    query_grad = jnp.zeros((block_rows, local_heads, HD), jnp.float32)
    pair_total = jnp.zeros((block_rows, 2, local_width), jnp.float32)
    remote = [own_block] + [shifted(own_block, "cp", distance) for distance in shifts[1:]]
    for distance, remote_block, key_mask in zip(shifts, remote, masks):
        pair_block_scores = scores_with(queries, remote_block, key_mask)
        pair_probs = jnp.exp(pair_block_scores - log_total[:, :, None])
        pair_key_part = remote_block[:, 0].reshape(block_rows, local_heads, HD)
        pair_value_part = remote_block[:, 1].reshape(block_rows, local_heads, HD)
        value_grad = jnp.einsum(
            "hqk,qhd->khd",
            pair_probs.astype(jnp.bfloat16),
            heads_back,
            preferred_element_type=jnp.float32,
        )
        prob_grad = jnp.einsum(
            "qhd,khd->hqk", heads_back, pair_value_part, preferred_element_type=jnp.float32
        )
        score_grad = (pair_probs * (prob_grad - delta[:, :, None])).astype(jnp.bfloat16)
        query_term = (
            jnp.einsum(
                "hqk,khd->qhd", score_grad, pair_key_part, preferred_element_type=jnp.float32
            )
            * score_scale
        )
        key_grad = (
            jnp.einsum("hqk,qhd->khd", score_grad, queries, preferred_element_type=jnp.float32)
            * score_scale
        )
        grad_pair = jnp.stack(
            [
                key_grad.reshape(block_rows, local_width),
                value_grad.reshape(block_rows, local_width),
            ],
            axis=1,
        )
        query_term, grad_pair = (query_term, grad_pair)
        query_grad = query_grad + query_term
        if distance == 0:
            pair_total = grad_pair
        else:
            pair_total = pair_total + shifted(
                grad_pair.astype(jnp.bfloat16), "cp", -distance
            ).astype(grad_pair.dtype)
    query_back = rotate_back(query_grad, cosine, sine).reshape(block_rows, local_width)
    key_back = rotate_back(
        pair_total[:, 0].reshape(block_rows, local_heads, HD), cosine, sine
    ).reshape(block_rows, local_width)
    raw_back = jnp.stack([query_back, key_back, pair_total[:, 1]], axis=1).astype(jnp.bfloat16)
    raw_back = lax.all_to_all(
        raw_back.reshape(block_rows, 3, 1, local_width),
        "hd",
        split_axis=0,
        concat_axis=2,
        tiled=True,
    )
    raw_back = raw_back.reshape(rows_here, 3 * model_width)
    qkv_sum = product(tokens.T, raw_back)
    tokens_grad = (dz_one + product(raw_back, qkv_full.T)).astype(jnp.bfloat16)
    summed = (
        lax.psum_scatter(qkv_sum, ("cp", "hd"), scatter_dimension=0, tiled=True),
        lax.psum_scatter(out_sum, ("cp", "hd"), scatter_dimension=0, tiled=True),
        lax.psum_scatter(gate_sum, ("cp", "hd"), scatter_dimension=0, tiled=True),
        lax.psum_scatter(up_sum, ("cp", "hd"), scatter_dimension=0, tiled=True),
        lax.psum_scatter(down_sum, ("cp", "hd"), scatter_dimension=0, tiled=True),
        lax.psum_scatter(gain_one_grad, ("cp", "hd"), scatter_dimension=0, tiled=True),
        lax.psum_scatter(bias_one_grad, ("cp", "hd"), scatter_dimension=0, tiled=True),
        lax.psum_scatter(gain_two_grad, ("cp", "hd"), scatter_dimension=0, tiled=True),
        lax.psum_scatter(bias_two_grad, ("cp", "hd"), scatter_dimension=0, tiled=True),
    )
    return (
        layer_out,
        tokens_grad,
        summed[0],
        summed[1],
        summed[2],
        summed[3],
        summed[4],
        summed[5],
        summed[6],
        summed[7],
        summed[8],
    )


MESH = pl.DeviceIdType.MESH
ZN, YN, CN, XN = 4, 2, 2, 2
BLOCKS = ZN * YN * CN * XN


def place():
    cp = lax.axis_index("cp")
    x = lax.axis_index("hd")
    return x, lax.rem(cp // CN, YN), cp // (YN * CN), lax.rem(cp, CN)


def device(x, y, z, c):
    return ((z * YN + y) * CN + c, x)


def block(x, y, z, c):
    return ((z * YN + y) * CN + c) * XN + x


def when(cond, fn):
    if cond is None:
        fn()
    else:
        pl.when(cond)(fn)


def both(a, b):
    if a is None:
        return b
    if b is None:
        return a
    return jnp.logical_and(a, b)


def halves(ref):
    rows, cols = ref.shape[-2:]
    if rows % 32 == 0:
        return ref.at[pl.ds(0, rows // 2)], ref.at[pl.ds(rows // 2, rows // 2)]
    if cols % 256 == 0:
        return ref.at[:, pl.ds(0, cols // 2)], ref.at[:, pl.ds(cols // 2, cols // 2)]
    return ref, None


def greet(x, y, z, c, far):
    barrier = pltpu.get_barrier_semaphore()
    for peer in (device(1 - x, y, z, c), device(x, 1 - y, z, c), device(x, y, z, 1 - c)):
        pl.semaphore_signal(barrier, inc=1, device_id=peer, device_id_type=MESH)
    count = 3
    if far:
        for k in range(1, ZN):
            peer = device(x, y, lax.rem(z + k, ZN), c)
            pl.semaphore_signal(barrier, inc=1, device_id=peer, device_id_type=MESH)
        count = count + ZN - 1
    else:
        pl.when(z > 0)(lambda: pl.semaphore_signal(barrier, inc=1, device_id=device(x, y, z - 1, c), device_id_type=MESH))
        pl.when(z < ZN - 1)(lambda: pl.semaphore_signal(barrier, inc=1, device_id=device(x, y, z + 1, c), device_id_type=MESH))
        count = count + (z > 0).astype(jnp.int32) + (z < ZN - 1).astype(jnp.int32)
    pl.semaphore_wait(barrier, count)


SENDS = 40
LITTLE = 16 << 20
RECVS = 36


BCAST, BY_X, BY_Y, CROSS, SWAP, REST_X, REST_Y, PAIR_X, PAIR_Y, REDUCE, PRODUCT, TURNED_PRODUCT = range(12)
ONWARD, BESIDE, ACROSS = range(3)
CHAINED = (BCAST, BY_X, BY_Y)
REST = (REST_X, REST_Y)


def take(refs, counts):
    groups = []
    for count in counts:
        groups.append(refs[:count])
        refs = refs[count:]
    return groups, refs


SHORT_PLAN = [
    (fn, 0, d - lag)
    for d in range(1, ZN + 2)
    for lag, fn in enumerate((ONWARD, BESIDE, ACROSS))
    if (d > 0 if lag else d < ZN) and 0 <= d - lag < ZN
]
PLAN = [
    (ONWARD, 0, 1),
    (BESIDE, 0, 0),
    (BESIDE, 1, 0),
    (ACROSS, 0, 0),
    (BESIDE, 0, 1),
    (ONWARD, 1, 1),
    (ACROSS, 1, 0),
    (ACROSS, 0, 1),
    (ONWARD, 1, 2),
    (ONWARD, 1, 3),
    (BESIDE, 1, 1),
    (ONWARD, 0, 2),
    (BESIDE, 1, 2),
    (BESIDE, 1, 3),
    (BESIDE, 0, 2),
    (ACROSS, 1, 1),
    (ONWARD, 0, 3),
    (ACROSS, 1, 2),
    (ACROSS, 1, 3),
    (ACROSS, 0, 2),
    (BESIDE, 0, 3),
    (ACROSS, 0, 3),
]


def gather_kernel(modes, *refs):
    n = len(modes)
    ins, refs = take(refs, [2 if mode in REST else 1 for mode in modes])
    outs, (lsem, ssem, rsem), bufs = refs[:n], refs[n : n + 3], list(refs[n + 3 :])
    bufs = {k: bufs.pop(0) for k, mode in enumerate(modes) if mode in REST}
    pairs, ins = ins, [group[0] for group in ins]
    x, y, z, c = place()
    ox, oy, oc = 1 - x, 1 - y, 1 - c
    greet(x, y, z, c, any(m in (SWAP, CROSS) for m in modes))
    sent = []

    def copy(k, src, dst, s, r, peer):
        return pltpu.make_async_remote_copy(
            src_ref=src,
            dst_ref=dst,
            send_sem=ssem.at[k, s],
            recv_sem=rsem.at[k, r],
            device_id=peer,
            device_id_type=MESH,
        )

    def send(cond, *args):
        when(cond, lambda: copy(*args).start())
        sent.append((cond, args))

    def arrived(cond, k, ref, r):
        when(cond, lambda: copy(k, ref, ref, 0, r, device(ox, y, z, c)).wait_recv())

    locals_ = []

    def keep(k, i, mine, spot):
        pltpu.make_async_copy(mine, spot, lsem.at[k, i]).start()
        locals_.append((k, i, mine, spot))

    def at(k, px, py, b):
        if modes[k] == BY_X:
            return outs[k].at[2 * b + px]
        if modes[k] == BY_Y:
            return outs[k].at[2 * b + py]
        return outs[k].at[block(px, py, b, c)]

    for k, mode in enumerate(modes):
        if mode in CHAINED:
            keep(k, 0, ins[k], at(k, x, y, z))
        elif mode == SWAP:
            keep(k, 0, ins[k].at[z], outs[k].at[z])
        elif mode == CROSS:
            keep(k, 0, ins[k].at[z], outs[k].at[block(x, y, z, c)])

    def share_of(k, i, core):
        b, j = i % 8 // 2, i % 2
        if modes[k] == REST_Y:
            return block(j, oy if i >= 8 else y, b, core)
        return block(ox if i >= 8 else x, j, b, core)

    def spread(k, cond, b, src, up, down):
        here = at(k, x, y, b)
        if modes[k] in CHAINED:
            if up is not False:
                send(both(cond, up), k, src, here, b, b, device(x, y, lax.rem(z + 1, ZN), c))
            if down is not False:
                send(both(cond, down), k, src, here, 4 + b, b, device(x, y, lax.rem(z + ZN - 1, ZN), c))
        if modes[k] != BY_Y:
            send(cond, k, src, here, 8 + b, 4 + b, device(ox, y, z, c))
        if modes[k] != BY_X:
            send(cond, k, src, here, 16 + b, 12 + b, device(x, oy, z, c))
        if modes[k] not in (BY_X, BY_Y):
            send(cond, k, src, here, 24 + b, 20 + b, device(x, y, z, oc))

    def sides(k, cond, b):
        fx, fy = at(k, ox, y, b), at(k, x, oy, b)
        full = modes[k] not in (BY_X, BY_Y)
        if modes[k] != BY_Y:
            arrived(cond, k, fx, 4 + b)
            first, _ = halves(fx)
            if full:
                send(cond, k, first, first, 20 + b, 16 + b, device(x, oy, z, c))
                send(cond, k, fx, fx, 28 + b, 24 + b, device(x, y, z, oc))
        if modes[k] != BY_X:
            arrived(cond, k, fy, 12 + b)
            _, second = halves(fy)
            if full and second is not None:
                send(cond, k, second, second, 12 + b, 8 + b, device(ox, y, z, c))
            if full:
                send(cond, k, fy, fy, 32 + b, 28 + b, device(x, y, z, oc))

    def corner(k, cond, b):
        far = outs[k].at[block(ox, oy, b, c)]
        first, second = halves(far)
        arrived(cond, k, first, 16 + b)
        if second is not None:
            arrived(cond, k, second, 8 + b)
        send(cond, k, far, far, 36 + b, 32 + b, device(x, y, z, oc))

    def steps(distance):
        if distance == 0:
            return [(None, z)]
        return [(z >= distance, jnp.maximum(z - distance, 0)), (z + distance < ZN, jnp.minimum(z + distance, ZN - 1))]

    chained = [k for k, mode in enumerate(modes) if mode in CHAINED]
    crossed = [k for k, mode in enumerate(modes) if mode == CROSS]
    swapped = [k for k, mode in enumerate(modes) if mode == SWAP]

    def exchange(ks):
        for k in ks:
            for d in range(1, ZN):
                to = lax.rem(z + d, ZN)
                spot = outs[k].at[z] if modes[k] == SWAP else outs[k].at[block(x, y, z, c)]
                send(None, k, ins[k].at[to], spot, to, z, device(x, y, to, c))

    for k in chained:
        spread(k, None, z, ins[k], z < ZN - 1, z > 0)
    if not chained:
        exchange(swapped)
        swapped = []
    for k, mode in enumerate(modes):
        if mode in REST:
            for i in range(16):
                src = pairs[k][i // 8].at[i % 8]
                pltpu.make_async_copy(src, bufs[k].at[i], lsem.at[k, i]).start()
                send(None, k, src, outs[k].at[share_of(k, i, c)], i, i, device(x, y, z, oc))
    for k in crossed:
        spread(k, None, z, ins[k].at[z], False, False)
    exchange(crossed)

    def onward(ks, distance):
        for side, (cond, b) in enumerate(steps(distance)):
            for k in ks:
                here = at(k, x, y, b)
                arrived(cond, k, here, b)
                spread(k, cond, b, here, z < ZN - 1 if side == 0 else False, z > 0 if side == 1 else False)

    def beside(ks, distance):
        for cond, b in steps(distance):
            for k in ks:
                sides(k, cond, b)

    def across(ks, distance):
        for cond, b in steps(distance):
            for k in ks:
                if modes[k] in (BCAST, CROSS):
                    corner(k, cond, b)

    plan = PLAN if crossed else SHORT_PLAN
    for fn, ks, distance in plan if chained else ():
        fn = {ONWARD: onward, BESIDE: beside, ACROSS: across}[fn]
        fn(chained if ks == 0 else crossed, distance)
        if fn is onward and distance == ZN - 1 and ks == 0:
            exchange(swapped)
            swapped = []
    exchange(swapped)
    for k in bufs:
        for i in range(16):
            pltpu.make_async_copy(pairs[k][0].at[0], bufs[k].at[i], lsem.at[k, i]).wait()
            keep(k, i, bufs[k].at[i], outs[k].at[share_of(k, i, c)])
    for k, mode in enumerate(modes):
        if mode == SWAP:
            for d in range(1, ZN):
                frm = lax.rem(z + d, ZN)
                arrived(None, k, outs[k].at[frm], frm)
        elif mode in REST:
            for i in range(16):
                arrived(None, k, outs[k].at[share_of(k, i, oc)], i)
        elif mode not in (BY_X, BY_Y):
            quads = (0, 1, 2, 3)
            for b in range(ZN):
                for j in quads:
                    px, py = ((x, y), (ox, y), (x, oy), (ox, oy))[j]
                    arrived(None, k, outs[k].at[block(px, py, b, oc)], 20 + 4 * j + b)
    for k, i, mine, spot in locals_:
        pltpu.make_async_copy(mine, spot, lsem.at[k, i]).wait()
    for cond, args in sent:
        when(cond, lambda args=args: copy(*args).wait_send())


def gather(arrays, modes, collective_id):
    shapes, inputs, operands, scratch = [], [], [], []
    anywhere, local = pl.BlockSpec(memory_space=pltpu.HBM), pl.BlockSpec(memory_space=pltpu.VMEM)
    for a, mode in zip(arrays, modes):
        inputs = inputs + ([anywhere] * 2 if mode in REST else [local])
        operands = operands + (list(a) if mode in REST else [a])
        if mode in REST:
            a = a[0]
            scratch.append(pltpu.VMEM((16,) + a.shape[1:], a.dtype))
        if mode == BCAST:
            shapes.append((BLOCKS,) + a.shape)
        elif mode in CHAINED:
            shapes.append((2 * ZN,) + a.shape)
        elif mode == SWAP:
            shapes.append(a.shape)
        else:
            shapes.append((BLOCKS,) + a.shape[1:])
    n = len(arrays)
    dtypes = [(a[0] if mode in REST else a).dtype for a, mode in zip(arrays, modes)]
    return pl.pallas_call(
        functools.partial(gather_kernel, tuple(modes)),
        out_shape=[jax.ShapeDtypeStruct(shape, dtype) for shape, dtype in zip(shapes, dtypes)],
        in_specs=inputs,
        out_specs=[anywhere] * n,
        scratch_shapes=[
            pltpu.SemaphoreType.DMA((n, 16)),
            pltpu.SemaphoreType.DMA((n, SENDS)),
            pltpu.SemaphoreType.DMA((n, RECVS)),
        ]
        + scratch,
        compiler_params=pltpu.CompilerParams(
            collective_id=collective_id, has_side_effects=True, vmem_limit_bytes=LITTLE if modes[0] == SWAP else 67043328
        ),
    )(*operands)


def chunk_of(cols):
    for size in (768, 640, 512, 384, 256, 128):
        if cols % size == 0:
            return size
    return cols


def add_up(dst, sources):
    rows, cols = dst.shape[-2:]
    tall = 32 if rows > 32 and rows % 32 == 0 else (16 if rows > 32 else rows)
    wide = cols if rows > 32 else chunk_of(cols)

    def step(i, carry):
        if rows > 32:
            spot = (pl.ds(pl.multiple_of(i * tall, tall), tall), slice(None))
        elif cols > wide:
            spot = (slice(None), pl.ds(pl.multiple_of(i * wide, wide), wide))
        else:
            spot = (slice(None), slice(None))
        total = sources[0][spot].astype(jnp.float32)
        for source in sources[1:]:
            total = total + source[spot].astype(jnp.float32)
        dst[spot] = total.astype(dst.dtype)
        return carry

    count = (rows // tall) * (cols // wide)
    if count == 1:
        step(0, 0)
    else:
        lax.fori_loop(0, count, step, 0)


BUFFERS = {PRODUCT: 5, TURNED_PRODUCT: 5, SWAP: 0, PAIR_X: 2, PAIR_Y: 2, CROSS: 3, REDUCE: 4, REST_X: 5, REST_Y: 5}
PAIR = (PAIR_X, PAIR_Y)
MADE = (PRODUCT, TURNED_PRODUCT)


def make(dst, left, right, turned):
    blocks, rows = dst.shape[:2]
    group = blocks // 8

    def step(i, carry):
        span = pl.ds(pl.multiple_of(i * group * rows, 32), group * rows)
        if turned:
            span = pl.ds(pl.multiple_of(i * group * rows, 128), group * rows)
            part = left[:, span].T
        else:
            part = left[span, :]
        total = jnp.dot(part, right[...], preferred_element_type=jnp.float32)
        for j in range(group):
            dst[i * group + j] = total[j * rows : (j + 1) * rows].astype(dst.dtype)
        return carry

    lax.fori_loop(0, blocks // group, step, 0)


def reduce_kernel(modes, *refs):
    n = len(modes)
    ins, refs = take(refs, [2 if mode in REST + MADE else 1 for mode in modes])
    outs, refs = refs[:n], refs[n:]
    (lsem, ssem, rsem), scratch = refs[:3], refs[3:]
    bufs, _ = take(scratch, [BUFFERS[mode] for mode in modes])
    others, ins = ins, [group[0] for group in ins]
    for k, mode in enumerate(modes):
        if mode in MADE:
            ins[k] = bufs[k][4]
    x, y, z, c = place()
    ox, oy, oc = 1 - x, 1 - y, 1 - c
    greet(x, y, z, c, any(m in (SWAP, CROSS) for m in modes))
    sent = []

    def copy(k, src, dst, s, r, peer):
        return pltpu.make_async_remote_copy(
            src_ref=src,
            dst_ref=dst,
            send_sem=ssem.at[k, s],
            recv_sem=rsem.at[k, r],
            device_id=peer,
            device_id_type=MESH,
        )

    def send(cond, *args):
        when(cond, lambda: copy(*args).start())
        sent.append((cond, args))

    def arrived(cond, k, ref, r):
        when(cond, lambda: copy(k, ref, ref, 0, r, device(ox, y, z, c)).wait_recv())

    half = z // 2
    order = [3 - 3 * half, 2 - half, 1 - z + 4 * half, z]
    quads = ((ox, oy), (ox, y), (x, oy), (x, y))
    active = [k for k, mode in enumerate(modes) if mode in (CROSS, REDUCE) + MADE]
    paired = [k for k, mode in enumerate(modes) if mode in PAIR]
    rest = [k for k, mode in enumerate(modes) if mode in REST]

    for k, mode in enumerate(modes):
        if mode == SWAP:
            for d in range(1, ZN):
                to = lax.rem(z + d, ZN)
                send(None, k, ins[k].at[to], outs[k].at[z], d, z, device(x, y, to, c))
            pltpu.make_async_copy(ins[k].at[z], outs[k].at[z], lsem.at[k, 0]).start()

    for k in rest:
        acc, rec, _, _, cor = bufs[k]
        for i, b in enumerate(order):
            for j in range(2):
                mine = (x, y)[modes[k] == REST_X]
                other = mine if j else 1 - mine
                px, py = (x, other) if modes[k] == REST_X else (other, y)
                at = 2 * i + j
                send(None, k, ins[k].at[block(px, py, b, oc)], cor.at[at], at, at, device(x, y, z, oc))
                pltpu.make_async_copy(ins[k].at[block(px, py, b, c)], acc.at[at], lsem.at[k, at]).start()
                pltpu.make_async_copy(others[k][1].at[2 * b + other], rec.at[at], lsem.at[k, 8 + at]).start()

    def begin(ks):
        for k in ks:
            if modes[k] in MADE:
                make(ins[k], *others[k], modes[k] == TURNED_PRODUCT)
            for i, b in enumerate(order):
                acc, cor = bufs[k][:2]
                for j, (px, py) in enumerate(quads):
                    send(None, k, ins[k].at[block(px, py, b, oc)], cor.at[4 * i + j], 4 * i + j, 4 * i + j, device(x, y, z, oc))
                    pltpu.make_async_copy(ins[k].at[block(px, py, b, c)], acc.at[4 * i + j], lsem.at[k, 4 * i + j]).start()

    begin([k for k in active if modes[k] == CROSS])

    for k in paired:
        acc, cor = bufs[k]
        for i in range(8):
            b, j = i // 2, i % 2
            px, py = (j, oy) if modes[k] == PAIR_Y else (ox, j)
            send(None, k, ins[k].at[block(px, py, b, oc)], cor.at[i], i, i, device(x, y, z, oc))
            pltpu.make_async_copy(ins[k].at[block(px, py, b, c)], acc.at[i], lsem.at[k, i]).start()

    def loaded(k, i, j):
        acc, cor = bufs[k][:2]
        pltpu.make_async_copy(ins[k].at[0], acc.at[4 * i + j], lsem.at[k, 4 * i + j]).wait()
        arrived(None, k, cor.at[4 * i + j], 4 * i + j)

    for k in paired:
        acc, cor = bufs[k]

        def join(i, carry, k=k, acc=acc, cor=cor):
            pltpu.make_async_copy(ins[k].at[0], acc.at[i], lsem.at[k, i]).wait()
            arrived(None, k, cor.at[i], i)
            add_up(outs[k].at[i], (acc.at[i], cor.at[i]))
            return carry

        lax.fori_loop(0, 8, join, 0)

    def fetched(k, i, j):
        acc, rec, _, _, cor = bufs[k]
        at = 2 * i + j
        pltpu.make_async_copy(ins[k].at[0], acc.at[at], lsem.at[k, at]).wait()
        pltpu.make_async_copy(ins[k].at[0], rec.at[at], lsem.at[k, 8 + at]).wait()
        arrived(None, k, cor.at[at], at)

    def ahead(k, i, b):
        acc, rec, side, _, cor = bufs[k]
        fetched(k, i, 0)
        add_up(acc.at[2 * i], (acc.at[2 * i], rec.at[2 * i], cor.at[2 * i]))
        peer = device(x, oy, z, c) if modes[k] == REST_X else device(ox, y, z, c)
        send(None, k, acc.at[2 * i], side.at[i], 16 + i, 16 + i, peer)

    def corner(k, i, b):
        acc, cor, side = bufs[k][:3]
        loaded(k, i, 0)
        add_up(acc.at[4 * i], (acc.at[4 * i], cor.at[4 * i]))
        first, second = halves(acc.at[4 * i])
        send(None, k, first, halves(side.at[i])[0], 16 + i, 16 + i, device(x, oy, z, c))
        if second is not None:
            send(None, k, second, halves(side.at[4 + i])[1], 20 + i, 20 + i, device(ox, y, z, c))

    def beside(k, i, b):
        acc, cor, side = bufs[k][:3]
        loaded(k, i, 1)
        add_up(acc.at[4 * i + 1], (acc.at[4 * i + 1], cor.at[4 * i + 1]))
        part = halves(side.at[i])[0]
        arrived(None, k, part, 16 + i)
        mine = halves(acc.at[4 * i + 1])[0]
        add_up(mine, (mine, part))
        send(None, k, acc.at[4 * i + 1], side.at[8 + i], 24 + i, 24 + i, device(ox, y, z, c))
        loaded(k, i, 2)
        add_up(acc.at[4 * i + 2], (acc.at[4 * i + 2], cor.at[4 * i + 2]))
        part = halves(side.at[4 + i])[1]
        if part is not None:
            arrived(None, k, part, 20 + i)
            mine = halves(acc.at[4 * i + 2])[1]
            add_up(mine, (mine, part))
        send(None, k, acc.at[4 * i + 2], side.at[12 + i], 28 + i, 28 + i, device(x, oy, z, c))

    def settle(k, i, b):
        side = bufs[k][2]
        if k in rest:
            acc, rec, _, _, cor = bufs[k]
            fetched(k, i, 1)
            arrived(None, k, side.at[i], 16 + i)
            own = acc.at[2 * i + 1]
            terms = (own, rec.at[2 * i + 1], cor.at[2 * i + 1], side.at[i])
        else:
            acc, cor = bufs[k][:2]
            loaded(k, i, 3)
            own = acc.at[4 * i + 3]
            arrived(None, k, side.at[8 + i], 24 + i)
            arrived(None, k, side.at[12 + i], 28 + i)
            terms = (own, cor.at[4 * i + 3], side.at[8 + i], side.at[12 + i])
        if modes[k] == CROSS:
            add_up(own, terms)
            if i < ZN - 1:
                send(None, k, own, outs[k].at[z], 32 + i, 32 + z, device(x, y, b, c))
            else:
                pltpu.make_async_copy(own, outs[k].at[z], lsem.at[k, 16]).start()
            return
        chain = bufs[k][3]
        if i == ZN - 1:
            add_up(outs[k], terms)

            def lower(k=k, chain=chain):
                arrived(None, k, chain.at[z], 32 + z)
                add_up(outs[k], (outs[k], chain.at[z]))

            def upper(k=k, chain=chain):
                arrived(None, k, chain.at[4 + z], 36 + z)
                add_up(outs[k], (outs[k], chain.at[4 + z]))

            pl.when(z > 0)(lower)
            pl.when(z < ZN - 1)(upper)
        else:
            add_up(own, terms)
            below = both(b > z, z > 0)
            above = both(b < z, z < ZN - 1)

            def lower(k=k, chain=chain, own=own, b=b):
                arrived(None, k, chain.at[b], 32 + b)
                add_up(own, (own, chain.at[b]))

            def upper(k=k, chain=chain, own=own, b=b):
                arrived(None, k, chain.at[4 + b], 36 + b)
                add_up(own, (own, chain.at[4 + b]))

            pl.when(below)(lower)
            pl.when(above)(upper)
            send(b > z, k, own, chain.at[b], 32 + i, 32 + b, device(x, y, lax.rem(z + 1, ZN), c))
            send(b < z, k, own, chain.at[4 + b], 32 + i, 36 + b, device(x, y, lax.rem(z + ZN - 1, ZN), c))

    crossed = [k for k in active if modes[k] == CROSS]
    plain = [k for k in active if modes[k] != CROSS]
    stages = [[(ahead, rest)], [(corner, crossed)], [(corner, plain)]]
    stages = stages + [[(settle, rest), (beside, crossed)], [(settle, crossed), (beside, plain)], [(settle, plain)]]
    for stage in stages:
        for i, b in enumerate(order):
            for fn, ks in stage:
                for k in ks:
                    fn(k, i, b)
        if stage is stages[0]:
            begin(plain)
    for k, mode in enumerate(modes):
        if mode not in (SWAP, CROSS):
            continue
        for d in range(1, ZN):
            frm = lax.rem(z + d, ZN)
            arrived(None, k, outs[k].at[frm], frm if mode == SWAP else 32 + frm)
        if mode == SWAP:
            pltpu.make_async_copy(ins[k].at[z], outs[k].at[z], lsem.at[k, 0]).wait()
        else:
            pltpu.make_async_copy(bufs[k][0].at[15], outs[k].at[z], lsem.at[k, 16]).wait()
    for cond, args in sent:
        when(cond, lambda args=args: copy(*args).wait_send())


def reduce(arrays, modes, collective_id):
    shapes, specs, scratch, operands, inputs = [], [], [], [], []
    anywhere, local = pl.BlockSpec(memory_space=pltpu.HBM), pl.BlockSpec(memory_space=pltpu.VMEM)
    for a, mode in zip(arrays, modes):
        operands = operands + (list(a) if mode in REST + MADE else [a])
        inputs = inputs + [local if mode in MADE + (SWAP,) else anywhere] * (2 if mode in REST + MADE else 1)
        if mode in MADE:
            tall = a[0].shape[1] if mode == TURNED_PRODUCT else a[0].shape[0]
            shape = (BLOCKS, tall // BLOCKS, a[1].shape[1])
        else:
            a = a[0] if mode in REST else a
            shape = a.shape
        rows, cols = shape[1:]
        dtype = jnp.bfloat16 if mode in MADE else a.dtype
        sizes = {SWAP: (), CROSS: (16, 16, 16), REDUCE: (16, 16, 16, 8)}
        sizes.update({PAIR_X: (8, 8), PAIR_Y: (8, 8), REST_X: (8, 8, 4, 8, 8), REST_Y: (8, 8, 4, 8, 8)})
        sizes = sizes[REDUCE] + (BLOCKS,) if mode in MADE else sizes[mode]
        scratch = scratch + [pltpu.VMEM((size, rows, cols), dtype) for size in sizes]
        if mode == SWAP:
            shapes.append(jax.ShapeDtypeStruct(a.shape, a.dtype))
            specs.append(anywhere)
        elif mode in PAIR:
            shapes.append(jax.ShapeDtypeStruct((8, rows, cols), a.dtype))
            specs.append(local)
        elif mode == CROSS:
            shapes.append(jax.ShapeDtypeStruct((ZN, rows, cols), a.dtype))
            specs.append(anywhere)
        else:
            shapes.append(jax.ShapeDtypeStruct((rows, cols), jnp.float32))
            specs.append(local)
    n = len(arrays)
    return pl.pallas_call(
        functools.partial(reduce_kernel, tuple(modes)),
        out_shape=shapes,
        in_specs=inputs,
        out_specs=specs,
        scratch_shapes=[
            pltpu.SemaphoreType.DMA((n, 17)),
            pltpu.SemaphoreType.DMA((n, SENDS)),
            pltpu.SemaphoreType.DMA((n, SENDS)),
        ]
        + scratch,
        compiler_params=pltpu.CompilerParams(
            collective_id=collective_id, has_side_effects=True, vmem_limit_bytes=LITTLE if modes[0] == SWAP else 67043328
        ),
    )(*operands)


HEAD = 64
GROUP = 3
TILE = 512
WIDE = 1024
EDGE = 128
SPAN = 4096
FAR = 1 << 30


def longest(lengths):
    begin, best, at = jnp.int32(0), lengths[0], jnp.int32(0)
    for j in range(lengths.shape[0]):
        length = lengths[j]
        at = jnp.where(length > best, begin, at)
        best = jnp.maximum(best, length)
        begin = begin + length
    return at, at + best


def lane_slots(lengths, count):
    x, y, z, c = place()
    lane = lax.broadcasted_iota(jnp.int32, (1, count), 1)
    begin, end = longest(lengths)
    spots = [block(x, y, b, c) * count + lane for b in range(ZN)]
    slots, before = [], jnp.zeros((1, count), jnp.int32)
    for b in range(ZN):
        big = jnp.logical_and(spots[b] >= begin, spots[b] < end)
        slots.append(jnp.where(big, before, ZN // 2 + b - before))
        before = before + big.astype(jnp.int32)
    return begin, end, spots, slots


def pick(slots, slot, parts):
    chosen = parts[-1]
    for b in range(len(parts) - 2, -1, -1):
        chosen = jnp.where(slots[b] == slot, parts[b], chosen)
    return chosen


def bounds_of(lengths, spot):
    low, high = jnp.zeros_like(spot), jnp.full_like(spot, FAR)
    begin = jnp.int32(0)
    for j in range(lengths.shape[0]):
        end = begin + lengths[j]
        low = jnp.where(spot >= begin, begin, low)
        high = jnp.where(spot < end, jnp.minimum(high, end), high)
        begin = end
    return low, high


def walk(big, begin, end, low, high, step, init):
    if big:
        base = begin // EDGE * EDGE

        def body(i, carry):
            at = pl.multiple_of(base + i * WIDE, EDGE)
            return step(at, WIDE, False, carry)

        carry = step(pl.multiple_of(base, EDGE), WIDE, True, init)
        carry = lax.fori_loop(1, SPAN // WIDE, body, carry)
        return lax.cond(
            begin > base,
            lambda c: step(pl.multiple_of(base + SPAN, EDGE), EDGE, True, c),
            lambda c: c,
            carry,
        )
    first = jnp.min(low) // TILE
    stop = (jnp.max(high) + TILE - 1) // TILE
    hole_first = jnp.maximum((begin + TILE - 1) // TILE, first)
    hole = jnp.maximum(jnp.minimum(end // TILE, stop) - hole_first, 0)

    def body(i, carry):
        tile = first + i
        tile = jnp.where(jnp.logical_and(hole > 0, tile >= hole_first), tile + hole, tile)
        return step(pl.multiple_of(tile * TILE, TILE), TILE, True, carry)

    return lax.fori_loop(0, stop - first - hole, body, init)


def keys_in(first, size, low, high):
    at = first + lax.broadcasted_iota(jnp.int32, (size, low.shape[1]), 0)
    return jnp.logical_and(at >= low, at < high)


def dot(a, b):
    return jnp.dot(a, b, preferred_element_type=jnp.float32)


def pad_heads(rows, h, slots):
    part = rows[h * HEAD : (h + 1) * HEAD]
    zero = jnp.zeros_like(part)
    return jnp.concatenate([part if s == h else zero for s in slots], axis=0)


Q_SLOTS = (0, 1, 2, -1)
V_SLOTS = (-1, 2, 0, 1)


def forward_kernel(lengths, qt, kv, low_out, out, lse_out, qm, acc, qs, os, ls):
    count = qt.shape[2]
    begin, end, spots, slots = lane_slots(lengths, count)
    for s in range(ZN):
        qs[s] = pick(slots, s, [qt[b] for b in range(ZN)])

    def one_block(big, s, carry):
        low, high = bounds_of(lengths, pick(slots, s, spots))
        rows = qs[s] * jnp.bfloat16(0.125)
        for h in range(GROUP):
            qm[h] = pad_heads(rows, h, Q_SLOTS)
        acc[...] = jnp.zeros_like(acc)

        def step(at, size, masked, stats):
            span = pl.ds(at, size)
            keys = kv[span, 0:256]
            values = kv[span, 128:384].T
            mask = keys_in(at, size, low, high) if masked else None
            fresh = []
            for h in range(GROUP):
                top, total = stats[2 * h], stats[2 * h + 1]
                scores = dot(keys, qm[h])
                if masked:
                    scores = jnp.where(mask, scores, -1e9)
                new_top = jnp.maximum(top, jnp.max(scores, axis=0, keepdims=True))
                shrink = jnp.exp(top - new_top)
                weights = jnp.exp(scores - new_top)
                total = total * shrink + jnp.sum(weights, axis=0, keepdims=True)
                row = V_SLOTS.index(h) * HEAD
                acc[h] = acc[h] * shrink + dot(values[row : row + HEAD], weights.astype(jnp.bfloat16))
                fresh = fresh + [new_top, total]
            return tuple(fresh)

        init = (jnp.full((1, count), -1e9, jnp.float32), jnp.zeros((1, count), jnp.float32)) * GROUP
        stats = walk(big, begin, end, low, high, step, init)
        for h in range(GROUP):
            top, total = stats[2 * h], stats[2 * h + 1]
            os[s, h * HEAD : (h + 1) * HEAD] = acc[h] / total
            ls[s, h : h + 1] = top + jnp.log(total)
        return carry

    lax.fori_loop(0, ZN // 2, functools.partial(one_block, True), 0)
    lax.fori_loop(ZN // 2, ZN, functools.partial(one_block, False), 0)
    for b in range(ZN):
        value = pick([jnp.full_like(slots[b], s) for s in range(ZN)], slots[b], [os[s] for s in range(ZN)])
        out[b] = value
        low_out[b] = value.astype(low_out.dtype)
        lse_out[b] = pick([jnp.full_like(slots[b], s) for s in range(ZN)], slots[b], [ls[s] for s in range(ZN)])


def attend(lengths, qt, kv):
    blocks, rows, count = qt.shape
    whole = pl.BlockSpec(memory_space=pltpu.VMEM)
    return pl.pallas_call(
        forward_kernel,
        out_shape=[
            jax.ShapeDtypeStruct(qt.shape, jnp.bfloat16),
            jax.ShapeDtypeStruct(qt.shape, jnp.float32),
            jax.ShapeDtypeStruct((blocks, 8, count), jnp.float32),
        ],
        in_specs=[pl.BlockSpec(memory_space=pltpu.SMEM), whole, whole],
        out_specs=[whole] * 3,
        scratch_shapes=[
            pltpu.VMEM((GROUP, 256, count), jnp.bfloat16),
            pltpu.VMEM((GROUP, HEAD, count), jnp.float32),
            pltpu.VMEM(qt.shape, jnp.bfloat16),
            pltpu.VMEM(qt.shape, jnp.float32),
            pltpu.VMEM((blocks, 8, count), jnp.float32),
        ],
        compiler_params=pltpu.CompilerParams(vmem_limit_bytes=67043328),
    )(lengths, qt, kv)


def backward_kernel(lengths, qt, kv, out, lse, dot_in, cosine, sine, dq_out, dkv_out, qmt, qm, dmt, dm, dq, acc, qs, ds, es, ls, dqs):
    count = qt.shape[2]
    tiles = kv.shape[0] // TILE

    def clear(tile, carry):
        acc[pl.ds(pl.multiple_of(tile * TILE, TILE), TILE), :] = jnp.zeros((TILE, acc.shape[1]), jnp.float32)
        return carry

    lax.fori_loop(0, tiles, clear, 0)

    begin, end, spots, slots = lane_slots(lengths, count)
    for b in range(ZN):
        product_rows = dot_in[b].astype(jnp.float32) * out[b]
        for h in range(GROUP):
            es[b, h : h + 1] = jnp.sum(product_rows[h * HEAD : (h + 1) * HEAD], axis=0, keepdims=True)
    for s in range(ZN):
        qs[s] = pick(slots, s, [qt[b] for b in range(ZN)])
        ds[s] = pick(slots, s, [dot_in[b] for b in range(ZN)])
        ls[s] = pick(slots, s, [lse[b] for b in range(ZN)])
    picked = [pick(slots, s, [es[b] for b in range(ZN)]) for s in range(ZN)]
    for s in range(ZN):
        es[s] = picked[s]

    def one_block(big, s, carry):
        low, high = bounds_of(lengths, pick(slots, s, spots))
        rows = qs[s] * jnp.bfloat16(0.125)
        grads = ds[s]
        deltas = [es[s, h : h + 1] for h in range(GROUP)]
        levels = [ls[s, h : h + 1] for h in range(GROUP)]
        for h in range(GROUP):
            padded = pad_heads(rows, h, Q_SLOTS)
            qmt[h] = padded
            qm[h * count : (h + 1) * count] = padded.T
            padded = pad_heads(grads, h, V_SLOTS)
            dmt[h] = padded
            dm[h * count : (h + 1) * count] = padded.T
        dq[...] = jnp.zeros_like(dq)

        def step(at, size, masked, inner):
            span = pl.ds(at, size)
            keys = kv[span, 0:256]
            values = kv[span, 128:384]
            turned = keys.T
            mask = keys_in(at, size, low, high) if masked else None
            probs, slopes = [], []
            for h in range(GROUP):
                weights = jnp.exp(dot(keys, qmt[h]) - levels[h])
                if masked:
                    weights = jnp.where(mask, weights, 0.0)
                slope = (weights * (dot(values, dmt[h]) - deltas[h])).astype(jnp.bfloat16)
                dq[h] += dot(turned[h * HEAD : (h + 1) * HEAD], slope)
                probs.append(weights.astype(jnp.bfloat16))
                slopes.append(slope)
            dv = dot(jnp.concatenate(probs, axis=1), dm[...])
            dk = dot(jnp.concatenate(slopes, axis=1), qm[...])
            acc[span, 0:128] += dk[:, :128]
            acc[span, 128:256] += dk[:, 128:] + dv[:, :128]
            acc[span, 256:384] += dv[:, 128:]
            return inner

        walk(big, begin, end, low, high, step, 0)
        for h in range(GROUP):
            dqs[s, h * HEAD : (h + 1) * HEAD] = dq[h] * 0.125
        return carry

    lax.fori_loop(0, ZN // 2, functools.partial(one_block, True), 0)
    lax.fori_loop(ZN // 2, ZN, functools.partial(one_block, False), 0)
    half = HEAD // 2
    for b in range(ZN):
        back = pick([jnp.full_like(slots[b], s) for s in range(ZN)], slots[b], [dqs[s] for s in range(ZN)])
        for h in range(GROUP):
            at = h * HEAD
            w1, w2 = back[at : at + half], back[at + half : at + HEAD]
            dq_out[b, at : at + half] = (w1 * cosine[b] + w2 * sine[b]).astype(dq_out.dtype)
            dq_out[b, at + half : at + HEAD] = (w2 * cosine[b] - w1 * sine[b]).astype(dq_out.dtype)

    def finish(tile, carry):
        span = pl.ds(pl.multiple_of(tile * TILE, TILE), TILE)
        dkv_out[span, :] = acc[span, :].astype(dkv_out.dtype)
        return carry

    lax.fori_loop(0, tiles, finish, 0)


def attend_back(lengths, qt, kv, out, lse, dots, cosine, sine):
    blocks, rows, count = qt.shape
    whole = pl.BlockSpec(memory_space=pltpu.VMEM)
    return pl.pallas_call(
        backward_kernel,
        out_shape=[
            jax.ShapeDtypeStruct(qt.shape, jnp.bfloat16),
            jax.ShapeDtypeStruct(kv.shape, jnp.bfloat16),
        ],
        in_specs=[pl.BlockSpec(memory_space=pltpu.SMEM)] + [whole] * 7,
        out_specs=[whole] * 2,
        scratch_shapes=[
            pltpu.VMEM((GROUP, 256, count), jnp.bfloat16),
            pltpu.VMEM((GROUP * count, 256), jnp.bfloat16),
            pltpu.VMEM((GROUP, 256, count), jnp.bfloat16),
            pltpu.VMEM((GROUP * count, 256), jnp.bfloat16),
            pltpu.VMEM((GROUP, HEAD, count), jnp.float32),
            pltpu.VMEM(kv.shape, jnp.float32),
            pltpu.VMEM(qt.shape, jnp.bfloat16),
            pltpu.VMEM(qt.shape, jnp.bfloat16),
            pltpu.VMEM((blocks, 8, count), jnp.float32),
            pltpu.VMEM((blocks, 8, count), jnp.float32),
            pltpu.VMEM(qt.shape, jnp.float32),
        ],
        compiler_params=pltpu.CompilerParams(vmem_limit_bytes=67043328),
    )(lengths, qt, kv, out, lse, dots, cosine, sine)


KV_SLOTS = (0, 1, 2, 5, 3, 4)


def turn(rows, cosine, sine):
    first, second = rows[:, 0], rows[:, 1]
    return jnp.stack([first * cosine - second * sine, second * cosine + first * sine], axis=1)


def turn_back(rows, cosine, sine):
    first, second = rows[:, 0], rows[:, 1]
    return jnp.stack([first * cosine + second * sine, second * cosine - first * sine], axis=1)


def tables(lengths, first, count):
    starts = jnp.cumsum(lengths) - lengths
    position = first[:, None] + jnp.arange(count, dtype=jnp.int32)[None, :]
    begun = position[..., None] >= starts
    offsets = position - jnp.max(jnp.where(begun, starts, 0), axis=-1)
    half = HEAD // 2
    frequency = rope_base ** (-(jnp.arange(half, dtype=jnp.float32) * 2.0) / HEAD)
    angles = offsets.astype(jnp.float32)[:, None, :] * frequency[None, :, None]
    return jnp.cos(angles), jnp.sin(angles)


def norm_back(upstream, scaled, inv_std, gain_vec):
    weighted = upstream * gain_vec
    inner = (
        weighted
        - jnp.mean(weighted, axis=-1, keepdims=True)
        - scaled * jnp.mean(weighted * scaled, axis=-1, keepdims=True)
    )
    sums = [jnp.sum(upstream * scaled, axis=0, keepdims=True), jnp.sum(upstream, axis=0, keepdims=True)]
    return inv_std * inner, sums


def contract(left, right, dims):
    return lax.dot_general(left, right, (dims, ((), ())), preferred_element_type=jnp.float32)


def copies_kernel(*refs):
    n = len(refs) // 3
    ins, outs, bufs, sems = refs[:n], refs[n : 2 * n], refs[2 * n : 3 * n], refs[3 * n]
    loads = [pltpu.make_async_copy(ins[k], bufs[k], sems.at[k]) for k in range(n)]
    stores = [pltpu.make_async_copy(bufs[k], outs[k], sems.at[n + k]) for k in range(n)]
    for load in loads:
        load.start()
    for load, store in zip(loads, stores):
        load.wait()
        store.start()
    for store in stores:
        store.wait()


def copies(arrays):
    n = len(arrays)
    anywhere = pl.BlockSpec(memory_space=pl.ANY)
    return pl.pallas_call(
        copies_kernel,
        out_shape=[jax.ShapeDtypeStruct(a.shape, a.dtype) for a in arrays],
        in_specs=[anywhere] * n,
        out_specs=[anywhere] * n,
        scratch_shapes=[pltpu.VMEM(a.shape, a.dtype) for a in arrays] + [pltpu.SemaphoreType.DMA((2 * n,))],
    )(*arrays)


def local_grid(
    tokens,
    qkv_weight,
    out_weight,
    gate_weight,
    up_weight,
    down_weight,
    first_gain,
    first_bias,
    second_gain,
    second_bias,
    lengths,
    cotangent,
):
    bf16 = jnp.bfloat16
    rows, width = tokens.shape
    share = first_gain.shape[0]
    heads = width // HEAD
    half = HEAD // 2
    x, y, z, c = place()
    spots = [(px, py, pz, pc) for pz in range(ZN) for py in range(YN) for pc in range(CN) for px in range(XN)]
    over_x = [(block(*p), block(1 - p[0], *p[1:])) for p in spots]
    over_y = [(block(*p), block(p[0], 1 - p[1], *p[2:])) for p in spots]
    small = jnp.stack([first_gain, first_bias, second_gain, second_bias])
    small = jnp.pad(small, ((0, 4), (0, 128 - share)))
    hidden_width = gate_weight.shape[1]

    (qkv_blocks,) = gather([qkv_weight], [BCAST], 1)
    qkv_full = qkv_blocks.reshape(width, 3 * width)
    turned = jnp.stack([block(x, y, b, c) for b in range(ZN)]) * rows
    cos_all, sin_all = tables(lengths, turned, rows)
    cosine = lax.dynamic_index_in_dim(cos_all, z, 0, keepdims=False)
    sine = lax.dynamic_index_in_dim(sin_all, z, 0, keepdims=False)

    raw = contract(qkv_full, tokens, ((0,), (1,))).astype(bf16)
    raw = raw.reshape(3, heads, 2, half, rows)
    queries = turn(raw[0].astype(jnp.float32), cosine, sine).astype(bf16)
    keys = turn(raw[1].astype(jnp.float32), cosine, sine).astype(bf16)
    queries = queries.reshape(ZN, GROUP * HEAD, rows)
    pairs = jnp.concatenate(
        [keys.reshape(ZN, GROUP, HEAD, rows), raw[2].reshape(ZN, GROUP, HEAD, rows)], axis=1
    )
    pairs = jnp.concatenate([pairs[:, s : s + 1] for s in KV_SLOTS], axis=1)
    pairs = jnp.swapaxes(pairs.reshape(ZN, 2 * GROUP * HEAD, rows), 1, 2)

    pairs_all, queries, out_full, down_full, small, gate_part, up_part = gather(
        [pairs, queries, out_weight, down_weight, small, gate_weight, up_weight],
        [CROSS, SWAP, BCAST, BCAST, BCAST, BY_X, BY_Y],
        2,
    )
    out_full = out_full.reshape(width, width)
    gate_rest = lax.ppermute(gate_part, ("cp", "hd"), over_y)
    up_rest = lax.ppermute(up_part, ("cp", "hd"), over_x)
    down_full = down_full.reshape(hidden_width, width)
    small = jnp.swapaxes(small[:, :4, :share], 0, 1).astype(jnp.float32).reshape(4, width)
    small = lax.optimization_barrier(small)
    gain_one, bias_one, gain_two, bias_two = [small[i] for i in range(4)]
    pairs_all = pairs_all.reshape(-1, 2 * GROUP * HEAD)
    low, attended, lse = attend(lengths, queries, pairs_all)
    low, gate_full, up_full = gather(
        [low, (gate_part, gate_rest), (up_part, up_rest)], [SWAP, REST_Y, REST_X], 3
    )
    gate_full = gate_full.reshape(width, hidden_width)
    up_full = up_full.reshape(width, hidden_width)
    low = low.reshape(width, rows)

    attn_out = contract(low, out_full, ((0,), (0,)))
    first, scaled_one, inv_one = normalize(tokens.astype(jnp.float32) + attn_out, gain_one, bias_one)
    first_low = first.astype(bf16)
    gate_proj = product(first_low, gate_full)
    up_proj = product(first_low, up_full)
    sigmoid_gate = jax.nn.sigmoid(gate_proj)
    silu_gate = gate_proj * sigmoid_gate
    hidden = (silu_gate * up_proj).astype(bf16)
    branch = product(hidden, down_full)
    second, scaled_two, inv_two = normalize(first + branch, gain_two, bias_two)
    layer_out = second.astype(bf16)

    upstream = cotangent.astype(jnp.float32)
    dz_two, sums_two = norm_back(upstream, scaled_two, inv_two, gain_two)
    dz_two_low = dz_two.astype(bf16)
    hidden_grad = contract(dz_two_low, down_full, ((1,), (1,)))
    gate_back = (
        hidden_grad * up_proj * sigmoid_gate * (1.0 + gate_proj * (1.0 - sigmoid_gate))
    ).astype(bf16)
    up_back = (hidden_grad * silu_gate).astype(bf16)
    gate_sum = contract(first_low, gate_back, ((0,), (0,))).astype(bf16)
    up_sum = contract(first_low, up_back, ((0,), (0,))).astype(bf16)
    first_back = (
        dz_two + contract(gate_back, gate_full, ((1,), (1,))) + contract(up_back, up_full, ((1,), (1,)))
    )
    dz_one, sums_one = norm_back(first_back, scaled_one, inv_one, gain_one)
    dz_one_low = dz_one.astype(bf16)
    attended_back = contract(out_full, dz_one_low, ((1,), (1,))).astype(bf16)
    gate_sum = gate_sum.reshape((BLOCKS,) + gate_weight.shape)
    up_sum = up_sum.reshape((BLOCKS,) + up_weight.shape)
    attended_back, gate_send, up_send = reduce(
        [attended_back.reshape(ZN, GROUP * HEAD, rows), gate_sum, up_sum], [SWAP, PAIR_Y, PAIR_X], 4
    )
    gate_rest = lax.ppermute(gate_send, ("cp", "hd"), over_y)
    up_rest = lax.ppermute(up_send, ("cp", "hd"), over_x)

    query_back, pair_back = attend_back(
        lengths, queries, pairs_all, attended, lse, attended_back, cos_all, sin_all
    )
    small_sum = lax.optimization_barrier(jnp.concatenate(sums_one + sums_two, axis=0))
    small_sum = jnp.swapaxes(small_sum.reshape(4, BLOCKS, share), 0, 1)
    small_sum = jnp.pad(small_sum, ((0, 0), (0, 4), (0, 128 - share)))
    pair_back, query_back, out_grad, down_grad, small_grad, gate_grad, up_grad = reduce(
        [
            pair_back.reshape(BLOCKS, rows, 2 * GROUP * HEAD),
            query_back,
            (low, dz_one_low),
            (hidden, dz_two_low),
            small_sum,
            (gate_sum, gate_rest),
            (up_sum, up_rest),
        ],
        [CROSS, SWAP, PRODUCT, TURNED_PRODUCT, REDUCE, REST_Y, REST_X],
        5,
    )
    pair_back = jnp.swapaxes(pair_back, 1, 2).reshape(ZN, 2 * GROUP, HEAD, rows)
    pair_back = [pair_back[:, KV_SLOTS.index(s)] for s in range(2 * GROUP)]
    key_back = jnp.stack(pair_back[:GROUP], axis=1).reshape(heads, 2, half, rows)
    key_back = turn_back(key_back.astype(jnp.float32), cosine, sine).astype(bf16)
    value_back = jnp.stack(pair_back[GROUP:], axis=1)
    raw_back = jnp.concatenate(
        [
            query_back.reshape(width, rows),
            key_back.reshape(width, rows),
            value_back.reshape(width, rows),
        ],
        axis=0,
    )
    qkv_sum = contract(tokens, raw_back, ((0,), (1,))).astype(bf16)
    tokens_grad = (dz_one + contract(raw_back, qkv_full, ((0,), (1,)))).astype(bf16)
    (qkv_grad,) = reduce([qkv_sum.reshape(BLOCKS, share, 3 * width)], [REDUCE], 6)
    qkv_grad, out_grad, gate_grad, up_grad, down_grad = copies([qkv_grad, out_grad, gate_grad, up_grad, down_grad])
    return (
        layer_out,
        tokens_grad,
        qkv_grad,
        out_grad,
        gate_grad,
        up_grad,
        down_grad,
        small_grad[0, :share],
        small_grad[1, :share],
        small_grad[2, :share],
        small_grad[3, :share],
    )


def solution(mesh):
    rows = P(("cp", "hd"), None)
    line = P(("cp", "hd"))
    local = local_grid if (mesh.shape["cp"], mesh.shape["hd"]) == (ZN * YN * CN, XN) else local_any
    return jax.shard_map(
        local,
        mesh=mesh,
        in_specs=(rows,) * 6 + (line,) * 4 + (P(), rows),
        out_specs=(rows,) * 7 + (line,) * 4,
        check_vma=False,
    )
```
